32 devices in a mesh: rep: 4 (over y, core), ep: 8 (over z, x).
Axes of the slice: x: 2, y: 2, z: 4, core: 2. Of those that a mesh axis runs over, the one named last changes fastest.
Arguments:
- tokens: bfloat16 [5120, 2048], P(('rep', 'ep')), may hold values from -6 to 6
- cotangent: bfloat16 [5120, 2048], P(('rep', 'ep')), may hold values from -6 to 6
- seq_lengths: int32 [4, 4], P('rep'), may hold values from 1 to 1024, 1120 in all within a row
- token_order: int32 [4, 1280], P('rep'), may hold values from 0 to 1279, each once within a row
- routes: int32 [5120, 8], P(('rep', 'ep')), may hold values from 0 to 15, as said below
- slot_index: int32 [5120, 8], P(('rep', 'ep')), may hold values from 0 to 100, as said below
- query_weight: bfloat16 [2048, 2048], P('ep'), may hold values from -0.125 to 0.125
- key_weight: bfloat16 [2048, 2048], P('ep'), may hold values from -0.125 to 0.125
- value_weight: bfloat16 [2048, 2048], P('ep'), may hold values from -0.125 to 0.125
- output_weight: bfloat16 [2048, 2048], P('ep'), may hold values from -1 to 1
- router_weight: bfloat16 [2048, 16], P('ep'), may hold values from -0.0625 to 0.0625
- prenorm_gain: float32 [2048], replicated, may hold values from 0.5 to 1.5
- querynorm_gain: float32 [128], replicated, may hold values from 0.6 to 1.4
- keynorm_gain: float32 [128], replicated, may hold values from 0.6 to 1.4
- postnorm_gain: float32 [2048], replicated, may hold values from 0.5 to 1.5
- gate_weight: bfloat16 [16, 2048, 1024], P('ep'), may hold values from -0.125 to 0.125
- up_weight: bfloat16 [16, 2048, 1024], P('ep'), may hold values from -0.125 to 0.125
- down_weight: bfloat16 [16, 1024, 2048], P('ep'), may hold values from -0.75 to 0.75
Outputs:
- layer_out: bfloat16 [5120, 2048], P(('rep', 'ep'))
- token_grad: float32 [5120, 2048], P(('rep', 'ep'))
- query_grad: float32 [2048, 2048], P('ep')
- key_grad: float32 [2048, 2048], P('ep')
- value_grad: float32 [2048, 2048], P('ep')
- output_grad: float32 [2048, 2048], P('ep')
- router_grad: float32 [2048, 16], P('ep')
- prenorm_grad: float32 [2048], P('ep')
- querynorm_grad: float32 [128], P('ep')
- keynorm_grad: float32 [128], P('ep')
- postnorm_grad: float32 [2048], P('ep')
- gate_grad: float32 [16, 2048, 1024], P('ep', 'rep')
- up_grad: float32 [16, 2048, 1024], P('ep', 'rep')
- down_grad: float32 [16, 1024, 2048], P('ep', 'rep')
The draws below stay inside these ranges and needn't reach their ends.
Inputs may be any that keep to these rules, and one draw needn't show every extreme that they name: `seq_lengths`: each group's 4 lengths sum to 1120, the largest is exactly 1024; group positions 1120 to 1279 are padding. `token_order`: each row is a permutation of the group positions 0 to 1279. `routes`: the 8 experts of a row are distinct; among the rows of each device some expert is named by more than 100 rows. `slot_index`: within the rows of one device, the pairs that name one expert carry 0, 1, 2, ... in row order; counts from 100 on are stored as 100, and those pairs are dropped.
All inputs are finite; a program needn't handle non-finite values.
Results may differ from the reference program's by a relative error of at most 0.025.
Values may be sent and summed in bfloat16 or wider, within the bound.
No kernel may reach another device: no remote copies, remote signals or barrier semaphores. Data moves between devices by JAX's collectives and lax.ppermute only.
A program may use at most 448 MiB of HBM per device.

```python
import math
import jax
import jax.numpy as jnp
import numpy as np
from jax import lax

D = 2048
H = 16
HD = 128
F = 1024
TOP = 8
TOK_DEV = 160
EXPERTS = 16
CAP = 100
GROUP_TOK = 1280
LIVE = 1120
SEQS = 4
MAXLEN = 1024
TOKENS = 5120
N_REP = 4
N_EP = 8


def route_draw(key):
    base_key = jax.random.fold_in(key, 11)
    score_key, bias_key, hot_key = jax.random.split(base_key, 3)
    random_part = jax.random.randint(score_key, (TOKENS, EXPERTS), 0, 65536)
    expert_lift = jax.random.randint(bias_key, (EXPERTS,), 0, 4) * 16384
    block_count = TOKENS // TOK_DEV
    hot_expert = jax.random.randint(hot_key, (block_count,), 0, EXPERTS)
    block_row = jnp.arange(TOKENS, dtype=jnp.int32) % TOK_DEV
    hot_rows = jnp.repeat(hot_expert, TOK_DEV)
    expert_ids = jnp.arange(EXPERTS, dtype=jnp.int32)
    forced = (block_row[:, None] <= CAP) & (expert_ids[None, :] == hot_rows[:, None])
    scores = (random_part + expert_lift[None, :]) * 2 + forced.astype(jnp.int32) * 1048576
    distinct = scores * EXPERTS + expert_ids[None, :]
    top_values, chosen = lax.top_k(distinct, TOP)
    return chosen.astype(jnp.int32)


def draw_routes(key, part):
    return route_draw(key)


def draw_slot_index(key, part):
    chosen = route_draw(key)
    blocks = chosen.reshape(TOKENS // TOK_DEV, TOK_DEV, TOP)
    expert_ids = jnp.arange(EXPERTS, dtype=jnp.int32)
    counts = jnp.sum((blocks[..., None] == expert_ids).astype(jnp.int32), axis=2)
    before = jnp.cumsum(counts, axis=1) - counts
    slot_values = jnp.take_along_axis(before, blocks, axis=2)
    return jnp.minimum(slot_values, CAP).reshape(TOKENS, TOP).astype(jnp.int32)


def level_of(stream_key, extent, cuts, smallest, high):
    gain, own = 1.0, jax.random.fold_in(stream_key, 6)
    for dim, parts in cuts:
        steps = jnp.exp(jax.random.uniform(jax.random.fold_in(own, dim), (parts,), jnp.float32, smallest / len(cuts), high / len(cuts)))
        gain = gain * jnp.repeat(steps, extent[dim] // parts).reshape([-1 if axis == dim else 1 for axis in range(len(extent))])
    return gain


def split_up(amount, total, bound, skew):
    weights = [(1 << 20) // math.isqrt(grade ** skew) + 1 for grade in range(2, amount + 1)]
    rest, holding = total - bound - (amount - 1), [1] * (amount - 1)
    while rest > 0:
        movable = [i for i in range(amount - 1) if holding[i] < bound]
        mass, remaining = sum([weights[i] for i in movable]), rest
        for i in movable:
            extra = min(bound - holding[i], max(1, remaining * weights[i] // mass), rest)
            holding[i] = holding[i] + extra
            rest = rest - extra
    return np.array([bound] + holding)


def uneven(own_key, count, total, limit, slope):
    if count == 2:
        one = jax.random.randint(own_key, (), max(1, total - limit), min(limit, total - 1) + 1)
        return jnp.stack([one, total - one])
    tallies = jnp.asarray(split_up(count, total, limit, slope), jnp.int32)
    twos = (count - 1) // 2
    giver, taker = tallies[1:1 + 2 * twos:2], tallies[2:2 + 2 * twos:2]
    margin = jnp.minimum(giver - 1, limit - taker)
    shifted = jax.random.randint(jax.random.fold_in(own_key, 1), (twos,), 0, 1 << 20) % (margin + 1)
    tallies = tallies.at[1:1 + 2 * twos:2].set(giver - shifted).at[2:2 + 2 * twos:2].set(taker + shifted)
    return tallies[jax.random.permutation(jax.random.fold_in(own_key, 2), count)]


def gaussian(stream_key, shape, scale, bound, pieces=(), kind=jnp.bfloat16):
    values = jax.random.normal(stream_key, shape, jnp.float32) * scale
    if len(pieces) > 0:
        values = level_of(stream_key, shape, pieces, -0.22, 0.18) * values
    return jnp.clip(values, min=-bound, max=bound).astype(kind)


def setup_inputs(seed: int = 0) -> dict:
    splits = jax.random.split(jax.random.key(seed), 19)
    tokens = gaussian(splits[0], (TOKENS, D), 1.0, 6.0, ((0, 32),))
    cotangent = gaussian(splits[1], (TOKENS, D), 1.0, 6.0, ((0, 32),))
    seq_lengths = jax.vmap(lambda own: uneven(own, SEQS, LIVE, MAXLEN, 1))(jax.random.split(splits[2], N_REP)).reshape((N_REP, SEQS)).astype(jnp.int32)
    token_order = jax.vmap(lambda own: jax.random.permutation(own, GROUP_TOK))(jax.random.split(splits[3], N_REP)).reshape((N_REP, GROUP_TOK)).astype(jnp.int32)
    routes = draw_routes(jax.random.fold_in(splits[18], 71), 0)
    slot_index = draw_slot_index(jax.random.fold_in(splits[18], 71), 0)
    query_weight = gaussian(splits[6], (D, D), D ** -0.5, 0.125, ((0, 8),))
    key_weight = gaussian(splits[7], (D, D), D ** -0.5, 0.125, ((0, 8),))
    value_weight = gaussian(splits[8], (D, D), D ** -0.5, 0.125, ((0, 8),))
    output_weight = gaussian(splits[9], (D, D), (D // 64) ** -0.5, 1.0, ((0, 8),))
    router_weight = gaussian(splits[10], (D, EXPERTS), (4 * D) ** -0.5, 0.0625, ((0, 8),))
    prenorm_gain = jnp.clip(jax.random.uniform(splits[11], (D,), jnp.float32, 0.5, 1.5), 0.5, 1.5)
    querynorm_gain = jnp.clip(jax.random.uniform(splits[12], (HD,), jnp.float32, 0.6, 1.4), 0.6, 1.4)
    keynorm_gain = jnp.clip(jax.random.uniform(splits[13], (HD,), jnp.float32, 0.6, 1.4), 0.6, 1.4)
    postnorm_gain = jnp.clip(jax.random.uniform(splits[14], (D,), jnp.float32, 0.5, 1.5), 0.5, 1.5)
    gate_weight = gaussian(splits[15], (EXPERTS, D, F), D ** -0.5, 0.125, ((0, 8),))
    up_weight = gaussian(splits[16], (EXPERTS, D, F), D ** -0.5, 0.125, ((0, 8),))
    down_weight = gaussian(splits[17], (EXPERTS, F, D), (F // 16) ** -0.5, 0.75, ((0, 8),))
    return dict(tokens=tokens, cotangent=cotangent, seq_lengths=seq_lengths, token_order=token_order, routes=routes, slot_index=slot_index, query_weight=query_weight, key_weight=key_weight, value_weight=value_weight, output_weight=output_weight, router_weight=router_weight, prenorm_gain=prenorm_gain, querynorm_gain=querynorm_gain, keynorm_gain=keynorm_gain, postnorm_gain=postnorm_gain, gate_weight=gate_weight, up_weight=up_weight, down_weight=down_weight)


highest = lax.Precision.HIGHEST
epsilon = 1e-05
rope_base = 10000.0
masked_value = -1e+30

@jax.custom_vjp
def low(v):
    return lax.optimization_barrier(v.astype(jnp.bfloat16)).astype(jnp.float32)

@jax.custom_vjp
def low_back(v):
    return v

def low_keep(v):
    return (low(v), None)

def low_pass(kept, grad):
    return (grad,)

def back_keep(v):
    return (v, None)

def back_low(kept, grad):
    return (low(grad),)
low.defvjp(low_keep, low_pass)
low_back.defvjp(back_keep, back_low)

def matmul(left_side, right_side):
    return jnp.dot(left_side, right_side, precision=highest)

def root_norm(values, gain_vector):
    inverse = lax.rsqrt(lax.optimization_barrier(jnp.mean(values * values, axis=-1, keepdims=True)) + epsilon)
    return values * inverse * gain_vector

def rope_tables(position, dimension):
    halfway = dimension // 2
    indices = jnp.arange(halfway, dtype=jnp.float32)
    frequency = rope_base ** (-2.0 * indices / dimension)
    angles = position.astype(jnp.float32)[:, None] * frequency[None, :]
    cosine = jnp.cos(angles)
    sine_part = jnp.sin(angles)
    return (jnp.concatenate([cosine, cosine], axis=-1)[:, None, :], jnp.concatenate([sine_part, sine_part], axis=-1)[:, None, :])

def turn_half(values):
    halfway = values.shape[-1] // 2
    return jnp.concatenate([-values[..., halfway:], values[..., :halfway]], axis=-1)

def rotate(values, cosine, sine_part):
    return values * cosine + turn_half(values) * sine_part

def row_meta(lengths, group_order):
    boundary = jnp.cumsum(lengths).astype(jnp.int32)
    passed = (group_order[:, None] >= boundary[None, :]).astype(jnp.int32)
    segment = lax.optimization_barrier(jnp.sum(passed, axis=1)).astype(jnp.int32)
    offset = lax.optimization_barrier(jnp.sum(passed * lengths[None, :], axis=1)).astype(jnp.int32)
    return (segment, (group_order - offset).astype(jnp.int32))

def group_layer(params, group_tokens, lengths, group_order, group_routes, group_slots):
    query_weight, key_weight, value_weight, output_weight, router_weight, prenorm_gain, querynorm_gain, keynorm_gain, postnorm_gain, gate_weight, up_weight, down_weight = params
    segment, position = row_meta(lengths, group_order)
    valid_rows = (segment < SEQS).astype(jnp.float32)[:, None]
    first_input = low(root_norm(group_tokens, prenorm_gain))
    query_raw = low_back(matmul(first_input, query_weight)).reshape(GROUP_TOK, H, HD)
    key_raw = low_back(matmul(first_input, key_weight)).reshape(GROUP_TOK, H, HD)
    value_low = low(low_back(matmul(first_input, value_weight))).reshape(GROUP_TOK, H, HD)
    cosine, sine_part = rope_tables(position, HD)
    query_low = low(rotate(root_norm(query_raw, querynorm_gain), cosine, sine_part))
    key_low = low(rotate(root_norm(key_raw, keynorm_gain), cosine, sine_part))
    pair_count = H // 2

    def split_pairs(values):
        return values.reshape(GROUP_TOK, pair_count, 2, HD).transpose(1, 0, 2, 3)
    allowed = segment[:, None] == segment[None, :]

    def attend(item):
        query_pair, key_pair, value_pair = item
        scores = low_back(jnp.einsum('qhd,khd->hqk', query_pair, key_pair, precision=highest) * HD ** (-0.5))
        scores = jnp.where(allowed[None], scores, masked_value)
        weights_low = low(jax.nn.softmax(scores, axis=-1))
        return jnp.einsum('hqk,khd->qhd', weights_low, value_pair, precision=highest)
    mixed_pairs = lax.map(jax.checkpoint(attend), (split_pairs(query_low), split_pairs(key_low), split_pairs(value_low)))
    mixed_heads = low(low_back(mixed_pairs.transpose(1, 0, 2, 3).reshape(GROUP_TOK, D)))
    residual = group_tokens + low_back(matmul(mixed_heads, output_weight))
    second_input = low(root_norm(residual, postnorm_gain))
    logits = low_back(matmul(second_input, router_weight))
    gates_low = low(jax.nn.softmax(jnp.take_along_axis(logits, group_routes, axis=1), axis=-1))
    slot_total = EXPERTS * CAP
    kept_pair = group_slots < CAP
    flat_slot = (group_routes * CAP + jnp.minimum(group_slots, CAP - 1)).astype(jnp.int32)
    slot_ids = jnp.arange(slot_total, dtype=jnp.int32)

    def tables(flat_device, kept_device, gates_device):
        spread = jnp.zeros((TOK_DEV, slot_total), jnp.float32)
        weighted = jnp.zeros((TOK_DEV, slot_total), jnp.float32)
        for column in range(TOP):
            matching = ((flat_device[:, column, None] == slot_ids[None, :]) & kept_device[:, column, None]).astype(jnp.float32)
            spread = spread + matching
            weighted = weighted + matching * gates_device[:, column, None]
        return (spread, weighted)
    spread, weighted = jax.vmap(tables)(flat_slot.reshape(N_EP, TOK_DEV, TOP), kept_pair.reshape(N_EP, TOK_DEV, TOP), gates_low.reshape(N_EP, TOK_DEV, TOP))
    device_input = second_input.reshape(N_EP, TOK_DEV, D)
    buffer = low_back(jnp.einsum('ntf,ntd->nfd', spread, device_input, precision=highest)).reshape(N_EP, EXPERTS, CAP, D)
    gate_linear = low_back(jnp.einsum('necd,edf->necf', buffer, gate_weight, precision=highest))
    up_linear = low_back(jnp.einsum('necd,edf->necf', buffer, up_weight, precision=highest))
    inner = low(jax.nn.silu(gate_linear) * up_linear)
    returned = low(low_back(jnp.einsum('necf,efd->necd', inner, down_weight, precision=highest))).reshape(N_EP, slot_total, D)
    mixture = jnp.einsum('ntf,nfd->ntd', weighted, returned, precision=highest).reshape(GROUP_TOK, D)
    return valid_rows * (residual + mixture)

def reference(tokens, cotangent, seq_lengths, token_order, routes, slot_index, query_weight, key_weight, value_weight, output_weight, router_weight, prenorm_gain, querynorm_gain, keynorm_gain, postnorm_gain, gate_weight, up_weight, down_weight):
    params = tuple((item.astype(jnp.float32) for item in (query_weight, key_weight, value_weight, output_weight, router_weight, prenorm_gain, querynorm_gain, keynorm_gain, postnorm_gain, gate_weight, up_weight, down_weight)))
    grouped = tokens.astype(jnp.float32).reshape(N_REP, GROUP_TOK, D)
    routes_grouped = routes.reshape(N_REP, GROUP_TOK, TOP)
    slots_grouped = slot_index.reshape(N_REP, GROUP_TOK, TOP)

    def forward(weights_all, inputs_all):

        def one_group(item):
            return group_layer(weights_all, item[0], item[1], item[2], item[3], item[4])
        return lax.map(jax.checkpoint(one_group), (inputs_all, seq_lengths, token_order, routes_grouped, slots_grouped))
    outputs, pullback = jax.vjp(forward, params, grouped)
    weight_grads, input_grads = pullback(cotangent.astype(jnp.float32).reshape(N_REP, GROUP_TOK, D))
    query_grad, key_grad, value_grad, output_grad, router_grad, prenorm_grad, querynorm_grad, keynorm_grad, postnorm_grad, gate_grad, up_grad, down_grad = weight_grads
    layer_out = outputs.reshape(TOKENS, D).astype(jnp.bfloat16)
    token_grad = input_grads.reshape(TOKENS, D)
    return (layer_out, token_grad, query_grad, key_grad, value_grad, output_grad, router_grad, prenorm_grad, querynorm_grad, keynorm_grad, postnorm_grad, gate_grad, up_grad, down_grad)
```

```python
import jax
import jax.numpy as jnp
from jax import lax
from jax.sharding import PartitionSpec as P

epsilon = 1e-05
rope_base = 10000.0
masked_value = -1e30
low_type = jnp.bfloat16
wide_type = jnp.float32


def inverse_rms(values):
    return lax.rsqrt(jnp.mean(values * values, axis=-1, keepdims=True) + epsilon)


def norm_backward(values, inverse, gain_vector, upstream):
    scaled = upstream * gain_vector
    inner_mean = jnp.mean(scaled * values, axis=-1, keepdims=True)
    result = inverse * scaled - values * (inverse * inverse * inverse) * inner_mean
    return (result, upstream * values * inverse)


def rope_tables(position, dimension):
    halfway = dimension // 2
    indices = jnp.arange(halfway, dtype=wide_type)
    frequency = rope_base ** (-2.0 * indices / dimension)
    angles = position.astype(wide_type)[:, None] * frequency[None, :]
    cosine = jnp.cos(angles)
    sine_part = jnp.sin(angles)
    return (
        jnp.concatenate([cosine, cosine], axis=-1),
        jnp.concatenate([sine_part, sine_part], axis=-1),
    )


def turn_half(values):
    halfway = values.shape[-1] // 2
    return jnp.concatenate([-values[..., halfway:], values[..., :halfway]], axis=-1)


def turn_back(values):
    halfway = values.shape[-1] // 2
    return jnp.concatenate([values[..., halfway:], -values[..., :halfway]], axis=-1)


def row_meta(lengths, group_order):
    boundary = jnp.cumsum(lengths)
    passed = (group_order[:, None] >= boundary[None, :]).astype(jnp.int32)
    segment = jnp.sum(passed, axis=1)
    offset = jnp.sum(passed * lengths[None, :], axis=1)
    return (segment, group_order - offset)


def mm(left, right, left_dim, right_dim):
    return lax.dot_general(
        left,
        right,
        (((left_dim,), (right_dim,)), ((), ())),
        preferred_element_type=wide_type,
    )


def gather_rows(values):
    return lax.all_gather(values, "ep", axis=0, tiled=True)


def scatter_rows(values):
    return lax.psum_scatter(
        values.astype(low_type), "ep", scatter_dimension=0, tiled=True
    ).astype(wide_type)


def body(
    tokens,
    cotangent,
    seq_lengths,
    token_order,
    routes,
    slot_index,
    query_weight,
    key_weight,
    value_weight,
    output_weight,
    router_weight,
    prenorm_gain,
    querynorm_gain,
    keynorm_gain,
    postnorm_gain,
    gate_weight,
    up_weight,
    down_weight,
):
    group_count = lax.axis_size("ep")
    device = lax.axis_index("ep")
    row_count, model_width = tokens.shape
    head_dim = querynorm_gain.shape[0]
    width_here = model_width // group_count
    heads_here = width_here // head_dim
    experts_here = gate_weight.shape[0]
    expert_total = experts_here * group_count
    top_count = routes.shape[1]
    capacity = row_count * top_count * 5 // (4 * expert_total)
    group_rows = row_count * group_count
    sequence_count = seq_lengths.shape[1]
    score_scale = head_dim ** (-0.5)

    segment, position = row_meta(seq_lengths[0], token_order[0])
    segment_own = lax.dynamic_slice_in_dim(segment, device * row_count, row_count)
    valid_own = (segment_own < sequence_count).astype(wide_type)[:, None]
    valid_all = (segment < sequence_count).astype(wide_type)[:, None]

    expert_ids = jnp.arange(expert_total, dtype=jnp.int32)
    route_code = jnp.zeros((row_count, expert_total), jnp.int32)
    for column in range(top_count):
        hit = routes[:, column, None] == expert_ids[None, :]
        kept = (slot_index[:, column, None] < capacity).astype(jnp.int32)
        route_code = route_code + jnp.where(hit, 1 + kept, 0)
    small_sent = jnp.concatenate([route_code.astype(low_type), router_weight], axis=0)

    token_all = gather_rows(tokens)
    projections = jnp.concatenate(
        [
            piece.reshape(width_here, group_count, width_here)
            for piece in (query_weight, key_weight, value_weight)
        ],
        axis=2,
    ).transpose(1, 0, 2)
    head_weight = lax.all_to_all(
        projections, "ep", split_axis=0, concat_axis=0, tiled=True
    ).reshape(model_width, 3 * width_here)
    small_all = gather_rows(small_sent).reshape(
        group_count, row_count + width_here, expert_total
    )
    code_all = small_all[:, :row_count].reshape(group_rows, expert_total)
    full_router = small_all[:, row_count:].reshape(model_width, expert_total)
    cot_all = gather_rows(cotangent)

    token_wide = token_all.astype(wide_type)
    inverse_all = inverse_rms(token_wide)
    first_all = (token_wide * inverse_all * prenorm_gain).astype(low_type)
    raw = mm(first_all, head_weight, 1, 0)
    cosine, sine_part = rope_tables(position, head_dim)

    up_stream = [mm(cot_all, down_weight[e], 1, 1) for e in range(experts_here)]

    allowed = segment[:, None] == segment[None, :]

    def head_columns(values, block, head):
        start = block * width_here + head * head_dim
        return values[:, start : start + head_dim]

    kept_heads = []
    mixed_parts = []
    for head in range(heads_here):
        query_raw = head_columns(raw, 0, head)
        key_raw = head_columns(raw, 1, head)
        query_inverse = inverse_rms(query_raw)
        key_inverse = inverse_rms(key_raw)
        query_normed = query_raw * query_inverse * querynorm_gain
        key_normed = key_raw * key_inverse * keynorm_gain
        query_low = (query_normed * cosine + turn_half(query_normed) * sine_part).astype(
            low_type
        )
        key_low = (key_normed * cosine + turn_half(key_normed) * sine_part).astype(low_type)
        value_low = head_columns(raw, 2, head).astype(low_type)
        scores = jnp.where(allowed, mm(query_low, key_low, 1, 1) * score_scale, masked_value)
        top_score = jnp.max(scores, axis=-1, keepdims=True)
        powers = jnp.exp(scores - top_score)
        log_total = top_score + jnp.log(jnp.sum(powers, axis=-1, keepdims=True))
        weights_low = jnp.exp(scores - log_total).astype(low_type)
        mixed_parts.append(mm(weights_low, value_low, 1, 0).astype(low_type))
        kept_heads.append(
            (query_raw, key_raw, query_inverse, key_inverse, query_low, key_low, value_low, log_total)
        )
    mixed_low = jnp.concatenate(mixed_parts, axis=1)

    attention = scatter_rows(mm(mixed_low, output_weight, 1, 0))
    residual = tokens.astype(wide_type) + attention
    inverse_two = inverse_rms(residual)
    second_input = (residual * inverse_two * postnorm_gain).astype(low_type)
    second_all = gather_rows(second_input)

    def gate_table(rows, code):
        logits = mm(rows, full_router, 1, 0)
        shifted = jnp.where(code > 0, logits, masked_value)
        powers = jnp.exp(shifted - jnp.max(shifted, axis=1, keepdims=True))
        return powers / jnp.sum(powers, axis=1, keepdims=True)

    gates_all = gate_table(second_all, code_all)
    masked_gates = jnp.where(code_all > 1, gates_all, 0.0) * valid_all
    gates_here = lax.dynamic_slice_in_dim(masked_gates, device * experts_here, experts_here, 1)
    kept_here = lax.dynamic_slice_in_dim(
        jnp.where(code_all > 1, valid_all, 0.0), device * experts_here, experts_here, 1
    )

    mixture_part = jnp.zeros((group_rows, model_width), wide_type)
    second_part = jnp.zeros((group_rows, model_width), wide_type)
    pair_parts = []
    gate_parts, up_parts, down_parts = [], [], []
    for e in range(experts_here):
        gate_linear = mm(second_all, gate_weight[e], 1, 0)
        up_linear = mm(second_all, up_weight[e], 1, 0)
        sigmoid_gate = jax.nn.sigmoid(gate_linear)
        silu_gate = gate_linear * sigmoid_gate
        inner = silu_gate * up_linear
        gate_column = gates_here[:, e : e + 1]
        inner_scaled = (gate_column * inner).astype(low_type)
        pair_parts.append(
            kept_here[:, e : e + 1] * jnp.sum(inner * up_stream[e], axis=1, keepdims=True)
        )
        hidden_grad = gate_column * up_stream[e]
        gate_back = (
            hidden_grad * up_linear * sigmoid_gate * (1.0 + gate_linear * (1.0 - sigmoid_gate))
        ).astype(low_type)
        up_back = (hidden_grad * silu_gate).astype(low_type)
        mixture_part = mixture_part + mm(inner_scaled, down_weight[e], 1, 0)
        second_part = (
            second_part + mm(gate_back, gate_weight[e], 1, 1) + mm(up_back, up_weight[e], 1, 1)
        )
        down_parts.append(mm(inner_scaled, cot_all, 0, 0).astype(low_type))
        gate_parts.append(mm(second_all, gate_back, 0, 0).astype(low_type))
        up_parts.append(mm(second_all, up_back, 0, 0).astype(low_type))

    pair_sent = jnp.concatenate(pair_parts, axis=1).reshape(
        group_count, row_count, experts_here
    )
    pair_grad = (
        lax.all_to_all(pair_sent, "ep", split_axis=0, concat_axis=0, tiled=True)
        .transpose(1, 0, 2)
        .reshape(row_count, expert_total)
    )
    second_scattered = scatter_rows(second_part)
    mixture = scatter_rows(mixture_part)
    layer_out = (valid_own * (residual + mixture)).astype(low_type)

    code_own = route_code
    gates_own = gate_table(second_input, code_own)
    chosen_grad = gates_own * (
        pair_grad - jnp.sum(gates_own * pair_grad, axis=1, keepdims=True)
    )
    logits_grad = jnp.where(code_own > 0, chosen_grad, 0.0).astype(low_type)
    router_part = mm(second_input, logits_grad, 0, 0)
    second_grad = mm(logits_grad, full_router, 1, 1) + second_scattered
    upstream = valid_own * cotangent.astype(wide_type)
    post_back, postnorm_part = norm_backward(residual, inverse_two, postnorm_gain, second_grad)
    residual_grad = upstream + post_back
    attention_low = residual_grad.astype(low_type)
    attention_all = gather_rows(attention_low)
    mixed_grad = mm(attention_all, output_weight, 1, 1).astype(low_type)
    output_part = mm(mixed_low, attention_all, 0, 0).astype(low_type)

    query_parts, key_parts, value_parts = [], [], []
    querynorm_part = jnp.zeros((head_dim,), wide_type)
    keynorm_part = jnp.zeros((head_dim,), wide_type)
    for head in range(heads_here):
        (query_raw, key_raw, query_inverse, key_inverse, query_low, key_low, value_low, log_total) = (
            kept_heads[head]
        )
        grad_head = mixed_grad[:, head * head_dim : (head + 1) * head_dim]
        scores = jnp.where(allowed, mm(query_low, key_low, 1, 1) * score_scale, masked_value)
        weights = jnp.exp(scores - log_total)
        weight_grad = mm(grad_head, value_low, 1, 1)
        row_dot = jnp.sum(weights * weight_grad, axis=-1, keepdims=True)
        score_grad = (weights * (weight_grad - row_dot)).astype(low_type)
        query_back = mm(score_grad, key_low, 1, 0) * score_scale
        key_back = mm(score_grad, query_low, 0, 0) * score_scale
        value_back = mm(weights.astype(low_type), grad_head, 0, 0)
        query_unturned = query_back * cosine + turn_back(query_back * sine_part)
        key_unturned = key_back * cosine + turn_back(key_back * sine_part)
        query_before, query_gain_part = norm_backward(
            query_raw, query_inverse, querynorm_gain, query_unturned
        )
        key_before, key_gain_part = norm_backward(
            key_raw, key_inverse, keynorm_gain, key_unturned
        )
        querynorm_part = querynorm_part + jnp.sum(query_gain_part, axis=0)
        keynorm_part = keynorm_part + jnp.sum(key_gain_part, axis=0)
        query_parts.append(query_before.astype(low_type))
        key_parts.append(key_before.astype(low_type))
        value_parts.append(value_back.astype(low_type))
    sent = jnp.concatenate(query_parts + key_parts + value_parts, axis=1)
    first_grad = scatter_rows(mm(sent, head_weight, 1, 1))
    head_part = mm(first_all, sent, 0, 0).astype(low_type)
    head_rows = lax.all_to_all(
        head_part.reshape(group_count, width_here, 3 * width_here),
        "ep",
        split_axis=0,
        concat_axis=0,
        tiled=True,
    )
    weight_sums = lax.psum(
        tuple(
            head_rows[:, :, block * width_here : (block + 1) * width_here]
            .transpose(1, 0, 2)
            .reshape(width_here, model_width)
            for block in range(3)
        )
        + (output_part,),
        "rep",
    )
    query_grad, key_grad, value_grad, output_grad = (
        piece.astype(wide_type) for piece in weight_sums
    )

    token_own = tokens.astype(wide_type)
    inverse_one = inverse_rms(token_own)
    pre_back, prenorm_part = norm_backward(token_own, inverse_one, prenorm_gain, first_grad)
    token_grad = residual_grad + pre_back

    small_parts = jnp.concatenate(
        [
            router_part.reshape(group_count, -1),
            jnp.sum(prenorm_part, axis=0).reshape(group_count, -1),
            jnp.sum(postnorm_part, axis=0).reshape(group_count, -1),
            querynorm_part.reshape(group_count, -1),
            keynorm_part.reshape(group_count, -1),
        ],
        axis=1,
    )
    small_sum = lax.psum(
        lax.psum_scatter(small_parts, "ep", scatter_dimension=0, tiled=True), "rep"
    ).reshape(-1)
    sizes = (width_here * expert_total, width_here, width_here) + 2 * (head_dim // group_count,)
    pieces = []
    start = 0
    for size in sizes:
        pieces.append(small_sum[start : start + size])
        start += size
    router_grad = pieces[0].reshape(width_here, expert_total)
    prenorm_grad, postnorm_grad, querynorm_grad, keynorm_grad = pieces[1:]

    gate_total, up_total, down_total = (
        lax.psum_scatter(
            jnp.stack(parts), "rep", scatter_dimension=1, tiled=True
        ).astype(wide_type)
        for parts in (gate_parts, up_parts, down_parts)
    )
    return (
        layer_out,
        token_grad,
        query_grad,
        key_grad,
        value_grad,
        output_grad,
        router_grad,
        prenorm_grad,
        querynorm_grad,
        keynorm_grad,
        postnorm_grad,
        gate_total,
        up_total,
        down_total,
    )


def solution(mesh):
    in_specs = (
        P(("rep", "ep"), None),
        P(("rep", "ep"), None),
        P("rep", None),
        P("rep", None),
        P(("rep", "ep"), None),
        P(("rep", "ep"), None),
        P("ep", None),
        P("ep", None),
        P("ep", None),
        P("ep", None),
        P("ep", None),
        P(),
        P(),
        P(),
        P(),
        P("ep", None, None),
        P("ep", None, None),
        P("ep", None, None),
    )
    out_specs = (
        P(("rep", "ep"), None),
        P(("rep", "ep"), None),
        P("ep", None),
        P("ep", None),
        P("ep", None),
        P("ep", None),
        P("ep", None),
        P("ep"),
        P("ep"),
        P("ep"),
        P("ep"),
        P("ep", "rep", None),
        P("ep", "rep", None),
        P("ep", "rep", None),
    )
    return jax.shard_map(body, mesh=mesh, in_specs=in_specs, out_specs=out_specs, check_vma=False)
```

```python
import jax
import jax.numpy as jnp
from jax import lax
from jax.sharding import PartitionSpec as P

epsilon = 1e-05
rope_base = 10000.0
masked_value = -1e30
low_type = jnp.bfloat16
wide_type = jnp.float32


def inverse_rms(values):
    return lax.rsqrt(jnp.mean(values * values, axis=-1, keepdims=True) + epsilon)


def norm_backward(values, inverse, gain_vector, upstream):
    scaled = upstream * gain_vector
    inner_mean = jnp.mean(scaled * values, axis=-1, keepdims=True)
    result = inverse * scaled - values * (inverse * inverse * inverse) * inner_mean
    return (result, upstream * values * inverse)


def rope_tables(position, dimension):
    halfway = dimension // 2
    indices = jnp.arange(halfway, dtype=wide_type)
    frequency = rope_base ** (-2.0 * indices / dimension)
    angles = position.astype(wide_type)[:, None] * frequency[None, :]
    cosine = jnp.cos(angles)
    sine_part = jnp.sin(angles)
    return (
        jnp.concatenate([cosine, cosine], axis=-1),
        jnp.concatenate([sine_part, sine_part], axis=-1),
    )


def turn_half(values):
    halfway = values.shape[-1] // 2
    return jnp.concatenate([-values[..., halfway:], values[..., :halfway]], axis=-1)


def turn_back(values):
    halfway = values.shape[-1] // 2
    return jnp.concatenate([values[..., halfway:], -values[..., :halfway]], axis=-1)


def row_meta(lengths, group_order):
    boundary = jnp.cumsum(lengths)
    passed = (group_order[:, None] >= boundary[None, :]).astype(jnp.int32)
    segment = jnp.sum(passed, axis=1)
    offset = jnp.sum(passed * lengths[None, :], axis=1)
    return (segment, group_order - offset)


def mm(left, right, left_dim, right_dim):
    return lax.dot_general(
        left,
        right,
        (((left_dim,), (right_dim,)), ((), ())),
        preferred_element_type=wide_type,
    )


def ring_order(count):
    return [i for i in range(count) if i % 2 == 0] + [i for i in reversed(range(count)) if i % 2]


def ring_slots(count):
    half = count // 2
    offsets = [0]
    for step in range(1, half):
        offsets += [step, -step]
    return offsets + [half]


def ring_shift(values, direction):
    order = ring_order(lax.axis_size("ep"))
    count = len(order)
    pairs = [(order[i], order[(i + direction) % count]) for i in range(count)]
    return lax.ppermute(values, "ep", pairs)


def ring_gather(values):
    half = lax.axis_size("ep") // 2
    middle = values.shape[0] // 2
    onward, backward = values, values
    blocks = [values]
    for _ in range(1, half):
        onward, backward = ring_shift(onward, 1), ring_shift(backward, -1)
        blocks += [backward, onward]
    far = [ring_shift(onward[:middle], 1), ring_shift(backward[middle:], -1)]
    return blocks + [jnp.concatenate(far, axis=0)]


def ring_scatter(partial):
    count = lax.axis_size("ep")
    half = count // 2
    rows = partial.shape[0] // count
    middle = rows // 2
    slot = {offset: j for j, offset in enumerate(ring_slots(count))}

    def block(offset):
        return partial[slot[offset] * rows : (slot[offset] + 1) * rows]

    onward = ring_shift(block(half)[:middle], 1)
    backward = ring_shift(block(half)[middle:], -1)
    up, down = block(half - 1), block(1 - half)
    onward = jnp.concatenate([add_low(onward, up[:middle]), up[middle:]], axis=0)
    backward = jnp.concatenate([down[:middle], add_low(backward, down[middle:])], axis=0)
    for step in range(half - 2, -1, -1):
        onward, backward = ring_shift(onward, 1), ring_shift(backward, -1)
        if step:
            onward = add_low(onward, block(step))
            backward = add_low(backward, block(-step))
    return (
        block(0).astype(wide_type) + onward.astype(wide_type) + backward.astype(wide_type)
    )


def add_low(left, right):
    return (left.astype(wide_type) + right.astype(wide_type)).astype(low_type)


def rep_exchange(values, distance):
    count = lax.axis_size("rep")
    return lax.ppermute(values, "rep", [(i, i ^ distance) for i in range(count)])


def rep_bit(distance):
    return (lax.axis_index("rep") // distance) % 2


def rep_gather(values):
    gathered = values[None]
    distance = lax.axis_size("rep") // 2
    while distance:
        other = rep_exchange(gathered, distance)
        mine_first = jnp.stack([gathered, other], axis=1)
        other_first = jnp.stack([other, gathered], axis=1)
        gathered = jnp.where(rep_bit(distance) == 0, mine_first, other_first)
        gathered = gathered.reshape((-1,) + values.shape)
        distance //= 2
    return gathered


def rep_scatter(values, axis):
    distance = 1
    count = lax.axis_size("rep")
    while distance < count:
        shape = values.shape
        pairs = values.reshape(shape[:axis] + (shape[axis] // 2, 2) + shape[axis + 1 :])
        bit = rep_bit(distance)
        keep = lax.dynamic_index_in_dim(pairs, bit, axis + 1, keepdims=False)
        send = lax.dynamic_index_in_dim(pairs, 1 - bit, axis + 1, keepdims=False)
        values = add_low(keep, rep_exchange(send, distance))
        distance *= 2
    return lax.index_in_dim(values, 0, axis, keepdims=False)


def swap_all(values):
    return lax.all_to_all(values, "ep", split_axis=0, concat_axis=0, tiled=True)


def body(
    tokens,
    cotangent,
    seq_lengths,
    token_order,
    routes,
    slot_index,
    query_weight,
    key_weight,
    value_weight,
    output_weight,
    router_weight,
    prenorm_gain,
    querynorm_gain,
    keynorm_gain,
    postnorm_gain,
    gate_weight,
    up_weight,
    down_weight,
):
    group_count = lax.axis_size("ep")
    device = lax.axis_index("ep")
    row_count, model_width = tokens.shape
    head_dim = querynorm_gain.shape[0]
    width_here = model_width // group_count
    heads_here = width_here // head_dim
    experts_here = gate_weight.shape[0]
    expert_total = experts_here * group_count
    top_count = routes.shape[1]
    capacity = row_count * top_count * 5 // (4 * expert_total)
    group_rows = row_count * group_count
    sequence_count = seq_lengths.shape[1]
    score_scale = head_dim ** (-0.5)

    replica_count = lax.axis_size("rep")
    replica = lax.axis_index("rep")
    share = width_here // replica_count

    order = ring_order(group_count)
    offsets = ring_slots(group_count)
    place_of = jnp.array([order.index(i) for i in range(group_count)], jnp.int32)
    place = place_of[device]
    device_of_slot = jnp.array(order, jnp.int32)[(place + jnp.array(offsets)) % group_count]
    slot_of_offset = jnp.array(
        [[j for j, o in enumerate(offsets) if o % group_count == i][0] for i in range(group_count)],
        jnp.int32,
    )
    slot_of_device = slot_of_offset[(place_of - place) % group_count]

    def reorder(blocks, index):
        return jnp.concatenate(
            [lax.dynamic_slice_in_dim(blocks, index[i], 1, 0) for i in range(group_count)], axis=0
        )

    group_order = reorder(token_order[0].reshape(group_count, row_count), device_of_slot)
    segment, position = row_meta(seq_lengths[0], group_order.reshape(group_rows))
    segment_own = segment[:row_count]
    valid_own = (segment_own < sequence_count).astype(wide_type)[:, None]
    valid_all = (segment < sequence_count).astype(wide_type)[:, None]

    expert_ids = jnp.arange(expert_total, dtype=jnp.int32)
    route_code = jnp.zeros((row_count, expert_total), jnp.int32)
    for column in range(top_count):
        hit = routes[:, column, None] == expert_ids[None, :]
        kept = (slot_index[:, column, None] < capacity).astype(jnp.int32)
        route_code = route_code + jnp.where(hit, 1 + kept, 0)
    small_sent = jnp.concatenate([route_code.astype(low_type), router_weight], axis=0)

    small_flat = small_sent.reshape(-1, head_dim)
    small_all = swap_all(
        jnp.broadcast_to(small_flat[None], (group_count,) + small_flat.shape)
    ).reshape(group_count, row_count + width_here, expert_total)
    code_all = reorder(small_all[:, :row_count], device_of_slot).reshape(
        group_rows, expert_total
    )
    full_router = small_all[:, row_count:].reshape(model_width, expert_total)

    projections = jnp.concatenate(
        [
            lax.dynamic_slice_in_dim(piece, replica * share, share, 0).reshape(
                share, group_count, width_here
            )
            for piece in (query_weight, key_weight, value_weight)
        ],
        axis=2,
    ).transpose(1, 0, 2)
    head_weight = (
        rep_gather(swap_all(projections))
        .transpose(1, 0, 2, 3)
        .reshape(model_width, 3 * width_here)
    )
    token_blocks = ring_gather(tokens)
    token_last, cot_own, output_weight_own = lax.optimization_barrier(
        (token_blocks[-1], cotangent, output_weight)
    )
    token_all = jnp.concatenate(token_blocks[:-1] + [token_last], axis=0)
    cot_all = jnp.concatenate(ring_gather(cot_own), axis=0)
    column_share = model_width // replica_count
    full_output = rep_gather(
        lax.all_gather(
            lax.dynamic_slice_in_dim(
                output_weight_own, replica * column_share, column_share, 1
            ),
            "ep",
            axis=0,
            tiled=True,
        )
    )

    token_wide = token_all.astype(wide_type)
    inverse_all = inverse_rms(token_wide)
    first_all = (token_wide * inverse_all * prenorm_gain).astype(low_type)
    raw = mm(first_all, head_weight, 1, 0)
    cosine, sine_part = rope_tables(position, head_dim)

    up_stream = [mm(cot_all, down_weight[e], 1, 1) for e in range(experts_here)]

    allowed = segment[:, None] == segment[None, :]

    def head_columns(values, block, head):
        start = block * width_here + head * head_dim
        return values[:, start : start + head_dim]

    kept_heads = []
    mixed_parts = []
    for head in range(heads_here):
        query_raw = head_columns(raw, 0, head)
        key_raw = head_columns(raw, 1, head)
        query_inverse = inverse_rms(query_raw)
        key_inverse = inverse_rms(key_raw)
        query_normed = query_raw * query_inverse * querynorm_gain
        key_normed = key_raw * key_inverse * keynorm_gain
        query_low = (query_normed * cosine + turn_half(query_normed) * sine_part).astype(
            low_type
        )
        key_low = (key_normed * cosine + turn_half(key_normed) * sine_part).astype(low_type)
        value_low = head_columns(raw, 2, head).astype(low_type)
        scores = jnp.where(allowed, mm(query_low, key_low, 1, 1) * score_scale, masked_value)
        top_score = jnp.max(scores, axis=-1, keepdims=True)
        powers = jnp.exp(scores - top_score)
        log_total = top_score + jnp.log(jnp.sum(powers, axis=-1, keepdims=True))
        weights_low = jnp.exp(scores - log_total).astype(low_type)
        mixed_parts.append(mm(weights_low, value_low, 1, 0).astype(low_type))
        kept_heads.append(
            (query_raw, key_raw, query_inverse, key_inverse, query_low, key_low, value_low, log_total)
        )
    mixed_low = jnp.concatenate(mixed_parts, axis=1)

    mixed_own = (
        swap_all(reorder(mixed_low.reshape(group_count, row_count, width_here), slot_of_device))
        .transpose(1, 0, 2)
        .reshape(row_count, model_width)
    )
    attention = lax.dot_general(
        mixed_own, full_output, (((1,), (1,)), ((), ())), preferred_element_type=wide_type
    ).reshape(row_count, model_width)
    residual = tokens.astype(wide_type) + attention
    inverse_two = inverse_rms(residual)
    second_input = (residual * inverse_two * postnorm_gain).astype(low_type)
    second_all = jnp.concatenate(ring_gather(second_input), axis=0)

    def gate_table(rows, code):
        logits = mm(rows, full_router, 1, 0)
        shifted = jnp.where(code > 0, logits, masked_value)
        powers = jnp.exp(shifted - jnp.max(shifted, axis=1, keepdims=True))
        return powers / jnp.sum(powers, axis=1, keepdims=True)

    gates_all = gate_table(second_all, code_all)
    masked_gates = jnp.where(code_all > 1, gates_all, 0.0) * valid_all
    gates_here = lax.dynamic_slice_in_dim(masked_gates, device * experts_here, experts_here, 1)
    kept_here = lax.dynamic_slice_in_dim(
        jnp.where(code_all > 1, valid_all, 0.0), device * experts_here, experts_here, 1
    )

    mixture_part = jnp.zeros((group_rows, model_width), wide_type)
    second_part = jnp.zeros((group_rows, model_width), wide_type)
    pair_parts = []
    gate_parts, up_parts, down_parts = [], [], []
    for e in range(experts_here):
        gate_linear = mm(second_all, gate_weight[e], 1, 0)
        up_linear = mm(second_all, up_weight[e], 1, 0)
        sigmoid_gate = jax.nn.sigmoid(gate_linear)
        silu_gate = gate_linear * sigmoid_gate
        inner = silu_gate * up_linear
        gate_column = gates_here[:, e : e + 1]
        inner_scaled = (gate_column * inner).astype(low_type)
        pair_parts.append(
            kept_here[:, e : e + 1] * jnp.sum(inner * up_stream[e], axis=1, keepdims=True)
        )
        hidden_grad = gate_column * up_stream[e]
        gate_back = (
            hidden_grad * up_linear * sigmoid_gate * (1.0 + gate_linear * (1.0 - sigmoid_gate))
        ).astype(low_type)
        up_back = (hidden_grad * silu_gate).astype(low_type)
        mixture_part = mixture_part + mm(inner_scaled, down_weight[e], 1, 0)
        second_part = (
            second_part + mm(gate_back, gate_weight[e], 1, 1) + mm(up_back, up_weight[e], 1, 1)
        )
        down_parts.append(mm(inner_scaled, cot_all, 0, 0).astype(low_type))
        gate_parts.append(mm(second_all, gate_back, 0, 0).astype(low_type))
        up_parts.append(mm(second_all, up_back, 0, 0).astype(low_type))

    pair_sent = jnp.concatenate(pair_parts, axis=1).reshape(
        group_count, row_count, experts_here
    )
    pair_grad = (
        swap_all(reorder(pair_sent, slot_of_device))
        .transpose(1, 0, 2)
        .reshape(row_count, expert_total)
    )
    second_scattered = ring_scatter(second_part.astype(low_type))
    code_own = route_code
    gates_own = gate_table(second_input, code_own)
    chosen_grad = gates_own * (
        pair_grad - jnp.sum(gates_own * pair_grad, axis=1, keepdims=True)
    )
    logits_grad = jnp.where(code_own > 0, chosen_grad, 0.0).astype(low_type)
    router_part = mm(second_input, logits_grad, 0, 0)
    second_grad = mm(logits_grad, full_router, 1, 1) + second_scattered
    upstream = valid_own * cotangent.astype(wide_type)
    post_back, postnorm_part = norm_backward(residual, inverse_two, postnorm_gain, second_grad)
    residual_grad = upstream + post_back
    attention_low = residual_grad.astype(low_type)
    mixed_grad_own = lax.dot_general(
        attention_low.reshape(row_count, replica_count, column_share),
        full_output,
        (((1, 2), (0, 2)), ((), ())),
        preferred_element_type=wide_type,
    ).astype(low_type)
    mixed_grad = reorder(
        swap_all(mixed_grad_own.reshape(row_count, group_count, width_here).transpose(1, 0, 2)),
        device_of_slot,
    ).reshape(group_rows, width_here)
    mixed_grad, attention_sent, mixture_low = lax.optimization_barrier(
        (mixed_grad, attention_low, mixture_part.astype(low_type))
    )
    attention_all = jnp.concatenate(ring_gather(attention_sent), axis=0)
    mixture = ring_scatter(mixture_low)
    layer_out = (valid_own * (residual + mixture)).astype(low_type)
    output_part = mm(mixed_low, attention_all, 0, 0).astype(low_type)

    query_parts, key_parts, value_parts = [], [], []
    querynorm_part = jnp.zeros((head_dim,), wide_type)
    keynorm_part = jnp.zeros((head_dim,), wide_type)
    for head in range(heads_here):
        (query_raw, key_raw, query_inverse, key_inverse, query_low, key_low, value_low, log_total) = (
            kept_heads[head]
        )
        grad_head = mixed_grad[:, head * head_dim : (head + 1) * head_dim]
        scores = jnp.where(allowed, mm(query_low, key_low, 1, 1) * score_scale, masked_value)
        weights = jnp.exp(scores - log_total)
        weight_grad = mm(grad_head, value_low, 1, 1)
        row_dot = jnp.sum(weights * weight_grad, axis=-1, keepdims=True)
        score_grad = (weights * (weight_grad - row_dot)).astype(low_type)
        query_back = mm(score_grad, key_low, 1, 0) * score_scale
        key_back = mm(score_grad, query_low, 0, 0) * score_scale
        value_back = mm(weights.astype(low_type), grad_head, 0, 0)
        query_unturned = query_back * cosine + turn_back(query_back * sine_part)
        key_unturned = key_back * cosine + turn_back(key_back * sine_part)
        query_before, query_gain_part = norm_backward(
            query_raw, query_inverse, querynorm_gain, query_unturned
        )
        key_before, key_gain_part = norm_backward(
            key_raw, key_inverse, keynorm_gain, key_unturned
        )
        querynorm_part = querynorm_part + jnp.sum(query_gain_part, axis=0)
        keynorm_part = keynorm_part + jnp.sum(key_gain_part, axis=0)
        query_parts.append(query_before.astype(low_type))
        key_parts.append(key_before.astype(low_type))
        value_parts.append(value_back.astype(low_type))
    sent = jnp.concatenate(query_parts + key_parts + value_parts, axis=1)
    first_part = mm(sent, head_weight, 1, 1)
    prenorm_part = jnp.sum(first_part * token_wide * inverse_all, axis=0)
    first_grad = ring_scatter(first_part.astype(low_type))
    head_part = mm(first_all, sent, 0, 0).astype(low_type)
    head_rows = rep_gather(
        swap_all(
            rep_scatter(
                head_part.reshape(group_count, replica_count, share, 3 * width_here), 1
            )
        )
    )
    query_grad, key_grad, value_grad = (
        head_rows[..., block * width_here : (block + 1) * width_here]
        .transpose(0, 2, 1, 3)
        .reshape(width_here, model_width)
        .astype(wide_type)
        for block in range(3)
    )
    output_grad = (
        rep_gather(rep_scatter(output_part.reshape(replica_count, share, model_width), 0))
        .reshape(width_here, model_width)
        .astype(wide_type)
    )

    token_own = tokens.astype(wide_type)
    inverse_one = inverse_rms(token_own)
    pre_back, _ = norm_backward(token_own, inverse_one, prenorm_gain, first_grad)
    token_grad = residual_grad + pre_back

    def small_sum(parts):
        flat = jnp.concatenate([part.reshape(group_count, -1) for part in parts], axis=1)
        total = lax.psum(
            lax.psum_scatter(flat, "ep", scatter_dimension=0, tiled=True), "rep"
        ).reshape(-1)
        pieces, start = [], 0
        for part in parts:
            size = part.size // group_count
            pieces.append(total[start : start + size])
            start += size
        return pieces

    router_grad, postnorm_grad = small_sum([router_part, jnp.sum(postnorm_part, axis=0)])
    router_grad = router_grad.reshape(width_here, expert_total)
    prenorm_grad, querynorm_grad, keynorm_grad = small_sum(
        [prenorm_part, querynorm_part, keynorm_part]
    )

    gate_total, up_total, down_total = (
        lax.psum_scatter(
            jnp.stack(parts), "rep", scatter_dimension=1, tiled=True
        ).astype(wide_type)
        for parts in (gate_parts, up_parts, down_parts)
    )
    return (
        layer_out,
        token_grad,
        query_grad,
        key_grad,
        value_grad,
        output_grad,
        router_grad,
        prenorm_grad,
        querynorm_grad,
        keynorm_grad,
        postnorm_grad,
        gate_total,
        up_total,
        down_total,
    )


def solution(mesh):
    in_specs = (
        P(("rep", "ep"), None),
        P(("rep", "ep"), None),
        P("rep", None),
        P("rep", None),
        P(("rep", "ep"), None),
        P(("rep", "ep"), None),
        P("ep", None),
        P("ep", None),
        P("ep", None),
        P("ep", None),
        P("ep", None),
        P(),
        P(),
        P(),
        P(),
        P("ep", None, None),
        P("ep", None, None),
        P("ep", None, None),
    )
    out_specs = (
        P(("rep", "ep"), None),
        P(("rep", "ep"), None),
        P("ep", None),
        P("ep", None),
        P("ep", None),
        P("ep", None),
        P("ep", None),
        P("ep"),
        P("ep"),
        P("ep"),
        P("ep"),
        P("ep", "rep", None),
        P("ep", "rep", None),
        P("ep", "rep", None),
    )
    return jax.shard_map(body, mesh=mesh, in_specs=in_specs, out_specs=out_specs, check_vma=False)
```

```python
import jax
import jax.numpy as jnp
from jax import lax
from jax.experimental import pallas as pl
from jax.experimental.pallas import tpu as pltpu
from jax.sharding import PartitionSpec as P

epsilon = 1e-05
rope_base = 10000.0
masked_value = -1e30
low_type = jnp.bfloat16
wide_type = jnp.float32


def inverse_rms(values):
    return lax.rsqrt(jnp.mean(values * values, axis=-1, keepdims=True) + epsilon)


def norm_backward(values, inverse, gain_vector, upstream):
    scaled = upstream * gain_vector
    inner_mean = jnp.mean(scaled * values, axis=-1, keepdims=True)
    result = inverse * scaled - values * (inverse * inverse * inverse) * inner_mean
    return (result, upstream * values * inverse)


def rope_tables(position, dimension):
    halfway = dimension // 2
    indices = jnp.arange(halfway, dtype=wide_type)
    frequency = rope_base ** (-2.0 * indices / dimension)
    angles = position.astype(wide_type)[:, None] * frequency[None, :]
    cosine = jnp.cos(angles)
    sine_part = jnp.sin(angles)
    return (
        jnp.concatenate([cosine, cosine], axis=-1),
        jnp.concatenate([sine_part, sine_part], axis=-1),
    )


def turn_half(values):
    halfway = values.shape[-1] // 2
    return jnp.concatenate([-values[..., halfway:], values[..., :halfway]], axis=-1)


def turn_back(values):
    halfway = values.shape[-1] // 2
    return jnp.concatenate([values[..., halfway:], -values[..., :halfway]], axis=-1)


def row_meta(lengths, group_order):
    boundary = jnp.cumsum(lengths)
    passed = (group_order[:, None] >= boundary[None, :]).astype(jnp.int32)
    segment = jnp.sum(passed, axis=1)
    offset = jnp.sum(passed * lengths[None, :], axis=1)
    return (segment, group_order - offset)


def mm(left, right, left_dim, right_dim):
    return lax.dot_general(
        left,
        right,
        (((left_dim,), (right_dim,)), ((), ())),
        preferred_element_type=wide_type,
    )


def gather_rows(values):
    return lax.all_gather(values, "ep", axis=0, tiled=True)


def ring_order(count):
    return [i for i in range(count) if i % 2 == 0] + [i for i in reversed(range(count)) if i % 2]


def ring_slots(count):
    half = count // 2
    offsets = [0]
    for step in range(1, half):
        offsets += [step, -step]
    return offsets + [half]


def ring_shift(values, direction):
    order = ring_order(lax.axis_size("ep"))
    count = len(order)
    pairs = [(order[i], order[(i + direction) % count]) for i in range(count)]
    return lax.ppermute(values, "ep", pairs)


def ring_gather(values):
    half = lax.axis_size("ep") // 2
    middle = values.shape[0] // 2
    onward, backward = values, values
    blocks = [values]
    for _ in range(1, half):
        onward, backward = ring_shift(onward, 1), ring_shift(backward, -1)
        blocks += [backward, onward]
    far = [ring_shift(onward[:middle], 1), ring_shift(backward[middle:], -1)]
    return blocks + [jnp.concatenate(far, axis=0)]


def ring_scatter(partial):
    count = lax.axis_size("ep")
    half = count // 2
    rows = partial.shape[0] // count
    middle = rows // 2
    slot = {offset: j for j, offset in enumerate(ring_slots(count))}

    def block(offset):
        return partial[slot[offset] * rows : (slot[offset] + 1) * rows]

    onward = ring_shift(block(half)[:middle], 1)
    backward = ring_shift(block(half)[middle:], -1)
    up, down = block(half - 1), block(1 - half)
    onward = jnp.concatenate([add_low(onward, up[:middle]), up[middle:]], axis=0)
    backward = jnp.concatenate([down[:middle], add_low(backward, down[middle:])], axis=0)
    for step in range(half - 2, -1, -1):
        onward, backward = ring_shift(onward, 1), ring_shift(backward, -1)
        if step:
            onward = add_low(onward, block(step))
            backward = add_low(backward, block(-step))
    return (
        block(0).astype(wide_type) + onward.astype(wide_type) + backward.astype(wide_type)
    )


def add_low(left, right):
    return (left.astype(wide_type) + right.astype(wide_type)).astype(low_type)


def ring_place(member, count):
    return jnp.where(member % 2 == 0, member // 2, count - 1 - member // 2)


def ring_member(place, count):
    return jnp.where(place < count // 2, 2 * place, 2 * (count - 1 - place) + 1)


def ring_indices(device, count):
    place = ring_place(device, count)
    half = count // 2
    members = [ring_member((place + offset) % count, count) for offset in ring_slots(count)]
    slots = []
    for other in range(count):
        ahead = (ring_place(jnp.int32(other), count) - place) % count
        slot = jnp.where(ahead < half, 2 * ahead - 1, 2 * (count - ahead))
        slots.append(jnp.where(ahead == 0, 0, jnp.where(ahead == half, count - 1, slot)))
    return members, slots


def rep_exchange(values, distance):
    count = lax.axis_size("rep")
    return lax.ppermute(values, "rep", [(i, i ^ distance) for i in range(count)])


def rep_bit(distance):
    return (lax.axis_index("rep") // distance) % 2


def rep_gather(values):
    gathered = values[None]
    distance = lax.axis_size("rep") // 2
    while distance:
        other = rep_exchange(gathered, distance)
        mine_first = jnp.stack([gathered, other], axis=1)
        other_first = jnp.stack([other, gathered], axis=1)
        gathered = jnp.where(rep_bit(distance) == 0, mine_first, other_first)
        gathered = gathered.reshape((-1,) + values.shape)
        distance //= 2
    return gathered


def rep_scatter(values, axis):
    distance = 1
    count = lax.axis_size("rep")
    while distance < count:
        shape = values.shape
        pairs = values.reshape(shape[:axis] + (shape[axis] // 2, 2) + shape[axis + 1 :])
        bit = rep_bit(distance)
        keep = lax.dynamic_index_in_dim(pairs, bit, axis + 1, keepdims=False)
        send = lax.dynamic_index_in_dim(pairs, 1 - bit, axis + 1, keepdims=False)
        values = add_low(keep, rep_exchange(send, distance))
        distance *= 2
    return lax.index_in_dim(values, 0, axis, keepdims=False)


def rep_pieces(values):
    pieces = {0: values}
    distance = lax.axis_size("rep") // 2
    while distance:
        for j in list(pieces):
            pieces[j ^ distance] = rep_exchange(pieces[j], distance)
        distance //= 2
    return pieces


def rep_sum(values):
    distance = 1
    while distance < lax.axis_size("rep"):
        values = values + rep_exchange(values, distance)
        distance *= 2
    return values


def swap_all(values):
    return lax.all_to_all(values, "ep", split_axis=0, concat_axis=0, tiled=True)


def expert_kernel(
    rows_ref, gate_ref, up_ref, stream_ref, gates_ref, inner_ref, gback_ref, uback_ref, pair_ref
):
    expert, step = pl.program_id(0), pl.program_id(1)
    rows = rows_ref[...]
    gate_linear = jnp.dot(rows, gate_ref[0], preferred_element_type=wide_type)
    up_linear = jnp.dot(rows, up_ref[0], preferred_element_type=wide_type)
    stream = stream_ref[...]
    column = gates_ref[:, 0:1]
    for other in range(1, gates_ref.shape[1]):
        column = jnp.where(expert == other, gates_ref[:, other : other + 1], column)
    sigmoid_gate = jax.nn.sigmoid(gate_linear)
    silu_gate = gate_linear * sigmoid_gate
    inner = silu_gate * up_linear
    inner_ref[...] = (column * inner).astype(low_type)
    hidden_grad = column * stream
    gback_ref[...] = (
        hidden_grad * up_linear * sigmoid_gate * (1.0 + gate_linear * (1.0 - sigmoid_gate))
    ).astype(low_type)
    uback_ref[...] = (hidden_grad * silu_gate).astype(low_type)
    product = inner * stream
    lanes = pair_ref.shape[2]
    folded = product[:, :lanes]
    for start in range(lanes, product.shape[1], lanes):
        folded = folded + product[:, start : start + lanes]

    @pl.when(step == 0)
    def _():
        pair_ref[0] = folded

    @pl.when(step > 0)
    def _():
        pair_ref[0] += folded


def expert_pass(rows, gate_weight, up_weight, stream, gates):
    count, depth = rows.shape
    experts, _, hidden = gate_weight.shape
    width = 256
    steps = hidden // width
    wide = pl.BlockSpec((count, width), lambda e, j: (0, e * steps + j))
    weight = pl.BlockSpec((1, depth, width), lambda e, j: (e, 0, j))
    return pl.pallas_call(
        expert_kernel,
        grid=(experts, steps),
        in_specs=[
            pl.BlockSpec((count, depth), lambda e, j: (0, 0)),
            weight,
            weight,
            wide,
            pl.BlockSpec(gates.shape, lambda e, j: (0, 0)),
        ],
        out_specs=[wide, wide, wide, pl.BlockSpec((1, count, 128), lambda e, j: (e, 0, 0))],
        out_shape=[jax.ShapeDtypeStruct((count, experts * hidden), low_type)] * 3
        + [jax.ShapeDtypeStruct((experts, count, 128), wide_type)],
        compiler_params=pltpu.CompilerParams(vmem_limit_bytes=56 << 20),
        cost_estimate=pl.CostEstimate(
            flops=4 * count * depth * experts * hidden,
            bytes_accessed=4 * depth * experts * hidden + 20 * count * depth,
            transcendentals=count * experts * hidden,
        ),
    )(rows, gate_weight, up_weight, stream, gates)


def expert_back_kernel(gback_ref, uback_ref, gate_ref, up_ref, out_ref):
    experts, _, hidden = gate_ref.shape
    total = None
    for e in range(experts):
        for grad_ref, weight_ref in ((gback_ref, gate_ref), (uback_ref, up_ref)):
            term = mm(grad_ref[:, e * hidden : (e + 1) * hidden], weight_ref[e], 1, 1)
            total = term if total is None else total + term
    out_ref[...] = total.astype(low_type)


def expert_back(gback, uback, gate_weight, up_weight):
    count = gback.shape[0]
    experts, depth, hidden = gate_weight.shape
    width = 256
    whole = pl.BlockSpec((count, experts * hidden), lambda j: (0, 0))
    weight = pl.BlockSpec((experts, width, hidden), lambda j: (0, j, 0))
    return pl.pallas_call(
        expert_back_kernel,
        grid=(depth // width,),
        in_specs=[whole, whole, weight, weight],
        out_specs=pl.BlockSpec((count, width), lambda j: (0, j)),
        out_shape=jax.ShapeDtypeStruct((count, depth), low_type),
        compiler_params=pltpu.CompilerParams(vmem_limit_bytes=56 << 20),
        cost_estimate=pl.CostEstimate(
            flops=4 * count * depth * experts * hidden,
            bytes_accessed=4 * depth * experts * hidden + 6 * count * depth,
            transcendentals=0,
        ),
    )(gback, uback, gate_weight, up_weight)


def body(
    tokens,
    cotangent,
    seq_lengths,
    token_order,
    routes,
    slot_index,
    query_weight,
    key_weight,
    value_weight,
    output_weight,
    router_weight,
    prenorm_gain,
    querynorm_gain,
    keynorm_gain,
    postnorm_gain,
    gate_weight,
    up_weight,
    down_weight,
):
    group_count = lax.axis_size("ep")
    device = lax.axis_index("ep")
    row_count, model_width = tokens.shape
    head_dim = querynorm_gain.shape[0]
    width_here = model_width // group_count
    heads_here = width_here // head_dim
    experts_here = gate_weight.shape[0]
    expert_total = experts_here * group_count
    top_count = routes.shape[1]
    capacity = row_count * top_count * 5 // (4 * expert_total)
    group_rows = row_count * group_count
    sequence_count = seq_lengths.shape[1]
    score_scale = head_dim ** (-0.5)

    replica_count = lax.axis_size("rep")
    replica = lax.axis_index("rep")
    share = width_here // replica_count

    device_of_slot, slot_of_device = ring_indices(device, group_count)

    def reorder(blocks, index):
        return jnp.concatenate(
            [lax.dynamic_slice_in_dim(blocks, index[i], 1, 0) for i in range(group_count)], axis=0
        )

    group_order = reorder(token_order[0].reshape(group_count, row_count), device_of_slot)
    segment, position = row_meta(seq_lengths[0], group_order.reshape(group_rows))
    segment_own = segment[:row_count]
    valid_own = (segment_own < sequence_count).astype(wide_type)[:, None]
    valid_all = (segment < sequence_count).astype(wide_type)[:, None]

    expert_ids = jnp.arange(expert_total, dtype=jnp.int32)
    route_code = jnp.zeros((row_count, expert_total), jnp.int32)
    for column in range(top_count):
        hit = routes[:, column, None] == expert_ids[None, :]
        kept = (slot_index[:, column, None] < capacity).astype(jnp.int32)
        route_code = route_code + jnp.where(hit, 1 + kept, 0)
    small_sent = jnp.concatenate([route_code.astype(low_type), router_weight], axis=0)

    small_flat = small_sent.reshape(-1, head_dim)
    small_all = swap_all(
        jnp.broadcast_to(small_flat[None], (group_count,) + small_flat.shape)
    ).reshape(group_count, row_count + width_here, expert_total)
    code_all = reorder(small_all[:, :row_count], device_of_slot).reshape(
        group_rows, expert_total
    )
    full_router = small_all[:, row_count:].reshape(model_width, expert_total)

    projections = jnp.concatenate(
        [
            lax.dynamic_slice_in_dim(piece, replica * share, share, 0).reshape(
                share, group_count, width_here
            )
            for piece in (query_weight, key_weight, value_weight)
        ],
        axis=2,
    ).transpose(1, 0, 2)
    head_weight = (
        rep_gather(swap_all(projections))
        .transpose(1, 0, 2, 3)
        .reshape(model_width, 3 * width_here)
    )
    token_all = jnp.concatenate(ring_gather(tokens), axis=0)
    column_share = model_width // replica_count
    output_pieces = rep_pieces(
        gather_rows(
            lax.dynamic_slice_in_dim(output_weight, replica * column_share, column_share, 1)
        )
    )

    def reorder_rows(rows, index):
        return reorder(
            rows.reshape(group_count, row_count, rows.shape[1]), index
        ).reshape(rows.shape)

    token_late, cot_own = lax.optimization_barrier((token_all, cotangent))
    token_all = token_late
    cot_ordered = gather_rows(cot_own)
    cot_all = reorder_rows(cot_ordered, device_of_slot)

    token_wide = token_all.astype(wide_type)
    inverse_all = inverse_rms(token_wide)
    first_all = (token_wide * inverse_all * prenorm_gain).astype(low_type)
    raw = mm(first_all, head_weight, 1, 0)
    cosine, sine_part = rope_tables(position, head_dim)

    hidden_here = down_weight.shape[1]
    flat_down = down_weight.reshape(experts_here * hidden_here, model_width)
    up_stream = mm(cot_all, flat_down, 1, 1)

    allowed = segment[:, None] == segment[None, :]

    def head_columns(values, block, head):
        start = block * width_here + head * head_dim
        return values[:, start : start + head_dim]

    kept_heads = []
    mixed_parts = []
    for head in range(heads_here):
        query_raw = head_columns(raw, 0, head)
        key_raw = head_columns(raw, 1, head)
        query_inverse = inverse_rms(query_raw)
        key_inverse = inverse_rms(key_raw)
        query_normed = query_raw * query_inverse * querynorm_gain
        key_normed = key_raw * key_inverse * keynorm_gain
        query_low = (query_normed * cosine + turn_half(query_normed) * sine_part).astype(
            low_type
        )
        key_low = (key_normed * cosine + turn_half(key_normed) * sine_part).astype(low_type)
        value_low = head_columns(raw, 2, head).astype(low_type)
        scores = jnp.where(allowed, mm(query_low, key_low, 1, 1) * score_scale, masked_value)
        top_score = jnp.max(scores, axis=-1, keepdims=True)
        powers = jnp.exp(scores - top_score)
        log_total = top_score + jnp.log(jnp.sum(powers, axis=-1, keepdims=True))
        weights_low = jnp.exp(scores - log_total).astype(low_type)
        mixed_parts.append(mm(weights_low, value_low, 1, 0).astype(low_type))
        kept_heads.append(
            (query_raw, key_raw, query_inverse, key_inverse, query_low, key_low, value_low, log_total)
        )
    mixed_low = jnp.concatenate(mixed_parts, axis=1)

    mixed_ordered = reorder_rows(mixed_low, slot_of_device)
    mixed_own = (
        swap_all(mixed_ordered.reshape(group_count, row_count, width_here))
        .transpose(1, 0, 2)
        .reshape(row_count, model_width)
    )
    attention = jnp.zeros((row_count, model_width), wide_type)
    for j, piece in output_pieces.items():
        attention = lax.dynamic_update_slice_in_dim(
            attention, mm(mixed_own, piece, 1, 0), (replica ^ j) * column_share, 1
        )
    residual = tokens.astype(wide_type) + attention
    inverse_two = inverse_rms(residual)
    second_input = (residual * inverse_two * postnorm_gain).astype(low_type)
    second_all = jnp.concatenate(ring_gather(second_input), axis=0)

    def gate_table(rows, code):
        logits = mm(rows, full_router, 1, 0)
        shifted = jnp.where(code > 0, logits, masked_value)
        powers = jnp.exp(shifted - jnp.max(shifted, axis=1, keepdims=True))
        return powers / jnp.sum(powers, axis=1, keepdims=True)

    gates_all = gate_table(second_all, code_all)
    masked_gates = jnp.where(code_all > 1, gates_all, 0.0) * valid_all
    gates_here = lax.dynamic_slice_in_dim(masked_gates, device * experts_here, experts_here, 1)
    kept_here = lax.dynamic_slice_in_dim(
        jnp.where(code_all > 1, valid_all, 0.0), device * experts_here, experts_here, 1
    )

    inner_all, gback_all, uback_all, pair_lanes = expert_pass(
        second_all, gate_weight, up_weight, up_stream, gates_here
    )
    second_part = expert_back(gback_all, uback_all, gate_weight, up_weight)
    pair_sent = (
        (kept_here * jnp.sum(pair_lanes, axis=2).transpose(1, 0))
    ).reshape(group_count, row_count, experts_here)
    down_part = mm(inner_all, cot_all, 0, 0).astype(low_type)
    gate_part = mm(second_all, gback_all, 0, 0).astype(low_type)
    pair_grad = (
        swap_all(reorder(pair_sent, slot_of_device))
        .transpose(1, 0, 2)
        .reshape(row_count, expert_total)
    )
    second_scattered, uback_late, inner_late = lax.optimization_barrier(
        (ring_scatter(second_part), uback_all, inner_all)
    )
    up_part = mm(second_all, uback_late, 0, 0).astype(low_type)
    mixture_part = mm(inner_late, flat_down, 1, 0).astype(low_type)
    code_own = route_code
    gates_own = gate_table(second_input, code_own)
    chosen_grad = gates_own * (
        pair_grad - jnp.sum(gates_own * pair_grad, axis=1, keepdims=True)
    )
    logits_grad = jnp.where(code_own > 0, chosen_grad, 0.0).astype(low_type)
    router_part = mm(second_input, logits_grad, 0, 0)
    second_grad = mm(logits_grad, full_router, 1, 1) + second_scattered
    upstream = valid_own * cotangent.astype(wide_type)
    post_back, postnorm_part = norm_backward(residual, inverse_two, postnorm_gain, second_grad)
    residual_grad = upstream + post_back
    attention_low = residual_grad.astype(low_type)
    attention_all = gather_rows(attention_low)
    mixed_grad_own = jnp.zeros((row_count, model_width), wide_type)
    for j, piece in output_pieces.items():
        mixed_grad_own = mixed_grad_own + mm(
            lax.dynamic_slice_in_dim(
                attention_low, (replica ^ j) * column_share, column_share, 1
            ),
            piece,
            1,
            1,
        )
    mixed_grad = reorder_rows(
        swap_all(
            mixed_grad_own.astype(low_type)
            .reshape(row_count, group_count, width_here)
            .transpose(1, 0, 2)
        ).reshape(group_rows, width_here),
        device_of_slot,
    )
    mixed_grad, mixture_low = lax.optimization_barrier((mixed_grad, mixture_part))
    mixture = ring_scatter(mixture_low)
    layer_out = (valid_own * (residual + mixture)).astype(low_type)
    output_part = mm(mixed_ordered, attention_all, 0, 0).astype(low_type)

    query_parts, key_parts, value_parts = [], [], []
    querynorm_part = jnp.zeros((head_dim,), wide_type)
    keynorm_part = jnp.zeros((head_dim,), wide_type)
    for head in range(heads_here):
        (query_raw, key_raw, query_inverse, key_inverse, query_low, key_low, value_low, log_total) = (
            kept_heads[head]
        )
        grad_head = mixed_grad[:, head * head_dim : (head + 1) * head_dim]
        scores = jnp.where(allowed, mm(query_low, key_low, 1, 1) * score_scale, masked_value)
        weights = jnp.exp(scores - log_total)
        weight_grad = mm(grad_head, value_low, 1, 1)
        row_dot = jnp.sum(weights * weight_grad, axis=-1, keepdims=True)
        score_grad = (weights * (weight_grad - row_dot)).astype(low_type)
        query_back = mm(score_grad, key_low, 1, 0) * score_scale
        key_back = mm(score_grad, query_low, 0, 0) * score_scale
        value_back = mm(weights.astype(low_type), grad_head, 0, 0)
        query_unturned = query_back * cosine + turn_back(query_back * sine_part)
        key_unturned = key_back * cosine + turn_back(key_back * sine_part)
        query_before, query_gain_part = norm_backward(
            query_raw, query_inverse, querynorm_gain, query_unturned
        )
        key_before, key_gain_part = norm_backward(
            key_raw, key_inverse, keynorm_gain, key_unturned
        )
        querynorm_part = querynorm_part + jnp.sum(query_gain_part, axis=0)
        keynorm_part = keynorm_part + jnp.sum(key_gain_part, axis=0)
        query_parts.append(query_before.astype(low_type))
        key_parts.append(key_before.astype(low_type))
        value_parts.append(value_back.astype(low_type))
    sent = jnp.concatenate(query_parts + key_parts + value_parts, axis=1)
    first_part = mm(sent, head_weight, 1, 1)
    prenorm_part = jnp.sum(first_part * token_wide * inverse_all, axis=0)
    first_grad = ring_scatter(first_part.astype(low_type))
    head_part = mm(first_all, sent, 0, 0).astype(low_type)
    head_rows = swap_all(
        rep_scatter(head_part.reshape(group_count, replica_count, share, 3 * width_here), 1)
    )
    head_rows = rep_gather(
        head_rows.reshape(group_count, share, 3, width_here)
        .transpose(2, 1, 0, 3)
        .reshape(3, share, model_width)
    )
    query_grad, key_grad, value_grad = (
        head_rows[:, block].reshape(width_here, model_width).astype(wide_type)
        for block in range(3)
    )
    output_grad = (
        rep_gather(rep_scatter(output_part.reshape(replica_count, share, model_width), 0))
        .reshape(width_here, model_width)
        .astype(wide_type)
    )

    token_own = tokens.astype(wide_type)
    inverse_one = inverse_rms(token_own)
    pre_back, _ = norm_backward(token_own, inverse_one, prenorm_gain, first_grad)
    token_grad = residual_grad + pre_back

    def small_sum(parts):
        flat = jnp.concatenate([part.reshape(group_count, -1) for part in parts], axis=1)
        total = rep_sum(jnp.sum(swap_all(flat), axis=0))
        pieces, start = [], 0
        for part in parts:
            size = part.size // group_count
            pieces.append(total[start : start + size])
            start += size
        return pieces

    router_grad, postnorm_grad = small_sum([router_part, jnp.sum(postnorm_part, axis=0)])
    router_grad = router_grad.reshape(width_here, expert_total)
    prenorm_grad, querynorm_grad, keynorm_grad = small_sum(
        [prenorm_part, querynorm_part, keynorm_part]
    )

    down_total = lax.psum_scatter(
        down_part.reshape(experts_here, hidden_here, model_width),
        "rep",
        scatter_dimension=1,
        tiled=True,
    ).astype(wide_type)
    gate_total, up_total = (
        lax.psum_scatter(part, "rep", scatter_dimension=0, tiled=True)
        .reshape(column_share, experts_here, hidden_here)
        .transpose(1, 0, 2)
        .astype(wide_type)
        for part in (gate_part, up_part)
    )
    return (
        layer_out,
        token_grad,
        query_grad,
        key_grad,
        value_grad,
        output_grad,
        router_grad,
        prenorm_grad,
        querynorm_grad,
        keynorm_grad,
        postnorm_grad,
        gate_total,
        up_total,
        down_total,
    )


def solution(mesh):
    in_specs = (
        P(("rep", "ep"), None),
        P(("rep", "ep"), None),
        P("rep", None),
        P("rep", None),
        P(("rep", "ep"), None),
        P(("rep", "ep"), None),
        P("ep", None),
        P("ep", None),
        P("ep", None),
        P("ep", None),
        P("ep", None),
        P(),
        P(),
        P(),
        P(),
        P("ep", None, None),
        P("ep", None, None),
        P("ep", None, None),
    )
    out_specs = (
        P(("rep", "ep"), None),
        P(("rep", "ep"), None),
        P("ep", None),
        P("ep", None),
        P("ep", None),
        P("ep", None),
        P("ep", None),
        P("ep"),
        P("ep"),
        P("ep"),
        P("ep"),
        P("ep", "rep", None),
        P("ep", "rep", None),
        P("ep", "rep", None),
    )
    return jax.shard_map(body, mesh=mesh, in_specs=in_specs, out_specs=out_specs, check_vma=False)
```

```python
import functools

import jax
import jax.numpy as jnp
from jax import lax
from jax.experimental import pallas as pl
from jax.experimental.pallas import tpu as pltpu
from jax.sharding import PartitionSpec as P

epsilon = 1e-05
rope_base = 10000.0
masked_value = -1e30
low_type = jnp.bfloat16
wide_type = jnp.float32


def inverse_rms(values):
    return lax.rsqrt(jnp.mean(values * values, axis=-1, keepdims=True) + epsilon)


def norm_backward(values, inverse, gain_vector, upstream):
    scaled = upstream * gain_vector
    inner_mean = jnp.mean(scaled * values, axis=-1, keepdims=True)
    result = inverse * scaled - values * (inverse * inverse * inverse) * inner_mean
    return (result, upstream * values * inverse)


def rope_tables(position, dimension):
    halfway = dimension // 2
    indices = jnp.arange(halfway, dtype=wide_type)
    frequency = rope_base ** (-2.0 * indices / dimension)
    angles = position.astype(wide_type)[:, None] * frequency[None, :]
    cosine = jnp.cos(angles)
    sine_part = jnp.sin(angles)
    return (
        jnp.concatenate([cosine, cosine], axis=-1),
        jnp.concatenate([sine_part, sine_part], axis=-1),
    )


def turn_half(values):
    halfway = values.shape[-1] // 2
    return jnp.concatenate([-values[..., halfway:], values[..., :halfway]], axis=-1)


def turn_back(values):
    halfway = values.shape[-1] // 2
    return jnp.concatenate([values[..., halfway:], -values[..., :halfway]], axis=-1)


def row_meta(lengths, group_order):
    boundary = jnp.cumsum(lengths)
    passed = (group_order[:, None] >= boundary[None, :]).astype(jnp.int32)
    segment = jnp.sum(passed, axis=1)
    offset = jnp.sum(passed * lengths[None, :], axis=1)
    return (segment, group_order - offset)


def mm(left, right, left_dim, right_dim):
    return lax.dot_general(
        left,
        right,
        (((left_dim,), (right_dim,)), ((), ())),
        preferred_element_type=wide_type,
    )


def gather_rows(values):
    return lax.all_gather(values, "ep", axis=0, tiled=True)


def ring_order(count):
    return [i for i in range(count) if i % 2 == 0] + [i for i in reversed(range(count)) if i % 2]


def ring_slots(count):
    half = count // 2
    offsets = [0]
    for step in range(1, half):
        offsets += [step, -step]
    return offsets + [half]


def ring_shift(values, direction):
    order = ring_order(lax.axis_size("ep"))
    count = len(order)
    pairs = [(order[i], order[(i + direction) % count]) for i in range(count)]
    return lax.ppermute(values, "ep", pairs)


def tie(*arrays):
    return lax.optimization_barrier(arrays)


def fill_window(fill, sent, received):
    if fill is None:
        return received, None
    work, inputs = fill
    inputs, _ = lax.optimization_barrier((inputs, sent))
    return lax.optimization_barrier((received, work(*inputs)))


def ring_gather(values, fills=()):
    half = lax.axis_size("ep") // 2
    middle = values.shape[0] // 2
    fills = dict(fills)
    onward, backward = values, values
    blocks, results = [values], {}
    for step in range(1, half + 1):
        if step == half:
            sent = (onward[:middle], backward[middle:])
        else:
            sent = (onward, backward)
        received = (ring_shift(sent[0], 1), ring_shift(sent[1], -1))
        fill = fills[step](blocks, results) if step in fills else None
        (onward, backward), results[step] = fill_window(fill, sent, received)
        if step < half:
            blocks = blocks + [backward, onward]
    return blocks + [jnp.concatenate([onward, backward], axis=0)], results


def ring_scatter(block, rows, fills=()):
    count = lax.axis_size("ep")
    half = count // 2
    middle = rows // 2
    fills = dict(fills)
    slot = {offset: j for j, offset in enumerate(ring_slots(count))}
    results = {}
    far = block(slot[half], results)
    onward, backward = far[:middle], far[middle:]
    for step in range(1, half + 1):
        sent = (onward, backward)
        received = (ring_shift(onward, 1), ring_shift(backward, -1))
        fill = fills[step](results) if step in fills else None
        (onward, backward), results[step] = fill_window(fill, sent, received)
        left = half - step
        if left:
            up, down = block(slot[left], results), block(slot[-left], results)
            if step == 1:
                onward = jnp.concatenate([add_low(onward, up[:middle]), up[middle:]], axis=0)
                backward = jnp.concatenate(
                    [down[:middle], add_low(backward, down[middle:])], axis=0
                )
            else:
                onward, backward = add_low(onward, up), add_low(backward, down)
    total = (
        block(slot[0], results).astype(wide_type)
        + onward.astype(wide_type)
        + backward.astype(wide_type)
    )
    return total, results


def add_low(left, right):
    return (left.astype(wide_type) + right.astype(wide_type)).astype(low_type)


def ring_place(member, count):
    return jnp.where(member % 2 == 0, member // 2, count - 1 - member // 2)


def ring_member(place, count):
    return jnp.where(place < count // 2, 2 * place, 2 * (count - 1 - place) + 1)


def ring_indices(device, count):
    place = ring_place(device, count)
    half = count // 2
    members = [ring_member((place + offset) % count, count) for offset in ring_slots(count)]
    slots = []
    for other in range(count):
        ahead = (ring_place(jnp.int32(other), count) - place) % count
        slot = jnp.where(ahead < half, 2 * ahead - 1, 2 * (count - ahead))
        slots.append(jnp.where(ahead == 0, 0, jnp.where(ahead == half, count - 1, slot)))
    return members, slots


def rep_exchange(values, distance):
    count = lax.axis_size("rep")
    return lax.ppermute(values, "rep", [(i, i ^ distance) for i in range(count)])


def rep_bit(distance):
    return (lax.axis_index("rep") // distance) % 2


def rep_gather(values):
    gathered = values[None]
    distance = lax.axis_size("rep") // 2
    while distance:
        other = rep_exchange(gathered, distance)
        mine_first = jnp.stack([gathered, other], axis=1)
        other_first = jnp.stack([other, gathered], axis=1)
        gathered = jnp.where(rep_bit(distance) == 0, mine_first, other_first)
        gathered = gathered.reshape((-1,) + values.shape)
        distance //= 2
    return gathered


def rep_scatter(values, axis):
    distance = 1
    count = lax.axis_size("rep")
    while distance < count:
        shape = values.shape
        pairs = values.reshape(shape[:axis] + (shape[axis] // 2, 2) + shape[axis + 1 :])
        bit = rep_bit(distance)
        keep = lax.dynamic_index_in_dim(pairs, bit, axis + 1, keepdims=False)
        send = lax.dynamic_index_in_dim(pairs, 1 - bit, axis + 1, keepdims=False)
        values = add_low(keep, rep_exchange(send, distance))
        distance *= 2
    return lax.index_in_dim(values, 0, axis, keepdims=False)


def rep_sum(values):
    distance = 1
    while distance < lax.axis_size("rep"):
        values = values + rep_exchange(values, distance)
        distance *= 2
    return values


def swap_all(values):
    return lax.all_to_all(values, "ep", split_axis=0, concat_axis=0, tiled=True)


def expert_kernel(rows_ref, gate_ref, up_ref, stream_ref, gates_ref, *refs):
    inner_ref, gback_ref, uback_ref, pair_ref = refs[-4:]
    expert, step = pl.program_id(0), pl.program_id(1)
    rows = rows_ref[...]
    gate_linear = jnp.dot(rows, gate_ref[0], preferred_element_type=wide_type)
    up_linear = jnp.dot(rows, up_ref[0], preferred_element_type=wide_type)
    stream = stream_ref[...]
    column = gates_ref[:, 0:1]
    for other in range(1, gates_ref.shape[1]):
        column = jnp.where(expert == other, gates_ref[:, other : other + 1], column)
    sigmoid_gate = jax.nn.sigmoid(gate_linear)
    silu_gate = gate_linear * sigmoid_gate
    inner = silu_gate * up_linear
    inner_ref[...] = (column * inner).astype(low_type)
    hidden_grad = column * stream
    gback_ref[...] = (
        hidden_grad * up_linear * sigmoid_gate * (1.0 + gate_linear * (1.0 - sigmoid_gate))
    ).astype(low_type)
    uback_ref[...] = (hidden_grad * silu_gate).astype(low_type)
    product = inner * stream
    lanes = pair_ref.shape[2]
    folded = product[:, :lanes]
    for start in range(lanes, product.shape[1], lanes):
        folded = folded + product[:, start : start + lanes]

    @pl.when(step == 0)
    def _():
        pair_ref[0] = folded

    @pl.when(step > 0)
    def _():
        pair_ref[0] += folded


def expert_pass(rows, gate_weight, up_weight, stream, gates, chunk, chunks, earlier=()):
    count, depth = rows.shape
    experts, _, hidden = gate_weight.shape
    width = 256
    steps = hidden // width
    weight = pl.BlockSpec((1, depth, width), lambda e, j: (e, 0, j))
    out = pl.BlockSpec((count, width), lambda e, j: (chunk, e * steps + j))
    return pl.pallas_call(
        expert_kernel,
        grid=(experts, steps),
        in_specs=[
            pl.BlockSpec((count, depth), lambda e, j: (0, 0)),
            weight,
            weight,
            pl.BlockSpec((count, width), lambda e, j: (0, e * steps + j)),
            pl.BlockSpec(gates.shape, lambda e, j: (0, 0)),
        ]
        + [pl.BlockSpec(memory_space=pl.ANY)] * len(earlier),
        out_specs=[out, out, out, pl.BlockSpec((1, count, 128), lambda e, j: (e, 0, 0))],
        out_shape=[jax.ShapeDtypeStruct((count * chunks, experts * hidden), low_type)] * 3
        + [jax.ShapeDtypeStruct((experts, count, 128), wide_type)],
        input_output_aliases={5 + i: i for i in range(len(earlier))},
        compiler_params=pltpu.CompilerParams(vmem_limit_bytes=56 << 20),
        cost_estimate=pl.CostEstimate(
            flops=4 * count * depth * experts * hidden,
            bytes_accessed=4 * depth * experts * hidden + 20 * count * depth,
            transcendentals=count * experts * hidden,
        ),
    )(rows, gate_weight, up_weight, stream, gates, *earlier)


def expert_back_kernel(gback_ref, uback_ref, gate_ref, up_ref, out_ref):
    experts, _, hidden = gate_ref.shape
    total = None
    for e in range(experts):
        for grad_ref, weight_ref in ((gback_ref, gate_ref), (uback_ref, up_ref)):
            term = mm(grad_ref[:, e * hidden : (e + 1) * hidden], weight_ref[e], 1, 1)
            total = term if total is None else total + term
    out_ref[...] = total.astype(low_type)


def expert_back(gback, uback, gate_weight, up_weight, chunk, chunks):
    count = gback.shape[0] // chunks
    experts, depth, hidden = gate_weight.shape
    width = 256
    whole = pl.BlockSpec((count, experts * hidden), lambda j: (chunk, 0))
    weight = pl.BlockSpec((experts, width, hidden), lambda j: (0, j, 0))
    return pl.pallas_call(
        expert_back_kernel,
        grid=(depth // width,),
        in_specs=[whole, whole, weight, weight],
        out_specs=pl.BlockSpec((count, width), lambda j: (0, j)),
        out_shape=jax.ShapeDtypeStruct((count, depth), low_type),
        compiler_params=pltpu.CompilerParams(vmem_limit_bytes=56 << 20),
        cost_estimate=pl.CostEstimate(
            flops=4 * count * depth * experts * hidden,
            bytes_accessed=4 * depth * experts * hidden + 6 * count * depth,
            transcendentals=0,
        ),
    )(gback, uback, gate_weight, up_weight)


def body(
    tokens,
    cotangent,
    seq_lengths,
    token_order,
    routes,
    slot_index,
    query_weight,
    key_weight,
    value_weight,
    output_weight,
    router_weight,
    prenorm_gain,
    querynorm_gain,
    keynorm_gain,
    postnorm_gain,
    gate_weight,
    up_weight,
    down_weight,
):
    group_count = lax.axis_size("ep")
    device = lax.axis_index("ep")
    row_count, model_width = tokens.shape
    head_dim = querynorm_gain.shape[0]
    width_here = model_width // group_count
    heads_here = width_here // head_dim
    experts_here = gate_weight.shape[0]
    expert_total = experts_here * group_count
    top_count = routes.shape[1]
    capacity = row_count * top_count * 5 // (4 * expert_total)
    group_rows = row_count * group_count
    sequence_count = seq_lengths.shape[1]
    score_scale = head_dim ** (-0.5)

    replica_count = lax.axis_size("rep")
    replica = lax.axis_index("rep")
    share = width_here // replica_count

    device_of_slot, slot_of_device = ring_indices(device, group_count)

    def reorder(blocks, index):
        return jnp.concatenate(
            [lax.dynamic_slice_in_dim(blocks, index[i], 1, 0) for i in range(group_count)], axis=0
        )

    group_order = reorder(token_order[0].reshape(group_count, row_count), device_of_slot)
    segment, position = row_meta(seq_lengths[0], group_order.reshape(group_rows))
    segment_own = segment[:row_count]
    valid_own = (segment_own < sequence_count).astype(wide_type)[:, None]
    valid_all = (segment < sequence_count).astype(wide_type)[:, None]

    expert_ids = jnp.arange(expert_total, dtype=jnp.int32)
    route_code = jnp.zeros((row_count, expert_total), jnp.int32)
    for column in range(top_count):
        hit = routes[:, column, None] == expert_ids[None, :]
        kept = (slot_index[:, column, None] < capacity).astype(jnp.int32)
        route_code = route_code + jnp.where(hit, 1 + kept, 0)
    small_sent = jnp.concatenate([route_code.astype(low_type), router_weight], axis=0)

    small_flat = small_sent.reshape(-1, head_dim)
    small_all = swap_all(
        jnp.broadcast_to(small_flat[None], (group_count,) + small_flat.shape)
    ).reshape(group_count, row_count + width_here, expert_total)
    code_all = reorder(small_all[:, :row_count], device_of_slot).reshape(
        group_rows, expert_total
    )
    full_router = small_all[:, row_count:].reshape(model_width, expert_total)

    projections = jnp.concatenate(
        [
            lax.dynamic_slice_in_dim(piece, replica * share, share, 0).reshape(
                share, group_count, width_here
            )
            for piece in (query_weight, key_weight, value_weight)
        ],
        axis=2,
    ).transpose(1, 0, 2)
    head_weight = (
        rep_gather(swap_all(projections))
        .transpose(1, 0, 2, 3)
        .reshape(model_width, 3 * width_here)
    )
    token_all = jnp.concatenate(ring_gather(tokens)[0], axis=0)
    column_share = model_width // replica_count
    output_share = gather_rows(
        lax.dynamic_slice_in_dim(output_weight, replica * column_share, column_share, 1)
    )

    def reorder_rows(rows, index):
        return reorder(
            rows.reshape(group_count, row_count, rows.shape[1]), index
        ).reshape(rows.shape)

    token_late, cot_own = lax.optimization_barrier((token_all, cotangent))
    token_all = token_late
    cot_ordered = gather_rows(cot_own)
    cot_all = reorder_rows(cot_ordered, device_of_slot)

    token_wide = token_all.astype(wide_type)
    inverse_all = inverse_rms(token_wide)
    first_all = (token_wide * inverse_all * prenorm_gain).astype(low_type)
    raw = mm(first_all, head_weight, 1, 0)
    cosine, sine_part = rope_tables(position, head_dim)

    hidden_here = down_weight.shape[1]
    flat_down = down_weight.reshape(experts_here * hidden_here, model_width)

    allowed = segment[:, None] == segment[None, :]

    def head_columns(values, block, head):
        start = block * width_here + head * head_dim
        return values[:, start : start + head_dim]

    kept_heads = []
    mixed_parts = []
    for head in range(heads_here):
        query_raw = head_columns(raw, 0, head)
        key_raw = head_columns(raw, 1, head)
        query_inverse = inverse_rms(query_raw)
        key_inverse = inverse_rms(key_raw)
        query_normed = query_raw * query_inverse * querynorm_gain
        key_normed = key_raw * key_inverse * keynorm_gain
        query_low = (query_normed * cosine + turn_half(query_normed) * sine_part).astype(
            low_type
        )
        key_low = (key_normed * cosine + turn_half(key_normed) * sine_part).astype(low_type)
        value_low = head_columns(raw, 2, head).astype(low_type)
        scores = jnp.where(allowed, mm(query_low, key_low, 1, 1) * score_scale, masked_value)
        top_score = jnp.max(scores, axis=-1, keepdims=True)
        powers = jnp.exp(scores - top_score)
        log_total = top_score + jnp.log(jnp.sum(powers, axis=-1, keepdims=True))
        weights_low = jnp.exp(scores - log_total).astype(low_type)
        mixed_parts.append(mm(weights_low, value_low, 1, 0).astype(low_type))
        kept_heads.append(
            (query_raw, key_raw, query_inverse, key_inverse, query_low, key_low, value_low, log_total)
        )
    mixed_low = jnp.concatenate(mixed_parts, axis=1)

    mixed_ordered = reorder_rows(mixed_low, slot_of_device)
    output_pieces = {0: output_share}
    distance = replica_count // 2
    while distance:
        for j in list(output_pieces):
            output_pieces[j ^ distance] = rep_exchange(output_pieces[j], distance)
        if distance == replica_count // 2:
            output_pieces[distance], mixed_ordered = tie(output_pieces[distance], mixed_ordered)
        distance //= 2
    mixed_own = (
        swap_all(mixed_ordered.reshape(group_count, row_count, width_here))
        .transpose(1, 0, 2)
        .reshape(row_count, model_width)
    )
    attention = jnp.zeros((row_count, model_width), wide_type)
    for j, piece in output_pieces.items():
        attention = lax.dynamic_update_slice_in_dim(
            attention, mm(mixed_own, piece, 1, 0), (replica ^ j) * column_share, 1
        )
    residual = tokens.astype(wide_type) + attention
    inverse_two = inverse_rms(residual)
    second_input = (residual * inverse_two * postnorm_gain).astype(low_type)

    def gate_table(rows, code):
        logits = mm(rows, full_router, 1, 0)
        shifted = jnp.where(code > 0, logits, masked_value)
        powers = jnp.exp(shifted - jnp.max(shifted, axis=1, keepdims=True))
        return powers / jnp.sum(powers, axis=1, keepdims=True)

    chunks = 2
    chunk_rows = group_rows // chunks
    kept_all = jnp.where(code_all > 1, valid_all, 0.0)
    kept_here = lax.dynamic_slice_in_dim(kept_all, device * experts_here, experts_here, 1)

    def chunk_of(array, chunk):
        return array[chunk * chunk_rows : (chunk + 1) * chunk_rows]

    def stream_of(chunk):
        return (lambda cot_part: (mm(cot_part, flat_down, 1, 1),)), (chunk_of(cot_all, chunk),)

    def expert_chunk(chunk, rows, stream, *earlier):
        gates = gate_table(rows, chunk_of(code_all, chunk)) * chunk_of(kept_all, chunk)
        gates_here = lax.dynamic_slice_in_dim(gates, device * experts_here, experts_here, 1)
        return expert_pass(
            rows, gate_weight, up_weight, stream, gates_here, chunk, chunks, earlier
        )

    blocks_here = group_count // chunks

    def first_chunk(blocks, results):
        rows = jnp.concatenate(blocks[:blocks_here], axis=0)
        return (
            lambda stream, rows: (rows,) + tuple(expert_chunk(0, rows, stream))
        ), (results[1][0], rows)

    blocks, results = ring_gather(
        second_input,
        {
            1: lambda blocks, results: stream_of(0),
            2: lambda blocks, results: stream_of(1),
            3: first_chunk,
        },
    )
    rows_first, *earlier, pair_first = results[3]
    rows_last = jnp.concatenate(blocks[blocks_here:], axis=0)
    inner_all, gback_all, uback_all, pair_last = expert_chunk(
        1, rows_last, results[2][0], *earlier
    )
    second_all = jnp.concatenate([rows_first, rows_last], axis=0)
    back_last = expert_back(gback_all, uback_all, gate_weight, up_weight, 1, chunks)

    def back_first(results):
        return (
            lambda gback, uback: (
                expert_back(gback, uback, gate_weight, up_weight, 0, chunks),
            )
        ), (gback_all, uback_all)

    def back_block(slot, results):
        part = back_last if slot >= blocks_here else results[1][0]
        start = (slot % blocks_here) * row_count
        return part[start : start + row_count]

    pair_lanes = jnp.concatenate([pair_first, pair_last], axis=1)
    pair_sent = (kept_here * jnp.sum(pair_lanes, axis=2).transpose(1, 0)).reshape(
        group_count, row_count, experts_here
    )
    code_own = route_code
    gates_own = gate_table(second_input, code_own)

    def grad_of(left, right):
        return mm(left, right, 0, 0).astype(low_type)

    def down_fill(results):
        return (
            lambda inner, pair: (grad_of(inner, cot_all), swap_all(reorder(pair, slot_of_device)))
        ), (inner_all, pair_sent)

    def gate_fill(results):
        def work(gback, pair):
            pair_grad = pair.transpose(1, 0, 2).reshape(row_count, expert_total)
            chosen_grad = gates_own * (
                pair_grad - jnp.sum(gates_own * pair_grad, axis=1, keepdims=True)
            )
            logits_grad = jnp.where(code_own > 0, chosen_grad, 0.0).astype(low_type)
            router_back = mm(logits_grad, full_router, 1, 1)
            return grad_of(second_all, gback), logits_grad, router_back

        return work, (gback_all, results[2][1])

    def up_fill(results):
        return (lambda uback: (grad_of(second_all, uback),)), (uback_all,)

    second_scattered, results = ring_scatter(
        back_block, row_count, {1: back_first, 2: down_fill, 3: gate_fill, 4: up_fill}
    )
    down_part = results[2][0]
    gate_part, logits_grad, router_back = results[3]
    up_part = results[4][0]
    router_part = mm(second_input, logits_grad, 0, 0)
    second_grad = router_back + second_scattered
    upstream = valid_own * cotangent.astype(wide_type)
    post_back, postnorm_part = norm_backward(residual, inverse_two, postnorm_gain, second_grad)
    residual_grad = upstream + post_back
    attention_low = residual_grad.astype(low_type)
    attention_all = gather_rows(attention_low)
    mixed_grad_own = jnp.zeros((row_count, model_width), wide_type)
    for j, piece in output_pieces.items():
        mixed_grad_own = mixed_grad_own + mm(
            lax.dynamic_slice_in_dim(
                attention_low, (replica ^ j) * column_share, column_share, 1
            ),
            piece,
            1,
            1,
        )
    swap_sent = (
        mixed_grad_own.astype(low_type)
        .reshape(row_count, group_count, width_here)
        .transpose(1, 0, 2)
    )
    mixed_swapped, (mixture_part,) = fill_window(
        ((lambda inner: (mm(inner, flat_down, 1, 0).astype(low_type),)), (inner_all,)),
        swap_sent,
        swap_all(swap_sent),
    )
    mixed_grad = reorder_rows(mixed_swapped.reshape(group_rows, width_here), device_of_slot)

    def mixture_block(slot, results):
        return mixture_part[slot * row_count : (slot + 1) * row_count]

    def head_backward(head, grad_head):
        (query_raw, key_raw, query_inverse, key_inverse, query_low, key_low, value_low, log_total) = (
            kept_heads[head]
        )
        scores = jnp.where(allowed, mm(query_low, key_low, 1, 1) * score_scale, masked_value)
        weights = jnp.exp(scores - log_total)
        weight_grad = mm(grad_head, value_low, 1, 1)
        row_dot = jnp.sum(weights * weight_grad, axis=-1, keepdims=True)
        score_grad = (weights * (weight_grad - row_dot)).astype(low_type)
        query_back = mm(score_grad, key_low, 1, 0) * score_scale
        key_back = mm(score_grad, query_low, 0, 0) * score_scale
        value_back = mm(weights.astype(low_type), grad_head, 0, 0)
        query_unturned = query_back * cosine + turn_back(query_back * sine_part)
        key_unturned = key_back * cosine + turn_back(key_back * sine_part)
        query_before, query_gain_part = norm_backward(
            query_raw, query_inverse, querynorm_gain, query_unturned
        )
        key_before, key_gain_part = norm_backward(
            key_raw, key_inverse, keynorm_gain, key_unturned
        )
        return (
            query_before.astype(low_type),
            key_before.astype(low_type),
            value_back.astype(low_type),
            jnp.sum(query_gain_part, axis=0),
            jnp.sum(key_gain_part, axis=0),
        )

    def head_fill(head):
        def fill(results):
            start = head * head_dim
            return functools.partial(head_backward, head), (
                mixed_grad[:, start : start + head_dim],
            )

        return fill

    mixture, results = ring_scatter(
        mixture_block, row_count, {2 + head: head_fill(head) for head in range(heads_here)}
    )
    layer_out = (valid_own * (residual + mixture)).astype(low_type)
    head_results = [results[2 + head] for head in range(heads_here)]
    sent = jnp.concatenate(
        [head_results[head][part] for part in range(3) for head in range(heads_here)], axis=1
    )
    querynorm_part = sum(result[3] for result in head_results)
    keynorm_part = sum(result[4] for result in head_results)
    first_part = mm(sent, head_weight, 1, 1)
    prenorm_part = jnp.sum(first_part * token_wide * inverse_all, axis=0)
    first_low = first_part.astype(low_type)

    def product_fill(results):
        return (
            lambda first, sent, mixed, attention: (grad_of(first, sent), grad_of(mixed, attention))
        ), (first_all, sent, mixed_ordered, attention_all)

    first_grad, results = ring_scatter(
        lambda slot, results: first_low[slot * row_count : (slot + 1) * row_count],
        row_count,
        {1: product_fill},
    )
    head_part, output_part = results[1]
    head_rows = swap_all(
        rep_scatter(head_part.reshape(group_count, replica_count, share, 3 * width_here), 1)
    )
    head_rows = rep_gather(
        head_rows.reshape(group_count, share, 3, width_here)
        .transpose(2, 1, 0, 3)
        .reshape(3, share, model_width)
    )
    query_grad, key_grad, value_grad = (
        head_rows[:, block].reshape(width_here, model_width).astype(wide_type)
        for block in range(3)
    )
    output_grad = (
        rep_gather(rep_scatter(output_part.reshape(replica_count, share, model_width), 0))
        .reshape(width_here, model_width)
        .astype(wide_type)
    )

    first_grad, query_grad, key_grad, value_grad, output_grad = tie(
        first_grad, query_grad, key_grad, value_grad, output_grad
    )
    token_own = tokens.astype(wide_type)
    inverse_one = inverse_rms(token_own)
    pre_back, _ = norm_backward(token_own, inverse_one, prenorm_gain, first_grad)
    token_grad = residual_grad + pre_back

    def small_sum(parts):
        flat = jnp.concatenate([part.reshape(group_count, -1) for part in parts], axis=1)
        total = rep_sum(jnp.sum(swap_all(flat), axis=0))
        pieces, start = [], 0
        for part in parts:
            size = part.size // group_count
            pieces.append(total[start : start + size])
            start += size
        return pieces

    router_grad, postnorm_grad = small_sum([router_part, jnp.sum(postnorm_part, axis=0)])
    router_grad = router_grad.reshape(width_here, expert_total)
    prenorm_grad, querynorm_grad, keynorm_grad = small_sum(
        [prenorm_part, querynorm_part, keynorm_part]
    )

    down_total = lax.psum_scatter(
        down_part.reshape(experts_here, hidden_here, model_width),
        "rep",
        scatter_dimension=1,
        tiled=True,
    ).astype(wide_type)
    gate_total, up_total = (
        jnp.stack(
            [
                total[:, e * hidden_here : (e + 1) * hidden_here].astype(wide_type)
                for e in range(experts_here)
            ]
        )
        for total in (
            lax.psum_scatter(part, "rep", scatter_dimension=0, tiled=True)
            for part in (gate_part, up_part)
        )
    )
    return (
        layer_out,
        token_grad,
        query_grad,
        key_grad,
        value_grad,
        output_grad,
        router_grad,
        prenorm_grad,
        querynorm_grad,
        keynorm_grad,
        postnorm_grad,
        gate_total,
        up_total,
        down_total,
    )


def solution(mesh):
    in_specs = (
        P(("rep", "ep"), None),
        P(("rep", "ep"), None),
        P("rep", None),
        P("rep", None),
        P(("rep", "ep"), None),
        P(("rep", "ep"), None),
        P("ep", None),
        P("ep", None),
        P("ep", None),
        P("ep", None),
        P("ep", None),
        P(),
        P(),
        P(),
        P(),
        P("ep", None, None),
        P("ep", None, None),
        P("ep", None, None),
    )
    out_specs = (
        P(("rep", "ep"), None),
        P(("rep", "ep"), None),
        P("ep", None),
        P("ep", None),
        P("ep", None),
        P("ep", None),
        P("ep", None),
        P("ep"),
        P("ep"),
        P("ep"),
        P("ep"),
        P("ep", "rep", None),
        P("ep", "rep", None),
        P("ep", "rep", None),
    )
    return jax.shard_map(body, mesh=mesh, in_specs=in_specs, out_specs=out_specs, check_vma=False)
```

```python
import jax
import jax.numpy as jnp
from jax import lax
from jax.experimental import pallas as pl
from jax.experimental.pallas import tpu as pltpu
from jax.sharding import PartitionSpec as P

epsilon = 1e-05
rope_base = 10000.0
masked_value = -1e30
low_type = jnp.bfloat16
wide_type = jnp.float32


def inverse_rms(values):
    return lax.rsqrt(jnp.mean(values * values, axis=-1, keepdims=True) + epsilon)


def norm_backward(values, inverse, gain_vector, upstream):
    scaled = upstream * gain_vector
    inner_mean = jnp.mean(scaled * values, axis=-1, keepdims=True)
    result = inverse * scaled - values * (inverse * inverse * inverse) * inner_mean
    return (result, upstream * values * inverse)


def rope_tables(position, dimension):
    halfway = dimension // 2
    indices = jnp.arange(halfway, dtype=wide_type)
    frequency = rope_base ** (-2.0 * indices / dimension)
    angles = position.astype(wide_type)[:, None] * frequency[None, :]
    cosine = jnp.cos(angles)
    sine_part = jnp.sin(angles)
    return (
        jnp.concatenate([cosine, cosine], axis=-1),
        jnp.concatenate([sine_part, sine_part], axis=-1),
    )


def turn_half(values):
    halfway = values.shape[-1] // 2
    return jnp.concatenate([-values[..., halfway:], values[..., :halfway]], axis=-1)


def turn_back(values):
    halfway = values.shape[-1] // 2
    return jnp.concatenate([values[..., halfway:], -values[..., :halfway]], axis=-1)


def row_meta(lengths, group_order):
    boundary = jnp.cumsum(lengths)
    passed = (group_order[:, None] >= boundary[None, :]).astype(jnp.int32)
    segment = jnp.sum(passed, axis=1)
    offset = jnp.sum(passed * lengths[None, :], axis=1)
    return (segment, group_order - offset)


def mm(left, right, left_dim, right_dim):
    return lax.dot_general(
        left,
        right,
        (((left_dim,), (right_dim,)), ((), ())),
        preferred_element_type=wide_type,
    )


def gather_rows(values):
    return lax.all_gather(values, "ep", axis=0, tiled=True)


def ring_order(count):
    return [i for i in range(count) if i % 2 == 0] + [i for i in reversed(range(count)) if i % 2]


def ring_slots(count):
    half = count // 2
    offsets = [0]
    for step in range(1, half):
        offsets += [step, -step]
    return offsets + [half]


def ring_shift(values, direction):
    order = ring_order(lax.axis_size("ep"))
    count = len(order)
    pairs = [(order[i], order[(i + direction) % count]) for i in range(count)]
    return lax.ppermute(values, "ep", pairs)


def tie(*arrays):
    return lax.optimization_barrier(arrays)


def fill_window(fill, sent, received):
    if fill is None:
        return received, None
    work, inputs = fill
    inputs, _ = lax.optimization_barrier((inputs, sent))
    return lax.optimization_barrier((received, work(*inputs)))


def ring_gather(values, fills=()):
    half = lax.axis_size("ep") // 2
    middle = values.shape[0] // 2
    fills = dict(fills)
    onward, backward = values, values
    blocks, results = [values], {}
    for step in range(1, half + 1):
        if step == half:
            sent = (onward[:middle], backward[middle:])
        else:
            sent = (onward, backward)
        received = (ring_shift(sent[0], 1), ring_shift(sent[1], -1))
        fill = fills[step](blocks, results) if step in fills else None
        (onward, backward), results[step] = fill_window(fill, sent, received)
        if step < half:
            blocks = blocks + [backward, onward]
    return blocks + [jnp.concatenate([onward, backward], axis=0)], results


class RingSum:
    def __init__(self, block, rows):
        count = lax.axis_size("ep")
        self.block, self.middle, self.step = block, rows // 2, 0
        self.half = count // 2
        self.slot = {offset: j for j, offset in enumerate(ring_slots(count))}
        far = block(self.slot[self.half])
        self.sent = (far[: self.middle], far[self.middle :])

    def start(self):
        self.received = (ring_shift(self.sent[0], 1), ring_shift(self.sent[1], -1))

    def finish(self):
        self.step += 1
        onward, backward = self.received
        left = self.half - self.step
        middle = self.middle
        if left:
            up, down = self.block(self.slot[left]), self.block(self.slot[-left])
            if self.step == 1:
                onward = jnp.concatenate([add_low(onward, up[:middle]), up[middle:]], axis=0)
                backward = jnp.concatenate(
                    [down[:middle], add_low(backward, down[middle:])], axis=0
                )
            else:
                onward, backward = add_low(onward, up), add_low(backward, down)
        self.sent = (onward, backward)

    def total(self):
        return (
            self.block(self.slot[0]).astype(wide_type)
            + self.sent[0].astype(wide_type)
            + self.sent[1].astype(wide_type)
        )


def window(rings, work, *inputs):
    for ring in rings:
        ring.start()
    inputs, _ = tie(inputs, [ring.sent for ring in rings])
    received, results = tie([ring.received for ring in rings], work(*inputs))
    for ring, pair in zip(rings, received):
        ring.received = pair
        ring.finish()
    return results


def add_low(left, right):
    return (left.astype(wide_type) + right.astype(wide_type)).astype(low_type)


def ring_place(member, count):
    return jnp.where(member % 2 == 0, member // 2, count - 1 - member // 2)


def ring_member(place, count):
    return jnp.where(place < count // 2, 2 * place, 2 * (count - 1 - place) + 1)


def ring_indices(device, count):
    place = ring_place(device, count)
    half = count // 2
    members = [ring_member((place + offset) % count, count) for offset in ring_slots(count)]
    slots = []
    for other in range(count):
        ahead = (ring_place(jnp.int32(other), count) - place) % count
        slot = jnp.where(ahead < half, 2 * ahead - 1, 2 * (count - ahead))
        slots.append(jnp.where(ahead == 0, 0, jnp.where(ahead == half, count - 1, slot)))
    return members, slots


def rep_exchange(values, distance):
    count = lax.axis_size("rep")
    return lax.ppermute(values, "rep", [(i, i ^ distance) for i in range(count)])


def rep_bit(distance):
    return (lax.axis_index("rep") // distance) % 2


def rep_gather(values):
    gathered = values[None]
    distance = lax.axis_size("rep") // 2
    while distance:
        other = rep_exchange(gathered, distance)
        mine_first = jnp.stack([gathered, other], axis=1)
        other_first = jnp.stack([other, gathered], axis=1)
        gathered = jnp.where(rep_bit(distance) == 0, mine_first, other_first)
        gathered = gathered.reshape((-1,) + values.shape)
        distance //= 2
    return gathered


def rep_scatter(values, axis):
    distance = 1
    count = lax.axis_size("rep")
    while distance < count:
        shape = values.shape
        pairs = values.reshape(shape[:axis] + (shape[axis] // 2, 2) + shape[axis + 1 :])
        bit = rep_bit(distance)
        keep = lax.dynamic_index_in_dim(pairs, bit, axis + 1, keepdims=False)
        send = lax.dynamic_index_in_dim(pairs, 1 - bit, axis + 1, keepdims=False)
        values = add_low(keep, rep_exchange(send, distance))
        distance *= 2
    return lax.index_in_dim(values, 0, axis, keepdims=False)


def rep_sum(values):
    distance = 1
    while distance < lax.axis_size("rep"):
        values = values + rep_exchange(values, distance)
        distance *= 2
    return values


def swap_all(values):
    return lax.all_to_all(values, "ep", split_axis=0, concat_axis=0, tiled=True)


def expert_kernel(rows_ref, gate_ref, up_ref, stream_ref, gates_ref, *refs):
    inner_ref, gback_ref, uback_ref, pair_ref = refs[-4:]
    expert, step = pl.program_id(0), pl.program_id(1)
    rows = rows_ref[...]
    gate_linear = jnp.dot(rows, gate_ref[0], preferred_element_type=wide_type)
    up_linear = jnp.dot(rows, up_ref[0], preferred_element_type=wide_type)
    stream = stream_ref[...]
    column = gates_ref[:, 0:1]
    for other in range(1, gates_ref.shape[1]):
        column = jnp.where(expert == other, gates_ref[:, other : other + 1], column)
    sigmoid_gate = jax.nn.sigmoid(gate_linear)
    silu_gate = gate_linear * sigmoid_gate
    inner = silu_gate * up_linear
    inner_ref[...] = (column * inner).astype(low_type)
    hidden_grad = column * stream
    gback_ref[...] = (
        hidden_grad * up_linear * sigmoid_gate * (1.0 + gate_linear * (1.0 - sigmoid_gate))
    ).astype(low_type)
    uback_ref[...] = (hidden_grad * silu_gate).astype(low_type)
    product = inner * stream
    lanes = pair_ref.shape[2]
    folded = product[:, :lanes]
    for start in range(lanes, product.shape[1], lanes):
        folded = folded + product[:, start : start + lanes]

    @pl.when(step == 0)
    def _():
        pair_ref[0] = folded

    @pl.when(step > 0)
    def _():
        pair_ref[0] += folded


def expert_pass(rows, gate_weight, up_weight, stream, gates, chunk, chunks, earlier=()):
    count, depth = rows.shape
    experts, _, hidden = gate_weight.shape
    width = 256
    steps = hidden // width
    weight = pl.BlockSpec((1, depth, width), lambda e, j: (e, 0, j))
    out = pl.BlockSpec((count, width), lambda e, j: (chunk, e * steps + j))
    return pl.pallas_call(
        expert_kernel,
        grid=(experts, steps),
        in_specs=[
            pl.BlockSpec((count, depth), lambda e, j: (0, 0)),
            weight,
            weight,
            pl.BlockSpec((count, width), lambda e, j: (0, e * steps + j)),
            pl.BlockSpec(gates.shape, lambda e, j: (0, 0)),
        ]
        + [pl.BlockSpec(memory_space=pl.ANY)] * len(earlier),
        out_specs=[out, out, out, pl.BlockSpec((1, count, 128), lambda e, j: (e, 0, 0))],
        out_shape=[jax.ShapeDtypeStruct((count * chunks, experts * hidden), low_type)] * 3
        + [jax.ShapeDtypeStruct((experts, count, 128), wide_type)],
        input_output_aliases={5 + i: i for i in range(len(earlier))},
        compiler_params=pltpu.CompilerParams(vmem_limit_bytes=56 << 20),
        cost_estimate=pl.CostEstimate(
            flops=4 * count * depth * experts * hidden,
            bytes_accessed=4 * depth * experts * hidden + 20 * count * depth,
            transcendentals=count * experts * hidden,
        ),
    )(rows, gate_weight, up_weight, stream, gates, *earlier)


def expert_back_kernel(gback_ref, uback_ref, gate_ref, up_ref, out_ref):
    experts, _, hidden = gate_ref.shape
    total = None
    for e in range(experts):
        for grad_ref, weight_ref in ((gback_ref, gate_ref), (uback_ref, up_ref)):
            term = mm(grad_ref[:, e * hidden : (e + 1) * hidden], weight_ref[e], 1, 1)
            total = term if total is None else total + term
    out_ref[...] = total.astype(low_type)


def expert_back(gback, uback, gate_weight, up_weight, chunk, chunks):
    count = gback.shape[0] // chunks
    experts, depth, hidden = gate_weight.shape
    width = 256
    whole = pl.BlockSpec((count, experts * hidden), lambda j: (chunk, 0))
    weight = pl.BlockSpec((experts, width, hidden), lambda j: (0, j, 0))
    return pl.pallas_call(
        expert_back_kernel,
        grid=(depth // width,),
        in_specs=[whole, whole, weight, weight],
        out_specs=pl.BlockSpec((count, width), lambda j: (0, j)),
        out_shape=jax.ShapeDtypeStruct((count, depth), low_type),
        compiler_params=pltpu.CompilerParams(vmem_limit_bytes=56 << 20),
        cost_estimate=pl.CostEstimate(
            flops=4 * count * depth * experts * hidden,
            bytes_accessed=4 * depth * experts * hidden + 6 * count * depth,
            transcendentals=0,
        ),
    )(gback, uback, gate_weight, up_weight)


def body(
    tokens,
    cotangent,
    seq_lengths,
    token_order,
    routes,
    slot_index,
    query_weight,
    key_weight,
    value_weight,
    output_weight,
    router_weight,
    prenorm_gain,
    querynorm_gain,
    keynorm_gain,
    postnorm_gain,
    gate_weight,
    up_weight,
    down_weight,
):
    group_count = lax.axis_size("ep")
    device = lax.axis_index("ep")
    row_count, model_width = tokens.shape
    head_dim = querynorm_gain.shape[0]
    width_here = model_width // group_count
    heads_here = width_here // head_dim
    experts_here = gate_weight.shape[0]
    expert_total = experts_here * group_count
    top_count = routes.shape[1]
    capacity = row_count * top_count * 5 // (4 * expert_total)
    group_rows = row_count * group_count
    sequence_count = seq_lengths.shape[1]
    score_scale = head_dim ** (-0.5)

    replica_count = lax.axis_size("rep")
    replica = lax.axis_index("rep")
    share = width_here // replica_count

    device_of_slot, slot_of_device = ring_indices(device, group_count)

    def reorder(blocks, index):
        return jnp.concatenate(
            [lax.dynamic_slice_in_dim(blocks, index[i], 1, 0) for i in range(group_count)], axis=0
        )

    group_order = reorder(token_order[0].reshape(group_count, row_count), device_of_slot)
    segment, position = row_meta(seq_lengths[0], group_order.reshape(group_rows))
    segment_own = segment[:row_count]
    valid_own = (segment_own < sequence_count).astype(wide_type)[:, None]
    valid_all = (segment < sequence_count).astype(wide_type)[:, None]

    expert_ids = jnp.arange(expert_total, dtype=jnp.int32)
    route_code = jnp.zeros((row_count, expert_total), jnp.int32)
    for column in range(top_count):
        hit = routes[:, column, None] == expert_ids[None, :]
        kept = (slot_index[:, column, None] < capacity).astype(jnp.int32)
        route_code = route_code + jnp.where(hit, 1 + kept, 0)
    small_sent = jnp.concatenate([route_code.astype(low_type), router_weight], axis=0)

    small_flat = small_sent.reshape(-1, head_dim)
    small_all = swap_all(
        jnp.broadcast_to(small_flat[None], (group_count,) + small_flat.shape)
    ).reshape(group_count, row_count + width_here, expert_total)
    code_all = reorder(small_all[:, :row_count], device_of_slot).reshape(
        group_rows, expert_total
    )
    full_router = small_all[:, row_count:].reshape(model_width, expert_total)

    projections = jnp.concatenate(
        [
            lax.dynamic_slice_in_dim(piece, replica * share, share, 0).reshape(
                share, group_count, width_here
            )
            for piece in (query_weight, key_weight, value_weight)
        ],
        axis=2,
    ).transpose(1, 0, 2)
    head_weight = (
        rep_gather(swap_all(projections))
        .transpose(1, 0, 2, 3)
        .reshape(model_width, 3 * width_here)
    )
    token_all = jnp.concatenate(ring_gather(tokens)[0], axis=0)
    column_share = model_width // replica_count
    halves = 2 if column_share % 256 == 0 else 1
    piece_width = column_share // halves
    token_all, output_own = tie(token_all, output_weight)
    output_shares = [
        gather_rows(
            lax.dynamic_slice_in_dim(
                output_own, replica * column_share + half * piece_width, piece_width, 1
            )
        )
        for half in range(halves)
    ]

    def reorder_rows(rows, index):
        return reorder(
            rows.reshape(group_count, row_count, rows.shape[1]), index
        ).reshape(rows.shape)

    output_shares[-1], cot_own = tie(output_shares[-1], cotangent)
    cot_ordered = gather_rows(cot_own)
    cot_all = reorder_rows(cot_ordered, device_of_slot)

    token_wide = token_all.astype(wide_type)
    inverse_all = inverse_rms(token_wide)
    first_all = (token_wide * inverse_all * prenorm_gain).astype(low_type)
    raw = mm(first_all, head_weight, 1, 0)
    cosine, sine_part = rope_tables(position, head_dim)

    hidden_here = down_weight.shape[1]
    flat_down = down_weight.reshape(experts_here * hidden_here, model_width)

    allowed = segment[:, None] == segment[None, :]

    def head_columns(values, block, head):
        start = block * width_here + head * head_dim
        return values[:, start : start + head_dim]

    kept_heads = []
    mixed_parts = []
    for head in range(heads_here):
        query_raw = head_columns(raw, 0, head)
        key_raw = head_columns(raw, 1, head)
        query_inverse = inverse_rms(query_raw)
        key_inverse = inverse_rms(key_raw)
        query_normed = query_raw * query_inverse * querynorm_gain
        key_normed = key_raw * key_inverse * keynorm_gain
        query_low = (query_normed * cosine + turn_half(query_normed) * sine_part).astype(
            low_type
        )
        key_low = (key_normed * cosine + turn_half(key_normed) * sine_part).astype(low_type)
        value_low = head_columns(raw, 2, head).astype(low_type)
        scores = jnp.where(allowed, mm(query_low, key_low, 1, 1) * score_scale, masked_value)
        top_score = jnp.max(scores, axis=-1, keepdims=True)
        powers = jnp.exp(scores - top_score)
        log_total = top_score + jnp.log(jnp.sum(powers, axis=-1, keepdims=True))
        weights_low = jnp.exp(scores - log_total).astype(low_type)
        mixed_parts.append(mm(weights_low, value_low, 1, 0).astype(low_type))
        kept_heads.append(
            (query_raw, key_raw, query_inverse, key_inverse, query_low, key_low, value_low, log_total)
        )
    mixed_low = jnp.concatenate(mixed_parts, axis=1)

    mixed_ordered = reorder_rows(mixed_low, slot_of_device)
    output_pieces = {(0, half): output_shares[half] for half in range(halves)}
    distance = replica_count // 2
    while distance:
        for j, half in list(output_pieces):
            output_pieces[j ^ distance, half] = rep_exchange(output_pieces[j, half], distance)
        if distance == replica_count // 2:
            for half in range(halves):
                output_pieces[distance, half], mixed_ordered = tie(
                    output_pieces[distance, half], mixed_ordered
                )
        distance //= 2

    def piece_start(j, half):
        return (replica ^ j) * column_share + half * piece_width

    mixed_own = (
        swap_all(mixed_ordered.reshape(group_count, row_count, width_here))
        .transpose(1, 0, 2)
        .reshape(row_count, model_width)
    )
    attention = jnp.zeros((row_count, model_width), wide_type)
    for place, piece in output_pieces.items():
        attention = lax.dynamic_update_slice_in_dim(
            attention, mm(mixed_own, piece, 1, 0), piece_start(*place), 1
        )
    residual = tokens.astype(wide_type) + attention
    inverse_two = inverse_rms(residual)
    second_input = (residual * inverse_two * postnorm_gain).astype(low_type)

    def gate_table(rows, code):
        logits = mm(rows, full_router, 1, 0)
        shifted = jnp.where(code > 0, logits, masked_value)
        powers = jnp.exp(shifted - jnp.max(shifted, axis=1, keepdims=True))
        return powers / jnp.sum(powers, axis=1, keepdims=True)

    chunks = 2
    chunk_rows = group_rows // chunks
    kept_all = jnp.where(code_all > 1, valid_all, 0.0)
    kept_here = lax.dynamic_slice_in_dim(kept_all, device * experts_here, experts_here, 1)

    def chunk_of(array, chunk):
        return array[chunk * chunk_rows : (chunk + 1) * chunk_rows]

    def stream_of(chunk):
        return (lambda cot_part: (mm(cot_part, flat_down, 1, 1),)), (chunk_of(cot_all, chunk),)

    def expert_chunk(chunk, rows, stream, *earlier):
        gates = gate_table(rows, chunk_of(code_all, chunk)) * chunk_of(kept_all, chunk)
        gates_here = lax.dynamic_slice_in_dim(gates, device * experts_here, experts_here, 1)
        return expert_pass(
            rows, gate_weight, up_weight, stream, gates_here, chunk, chunks, earlier
        )

    blocks_here = group_count // chunks

    def first_chunk(blocks, results):
        rows = jnp.concatenate(blocks[:blocks_here], axis=0)
        return (
            lambda stream, rows: (rows,) + tuple(expert_chunk(0, rows, stream))
        ), (results[1][0], rows)

    blocks, results = ring_gather(
        second_input,
        {
            1: lambda blocks, results: stream_of(0),
            2: lambda blocks, results: stream_of(1),
            3: first_chunk,
        },
    )
    rows_first, *earlier, pair_first = results[3]
    rows_last = jnp.concatenate(blocks[blocks_here:], axis=0)
    inner_all, gback_all, uback_all, pair_last = expert_chunk(
        1, rows_last, results[2][0], *earlier
    )
    second_all = jnp.concatenate([rows_first, rows_last], axis=0)
    back_last = expert_back(gback_all, uback_all, gate_weight, up_weight, 1, chunks)

    back_parts = {1: back_last}

    def back_block(slot):
        start = (slot % blocks_here) * row_count
        return back_parts[slot // blocks_here][start : start + row_count]

    def grad_of(left, right):
        return mm(left, right, 0, 0).astype(low_type)

    pair_lanes = jnp.concatenate([pair_first, pair_last], axis=1)
    pair_sent = (kept_here * jnp.sum(pair_lanes, axis=2).transpose(1, 0)).reshape(
        group_count, row_count, experts_here
    )
    code_own = route_code
    gates_own = gate_table(second_input, code_own)

    second_ring = RingSum(back_block, row_count)
    second_ring.start()
    (gback_tied, uback_tied), _ = tie((gback_all, uback_all), second_ring.sent)
    second_ring.received, back_parts[0] = tie(
        second_ring.received,
        expert_back(gback_tied, uback_tied, gate_weight, up_weight, 0, chunks),
    )
    second_ring.finish()

    def mixture_work(inner, pair):
        return (
            mm(inner, flat_down, 1, 0).astype(low_type),
            swap_all(reorder(pair, slot_of_device)),
        )

    mixture_part, pair_grad = window([second_ring], mixture_work, inner_all, pair_sent)
    mixture_ring = RingSum(
        lambda slot: mixture_part[slot * row_count : (slot + 1) * row_count], row_count
    )

    def down_work(inner, pair):
        pair_grad = pair.transpose(1, 0, 2).reshape(row_count, expert_total)
        chosen_grad = gates_own * (
            pair_grad - jnp.sum(gates_own * pair_grad, axis=1, keepdims=True)
        )
        logits_grad = jnp.where(code_own > 0, chosen_grad, 0.0).astype(low_type)
        router_back = mm(logits_grad, full_router, 1, 1)
        router_part = mm(second_input, logits_grad, 0, 0)
        return grad_of(inner, cot_all), router_back, router_part

    down_part, router_back, router_part = window(
        [second_ring, mixture_ring], down_work, inner_all, pair_grad
    )
    gate_part = window(
        [second_ring, mixture_ring], lambda gback: grad_of(second_all, gback), gback_all
    )
    second_scattered = second_ring.total()
    second_grad = router_back + second_scattered
    upstream = valid_own * cotangent.astype(wide_type)
    def residual_work(second_grad):
        post_back, postnorm_part = norm_backward(
            residual, inverse_two, postnorm_gain, second_grad
        )
        residual_grad = upstream + post_back
        attention_low = residual_grad.astype(low_type)
        mixed_grad_own = jnp.zeros((row_count, model_width), wide_type)
        for place, piece in output_pieces.items():
            mixed_grad_own = mixed_grad_own + mm(
                lax.dynamic_slice_in_dim(attention_low, piece_start(*place), piece_width, 1),
                piece,
                1,
                1,
            )
        swap_sent = (
            mixed_grad_own.astype(low_type)
            .reshape(row_count, group_count, width_here)
            .transpose(1, 0, 2)
        )
        return swap_sent, residual_grad, attention_low, jnp.sum(postnorm_part, axis=0)

    swap_sent, residual_grad, attention_low, postnorm_part = window(
        [mixture_ring], residual_work, second_grad
    )
    attention_all = gather_rows(attention_low)
    mixed_swapped = swap_all(swap_sent)
    up_part = window([mixture_ring], lambda uback: grad_of(second_all, uback), uback_all)
    mixture = mixture_ring.total()
    layer_out = (valid_own * (residual + mixture)).astype(low_type)
    mixed_swapped, up_part = tie(mixed_swapped, up_part)
    mixed_grad = reorder_rows(mixed_swapped.reshape(group_rows, width_here), device_of_slot)

    def head_backward(head, grad_head):
        (query_raw, key_raw, query_inverse, key_inverse, query_low, key_low, value_low, log_total) = (
            kept_heads[head]
        )
        scores = jnp.where(allowed, mm(query_low, key_low, 1, 1) * score_scale, masked_value)
        weights = jnp.exp(scores - log_total)
        weight_grad = mm(grad_head, value_low, 1, 1)
        row_dot = jnp.sum(weights * weight_grad, axis=-1, keepdims=True)
        score_grad = (weights * (weight_grad - row_dot)).astype(low_type)
        query_back = mm(score_grad, key_low, 1, 0) * score_scale
        key_back = mm(score_grad, query_low, 0, 0) * score_scale
        value_back = mm(weights.astype(low_type), grad_head, 0, 0)
        query_unturned = query_back * cosine + turn_back(query_back * sine_part)
        key_unturned = key_back * cosine + turn_back(key_back * sine_part)
        query_before, query_gain_part = norm_backward(
            query_raw, query_inverse, querynorm_gain, query_unturned
        )
        key_before, key_gain_part = norm_backward(
            key_raw, key_inverse, keynorm_gain, key_unturned
        )
        return (
            query_before.astype(low_type),
            key_before.astype(low_type),
            value_back.astype(low_type),
            jnp.sum(query_gain_part, axis=0),
            jnp.sum(key_gain_part, axis=0),
        )

    head_results = [
        head_backward(head, mixed_grad[:, head * head_dim : (head + 1) * head_dim])
        for head in range(heads_here)
    ]
    sent = jnp.concatenate(
        [head_results[head][part] for part in range(3) for head in range(heads_here)], axis=1
    )
    down_sum = lax.psum_scatter(
        down_part.reshape(experts_here, hidden_here, model_width),
        "rep",
        scatter_dimension=1,
        tiled=True,
    )
    sent, down_sum = tie(sent, down_sum)
    querynorm_part = sum(result[3] for result in head_results)
    keynorm_part = sum(result[4] for result in head_results)
    first_part = mm(sent, head_weight, 1, 1)
    prenorm_part = jnp.sum(first_part * token_wide * inverse_all, axis=0)
    first_low = first_part.astype(low_type)

    def small_swap(parts):
        return swap_all(
            jnp.concatenate([part.reshape(group_count, -1) for part in parts], axis=1)
        )

    def small_pieces(swapped, parts):
        total = rep_sum(jnp.sum(swapped, axis=0))
        pieces, start = [], 0
        for part in parts:
            size = part.size // group_count
            pieces.append(total[start : start + size])
            start += size
        return pieces

    first_ring = RingSum(
        lambda slot: first_low[slot * row_count : (slot + 1) * row_count], row_count
    )
    head_part, output_part = window(
        [first_ring],
        lambda first, sent, mixed, attention: (grad_of(first, sent), grad_of(mixed, attention)),
        first_all,
        sent,
        mixed_ordered,
        attention_all,
    )
    small_parts = [router_part, postnorm_part, prenorm_part, querynorm_part, keynorm_part]
    head_rows, output_rows, small_swapped = window(
        [first_ring],
        lambda head, output, *small: (
            rep_scatter(head, 1),
            rep_scatter(output, 0),
            small_swap(small),
        ),
        head_part.reshape(group_count, replica_count, share, 3 * width_here),
        output_part.reshape(replica_count, share, model_width),
        *small_parts,
    )
    head_rows, output_rows, small_sums = window(
        [first_ring],
        lambda head, output, small: (
            swap_all(head)
            .reshape(group_count, share, 3, width_here)
            .transpose(2, 1, 0, 3)
            .reshape(3, share, model_width),
            rep_gather(output),
            small_pieces(small, small_parts),
        ),
        head_rows,
        output_rows,
        small_swapped,
    )
    gate_sum = lax.psum_scatter(gate_part, "rep", scatter_dimension=0, tiled=True)
    head_rows, gate_sum = tie(head_rows, gate_sum)
    up_sum = lax.psum_scatter(up_part, "rep", scatter_dimension=0, tiled=True)
    head_rows, output_grad = window(
        [first_ring],
        lambda head, output: (
            rep_gather(head),
            output.reshape(width_here, model_width).astype(wide_type),
        ),
        head_rows,
        output_rows,
    )
    first_grad = first_ring.total()
    query_grad, key_grad, value_grad = (
        head_rows[:, block].reshape(width_here, model_width).astype(wide_type)
        for block in range(3)
    )
    router_grad, postnorm_grad, prenorm_grad, querynorm_grad, keynorm_grad = small_sums
    router_grad = router_grad.reshape(width_here, expert_total)

    token_own = tokens.astype(wide_type)
    inverse_one = inverse_rms(token_own)
    pre_back, _ = norm_backward(token_own, inverse_one, prenorm_gain, first_grad)
    token_grad = residual_grad + pre_back

    down_total = down_sum.astype(wide_type)
    gate_total, up_total = (
        jnp.stack(
            [
                total[:, e * hidden_here : (e + 1) * hidden_here].astype(wide_type)
                for e in range(experts_here)
            ]
        )
        for total in (gate_sum, up_sum)
    )
    return (
        layer_out,
        token_grad,
        query_grad,
        key_grad,
        value_grad,
        output_grad,
        router_grad,
        prenorm_grad,
        querynorm_grad,
        keynorm_grad,
        postnorm_grad,
        gate_total,
        up_total,
        down_total,
    )


def solution(mesh):
    in_specs = (
        P(("rep", "ep"), None),
        P(("rep", "ep"), None),
        P("rep", None),
        P("rep", None),
        P(("rep", "ep"), None),
        P(("rep", "ep"), None),
        P("ep", None),
        P("ep", None),
        P("ep", None),
        P("ep", None),
        P("ep", None),
        P(),
        P(),
        P(),
        P(),
        P("ep", None, None),
        P("ep", None, None),
        P("ep", None, None),
    )
    out_specs = (
        P(("rep", "ep"), None),
        P(("rep", "ep"), None),
        P("ep", None),
        P("ep", None),
        P("ep", None),
        P("ep", None),
        P("ep", None),
        P("ep"),
        P("ep"),
        P("ep"),
        P("ep"),
        P("ep", "rep", None),
        P("ep", "rep", None),
        P("ep", "rep", None),
    )
    return jax.shard_map(body, mesh=mesh, in_specs=in_specs, out_specs=out_specs, check_vma=False)
```

```python
import jax
import jax.numpy as jnp
from jax import lax
from jax.experimental import pallas as pl
from jax.experimental.pallas import tpu as pltpu
from jax.sharding import PartitionSpec as P

epsilon = 1e-05
rope_base = 10000.0
masked_value = -1e30
low_type = jnp.bfloat16
wide_type = jnp.float32


def inverse_rms(values):
    return lax.rsqrt(jnp.mean(values * values, axis=-1, keepdims=True) + epsilon)


def norm_backward(values, inverse, gain_vector, upstream):
    scaled = upstream * gain_vector
    inner_mean = jnp.mean(scaled * values, axis=-1, keepdims=True)
    result = inverse * scaled - values * (inverse * inverse * inverse) * inner_mean
    return (result, upstream * values * inverse)


def rope_tables(position, dimension):
    halfway = dimension // 2
    indices = jnp.arange(halfway, dtype=wide_type)
    frequency = rope_base ** (-2.0 * indices / dimension)
    angles = position.astype(wide_type)[:, None] * frequency[None, :]
    cosine = jnp.cos(angles)
    sine_part = jnp.sin(angles)
    return (
        jnp.concatenate([cosine, cosine], axis=-1),
        jnp.concatenate([sine_part, sine_part], axis=-1),
    )


def turn_half(values):
    halfway = values.shape[-1] // 2
    return jnp.concatenate([-values[..., halfway:], values[..., :halfway]], axis=-1)


def turn_back(values):
    halfway = values.shape[-1] // 2
    return jnp.concatenate([values[..., halfway:], -values[..., :halfway]], axis=-1)


def row_meta(lengths, group_order):
    boundary = jnp.cumsum(lengths)
    passed = (group_order[:, None] >= boundary[None, :]).astype(jnp.int32)
    segment = jnp.sum(passed, axis=1)
    offset = jnp.sum(passed * lengths[None, :], axis=1)
    return (segment, group_order - offset)


def mm(left, right, left_dim, right_dim):
    return lax.dot_general(
        left,
        right,
        (((left_dim,), (right_dim,)), ((), ())),
        preferred_element_type=wide_type,
    )


def gather_rows(values):
    return lax.all_gather(values, "ep", axis=0, tiled=True)


def ring_order(count):
    return [i for i in range(count) if i % 2 == 0] + [i for i in reversed(range(count)) if i % 2]


def ring_slots(count):
    half = count // 2
    offsets = [0]
    for step in range(1, half):
        offsets += [step, -step]
    return offsets + [half]


def ring_shift(values, direction):
    order = ring_order(lax.axis_size("ep"))
    count = len(order)
    pairs = [(order[i], order[(i + direction) % count]) for i in range(count)]
    return lax.ppermute(values, "ep", pairs)


def tie(*arrays):
    return lax.optimization_barrier(arrays)


class RingGather:
    def __init__(self, values):
        self.middle = values.shape[0] // 2
        self.half, self.step = lax.axis_size("ep") // 2, 0
        self.sent = (values, values)
        self.blocks = [values]

    def start(self):
        if self.step == self.half - 1:
            self.sent = (self.sent[0][: self.middle], self.sent[1][self.middle :])
        self.received = (ring_shift(self.sent[0], 1), ring_shift(self.sent[1], -1))

    def finish(self):
        self.step += 1
        onward, backward = self.sent = self.received
        if self.step < self.half:
            self.blocks += [backward, onward]
        else:
            self.blocks += [jnp.concatenate([onward, backward], axis=0)]


class Exchange:
    def __init__(self, values, distance):
        self.sent, self.distance = values, distance

    def start(self):
        self.received = rep_exchange(self.sent, self.distance)

    def finish(self):
        pass


class RingSum:
    def __init__(self, block, rows):
        count = lax.axis_size("ep")
        self.block, self.middle, self.step = block, rows // 2, 0
        self.half = count // 2
        self.slot = {offset: j for j, offset in enumerate(ring_slots(count))}
        far = block(self.slot[self.half])
        self.sent = (far[: self.middle], far[self.middle :])

    def start(self):
        self.received = (ring_shift(self.sent[0], 1), ring_shift(self.sent[1], -1))

    def finish(self):
        self.step += 1
        onward, backward = self.received
        left = self.half - self.step
        middle = self.middle
        if left:
            up, down = self.block(self.slot[left]), self.block(self.slot[-left])
            if self.step == 1:
                onward = jnp.concatenate([add_low(onward, up[:middle]), up[middle:]], axis=0)
                backward = jnp.concatenate(
                    [down[:middle], add_low(backward, down[middle:])], axis=0
                )
            else:
                onward, backward = add_low(onward, up), add_low(backward, down)
        self.sent = (onward, backward)

    def total(self):
        return (
            self.block(self.slot[0]).astype(wide_type)
            + self.sent[0].astype(wide_type)
            + self.sent[1].astype(wide_type)
        )


def window(rings, work, *inputs):
    for ring in rings:
        ring.start()
    inputs, _ = tie(inputs, [ring.sent for ring in rings])
    received, results = tie([ring.received for ring in rings], work(*inputs))
    for ring, pair in zip(rings, received):
        ring.received = pair
        ring.finish()
    return results


def add_low(left, right):
    return (left.astype(wide_type) + right.astype(wide_type)).astype(low_type)


def ring_place(member, count):
    return jnp.where(member % 2 == 0, member // 2, count - 1 - member // 2)


def ring_member(place, count):
    return jnp.where(place < count // 2, 2 * place, 2 * (count - 1 - place) + 1)


def ring_indices(device, count):
    place = ring_place(device, count)
    half = count // 2
    members = [ring_member((place + offset) % count, count) for offset in ring_slots(count)]
    slots = []
    for other in range(count):
        ahead = (ring_place(jnp.int32(other), count) - place) % count
        slot = jnp.where(ahead < half, 2 * ahead - 1, 2 * (count - ahead))
        slots.append(jnp.where(ahead == 0, 0, jnp.where(ahead == half, count - 1, slot)))
    return members, slots


def rep_exchange(values, distance):
    count = lax.axis_size("rep")
    return lax.ppermute(values, "rep", [(i, i ^ distance) for i in range(count)])


def rep_bit(distance):
    return (lax.axis_index("rep") // distance) % 2


def rep_gather(values):
    gathered = values[None]
    distance = lax.axis_size("rep") // 2
    while distance:
        other = rep_exchange(gathered, distance)
        mine_first = jnp.stack([gathered, other], axis=1)
        other_first = jnp.stack([other, gathered], axis=1)
        gathered = jnp.where(rep_bit(distance) == 0, mine_first, other_first)
        gathered = gathered.reshape((-1,) + values.shape)
        distance //= 2
    return gathered


def rep_scatter(values, axis):
    distance = 1
    count = lax.axis_size("rep")
    while distance < count:
        shape = values.shape
        pairs = values.reshape(shape[:axis] + (shape[axis] // 2, 2) + shape[axis + 1 :])
        bit = rep_bit(distance)
        keep = lax.dynamic_index_in_dim(pairs, bit, axis + 1, keepdims=False)
        send = lax.dynamic_index_in_dim(pairs, 1 - bit, axis + 1, keepdims=False)
        values = add_low(keep, rep_exchange(send, distance))
        distance *= 2
    return lax.index_in_dim(values, 0, axis, keepdims=False)


def rep_sum(values):
    distance = 1
    while distance < lax.axis_size("rep"):
        values = values + rep_exchange(values, distance)
        distance *= 2
    return values


def swap_all(values):
    return lax.all_to_all(values, "ep", split_axis=0, concat_axis=0, tiled=True)


def expert_kernel(rows_ref, gate_ref, up_ref, stream_ref, gates_ref, *refs):
    inner_ref, gback_ref, uback_ref, pair_ref = refs[-4:]
    expert, step = pl.program_id(0), pl.program_id(1)
    rows = rows_ref[...]
    gate_linear = jnp.dot(rows, gate_ref[0], preferred_element_type=wide_type)
    up_linear = jnp.dot(rows, up_ref[0], preferred_element_type=wide_type)
    stream = stream_ref[...]
    column = gates_ref[:, 0:1]
    for other in range(1, gates_ref.shape[1]):
        column = jnp.where(expert == other, gates_ref[:, other : other + 1], column)
    sigmoid_gate = jax.nn.sigmoid(gate_linear)
    silu_gate = gate_linear * sigmoid_gate
    inner = silu_gate * up_linear
    inner_ref[...] = (column * inner).astype(low_type)
    hidden_grad = column * stream
    gback_ref[...] = (
        hidden_grad * up_linear * sigmoid_gate * (1.0 + gate_linear * (1.0 - sigmoid_gate))
    ).astype(low_type)
    uback_ref[...] = (hidden_grad * silu_gate).astype(low_type)
    product = inner * stream
    lanes = pair_ref.shape[2]
    folded = product[:, :lanes]
    for start in range(lanes, product.shape[1], lanes):
        folded = folded + product[:, start : start + lanes]

    @pl.when(step == 0)
    def _():
        pair_ref[0] = folded

    @pl.when(step > 0)
    def _():
        pair_ref[0] += folded


def expert_pass(rows, gate_weight, up_weight, stream, gates, chunk, chunks, earlier=()):
    count, depth = rows.shape
    experts, _, hidden = gate_weight.shape
    width = 256
    steps = hidden // width
    weight = pl.BlockSpec((1, depth, width), lambda e, j: (e, 0, j))
    out = pl.BlockSpec((count, width), lambda e, j: (chunk, e * steps + j))
    return pl.pallas_call(
        expert_kernel,
        grid=(experts, steps),
        in_specs=[
            pl.BlockSpec((count, depth), lambda e, j: (0, 0)),
            weight,
            weight,
            pl.BlockSpec((count, width), lambda e, j: (0, e * steps + j)),
            pl.BlockSpec(gates.shape, lambda e, j: (0, 0)),
        ]
        + [pl.BlockSpec(memory_space=pl.ANY)] * len(earlier),
        out_specs=[out, out, out, pl.BlockSpec((1, count, 128), lambda e, j: (e, 0, 0))],
        out_shape=[jax.ShapeDtypeStruct((count * chunks, experts * hidden), low_type)] * 3
        + [jax.ShapeDtypeStruct((experts, count, 128), wide_type)],
        input_output_aliases={5 + i: i for i in range(len(earlier))},
        compiler_params=pltpu.CompilerParams(vmem_limit_bytes=56 << 20),
        cost_estimate=pl.CostEstimate(
            flops=4 * count * depth * experts * hidden,
            bytes_accessed=4 * depth * experts * hidden + 20 * count * depth,
            transcendentals=count * experts * hidden,
        ),
    )(rows, gate_weight, up_weight, stream, gates, *earlier)


def expert_back_kernel(gback_ref, uback_ref, gate_ref, up_ref, out_ref):
    experts, _, hidden = gate_ref.shape
    total = None
    for e in range(experts):
        for grad_ref, weight_ref in ((gback_ref, gate_ref), (uback_ref, up_ref)):
            term = mm(grad_ref[:, e * hidden : (e + 1) * hidden], weight_ref[e], 1, 1)
            total = term if total is None else total + term
    out_ref[...] = total.astype(low_type)


def expert_back(gback, uback, gate_weight, up_weight, chunk, chunks):
    count = gback.shape[0] // chunks
    experts, depth, hidden = gate_weight.shape
    width = 256
    whole = pl.BlockSpec((count, experts * hidden), lambda j: (chunk, 0))
    weight = pl.BlockSpec((experts, width, hidden), lambda j: (0, j, 0))
    return pl.pallas_call(
        expert_back_kernel,
        grid=(depth // width,),
        in_specs=[whole, whole, weight, weight],
        out_specs=pl.BlockSpec((count, width), lambda j: (0, j)),
        out_shape=jax.ShapeDtypeStruct((count, depth), low_type),
        compiler_params=pltpu.CompilerParams(vmem_limit_bytes=56 << 20),
        cost_estimate=pl.CostEstimate(
            flops=4 * count * depth * experts * hidden,
            bytes_accessed=4 * depth * experts * hidden + 6 * count * depth,
            transcendentals=0,
        ),
    )(gback, uback, gate_weight, up_weight)


def body(
    tokens,
    cotangent,
    seq_lengths,
    token_order,
    routes,
    slot_index,
    query_weight,
    key_weight,
    value_weight,
    output_weight,
    router_weight,
    prenorm_gain,
    querynorm_gain,
    keynorm_gain,
    postnorm_gain,
    gate_weight,
    up_weight,
    down_weight,
):
    group_count = lax.axis_size("ep")
    device = lax.axis_index("ep")
    row_count, model_width = tokens.shape
    head_dim = querynorm_gain.shape[0]
    width_here = model_width // group_count
    heads_here = width_here // head_dim
    experts_here = gate_weight.shape[0]
    expert_total = experts_here * group_count
    top_count = routes.shape[1]
    capacity = row_count * top_count * 5 // (4 * expert_total)
    group_rows = row_count * group_count
    sequence_count = seq_lengths.shape[1]
    score_scale = head_dim ** (-0.5)

    replica_count = lax.axis_size("rep")
    replica = lax.axis_index("rep")
    share = width_here // replica_count

    device_of_slot, slot_of_device = ring_indices(device, group_count)

    def reorder(blocks, index):
        return jnp.concatenate(
            [lax.dynamic_slice_in_dim(blocks, index[i], 1, 0) for i in range(group_count)], axis=0
        )

    group_order = reorder(token_order[0].reshape(group_count, row_count), device_of_slot)
    segment, position = row_meta(seq_lengths[0], group_order.reshape(group_rows))
    segment_own = segment[:row_count]
    valid_own = (segment_own < sequence_count).astype(wide_type)[:, None]
    valid_all = (segment < sequence_count).astype(wide_type)[:, None]

    expert_ids = jnp.arange(expert_total, dtype=jnp.int32)
    route_code = jnp.zeros((row_count, expert_total), jnp.int32)
    for column in range(top_count):
        hit = routes[:, column, None] == expert_ids[None, :]
        kept = (slot_index[:, column, None] < capacity).astype(jnp.int32)
        route_code = route_code + jnp.where(hit, 1 + kept, 0)
    small_sent = jnp.concatenate([route_code.astype(low_type), router_weight], axis=0)

    small_flat = small_sent.reshape(-1, head_dim)
    projections = jnp.concatenate(
        [
            lax.dynamic_slice_in_dim(piece, replica * share, share, 0).reshape(
                share, group_count, width_here
            )
            for piece in (query_weight, key_weight, value_weight)
        ],
        axis=2,
    ).transpose(1, 0, 2)
    cosine, sine_part = rope_tables(position, head_dim)
    chunks = 2
    chunk_rows = group_rows // chunks
    blocks_here = group_count // chunks

    def chunk_of(array, chunk):
        return array[chunk * chunk_rows : (chunk + 1) * chunk_rows]

    def normed_rows(rows):
        wide = rows.astype(wide_type)
        return (wide * inverse_rms(wide) * prenorm_gain).astype(low_type)

    def head_columns(values, block, head):
        start = block * width_here + head * head_dim
        return values[:, start : start + head_dim]

    def project(first, weight, chunk):
        raw = mm(first, weight, 1, 0)
        turns = chunk_of(cosine, chunk), chunk_of(sine_part, chunk)
        results = []
        for head in range(heads_here):
            for block, gain in ((0, querynorm_gain), (1, keynorm_gain)):
                part = head_columns(raw, block, head)
                normed = part * inverse_rms(part) * gain
                turned = (normed * turns[0] + turn_half(normed) * turns[1]).astype(low_type)
                results += [part, turned]
            results.append(head_columns(raw, 2, head).astype(low_type))
        return results

    token_ring = RingGather(tokens)
    swapped = window([token_ring], swap_all, projections)
    head_pieces, small_all = window(
        [token_ring],
        lambda pieces, small: (
            rep_gather(pieces),
            swap_all(jnp.broadcast_to(small[None], (group_count,) + small.shape)),
        ),
        swapped,
        small_flat,
    )
    head_weight, first_rows = window(
        [token_ring],
        lambda pieces, *blocks: (
            pieces.transpose(1, 0, 2, 3).reshape(model_width, 3 * width_here),
            normed_rows(jnp.concatenate(blocks, axis=0)),
        ),
        head_pieces,
        *token_ring.blocks[:blocks_here],
    )
    early_heads = window(
        [token_ring],
        lambda first, weight: project(first, weight, 0),
        first_rows,
        head_weight,
    )
    token_blocks = token_ring.blocks
    last_rows = normed_rows(jnp.concatenate(token_blocks[blocks_here:], axis=0))
    late_heads = project(last_rows, head_weight, 1)
    first_all = jnp.concatenate([first_rows, last_rows], axis=0)
    token_all = jnp.concatenate(token_blocks, axis=0)
    token_wide = token_all.astype(wide_type)
    inverse_all = inverse_rms(token_wide)

    small_all = small_all.reshape(group_count, row_count + width_here, expert_total)
    code_all = reorder(small_all[:, :row_count], device_of_slot).reshape(
        group_rows, expert_total
    )
    full_router = small_all[:, row_count:].reshape(model_width, expert_total)

    def reorder_rows(rows, index):
        return reorder(
            rows.reshape(group_count, row_count, rows.shape[1]), index
        ).reshape(rows.shape)

    late_heads[0], cot_own = tie(late_heads[0], cotangent)
    cot_ordered = gather_rows(cot_own)
    cot_all = reorder_rows(cot_ordered, device_of_slot)
    column_share = model_width // replica_count
    cot_ordered, output_own = tie(cot_ordered, output_weight)
    output_share = gather_rows(
        lax.dynamic_slice_in_dim(output_own, replica * column_share, column_share, 1)
    )

    hidden_here = down_weight.shape[1]
    flat_down = down_weight.reshape(experts_here * hidden_here, model_width)

    allowed = segment[:, None] == segment[None, :]

    kept_heads = []
    mixed_parts = []
    for head in range(heads_here):
        query_raw, query_low, key_raw, key_low, value_low = (
            jnp.concatenate([early_heads[5 * head + i], late_heads[5 * head + i]], axis=0)
            for i in range(5)
        )
        scores = jnp.where(allowed, mm(query_low, key_low, 1, 1) * score_scale, masked_value)
        top_score = jnp.max(scores, axis=-1, keepdims=True)
        powers = jnp.exp(scores - top_score)
        log_total = top_score + jnp.log(jnp.sum(powers, axis=-1, keepdims=True))
        weights_low = jnp.exp(scores - log_total).astype(low_type)
        mixed_parts.append(mm(weights_low, value_low, 1, 0).astype(low_type))
        kept_heads.append((query_raw, key_raw, query_low, key_low, value_low, log_total))
    mixed_low = jnp.concatenate(mixed_parts, axis=1)

    def slot_rows(array):
        return lambda slot: array[slot * row_count : (slot + 1) * row_count]

    attention_ring = RingSum(slot_rows(mm(mixed_low, output_weight, 1, 0).astype(low_type)), row_count)
    for _ in range(group_count // 2):
        window([attention_ring], lambda: ())
    attention = attention_ring.total()
    residual = tokens.astype(wide_type) + attention
    inverse_two = inverse_rms(residual)
    second_input = (residual * inverse_two * postnorm_gain).astype(low_type)

    def gate_table(rows, code):
        logits = mm(rows, full_router, 1, 0)
        shifted = jnp.where(code > 0, logits, masked_value)
        powers = jnp.exp(shifted - jnp.max(shifted, axis=1, keepdims=True))
        return powers / jnp.sum(powers, axis=1, keepdims=True)

    kept_all = jnp.where(code_all > 1, valid_all, 0.0)
    kept_here = lax.dynamic_slice_in_dim(kept_all, device * experts_here, experts_here, 1)

    def stream_of(cot_part):
        return mm(cot_part, flat_down, 1, 1)

    def expert_chunk(chunk, rows, stream, *earlier):
        gates = gate_table(rows, chunk_of(code_all, chunk)) * chunk_of(kept_all, chunk)
        gates_here = lax.dynamic_slice_in_dim(gates, device * experts_here, experts_here, 1)
        return expert_pass(
            rows, gate_weight, up_weight, stream, gates_here, chunk, chunks, earlier
        )

    halves = 2 if column_share % 256 == 0 else 1
    piece_width = column_share // halves
    shares = [output_share[:, i * piece_width : (i + 1) * piece_width] for i in range(halves)]
    far = replica_count // 2

    second_ring = RingGather(second_input)
    stream_first = window([second_ring], lambda part: stream_of(part), chunk_of(cot_all, 0))
    stream_last = window([second_ring], lambda part: stream_of(part), chunk_of(cot_all, 1))
    rows_first = jnp.concatenate(second_ring.blocks[:blocks_here], axis=0)
    exchanges = [Exchange(piece, far) for piece in shares]
    *earlier, pair_first = window(
        [second_ring, exchanges[0]],
        lambda rows, stream: expert_chunk(0, rows, stream),
        rows_first,
        stream_first,
    )
    window([second_ring], lambda: ())
    rows_last = jnp.concatenate(second_ring.blocks[blocks_here:], axis=0)
    inner_all, gback_all, uback_all, pair_last = window(
        exchanges[1:],
        lambda rows, stream, *earlier: expert_chunk(1, rows, stream, *earlier),
        rows_last,
        stream_last,
        *earlier,
    )
    second_all = jnp.concatenate([rows_first, rows_last], axis=0)
    output_pieces = {}
    for half in range(halves):
        output_pieces[0, half] = shares[half]
        output_pieces[far, half] = exchanges[half].received
    near = []
    distance = far // 2
    while distance:
        near += [
            (j ^ distance, half, Exchange(output_pieces[j, half], distance))
            for j, half in output_pieces
        ]
        if distance > 1:
            for j, half, exchange in near:
                window([exchange], lambda: ())
                output_pieces[j, half] = exchange.received
            near = []
        distance //= 2
    back_last = window(
        [exchange for _, _, exchange in near],
        lambda gback, uback: expert_back(gback, uback, gate_weight, up_weight, 1, chunks),
        gback_all,
        uback_all,
    )
    for j, half, exchange in near:
        output_pieces[j, half] = exchange.received

    def piece_start(j, half):
        return (replica ^ j) * column_share + half * piece_width

    back_parts = {1: back_last}

    def back_block(slot):
        start = (slot % blocks_here) * row_count
        return back_parts[slot // blocks_here][start : start + row_count]

    def grad_of(left, right):
        return mm(left, right, 0, 0).astype(low_type)

    pair_lanes = jnp.concatenate([pair_first, pair_last], axis=1)
    pair_sent = (kept_here * jnp.sum(pair_lanes, axis=2).transpose(1, 0)).reshape(
        group_count, row_count, experts_here
    )
    code_own = route_code
    gates_own = gate_table(second_input, code_own)

    back_ring = RingSum(back_block, row_count)
    back_parts[0] = window(
        [back_ring],
        lambda gback, uback: expert_back(gback, uback, gate_weight, up_weight, 0, chunks),
        gback_all,
        uback_all,
    )

    def mixture_work(inner, pair):
        return (
            mm(inner, flat_down, 1, 0).astype(low_type),
            swap_all(reorder(pair, slot_of_device)),
        )

    mixture_part, pair_grad = window([back_ring], mixture_work, inner_all, pair_sent)
    mixture_ring = RingSum(slot_rows(mixture_part), row_count)

    def down_work(inner, pair):
        pair_grad = pair.transpose(1, 0, 2).reshape(row_count, expert_total)
        chosen_grad = gates_own * (
            pair_grad - jnp.sum(gates_own * pair_grad, axis=1, keepdims=True)
        )
        logits_grad = jnp.where(code_own > 0, chosen_grad, 0.0).astype(low_type)
        router_back = mm(logits_grad, full_router, 1, 1)
        router_part = mm(second_input, logits_grad, 0, 0)
        return grad_of(inner, cot_all), router_back, router_part

    down_part, router_back, router_part = window(
        [back_ring, mixture_ring], down_work, inner_all, pair_grad
    )
    window([back_ring, mixture_ring], lambda: ())
    second_scattered = back_ring.total()
    second_grad = router_back + second_scattered
    upstream = valid_own * cotangent.astype(wide_type)
    def residual_work(second_grad):
        post_back, postnorm_part = norm_backward(
            residual, inverse_two, postnorm_gain, second_grad
        )
        residual_grad = upstream + post_back
        attention_low = residual_grad.astype(low_type)
        mixed_grad_own = jnp.zeros((row_count, model_width), wide_type)
        for place, piece in output_pieces.items():
            mixed_grad_own = mixed_grad_own + mm(
                lax.dynamic_slice_in_dim(attention_low, piece_start(*place), piece_width, 1),
                piece,
                1,
                1,
            )
        swap_sent = (
            mixed_grad_own.astype(low_type)
            .reshape(row_count, group_count, width_here)
            .transpose(1, 0, 2)
        )
        return swap_sent, residual_grad, attention_low, jnp.sum(postnorm_part, axis=0)

    swap_sent, residual_grad, attention_low, postnorm_part = window(
        [mixture_ring], residual_work, second_grad
    )
    class Swap(Exchange):
        def start(self):
            self.received = swap_all(self.sent)

    swap = Swap(swap_sent, 0)
    gate_part, up_part = window(
        [mixture_ring, swap],
        lambda gback, uback: (grad_of(second_all, gback), grad_of(second_all, uback)),
        gback_all,
        uback_all,
    )
    mixture = mixture_ring.total()
    layer_out = (valid_own * (residual + mixture)).astype(low_type)
    mixed_grad = reorder_rows(swap.received.reshape(group_rows, width_here), device_of_slot)

    def head_backward(head, grad_head):
        query_raw, key_raw, query_low, key_low, value_low, log_total = kept_heads[head]
        query_inverse, key_inverse = inverse_rms(query_raw), inverse_rms(key_raw)
        scores = jnp.where(allowed, mm(query_low, key_low, 1, 1) * score_scale, masked_value)
        weights = jnp.exp(scores - log_total)
        weight_grad = mm(grad_head, value_low, 1, 1)
        row_dot = jnp.sum(weights * weight_grad, axis=-1, keepdims=True)
        score_grad = (weights * (weight_grad - row_dot)).astype(low_type)
        query_back = mm(score_grad, key_low, 1, 0) * score_scale
        key_back = mm(score_grad, query_low, 0, 0) * score_scale
        value_back = mm(weights.astype(low_type), grad_head, 0, 0)
        query_unturned = query_back * cosine + turn_back(query_back * sine_part)
        key_unturned = key_back * cosine + turn_back(key_back * sine_part)
        query_before, query_gain_part = norm_backward(
            query_raw, query_inverse, querynorm_gain, query_unturned
        )
        key_before, key_gain_part = norm_backward(
            key_raw, key_inverse, keynorm_gain, key_unturned
        )
        return (
            query_before.astype(low_type),
            key_before.astype(low_type),
            value_back.astype(low_type),
            jnp.sum(query_gain_part, axis=0),
            jnp.sum(key_gain_part, axis=0),
        )

    attention_gather = RingGather(attention_low)
    head_results = []
    for head in range(heads_here):
        head_results.append(
            window(
                [attention_gather],
                lambda grad_head: head_backward(head, grad_head),
                mixed_grad[:, head * head_dim : (head + 1) * head_dim],
            )
        )
    sent = jnp.concatenate(
        [head_results[head][part] for part in range(3) for head in range(heads_here)], axis=1
    )
    down_sum = lax.psum_scatter(
        down_part.reshape(experts_here, hidden_here, model_width),
        "rep",
        scatter_dimension=1,
        tiled=True,
    )
    sent, down_sum = tie(sent, down_sum)
    querynorm_part = sum(result[3] for result in head_results)
    keynorm_part = sum(result[4] for result in head_results)
    def first_work(sent):
        first_part = mm(sent, head_weight, 1, 1)
        prenorm_part = jnp.sum(first_part * token_wide * inverse_all, axis=0)
        return first_part.astype(low_type), prenorm_part

    while attention_gather.step < group_count // 2 - 2:
        window([attention_gather], lambda: ())
    first_low, prenorm_part = window([attention_gather], first_work, sent)

    def small_swap(parts):
        return swap_all(
            jnp.concatenate([part.reshape(group_count, -1) for part in parts], axis=1)
        )

    def small_pieces(swapped, parts):
        total = rep_sum(jnp.sum(swapped, axis=0))
        pieces, start = [], 0
        for part in parts:
            size = part.size // group_count
            pieces.append(total[start : start + size])
            start += size
        return pieces

    first_ring = RingSum(slot_rows(first_low), row_count)
    head_part = window([attention_gather, first_ring], grad_of, first_all, sent)
    attention_all = jnp.concatenate(attention_gather.blocks, axis=0)
    output_part = grad_of(mixed_low, attention_all)
    small_parts = [router_part, postnorm_part, prenorm_part, querynorm_part, keynorm_part]
    head_rows, output_rows, small_swapped = window(
        [first_ring],
        lambda head, output, *small: (
            rep_scatter(head, 1),
            rep_scatter(output, 0),
            small_swap(small),
        ),
        head_part.reshape(group_count, replica_count, share, 3 * width_here),
        output_part.reshape(replica_count, share, model_width),
        *small_parts,
    )
    head_rows, output_rows, small_sums = window(
        [first_ring],
        lambda head, output, small: (
            swap_all(head)
            .reshape(group_count, share, 3, width_here)
            .transpose(2, 1, 0, 3)
            .reshape(3, share, model_width),
            rep_gather(output),
            small_pieces(small, small_parts),
        ),
        head_rows,
        output_rows,
        small_swapped,
    )
    gate_sum = lax.psum_scatter(gate_part, "rep", scatter_dimension=0, tiled=True)
    head_rows, gate_sum = tie(head_rows, gate_sum)
    up_sum = lax.psum_scatter(up_part, "rep", scatter_dimension=0, tiled=True)
    head_rows, output_grad = window(
        [first_ring],
        lambda head, output: (
            rep_gather(head),
            output.reshape(width_here, model_width).astype(wide_type),
        ),
        head_rows,
        output_rows,
    )
    first_grad = first_ring.total()
    query_grad, key_grad, value_grad = (
        head_rows[:, block].reshape(width_here, model_width).astype(wide_type)
        for block in range(3)
    )
    router_grad, postnorm_grad, prenorm_grad, querynorm_grad, keynorm_grad = small_sums
    router_grad = router_grad.reshape(width_here, expert_total)

    token_own = tokens.astype(wide_type)
    inverse_one = inverse_rms(token_own)
    pre_back, _ = norm_backward(token_own, inverse_one, prenorm_gain, first_grad)
    token_grad = residual_grad + pre_back

    down_total = down_sum.astype(wide_type)
    gate_total, up_total = (
        jnp.stack(
            [
                total[:, e * hidden_here : (e + 1) * hidden_here].astype(wide_type)
                for e in range(experts_here)
            ]
        )
        for total in (gate_sum, up_sum)
    )
    return (
        layer_out,
        token_grad,
        query_grad,
        key_grad,
        value_grad,
        output_grad,
        router_grad,
        prenorm_grad,
        querynorm_grad,
        keynorm_grad,
        postnorm_grad,
        gate_total,
        up_total,
        down_total,
    )


def solution(mesh):
    in_specs = (
        P(("rep", "ep"), None),
        P(("rep", "ep"), None),
        P("rep", None),
        P("rep", None),
        P(("rep", "ep"), None),
        P(("rep", "ep"), None),
        P("ep", None),
        P("ep", None),
        P("ep", None),
        P("ep", None),
        P("ep", None),
        P(),
        P(),
        P(),
        P(),
        P("ep", None, None),
        P("ep", None, None),
        P("ep", None, None),
    )
    out_specs = (
        P(("rep", "ep"), None),
        P(("rep", "ep"), None),
        P("ep", None),
        P("ep", None),
        P("ep", None),
        P("ep", None),
        P("ep", None),
        P("ep"),
        P("ep"),
        P("ep"),
        P("ep"),
        P("ep", "rep", None),
        P("ep", "rep", None),
        P("ep", "rep", None),
    )
    return jax.shard_map(body, mesh=mesh, in_specs=in_specs, out_specs=out_specs, check_vma=False)
```

```python
import jax
import jax.numpy as jnp
from jax import lax
from jax.experimental import pallas as pl
from jax.experimental.pallas import tpu as pltpu
from jax.sharding import PartitionSpec as P

epsilon = 1e-05
rope_base = 10000.0
masked_value = -1e30
low_type = jnp.bfloat16
wide_type = jnp.float32


def inverse_rms(values):
    return lax.rsqrt(jnp.mean(values * values, axis=-1, keepdims=True) + epsilon)


def norm_backward(values, inverse, gain_vector, upstream):
    scaled = upstream * gain_vector
    inner_mean = jnp.mean(scaled * values, axis=-1, keepdims=True)
    result = inverse * scaled - values * (inverse * inverse * inverse) * inner_mean
    return (result, upstream * values * inverse)


def rope_tables(position, dimension):
    halfway = dimension // 2
    indices = jnp.arange(halfway, dtype=wide_type)
    frequency = rope_base ** (-2.0 * indices / dimension)
    angles = position.astype(wide_type)[:, None] * frequency[None, :]
    cosine = jnp.cos(angles)
    sine_part = jnp.sin(angles)
    return (
        jnp.concatenate([cosine, cosine], axis=-1),
        jnp.concatenate([sine_part, sine_part], axis=-1),
    )


def turn_half(values):
    halfway = values.shape[-1] // 2
    return jnp.concatenate([-values[..., halfway:], values[..., :halfway]], axis=-1)


def turn_back(values):
    halfway = values.shape[-1] // 2
    return jnp.concatenate([values[..., halfway:], -values[..., :halfway]], axis=-1)


def row_meta(lengths, group_order):
    boundary = jnp.cumsum(lengths)
    passed = (group_order[:, None] >= boundary[None, :]).astype(jnp.int32)
    segment = jnp.sum(passed, axis=1)
    offset = jnp.sum(passed * lengths[None, :], axis=1)
    return (segment, group_order - offset)


def mm(left, right, left_dim, right_dim):
    return lax.dot_general(
        left,
        right,
        (((left_dim,), (right_dim,)), ((), ())),
        preferred_element_type=wide_type,
    )


def gather_rows(values):
    return lax.all_gather(values, "ep", axis=0, tiled=True)


def ring_order(count):
    return [i for i in range(count) if i % 2 == 0] + [i for i in reversed(range(count)) if i % 2]


def ring_slots(count):
    half = count // 2
    offsets = [0]
    for step in range(1, half):
        offsets += [step, -step]
    return offsets + [half]


def ring_shift(values, direction):
    order = ring_order(lax.axis_size("ep"))
    count = len(order)
    pairs = [(order[i], order[(i + direction) % count]) for i in range(count)]
    return lax.ppermute(values, "ep", pairs)


def tie(*arrays):
    return lax.optimization_barrier(arrays)


def after(value, *others):
    return lax.optimization_barrier((value,) + others)[0]


class RingGather:
    def __init__(self, values):
        self.middle = values.shape[0] // 2
        self.half, self.step = lax.axis_size("ep") // 2, 0
        self.sent = (values, values)
        self.blocks = [values]

    def start(self):
        if self.step == self.half - 1:
            self.sent = (self.sent[0][: self.middle], self.sent[1][self.middle :])
        self.received = (ring_shift(self.sent[0], 1), ring_shift(self.sent[1], -1))

    def finish(self):
        self.step += 1
        onward, backward = self.sent = self.received
        if self.step < self.half:
            self.blocks += [backward, onward]
        else:
            self.blocks += [jnp.concatenate([onward, backward], axis=0)]


class Exchange:
    def __init__(self, values, distance):
        self.sent, self.distance = values, distance

    def start(self):
        self.received = rep_exchange(self.sent, self.distance)

    def finish(self):
        pass


class RingSum:
    def __init__(self, block, rows):
        count = lax.axis_size("ep")
        self.block, self.middle, self.step = block, rows // 2, 0
        self.half = count // 2
        self.slot = {offset: j for j, offset in enumerate(ring_slots(count))}
        far = block(self.slot[self.half])
        self.sent = (far[: self.middle], far[self.middle :])

    def start(self):
        self.received = (ring_shift(self.sent[0], 1), ring_shift(self.sent[1], -1))

    def finish(self):
        self.step += 1
        onward, backward = self.received
        left = self.half - self.step
        middle = self.middle
        if left:
            up, down = self.block(self.slot[left]), self.block(self.slot[-left])
            if self.step == 1:
                onward = jnp.concatenate([add_low(onward, up[:middle]), up[middle:]], axis=0)
                backward = jnp.concatenate(
                    [down[:middle], add_low(backward, down[middle:])], axis=0
                )
            else:
                onward, backward = add_low(onward, up), add_low(backward, down)
        self.sent = (onward, backward)

    def total(self):
        return (
            self.block(self.slot[0]).astype(wide_type)
            + self.sent[0].astype(wide_type)
            + self.sent[1].astype(wide_type)
        )


def window(rings, work, *inputs):
    for ring in rings:
        ring.start()
    inputs, _ = tie(inputs, [ring.sent for ring in rings])
    received, results = tie([ring.received for ring in rings], work(*inputs))
    for ring, pair in zip(rings, received):
        ring.received = pair
        ring.finish()
    return results


def add_low(left, right):
    return (left.astype(wide_type) + right.astype(wide_type)).astype(low_type)


def ring_place(member, count):
    return jnp.where(member % 2 == 0, member // 2, count - 1 - member // 2)


def ring_member(place, count):
    return jnp.where(place < count // 2, 2 * place, 2 * (count - 1 - place) + 1)


def ring_indices(device, count):
    place = ring_place(device, count)
    half = count // 2
    members = [ring_member((place + offset) % count, count) for offset in ring_slots(count)]
    slots = []
    for other in range(count):
        ahead = (ring_place(jnp.int32(other), count) - place) % count
        slot = jnp.where(ahead < half, 2 * ahead - 1, 2 * (count - ahead))
        slots.append(jnp.where(ahead == 0, 0, jnp.where(ahead == half, count - 1, slot)))
    return members, slots


def rep_exchange(values, distance):
    count = lax.axis_size("rep")
    return lax.ppermute(values, "rep", [(i, i ^ distance) for i in range(count)])


def rep_bit(distance):
    return (lax.axis_index("rep") // distance) % 2


def rep_gather(values):
    gathered = values[None]
    distance = lax.axis_size("rep") // 2
    while distance:
        other = rep_exchange(gathered, distance)
        mine_first = jnp.stack([gathered, other], axis=1)
        other_first = jnp.stack([other, gathered], axis=1)
        gathered = jnp.where(rep_bit(distance) == 0, mine_first, other_first)
        gathered = gathered.reshape((-1,) + values.shape)
        distance //= 2
    return gathered


def rep_scatter(values, axis):
    distance = 1
    count = lax.axis_size("rep")
    while distance < count:
        shape = values.shape
        pairs = values.reshape(shape[:axis] + (shape[axis] // 2, 2) + shape[axis + 1 :])
        bit = rep_bit(distance)
        keep = lax.dynamic_index_in_dim(pairs, bit, axis + 1, keepdims=False)
        send = lax.dynamic_index_in_dim(pairs, 1 - bit, axis + 1, keepdims=False)
        values = add_low(keep, rep_exchange(send, distance))
        distance *= 2
    return lax.index_in_dim(values, 0, axis, keepdims=False)


def rep_sum(values):
    distance = 1
    while distance < lax.axis_size("rep"):
        values = values + rep_exchange(values, distance)
        distance *= 2
    return values


def swap_all(values):
    return lax.all_to_all(values, "ep", split_axis=0, concat_axis=0, tiled=True)


def expert_kernel(rows_ref, gate_ref, up_ref, stream_ref, gates_ref, *refs):
    inner_ref, gback_ref, uback_ref, pair_ref = refs[-4:]
    expert, step = pl.program_id(0), pl.program_id(1)
    rows = rows_ref[...]
    gate_linear = jnp.dot(rows, gate_ref[0], preferred_element_type=wide_type)
    up_linear = jnp.dot(rows, up_ref[0], preferred_element_type=wide_type)
    stream = stream_ref[...]
    column = gates_ref[:, 0:1]
    for other in range(1, gates_ref.shape[1]):
        column = jnp.where(expert == other, gates_ref[:, other : other + 1], column)
    sigmoid_gate = jax.nn.sigmoid(gate_linear)
    silu_gate = gate_linear * sigmoid_gate
    inner = silu_gate * up_linear
    inner_ref[...] = (column * inner).astype(low_type)
    hidden_grad = column * stream
    gback_ref[...] = (
        hidden_grad * up_linear * sigmoid_gate * (1.0 + gate_linear * (1.0 - sigmoid_gate))
    ).astype(low_type)
    uback_ref[...] = (hidden_grad * silu_gate).astype(low_type)
    product = inner * stream
    lanes = pair_ref.shape[2]
    folded = product[:, :lanes]
    for start in range(lanes, product.shape[1], lanes):
        folded = folded + product[:, start : start + lanes]

    @pl.when(step == 0)
    def _():
        pair_ref[0] = folded

    @pl.when(step > 0)
    def _():
        pair_ref[0] += folded


def expert_pass(rows, gate_weight, up_weight, stream, gates, chunk, chunks, earlier=()):
    count, depth = rows.shape
    experts, _, hidden = gate_weight.shape
    width = 256
    steps = hidden // width
    weight = pl.BlockSpec((1, depth, width), lambda e, j: (e, 0, j))
    out = pl.BlockSpec((count, width), lambda e, j: (chunk, e * steps + j))
    return pl.pallas_call(
        expert_kernel,
        grid=(experts, steps),
        in_specs=[
            pl.BlockSpec((count, depth), lambda e, j: (0, 0)),
            weight,
            weight,
            pl.BlockSpec((count, width), lambda e, j: (0, e * steps + j)),
            pl.BlockSpec(gates.shape, lambda e, j: (0, 0)),
        ]
        + [pl.BlockSpec(memory_space=pl.ANY)] * len(earlier),
        out_specs=[out, out, out, pl.BlockSpec((1, count, 128), lambda e, j: (e, 0, 0))],
        out_shape=[jax.ShapeDtypeStruct((count * chunks, experts * hidden), low_type)] * 3
        + [jax.ShapeDtypeStruct((experts, count, 128), wide_type)],
        input_output_aliases={5 + i: i for i in range(len(earlier))},
        compiler_params=pltpu.CompilerParams(vmem_limit_bytes=56 << 20),
        cost_estimate=pl.CostEstimate(
            flops=4 * count * depth * experts * hidden,
            bytes_accessed=4 * depth * experts * hidden + 20 * count * depth,
            transcendentals=count * experts * hidden,
        ),
    )(rows, gate_weight, up_weight, stream, gates, *earlier)


def expert_back_kernel(gback_ref, uback_ref, gate_ref, up_ref, out_ref):
    experts, _, hidden = gate_ref.shape
    total = None
    for e in range(experts):
        for grad_ref, weight_ref in ((gback_ref, gate_ref), (uback_ref, up_ref)):
            term = mm(grad_ref[:, e * hidden : (e + 1) * hidden], weight_ref[e], 1, 1)
            total = term if total is None else total + term
    out_ref[...] = total.astype(low_type)


def expert_back(gback, uback, gate_weight, up_weight, chunk, chunks):
    count = gback.shape[0] // chunks
    experts, depth, hidden = gate_weight.shape
    width = 256
    whole = pl.BlockSpec((count, experts * hidden), lambda j: (chunk, 0))
    weight = pl.BlockSpec((experts, width, hidden), lambda j: (0, j, 0))
    return pl.pallas_call(
        expert_back_kernel,
        grid=(depth // width,),
        in_specs=[whole, whole, weight, weight],
        out_specs=pl.BlockSpec((count, width), lambda j: (0, j)),
        out_shape=jax.ShapeDtypeStruct((count, depth), low_type),
        compiler_params=pltpu.CompilerParams(vmem_limit_bytes=56 << 20),
        cost_estimate=pl.CostEstimate(
            flops=4 * count * depth * experts * hidden,
            bytes_accessed=4 * depth * experts * hidden + 6 * count * depth,
            transcendentals=0,
        ),
    )(gback, uback, gate_weight, up_weight)


def body(
    tokens,
    cotangent,
    seq_lengths,
    token_order,
    routes,
    slot_index,
    query_weight,
    key_weight,
    value_weight,
    output_weight,
    router_weight,
    prenorm_gain,
    querynorm_gain,
    keynorm_gain,
    postnorm_gain,
    gate_weight,
    up_weight,
    down_weight,
):
    group_count = lax.axis_size("ep")
    device = lax.axis_index("ep")
    row_count, model_width = tokens.shape
    head_dim = querynorm_gain.shape[0]
    width_here = model_width // group_count
    heads_here = width_here // head_dim
    experts_here = gate_weight.shape[0]
    expert_total = experts_here * group_count
    top_count = routes.shape[1]
    capacity = row_count * top_count * 5 // (4 * expert_total)
    group_rows = row_count * group_count
    sequence_count = seq_lengths.shape[1]
    score_scale = head_dim ** (-0.5)

    replica_count = lax.axis_size("rep")
    replica = lax.axis_index("rep")
    share = width_here // replica_count

    device_of_slot, slot_of_device = ring_indices(device, group_count)

    def reorder(blocks, index):
        return jnp.concatenate(
            [lax.dynamic_slice_in_dim(blocks, index[i], 1, 0) for i in range(group_count)], axis=0
        )

    group_order = reorder(token_order[0].reshape(group_count, row_count), device_of_slot)
    segment, position = row_meta(seq_lengths[0], group_order.reshape(group_rows))
    segment_own = segment[:row_count]
    valid_own = (segment_own < sequence_count).astype(wide_type)[:, None]
    valid_all = (segment < sequence_count).astype(wide_type)[:, None]

    expert_ids = jnp.arange(expert_total, dtype=jnp.int32)
    route_code = jnp.zeros((row_count, expert_total), jnp.int32)
    for column in range(top_count):
        hit = routes[:, column, None] == expert_ids[None, :]
        kept = (slot_index[:, column, None] < capacity).astype(jnp.int32)
        route_code = route_code + jnp.where(hit, 1 + kept, 0)
    small_sent = jnp.concatenate([route_code.astype(low_type), router_weight], axis=0)

    small_flat = small_sent.reshape(-1, head_dim)
    small_all = swap_all(
        jnp.broadcast_to(small_flat[None], (group_count,) + small_flat.shape)
    ).reshape(group_count, row_count + width_here, expert_total)
    code_all = reorder(small_all[:, :row_count], device_of_slot).reshape(
        group_rows, expert_total
    )
    full_router = small_all[:, row_count:].reshape(model_width, expert_total)

    projections = jnp.concatenate(
        [
            lax.dynamic_slice_in_dim(piece, replica * share, share, 0).reshape(
                share, group_count, width_here
            )
            for piece in (query_weight, key_weight, value_weight)
        ],
        axis=2,
    ).transpose(1, 0, 2)
    head_weight = (
        rep_gather(swap_all(projections))
        .transpose(1, 0, 2, 3)
        .reshape(model_width, 3 * width_here)
    )
    column_share = model_width // replica_count
    output_share = gather_rows(
        lax.dynamic_slice_in_dim(output_weight, replica * column_share, column_share, 1)
    )
    chunks = 2
    chunk_rows = group_rows // chunks
    blocks_here = group_count // chunks

    def chunk_of(array, chunk):
        return array[chunk * chunk_rows : (chunk + 1) * chunk_rows]

    def gather_ring(values):
        ring = RingGather(values)
        for _ in range(group_count // 2):
            ring.start()
            ring.finish()
        return ring.blocks

    def slot_rows(array):
        return lambda slot: array[slot * row_count : (slot + 1) * row_count]

    def reorder_rows(rows, index):
        return reorder(
            rows.reshape(group_count, row_count, rows.shape[1]), index
        ).reshape(rows.shape)

    token_all = jnp.concatenate(gather_ring(tokens), axis=0)
    token_late, cot_own = lax.optimization_barrier((token_all, cotangent))
    token_all = token_late
    cot_ordered = gather_rows(cot_own)
    cot_all = reorder_rows(cot_ordered, device_of_slot)

    token_wide = token_all.astype(wide_type)
    inverse_all = inverse_rms(token_wide)
    first_all = (token_wide * inverse_all * prenorm_gain).astype(low_type)
    raw = mm(first_all, head_weight, 1, 0)
    cosine, sine_part = rope_tables(position, head_dim)

    hidden_here = down_weight.shape[1]
    flat_down = down_weight.reshape(experts_here * hidden_here, model_width)

    allowed = segment[:, None] == segment[None, :]

    def head_columns(values, block, head):
        start = block * width_here + head * head_dim
        return values[:, start : start + head_dim]

    kept_heads = []
    mixed_parts = []
    for head in range(heads_here):
        query_raw = head_columns(raw, 0, head)
        key_raw = head_columns(raw, 1, head)
        query_inverse = inverse_rms(query_raw)
        key_inverse = inverse_rms(key_raw)
        query_normed = query_raw * query_inverse * querynorm_gain
        key_normed = key_raw * key_inverse * keynorm_gain
        query_low = (query_normed * cosine + turn_half(query_normed) * sine_part).astype(
            low_type
        )
        key_low = (key_normed * cosine + turn_half(key_normed) * sine_part).astype(low_type)
        value_low = head_columns(raw, 2, head).astype(low_type)
        scores = jnp.where(allowed, mm(query_low, key_low, 1, 1) * score_scale, masked_value)
        top_score = jnp.max(scores, axis=-1, keepdims=True)
        powers = jnp.exp(scores - top_score)
        log_total = top_score + jnp.log(jnp.sum(powers, axis=-1, keepdims=True))
        weights_low = jnp.exp(scores - log_total).astype(low_type)
        mixed_parts.append(mm(weights_low, value_low, 1, 0).astype(low_type))
        kept_heads.append(
            (query_raw, key_raw, query_low, key_low, value_low, log_total)
        )
    mixed_low = jnp.concatenate(mixed_parts, axis=1)

    mixed_ordered = reorder_rows(mixed_low, slot_of_device)
    output_pieces = {0: output_share}
    distance = replica_count // 2
    while distance:
        for j in list(output_pieces):
            output_pieces[j ^ distance] = rep_exchange(output_pieces[j], distance)
        if distance == replica_count // 2:
            output_pieces[distance] = after(output_pieces[distance], mixed_ordered)
        distance //= 2
    mixed_own = (
        swap_all(mixed_ordered.reshape(group_count, row_count, width_here))
        .transpose(1, 0, 2)
        .reshape(row_count, model_width)
    )
    attention = jnp.zeros((row_count, model_width), wide_type)
    for j, piece in output_pieces.items():
        attention = lax.dynamic_update_slice_in_dim(
            attention, mm(mixed_own, piece, 1, 0), (replica ^ j) * column_share, 1
        )
    residual = tokens.astype(wide_type) + attention
    inverse_two = inverse_rms(residual)
    second_input = (residual * inverse_two * postnorm_gain).astype(low_type)

    def gate_table(rows, code):
        logits = mm(rows, full_router, 1, 0)
        shifted = jnp.where(code > 0, logits, masked_value)
        powers = jnp.exp(shifted - jnp.max(shifted, axis=1, keepdims=True))
        return powers / jnp.sum(powers, axis=1, keepdims=True)

    kept_all = jnp.where(code_all > 1, valid_all, 0.0)
    kept_here = lax.dynamic_slice_in_dim(kept_all, device * experts_here, experts_here, 1)

    def stream_of(cot_part):
        return mm(cot_part, flat_down, 1, 1)

    def expert_chunk(chunk, rows, stream, *earlier):
        gates = gate_table(rows, chunk_of(code_all, chunk)) * chunk_of(kept_all, chunk)
        gates_here = lax.dynamic_slice_in_dim(gates, device * experts_here, experts_here, 1)
        return expert_pass(
            rows, gate_weight, up_weight, stream, gates_here, chunk, chunks, earlier
        )

    second_ring = RingGather(second_input)
    stream_first = window([second_ring], lambda part: stream_of(part), chunk_of(cot_all, 0))
    stream_last = window([second_ring], lambda part: stream_of(part), chunk_of(cot_all, 1))
    rows_first = jnp.concatenate(second_ring.blocks[:blocks_here], axis=0)
    *earlier, pair_first = window(
        [second_ring],
        lambda rows, stream: expert_chunk(0, rows, stream),
        rows_first,
        stream_first,
    )
    window([second_ring], lambda: ())
    rows_last = jnp.concatenate(second_ring.blocks[blocks_here:], axis=0)
    inner_all, gback_all, uback_all, pair_last = expert_chunk(
        1, rows_last, stream_last, *earlier
    )
    second_all = jnp.concatenate([rows_first, rows_last], axis=0)
    back_last = expert_back(gback_all, uback_all, gate_weight, up_weight, 1, chunks)
    back_parts = {1: back_last}

    def back_block(slot):
        start = (slot % blocks_here) * row_count
        return back_parts[slot // blocks_here][start : start + row_count]

    def grad_of(left, right):
        return mm(left, right, 0, 0).astype(low_type)

    pair_lanes = jnp.concatenate([pair_first, pair_last], axis=1)
    pair_sent = (kept_here * jnp.sum(pair_lanes, axis=2).transpose(1, 0)).reshape(
        group_count, row_count, experts_here
    )
    code_own = route_code
    gates_own = gate_table(second_input, code_own)

    back_ring = RingSum(back_block, row_count)
    back_parts[0] = window(
        [back_ring],
        lambda gback, uback: expert_back(gback, uback, gate_weight, up_weight, 0, chunks),
        gback_all,
        uback_all,
    )

    def mixture_work(inner, pair):
        return (
            mm(inner, flat_down, 1, 0).astype(low_type),
            swap_all(reorder(pair, slot_of_device)),
        )

    mixture_part, pair_grad = window([back_ring], mixture_work, inner_all, pair_sent)
    mixture_ring = RingSum(slot_rows(mixture_part), row_count)

    def down_work(inner, pair):
        pair_grad = pair.transpose(1, 0, 2).reshape(row_count, expert_total)
        chosen_grad = gates_own * (
            pair_grad - jnp.sum(gates_own * pair_grad, axis=1, keepdims=True)
        )
        logits_grad = jnp.where(code_own > 0, chosen_grad, 0.0).astype(low_type)
        router_back = mm(logits_grad, full_router, 1, 1)
        router_part = mm(second_input, logits_grad, 0, 0)
        return grad_of(inner, cot_all), router_back, router_part

    down_part, router_back, router_part = window(
        [back_ring, mixture_ring], down_work, inner_all, pair_grad
    )
    gate_part = window(
        [back_ring, mixture_ring], lambda gback: grad_of(second_all, gback), gback_all
    )
    second_scattered = back_ring.total()
    second_grad = router_back + second_scattered
    upstream = valid_own * cotangent.astype(wide_type)
    def residual_work(second_grad):
        post_back, postnorm_part = norm_backward(
            residual, inverse_two, postnorm_gain, second_grad
        )
        residual_grad = upstream + post_back
        attention_low = residual_grad.astype(low_type)
        mixed_grad_own = jnp.zeros((row_count, model_width), wide_type)
        for j, piece in output_pieces.items():
            mixed_grad_own = mixed_grad_own + mm(
                lax.dynamic_slice_in_dim(
                    attention_low, (replica ^ j) * column_share, column_share, 1
                ),
                piece,
                1,
                1,
            )
        swap_sent = (
            mixed_grad_own.astype(low_type)
            .reshape(row_count, group_count, width_here)
            .transpose(1, 0, 2)
        )
        return swap_sent, residual_grad, attention_low, jnp.sum(postnorm_part, axis=0)

    swap_sent, residual_grad, attention_low, postnorm_part = window(
        [mixture_ring], residual_work, second_grad
    )
    class Swap(Exchange):
        def start(self):
            self.received = swap_all(self.sent)

    swap = Swap(swap_sent, 0)
    up_part = window(
        [mixture_ring, swap], lambda uback: grad_of(second_all, uback), uback_all
    )
    mixture = mixture_ring.total()
    layer_out = (valid_own * (residual + mixture)).astype(low_type)
    mixed_grad = reorder_rows(swap.received.reshape(group_rows, width_here), device_of_slot)

    def head_backward(head, grad_head):
        query_raw, key_raw, query_low, key_low, value_low, log_total = kept_heads[head]
        query_inverse, key_inverse = inverse_rms(query_raw), inverse_rms(key_raw)
        scores = jnp.where(allowed, mm(query_low, key_low, 1, 1) * score_scale, masked_value)
        weights = jnp.exp(scores - log_total)
        weight_grad = mm(grad_head, value_low, 1, 1)
        row_dot = jnp.sum(weights * weight_grad, axis=-1, keepdims=True)
        score_grad = (weights * (weight_grad - row_dot)).astype(low_type)
        query_back = mm(score_grad, key_low, 1, 0) * score_scale
        key_back = mm(score_grad, query_low, 0, 0) * score_scale
        value_back = mm(weights.astype(low_type), grad_head, 0, 0)
        query_unturned = query_back * cosine + turn_back(query_back * sine_part)
        key_unturned = key_back * cosine + turn_back(key_back * sine_part)
        query_before, query_gain_part = norm_backward(
            query_raw, query_inverse, querynorm_gain, query_unturned
        )
        key_before, key_gain_part = norm_backward(
            key_raw, key_inverse, keynorm_gain, key_unturned
        )
        return (
            query_before.astype(low_type),
            key_before.astype(low_type),
            value_back.astype(low_type),
            jnp.sum(query_gain_part, axis=0),
            jnp.sum(key_gain_part, axis=0),
        )

    attention_gather = RingGather(attention_low)
    head_results = []
    for head in range(heads_here):
        head_results.append(
            window(
                [attention_gather],
                lambda grad_head: head_backward(head, grad_head),
                mixed_grad[:, head * head_dim : (head + 1) * head_dim],
            )
        )
    sent = jnp.concatenate(
        [head_results[head][part] for part in range(3) for head in range(heads_here)], axis=1
    )
    down_sum = lax.psum_scatter(
        down_part.reshape(experts_here, hidden_here, model_width),
        "rep",
        scatter_dimension=1,
        tiled=True,
    )
    sent, down_sum = tie(sent, down_sum)
    querynorm_part = sum(result[3] for result in head_results)
    keynorm_part = sum(result[4] for result in head_results)
    def first_work(sent):
        first_part = mm(sent, head_weight, 1, 1)
        prenorm_part = jnp.sum(first_part * token_wide * inverse_all, axis=0)
        return first_part.astype(low_type), prenorm_part

    while attention_gather.step < group_count // 2 - 2:
        window([attention_gather], lambda: ())
    first_low, prenorm_part = window([attention_gather], first_work, sent)

    def small_swap(parts):
        return swap_all(
            jnp.concatenate([part.reshape(group_count, -1) for part in parts], axis=1)
        )

    def small_pieces(swapped, parts):
        total = rep_sum(jnp.sum(swapped, axis=0))
        pieces, start = [], 0
        for part in parts:
            size = part.size // group_count
            pieces.append(total[start : start + size])
            start += size
        return pieces

    first_ring = RingSum(slot_rows(first_low), row_count)
    head_part = window(
        [attention_gather, first_ring],
        grad_of,
        first_all,
        sent,
    )
    attention_all = jnp.concatenate(attention_gather.blocks, axis=0)
    output_part = window([first_ring], grad_of, mixed_low, attention_all)
    gate_sum = lax.psum_scatter(gate_part, "rep", scatter_dimension=0, tiled=True)
    up_sum = lax.psum_scatter(up_part, "rep", scatter_dimension=0, tiled=True)
    for _ in range(2, group_count // 2):
        first_ring.start()
        first_ring.finish()
    first_grad = first_ring.total()
    head_rows = rep_gather(
        swap_all(
            rep_scatter(
                head_part.reshape(group_count, replica_count, share, 3 * width_here), 1
            )
        )
        .reshape(group_count, share, 3, width_here)
        .transpose(2, 1, 0, 3)
        .reshape(3, share, model_width)
    )
    output_grad = (
        rep_gather(rep_scatter(output_part.reshape(replica_count, share, model_width), 0))
        .reshape(width_here, model_width)
        .astype(wide_type)
    )
    small_parts = [router_part, postnorm_part, prenorm_part, querynorm_part, keynorm_part]
    small_sums = small_pieces(small_swap(small_parts), small_parts)
    query_grad, key_grad, value_grad = (
        head_rows[:, block].reshape(width_here, model_width).astype(wide_type)
        for block in range(3)
    )
    router_grad, postnorm_grad, prenorm_grad, querynorm_grad, keynorm_grad = small_sums
    router_grad = router_grad.reshape(width_here, expert_total)

    token_own = tokens.astype(wide_type)
    inverse_one = inverse_rms(token_own)
    pre_back, _ = norm_backward(token_own, inverse_one, prenorm_gain, first_grad)
    token_grad = residual_grad + pre_back

    down_total = down_sum.astype(wide_type)
    gate_total, up_total = (
        jnp.stack(
            [
                total[:, e * hidden_here : (e + 1) * hidden_here].astype(wide_type)
                for e in range(experts_here)
            ]
        )
        for total in (gate_sum, up_sum)
    )
    return (
        layer_out,
        token_grad,
        query_grad,
        key_grad,
        value_grad,
        output_grad,
        router_grad,
        prenorm_grad,
        querynorm_grad,
        keynorm_grad,
        postnorm_grad,
        gate_total,
        up_total,
        down_total,
    )


def solution(mesh):
    in_specs = (
        P(("rep", "ep"), None),
        P(("rep", "ep"), None),
        P("rep", None),
        P("rep", None),
        P(("rep", "ep"), None),
        P(("rep", "ep"), None),
        P("ep", None),
        P("ep", None),
        P("ep", None),
        P("ep", None),
        P("ep", None),
        P(),
        P(),
        P(),
        P(),
        P("ep", None, None),
        P("ep", None, None),
        P("ep", None, None),
    )
    out_specs = (
        P(("rep", "ep"), None),
        P(("rep", "ep"), None),
        P("ep", None),
        P("ep", None),
        P("ep", None),
        P("ep", None),
        P("ep", None),
        P("ep"),
        P("ep"),
        P("ep"),
        P("ep"),
        P("ep", "rep", None),
        P("ep", "rep", None),
        P("ep", "rep", None),
    )
    return jax.shard_map(body, mesh=mesh, in_specs=in_specs, out_specs=out_specs, check_vma=False)
```

```python
import functools

import jax
import jax.numpy as jnp
from jax import lax
from jax.experimental import pallas as pl
from jax.experimental.pallas import tpu as pltpu
from jax.sharding import PartitionSpec as P

epsilon = 1e-05
rope_base = 10000.0
masked_value = -1e30
low_type = jnp.bfloat16
wide_type = jnp.float32


def inverse_rms(values):
    return lax.rsqrt(jnp.mean(values * values, axis=-1, keepdims=True) + epsilon)


def norm_backward(values, inverse, gain_vector, upstream):
    scaled = upstream * gain_vector
    inner_mean = jnp.mean(scaled * values, axis=-1, keepdims=True)
    result = inverse * scaled - values * (inverse * inverse * inverse) * inner_mean
    return (result, upstream * values * inverse)


def rope_tables(position, dimension):
    halfway = dimension // 2
    indices = jnp.arange(halfway, dtype=wide_type)
    frequency = rope_base ** (-2.0 * indices / dimension)
    angles = position.astype(wide_type)[:, None] * frequency[None, :]
    cosine = jnp.cos(angles)
    sine_part = jnp.sin(angles)
    return (
        jnp.concatenate([cosine, cosine], axis=-1),
        jnp.concatenate([sine_part, sine_part], axis=-1),
    )


def turn_half(values):
    halfway = values.shape[-1] // 2
    return jnp.concatenate([-values[..., halfway:], values[..., :halfway]], axis=-1)


def turn_back(values):
    halfway = values.shape[-1] // 2
    return jnp.concatenate([values[..., halfway:], -values[..., :halfway]], axis=-1)


def row_meta(lengths, group_order):
    boundary = jnp.cumsum(lengths)
    passed = (group_order[:, None] >= boundary[None, :]).astype(jnp.int32)
    segment = jnp.sum(passed, axis=1)
    offset = jnp.sum(passed * lengths[None, :], axis=1)
    return (segment, group_order - offset)


def mm(left, right, left_dim, right_dim):
    return lax.dot_general(
        left,
        right,
        (((left_dim,), (right_dim,)), ((), ())),
        preferred_element_type=wide_type,
    )


def gather_rows(values):
    return lax.all_gather(values, "ep", axis=0, tiled=True)


def ring_order(count):
    return [i for i in range(count) if i % 2 == 0] + [i for i in reversed(range(count)) if i % 2]


def ring_slots(count):
    half = count // 2
    offsets = [0]
    for step in range(1, half):
        offsets += [step, -step]
    return offsets + [half]


def ring_shift(values, direction):
    order = ring_order(lax.axis_size("ep"))
    count = len(order)
    pairs = [(order[i], order[(i + direction) % count]) for i in range(count)]
    return lax.ppermute(values, "ep", pairs)


def tie(*arrays):
    return lax.optimization_barrier(arrays)


def after(value, *others):
    return lax.optimization_barrier((value,) + others)[0]


class RingGather:
    def __init__(self, values):
        self.middle = values.shape[0] // 2
        self.half, self.step = lax.axis_size("ep") // 2, 0
        self.sent = (values, values)
        self.blocks = [values]

    def start(self):
        if self.step == self.half - 1:
            self.sent = (self.sent[0][: self.middle], self.sent[1][self.middle :])
        self.received = (ring_shift(self.sent[0], 1), ring_shift(self.sent[1], -1))

    def finish(self):
        self.step += 1
        onward, backward = self.sent = self.received
        if self.step < self.half:
            self.blocks += [backward, onward]
        else:
            self.blocks += [jnp.concatenate([onward, backward], axis=0)]


class Exchange:
    def __init__(self, values, distance):
        self.sent, self.distance = values, distance

    def start(self):
        self.received = rep_exchange(self.sent, self.distance)

    def finish(self):
        pass


class RingSum:
    def __init__(self, block, rows):
        count = lax.axis_size("ep")
        self.block, self.middle, self.step = block, rows // 2, 0
        self.half = count // 2
        self.slot = {offset: j for j, offset in enumerate(ring_slots(count))}
        far = block(self.slot[self.half])
        self.sent = (far[: self.middle], far[self.middle :])

    def start(self):
        self.received = (ring_shift(self.sent[0], 1), ring_shift(self.sent[1], -1))

    def finish(self):
        self.step += 1
        onward, backward = self.received
        left = self.half - self.step
        middle = self.middle
        if left:
            up, down = self.block(self.slot[left]), self.block(self.slot[-left])
            if self.step == 1:
                onward = jnp.concatenate([add_low(onward, up[:middle]), up[middle:]], axis=0)
                backward = jnp.concatenate(
                    [down[:middle], add_low(backward, down[middle:])], axis=0
                )
            else:
                onward, backward = add_low(onward, up), add_low(backward, down)
        self.sent = (onward, backward)

    def total(self):
        return (
            self.block(self.slot[0]).astype(wide_type)
            + self.sent[0].astype(wide_type)
            + self.sent[1].astype(wide_type)
        )


def window(rings, work, *inputs):
    for ring in rings:
        ring.start()
    inputs, _ = tie(inputs, [ring.sent for ring in rings])
    received, results = tie([ring.received for ring in rings], work(*inputs))
    for ring, pair in zip(rings, received):
        ring.received = pair
        ring.finish()
    return results


def add_low(left, right):
    return (left.astype(wide_type) + right.astype(wide_type)).astype(low_type)


def ring_place(member, count):
    return jnp.where(member % 2 == 0, member // 2, count - 1 - member // 2)


def ring_member(place, count):
    return jnp.where(place < count // 2, 2 * place, 2 * (count - 1 - place) + 1)


def ring_indices(device, count):
    place = ring_place(device, count)
    half = count // 2
    members = [ring_member((place + offset) % count, count) for offset in ring_slots(count)]
    slots = []
    for other in range(count):
        ahead = (ring_place(jnp.int32(other), count) - place) % count
        slot = jnp.where(ahead < half, 2 * ahead - 1, 2 * (count - ahead))
        slots.append(jnp.where(ahead == 0, 0, jnp.where(ahead == half, count - 1, slot)))
    return members, slots


def rep_exchange(values, distance):
    count = lax.axis_size("rep")
    return lax.ppermute(values, "rep", [(i, i ^ distance) for i in range(count)])


def rep_bit(distance):
    return (lax.axis_index("rep") // distance) % 2


def rep_distances():
    count, distance, distances = lax.axis_size("rep"), 1, []
    while distance < count:
        distances.append(distance)
        distance *= 2
    return distances


def rep_gather(gathered, distances):
    for distance in distances:
        shape = gathered.shape[1:]
        other = rep_exchange(gathered, distance)
        mine_first = jnp.stack([gathered, other], axis=1)
        other_first = jnp.stack([other, gathered], axis=1)
        gathered = jnp.where(rep_bit(distance) == 0, mine_first, other_first)
        gathered = gathered.reshape((-1,) + shape)
    return gathered


def rep_scatter(values, axis, distances):
    for distance in distances:
        shape = values.shape
        pairs = values.reshape(shape[:axis] + (shape[axis] // 2, 2) + shape[axis + 1 :])
        bit = rep_bit(distance)
        keep = lax.dynamic_index_in_dim(pairs, bit, axis + 1, keepdims=False)
        send = lax.dynamic_index_in_dim(pairs, 1 - bit, axis + 1, keepdims=False)
        values = add_low(keep, rep_exchange(send, distance))
    return values


def rep_sum(values):
    distance = 1
    while distance < lax.axis_size("rep"):
        values = values + rep_exchange(values, distance)
        distance *= 2
    return values


def swap_all(values):
    return lax.all_to_all(values, "ep", split_axis=0, concat_axis=0, tiled=True)


def expert_kernel(rows_ref, gate_ref, up_ref, stream_ref, gates_ref, *refs):
    inner_ref, gback_ref, uback_ref, pair_ref = refs[-4:]
    expert, step = pl.program_id(0), pl.program_id(1)
    rows = rows_ref[...]
    gate_linear = jnp.dot(rows, gate_ref[0], preferred_element_type=wide_type)
    up_linear = jnp.dot(rows, up_ref[0], preferred_element_type=wide_type)
    stream = stream_ref[...]
    column = gates_ref[:, 0:1]
    for other in range(1, gates_ref.shape[1]):
        column = jnp.where(expert == other, gates_ref[:, other : other + 1], column)
    sigmoid_gate = jax.nn.sigmoid(gate_linear)
    silu_gate = gate_linear * sigmoid_gate
    inner = silu_gate * up_linear
    inner_ref[...] = (column * inner).astype(low_type)
    hidden_grad = column * stream
    gback_ref[...] = (
        hidden_grad * up_linear * sigmoid_gate * (1.0 + gate_linear * (1.0 - sigmoid_gate))
    ).astype(low_type)
    uback_ref[...] = (hidden_grad * silu_gate).astype(low_type)
    product = inner * stream
    lanes = pair_ref.shape[2]
    folded = product[:, :lanes]
    for start in range(lanes, product.shape[1], lanes):
        folded = folded + product[:, start : start + lanes]

    @pl.when(step == 0)
    def _():
        pair_ref[0] = folded

    @pl.when(step > 0)
    def _():
        pair_ref[0] += folded


def expert_pass(rows, gate_weight, up_weight, stream, gates, chunk, chunks, earlier=()):
    count, depth = rows.shape
    experts, _, hidden = gate_weight.shape
    width = 256
    steps = hidden // width
    weight = pl.BlockSpec((1, depth, width), lambda e, j: (e, 0, j))
    out = pl.BlockSpec((count, width), lambda e, j: (chunk, e * steps + j))
    return pl.pallas_call(
        expert_kernel,
        grid=(experts, steps),
        in_specs=[
            pl.BlockSpec((count, depth), lambda e, j: (0, 0)),
            weight,
            weight,
            pl.BlockSpec((count, width), lambda e, j: (0, e * steps + j)),
            pl.BlockSpec(gates.shape, lambda e, j: (0, 0)),
        ]
        + [pl.BlockSpec(memory_space=pl.ANY)] * len(earlier),
        out_specs=[out, out, out, pl.BlockSpec((1, count, 128), lambda e, j: (e, 0, 0))],
        out_shape=[jax.ShapeDtypeStruct((count * chunks, experts * hidden), low_type)] * 3
        + [jax.ShapeDtypeStruct((experts, count, 128), wide_type)],
        input_output_aliases={5 + i: i for i in range(len(earlier))},
        compiler_params=pltpu.CompilerParams(vmem_limit_bytes=56 << 20),
        cost_estimate=pl.CostEstimate(
            flops=4 * count * depth * experts * hidden,
            bytes_accessed=4 * depth * experts * hidden + 20 * count * depth,
            transcendentals=count * experts * hidden,
        ),
    )(rows, gate_weight, up_weight, stream, gates, *earlier)


def expert_back_kernel(gback_ref, uback_ref, gate_ref, up_ref, out_ref):
    experts, _, hidden = gate_ref.shape
    total = None
    for e in range(experts):
        for grad_ref, weight_ref in ((gback_ref, gate_ref), (uback_ref, up_ref)):
            term = mm(grad_ref[:, e * hidden : (e + 1) * hidden], weight_ref[e], 1, 1)
            total = term if total is None else total + term
    out_ref[...] = total.astype(low_type)


def expert_back(gback, uback, gate_weight, up_weight, chunk, chunks):
    count = gback.shape[0] // chunks
    experts, depth, hidden = gate_weight.shape
    width = 256
    whole = pl.BlockSpec((count, experts * hidden), lambda j: (chunk, 0))
    weight = pl.BlockSpec((experts, width, hidden), lambda j: (0, j, 0))
    return pl.pallas_call(
        expert_back_kernel,
        grid=(depth // width,),
        in_specs=[whole, whole, weight, weight],
        out_specs=pl.BlockSpec((count, width), lambda j: (0, j)),
        out_shape=jax.ShapeDtypeStruct((count, depth), low_type),
        compiler_params=pltpu.CompilerParams(vmem_limit_bytes=56 << 20),
        cost_estimate=pl.CostEstimate(
            flops=4 * count * depth * experts * hidden,
            bytes_accessed=4 * depth * experts * hidden + 6 * count * depth,
            transcendentals=0,
        ),
    )(gback, uback, gate_weight, up_weight)


def attention_back_kernel(
    block, scale, query_ref, key_ref, value_ref, grad_ref, total_ref, column_ref, line_ref,
    query_raw_ref, key_raw_ref, gains_ref, cosine_ref, sine_ref, sent_ref, part_ref, key_sum, value_sum
):
    head, heads = pl.program_id(0), pl.num_programs(0)
    rows, depth = query_ref.shape
    lane = lax.broadcasted_iota(jnp.int32, (1, depth), 1)
    sign = jnp.where(lane < depth // 2, 1.0, -1.0)
    key_sum[...] = jnp.zeros_like(key_sum)
    value_sum[...] = jnp.zeros_like(value_sum)

    @pl.when(head == 0)
    def _():
        part_ref[...] = jnp.zeros_like(part_ref)

    def finish(back, raw, gain, cosine, sine, row, column, which):
        turned = back * cosine + pltpu.roll(back * sine, depth // 2, axis=1) * sign
        inverse = lax.rsqrt(jnp.mean(raw * raw, axis=-1, keepdims=True) + 1e-5)
        result, part = norm_backward(raw, inverse, gain, turned)
        sent_ref[row, pl.ds(pl.multiple_of(column * depth, depth), depth)] = result.astype(low_type)
        part_ref[which : which + 1, :] += jnp.sum(part, axis=0, keepdims=True)

    @pl.loop(0, rows // block)
    def _(step):
        row = pl.ds(pl.multiple_of(step * block, block), block)
        query, grad = query_ref[row, :], grad_ref[row, :]
        scores = mm(query, key_ref[...], 1, 1) * scale
        scores = jnp.where(column_ref[row, :] == line_ref[...], scores, masked_value)
        weights = jnp.exp(scores - total_ref[row, pl.ds(0, 1)])
        weight_grad = mm(grad, value_ref[...], 1, 1)
        row_dot = jnp.sum(weights * weight_grad, axis=-1, keepdims=True)
        score_grad = (weights * (weight_grad - row_dot)).astype(low_type)
        key_sum[...] += mm(score_grad, query, 0, 0)
        value_sum[...] += mm(weights.astype(low_type), grad, 0, 0)
        query_back = mm(score_grad, key_ref[...], 1, 0) * scale
        finish(query_back, query_raw_ref[row, :], gains_ref[0:1, :], cosine_ref[row, :], sine_ref[row, :], row, head, 0)

    @pl.loop(0, rows // block)
    def _(step):
        row = pl.ds(pl.multiple_of(step * block, block), block)
        finish(key_sum[row, :] * scale, key_raw_ref[row, :], gains_ref[1:2, :], cosine_ref[row, :], sine_ref[row, :], row, heads + head, 1)
        sent_ref[row, pl.ds(pl.multiple_of((2 * heads + head) * depth, depth), depth)] = value_sum[row, :].astype(low_type)


def attention_back(query, key, value, grad, totals, segment, query_raw, key_raw, gains, cosine, sine, block=256):
    rows, width = query.shape
    depth = cosine.shape[1]
    heads = width // depth
    by_head = pl.BlockSpec((rows, depth), lambda h: (0, h))
    def whole(array):
        return pl.BlockSpec(array.shape, lambda h: (0, 0))
    column, line = segment[:, None], segment[None, :]
    return pl.pallas_call(
        functools.partial(attention_back_kernel, block, depth ** -0.5),
        grid=(heads,),
        in_specs=[by_head] * 4 + [pl.BlockSpec((None, rows, 1), lambda h: (h, 0, 0)), whole(column), whole(line), by_head, by_head, whole(gains), whole(cosine), whole(sine)],
        out_specs=[pl.BlockSpec((rows, 3 * width), lambda h: (0, 0)), pl.BlockSpec((2, depth), lambda h: (0, 0))],
        out_shape=[jax.ShapeDtypeStruct((rows, 3 * width), low_type), jax.ShapeDtypeStruct((2, depth), wide_type)],
        scratch_shapes=[pltpu.VMEM((rows, depth), wide_type)] * 2,
        compiler_params=pltpu.CompilerParams(vmem_limit_bytes=56 << 20),
        cost_estimate=pl.CostEstimate(flops=10 * rows * rows * width, bytes_accessed=30 * rows * width, transcendentals=heads * rows * rows),
    )(query, key, value, grad, totals, column, line, query_raw, key_raw, gains, cosine, sine)


def block_product_kernel(left_ref, *refs):
    out_ref = refs[-1]
    rows = refs[0].shape[0]
    total = None
    for j, ref in enumerate(refs[:-1]):
        term = mm(left_ref[j * rows : (j + 1) * rows, :], ref[...], 0, 0)
        total = term if total is None else total + term
    out_ref[...] = total.astype(low_type)


def block_product(left, blocks):
    rows, width = blocks[0].shape
    tile = 512
    return pl.pallas_call(
        block_product_kernel,
        grid=(width // tile,),
        in_specs=[pl.BlockSpec(left.shape, lambda j: (0, 0))] + [pl.BlockSpec((rows, tile), lambda j: (0, j))] * len(blocks),
        out_specs=pl.BlockSpec((left.shape[1], tile), lambda j: (0, j)),
        out_shape=jax.ShapeDtypeStruct((left.shape[1], width), low_type),
        cost_estimate=pl.CostEstimate(flops=2 * left.size * width, bytes_accessed=2 * left.size + 2 * len(blocks) * rows * width, transcendentals=0),
    )(left, *blocks)


def body(
    tokens,
    cotangent,
    seq_lengths,
    token_order,
    routes,
    slot_index,
    query_weight,
    key_weight,
    value_weight,
    output_weight,
    router_weight,
    prenorm_gain,
    querynorm_gain,
    keynorm_gain,
    postnorm_gain,
    gate_weight,
    up_weight,
    down_weight,
):
    group_count = lax.axis_size("ep")
    device = lax.axis_index("ep")
    row_count, model_width = tokens.shape
    head_dim = querynorm_gain.shape[0]
    width_here = model_width // group_count
    heads_here = width_here // head_dim
    experts_here = gate_weight.shape[0]
    expert_total = experts_here * group_count
    top_count = routes.shape[1]
    capacity = row_count * top_count * 5 // (4 * expert_total)
    group_rows = row_count * group_count
    sequence_count = seq_lengths.shape[1]
    score_scale = head_dim ** (-0.5)

    replica_count = lax.axis_size("rep")
    replica = lax.axis_index("rep")
    share = width_here // replica_count

    device_of_slot, slot_of_device = ring_indices(device, group_count)

    def reorder(blocks, index):
        return jnp.concatenate(
            [lax.dynamic_slice_in_dim(blocks, index[i], 1, 0) for i in range(group_count)], axis=0
        )

    group_order = reorder(token_order[0].reshape(group_count, row_count), device_of_slot)
    segment, position = row_meta(seq_lengths[0], group_order.reshape(group_rows))
    segment_own = segment[:row_count]
    valid_own = (segment_own < sequence_count).astype(wide_type)[:, None]
    valid_all = (segment < sequence_count).astype(wide_type)[:, None]

    expert_ids = jnp.arange(expert_total, dtype=jnp.int32)
    route_code = jnp.zeros((row_count, expert_total), jnp.int32)
    for column in range(top_count):
        hit = routes[:, column, None] == expert_ids[None, :]
        kept = (slot_index[:, column, None] < capacity).astype(jnp.int32)
        route_code = route_code + jnp.where(hit, 1 + kept, 0)
    small_sent = jnp.concatenate([route_code.astype(low_type), router_weight], axis=0)

    projections = jnp.concatenate(
        [
            lax.dynamic_slice_in_dim(piece, replica * share, share, 0).reshape(
                share, group_count, width_here
            )
            for piece in (query_weight, key_weight, value_weight)
        ],
        axis=2,
    ).transpose(1, 0, 2)
    scatter_order = rep_distances()
    gather_order = scatter_order[::-1]
    swapped = swap_all(projections)
    head_weight = (
        rep_gather(swapped[None], gather_order)
        .transpose(1, 0, 2, 3)
        .reshape(model_width, 3 * width_here)
    )
    small_flat = after(small_sent.reshape(-1, head_dim), swapped)
    small_all = swap_all(
        jnp.broadcast_to(small_flat[None], (group_count,) + small_flat.shape)
    ).reshape(group_count, row_count + width_here, expert_total)
    code_all = reorder(small_all[:, :row_count], device_of_slot).reshape(
        group_rows, expert_total
    )
    full_router = small_all[:, row_count:].reshape(model_width, expert_total)
    column_share = model_width // replica_count
    output_share = gather_rows(
        lax.dynamic_slice_in_dim(output_weight, replica * column_share, column_share, 1)
    )
    chunks = 2
    chunk_rows = group_rows // chunks
    blocks_here = group_count // chunks

    def chunk_of(array, chunk):
        return array[chunk * chunk_rows : (chunk + 1) * chunk_rows]

    def slot_rows(array):
        return lambda slot: array[slot * row_count : (slot + 1) * row_count]

    def reorder_rows(rows, index):
        return reorder(
            rows.reshape(group_count, row_count, rows.shape[1]), index
        ).reshape(rows.shape)

    token_ring = RingGather(tokens)
    for step in range(group_count // 2):
        if step == group_count // 2 - 1:
            token_ring.sent = (after(token_ring.sent[0], output_share), token_ring.sent[1])
        token_ring.start()
        token_ring.finish()
    token_all = jnp.concatenate(token_ring.blocks, axis=0)
    token_late, cot_own = lax.optimization_barrier((token_all, cotangent))
    token_all = token_late
    cot_ordered = gather_rows(cot_own)
    cot_all = reorder_rows(cot_ordered, device_of_slot)

    halves = 2 if column_share % 256 == 0 else 1
    piece_width = column_share // halves
    far = replica_count // 2
    far_pieces = [
        rep_exchange(output_share[:, i * piece_width : (i + 1) * piece_width], far)
        for i in range(halves)
    ]
    head_weight = after(head_weight, far_pieces[0])
    token_wide = token_all.astype(wide_type)
    inverse_all = inverse_rms(token_wide)
    first_all = (token_wide * inverse_all * prenorm_gain).astype(low_type)
    raw = mm(first_all, head_weight, 1, 0)
    cosine, sine_part = rope_tables(position, head_dim)

    hidden_here = down_weight.shape[1]
    flat_down = down_weight.reshape(experts_here * hidden_here, model_width)

    allowed = segment[:, None] == segment[None, :]

    def head_columns(values, block, head):
        start = block * width_here + head * head_dim
        return values[:, start : start + head_dim]

    kept_heads = []
    mixed_parts = []
    for head in range(heads_here):
        query_raw = head_columns(raw, 0, head)
        key_raw = head_columns(raw, 1, head)
        query_inverse = inverse_rms(query_raw)
        key_inverse = inverse_rms(key_raw)
        query_normed = query_raw * query_inverse * querynorm_gain
        key_normed = key_raw * key_inverse * keynorm_gain
        query_low = (query_normed * cosine + turn_half(query_normed) * sine_part).astype(
            low_type
        )
        key_low = (key_normed * cosine + turn_half(key_normed) * sine_part).astype(low_type)
        value_low = head_columns(raw, 2, head).astype(low_type)
        scores = jnp.where(allowed, mm(query_low, key_low, 1, 1) * score_scale, masked_value)
        top_score = jnp.max(scores, axis=-1, keepdims=True)
        powers = jnp.exp(scores - top_score)
        log_total = top_score + jnp.log(jnp.sum(powers, axis=-1, keepdims=True))
        weights_low = jnp.exp(scores - log_total).astype(low_type)
        mixed_parts.append(mm(weights_low, value_low, 1, 0).astype(low_type))
        kept_heads.append(
            (query_raw, key_raw, query_low, key_low, value_low, log_total)
        )
    mixed_low = jnp.concatenate(mixed_parts, axis=1)

    mixed_ordered = reorder_rows(mixed_low, slot_of_device)
    output_pieces = {(0, 0): output_share}
    for i in range(halves):
        output_pieces[far, i * piece_width] = after(far_pieces[i], mixed_ordered)
    for distance in gather_order[1:]:
        for j, start in list(output_pieces):
            output_pieces[j ^ distance, start] = rep_exchange(
                after(output_pieces[j, start], mixed_ordered), distance
            )
    mixed_own = (
        swap_all(mixed_ordered.reshape(group_count, row_count, width_here))
        .transpose(1, 0, 2)
        .reshape(row_count, model_width)
    )
    attention = jnp.zeros((row_count, model_width), wide_type)
    for (j, start), piece in output_pieces.items():
        attention = lax.dynamic_update_slice_in_dim(
            attention, mm(mixed_own, piece, 1, 0), (replica ^ j) * column_share + start, 1
        )
    residual = tokens.astype(wide_type) + attention
    inverse_two = inverse_rms(residual)
    second_input = (residual * inverse_two * postnorm_gain).astype(low_type)

    def gate_table(rows, code):
        logits = mm(rows, full_router, 1, 0)
        shifted = jnp.where(code > 0, logits, masked_value)
        powers = jnp.exp(shifted - jnp.max(shifted, axis=1, keepdims=True))
        return powers / jnp.sum(powers, axis=1, keepdims=True)

    kept_all = jnp.where(code_all > 1, valid_all, 0.0)
    kept_here = lax.dynamic_slice_in_dim(kept_all, device * experts_here, experts_here, 1)

    def stream_of(cot_part):
        return mm(cot_part, flat_down, 1, 1)

    def expert_chunk(chunk, rows, stream, *earlier):
        gates = gate_table(rows, chunk_of(code_all, chunk)) * chunk_of(kept_all, chunk)
        gates_here = lax.dynamic_slice_in_dim(gates, device * experts_here, experts_here, 1)
        return expert_pass(
            rows, gate_weight, up_weight, stream, gates_here, chunk, chunks, earlier
        )

    second_ring = RingGather(second_input)
    stream_first = window([second_ring], lambda part: stream_of(part), chunk_of(cot_all, 0))
    stream_last = window([second_ring], lambda part: stream_of(part), chunk_of(cot_all, 1))
    rows_first = jnp.concatenate(second_ring.blocks[:blocks_here], axis=0)
    *earlier, pair_first = window(
        [second_ring],
        lambda rows, stream: expert_chunk(0, rows, stream),
        rows_first,
        stream_first,
    )
    window([second_ring], lambda: ())
    rows_last = jnp.concatenate(second_ring.blocks[blocks_here:], axis=0)
    inner_all, gback_all, uback_all, pair_last = expert_chunk(
        1, rows_last, stream_last, *earlier
    )
    second_all = jnp.concatenate([rows_first, rows_last], axis=0)
    back_last = expert_back(gback_all, uback_all, gate_weight, up_weight, 1, chunks)
    back_parts = {1: back_last}

    def back_block(slot):
        start = (slot % blocks_here) * row_count
        return back_parts[slot // blocks_here][start : start + row_count]

    def grad_of(left, right):
        return mm(left, right, 0, 0).astype(low_type)

    pair_lanes = jnp.concatenate([pair_first, pair_last], axis=1)
    pair_sent = (kept_here * jnp.sum(pair_lanes, axis=2).transpose(1, 0)).reshape(
        group_count, row_count, experts_here
    )
    code_own = route_code
    gates_own = gate_table(second_input, code_own)

    back_ring = RingSum(back_block, row_count)
    back_parts[0] = window(
        [back_ring],
        lambda gback, uback: expert_back(gback, uback, gate_weight, up_weight, 0, chunks),
        gback_all,
        uback_all,
    )

    def mixture_work(inner, pair):
        return (
            mm(inner, flat_down, 1, 0).astype(low_type),
            swap_all(reorder(pair, slot_of_device)),
        )

    mixture_part, pair_grad = window([back_ring], mixture_work, inner_all, pair_sent)
    mixture_ring = RingSum(slot_rows(mixture_part), row_count)

    def down_work(inner, pair):
        pair_grad = pair.transpose(1, 0, 2).reshape(row_count, expert_total)
        chosen_grad = gates_own * (
            pair_grad - jnp.sum(gates_own * pair_grad, axis=1, keepdims=True)
        )
        logits_grad = jnp.where(code_own > 0, chosen_grad, 0.0).astype(low_type)
        router_back = mm(logits_grad, full_router, 1, 1)
        router_part = mm(second_input, logits_grad, 0, 0)
        return grad_of(inner, cot_all), router_back, router_part

    down_part, router_back, router_part = window(
        [back_ring, mixture_ring], down_work, inner_all, pair_grad
    )
    gate_part = window(
        [back_ring, mixture_ring], lambda gback: grad_of(second_all, gback), gback_all
    )
    second_scattered = back_ring.total()
    second_grad = router_back + second_scattered
    upstream = valid_own * cotangent.astype(wide_type)
    def residual_work(second_grad):
        post_back, postnorm_part = norm_backward(
            residual, inverse_two, postnorm_gain, second_grad
        )
        residual_grad = upstream + post_back
        attention_low = residual_grad.astype(low_type)
        mixed_grad_own = jnp.zeros((row_count, model_width), wide_type)
        for (j, start), piece in output_pieces.items():
            mixed_grad_own = mixed_grad_own + mm(
                lax.dynamic_slice_in_dim(
                    attention_low, (replica ^ j) * column_share + start, piece.shape[1], 1
                ),
                piece,
                1,
                1,
            )
        swap_sent = (
            mixed_grad_own.astype(low_type)
            .reshape(row_count, group_count, width_here)
            .transpose(1, 0, 2)
        )
        return swap_sent, residual_grad, attention_low, jnp.sum(postnorm_part, axis=0)

    swap_sent, residual_grad, attention_low, postnorm_part = window(
        [mixture_ring], residual_work, second_grad
    )
    class Swap(Exchange):
        def start(self):
            self.received = swap_all(self.sent)

    swap = Swap(swap_sent, 0)
    up_part = window(
        [mixture_ring, swap], lambda uback: grad_of(second_all, uback), uback_all
    )
    mixture = mixture_ring.total()
    layer_out = (valid_own * (residual + mixture)).astype(low_type)
    mixed_grad = reorder_rows(swap.received.reshape(group_rows, width_here), device_of_slot)

    query_raws, key_raws, query_lows, key_lows, value_lows = (
        jnp.concatenate([kept[i] for kept in kept_heads], axis=1) for i in range(5)
    )
    log_totals = jnp.stack([kept[5] for kept in kept_heads])
    attention_gather = RingGather(attention_low)
    sent, gain_parts = window(
        [attention_gather],
        lambda grads: tuple(
            attention_back(
                query_lows,
                key_lows,
                value_lows,
                grads,
                log_totals,
                segment,
                query_raws,
                key_raws,
                jnp.stack([querynorm_gain, keynorm_gain]),
                cosine,
                sine_part,
            )
        ),
        mixed_grad,
    )
    querynorm_part, keynorm_part = gain_parts[0], gain_parts[1]
    down_sum = lax.psum_scatter(
        down_part.reshape(experts_here, hidden_here, model_width),
        "rep",
        scatter_dimension=1,
        tiled=True,
    )
    sent, down_sum = tie(sent, down_sum)

    def first_work(sent, head):
        first_part = mm(sent, head_weight, 1, 1)
        prenorm_part = jnp.sum(first_part * token_wide * inverse_all, axis=0)
        return first_part.astype(low_type), prenorm_part, rep_scatter(head, 1, scatter_order[:1])

    head_part = window([attention_gather], grad_of, first_all, sent)
    first_low, prenorm_part, head_part = window(
        [attention_gather],
        first_work,
        sent,
        head_part.reshape(group_count, replica_count, share, 3 * width_here),
    )

    def small_swap(parts):
        return swap_all(
            jnp.concatenate([part.reshape(group_count, -1) for part in parts], axis=1)
        )

    def small_pieces(swapped, parts):
        total = rep_sum(jnp.sum(swapped, axis=0))
        pieces, start = [], 0
        for part in parts:
            size = part.size // group_count
            pieces.append(total[start : start + size])
            start += size
        return pieces

    first_ring = RingSum(slot_rows(first_low), row_count)
    small_parts = [router_part, postnorm_part, prenorm_part, querynorm_part, keynorm_part]
    head_part, small_swapped = window(
        [attention_gather, first_ring],
        lambda head, *small: (rep_scatter(head, 1, scatter_order[1:]), small_swap(small)),
        head_part,
        *small_parts,
    )
    gate_sum = lax.psum_scatter(gate_part, "rep", scatter_dimension=0, tiled=True)
    up_sum = lax.psum_scatter(up_part, "rep", scatter_dimension=0, tiled=True)
    head_swap = Swap(head_part.reshape(group_count, share, 3 * width_here), 0)
    output_part = window(
        [first_ring, head_swap],
        lambda mixed, *blocks: block_product(mixed, blocks),
        mixed_low,
        *attention_gather.blocks,
    )
    head_rows, output_part, small_sums = window(
        [first_ring],
        lambda head, output, small: (
            rep_gather(
                head.reshape(group_count, share, 3, width_here)
                .transpose(2, 1, 0, 3)
                .reshape(1, 3, share, model_width),
                gather_order[:-1],
            ),
            rep_scatter(output, 0, scatter_order[:1]),
            small_pieces(small, small_parts),
        ),
        head_swap.received,
        output_part.reshape(replica_count, share, model_width),
        small_swapped,
    )
    head_rows, output_part = window(
        [first_ring],
        lambda head, output: (
            rep_gather(head, gather_order[-1:]),
            rep_scatter(output, 0, scatter_order[1:]),
        ),
        head_rows,
        output_part,
    )
    first_grad = first_ring.total()
    output_grad = (
        rep_gather(output_part, gather_order)
        .reshape(width_here, model_width)
        .astype(wide_type)
    )
    query_grad, key_grad, value_grad = (
        head_rows[:, block].reshape(width_here, model_width).astype(wide_type)
        for block in range(3)
    )
    router_grad, postnorm_grad, prenorm_grad, querynorm_grad, keynorm_grad = small_sums
    router_grad = router_grad.reshape(width_here, expert_total)

    token_own = tokens.astype(wide_type)
    inverse_one = inverse_rms(token_own)
    pre_back, _ = norm_backward(token_own, inverse_one, prenorm_gain, first_grad)
    token_grad = residual_grad + pre_back

    down_total = down_sum.astype(wide_type)
    gate_total, up_total = (
        jnp.stack(
            [
                total[:, e * hidden_here : (e + 1) * hidden_here].astype(wide_type)
                for e in range(experts_here)
            ]
        )
        for total in (gate_sum, up_sum)
    )
    return (
        layer_out,
        token_grad,
        query_grad,
        key_grad,
        value_grad,
        output_grad,
        router_grad,
        prenorm_grad,
        querynorm_grad,
        keynorm_grad,
        postnorm_grad,
        gate_total,
        up_total,
        down_total,
    )


def solution(mesh):
    in_specs = (
        P(("rep", "ep"), None),
        P(("rep", "ep"), None),
        P("rep", None),
        P("rep", None),
        P(("rep", "ep"), None),
        P(("rep", "ep"), None),
        P("ep", None),
        P("ep", None),
        P("ep", None),
        P("ep", None),
        P("ep", None),
        P(),
        P(),
        P(),
        P(),
        P("ep", None, None),
        P("ep", None, None),
        P("ep", None, None),
    )
    out_specs = (
        P(("rep", "ep"), None),
        P(("rep", "ep"), None),
        P("ep", None),
        P("ep", None),
        P("ep", None),
        P("ep", None),
        P("ep", None),
        P("ep"),
        P("ep"),
        P("ep"),
        P("ep"),
        P("ep", "rep", None),
        P("ep", "rep", None),
        P("ep", "rep", None),
    )
    return jax.shard_map(body, mesh=mesh, in_specs=in_specs, out_specs=out_specs, check_vma=False)
```

```python
import functools

import jax
import jax.numpy as jnp
from jax import lax
from jax.experimental import pallas as pl
from jax.experimental.pallas import tpu as pltpu
from jax.sharding import PartitionSpec as P

epsilon = 1e-05
rope_base = 10000.0
masked_value = -1e30
low_type = jnp.bfloat16
wide_type = jnp.float32


def inverse_rms(values):
    return lax.rsqrt(jnp.mean(values * values, axis=-1, keepdims=True) + epsilon)


def norm_backward(values, inverse, gain_vector, upstream):
    scaled = upstream * gain_vector
    inner_mean = jnp.mean(scaled * values, axis=-1, keepdims=True)
    result = inverse * scaled - values * (inverse * inverse * inverse) * inner_mean
    return (result, upstream * values * inverse)


def rope_tables(position, dimension):
    halfway = dimension // 2
    indices = jnp.arange(halfway, dtype=wide_type)
    frequency = rope_base ** (-2.0 * indices / dimension)
    angles = position.astype(wide_type)[:, None] * frequency[None, :]
    cosine = jnp.cos(angles)
    sine_part = jnp.sin(angles)
    return (
        jnp.concatenate([cosine, cosine], axis=-1),
        jnp.concatenate([sine_part, sine_part], axis=-1),
    )


def turn_half(values):
    halfway = values.shape[-1] // 2
    return jnp.concatenate([-values[..., halfway:], values[..., :halfway]], axis=-1)


def turn_back(values):
    halfway = values.shape[-1] // 2
    return jnp.concatenate([values[..., halfway:], -values[..., :halfway]], axis=-1)


def row_meta(lengths, group_order):
    boundary = jnp.cumsum(lengths)
    passed = (group_order[:, None] >= boundary[None, :]).astype(jnp.int32)
    segment = jnp.sum(passed, axis=1)
    offset = jnp.sum(passed * lengths[None, :], axis=1)
    return (segment, group_order - offset)


def mm(left, right, left_dim, right_dim):
    return lax.dot_general(
        left,
        right,
        (((left_dim,), (right_dim,)), ((), ())),
        preferred_element_type=wide_type,
    )


def gather_rows(values):
    return lax.all_gather(values, "ep", axis=0, tiled=True)


def ring_order(count):
    return [i for i in range(count) if i % 2 == 0] + [i for i in reversed(range(count)) if i % 2]


def ring_slots(count):
    half = count // 2
    offsets = [0]
    for step in range(1, half):
        offsets += [step, -step]
    return offsets + [half]


def ring_shift(values, direction):
    order = ring_order(lax.axis_size("ep"))
    count = len(order)
    pairs = [(order[i], order[(i + direction) % count]) for i in range(count)]
    return lax.ppermute(values, "ep", pairs)


def tie(*arrays):
    return lax.optimization_barrier(arrays)


def after(value, *others):
    return lax.optimization_barrier((value,) + others)[0]


class RingGather:
    def __init__(self, values):
        self.middle = values.shape[0] // 2
        self.half, self.step = lax.axis_size("ep") // 2, 0
        self.sent = (values, values)
        self.blocks = [values]

    def start(self):
        if self.step == self.half - 1:
            self.sent = (self.sent[0][: self.middle], self.sent[1][self.middle :])
        self.received = (ring_shift(self.sent[0], 1), ring_shift(self.sent[1], -1))

    def finish(self):
        self.step += 1
        onward, backward = self.sent = self.received
        if self.step < self.half:
            self.blocks += [backward, onward]
        else:
            self.blocks += [jnp.concatenate([onward, backward], axis=0)]


class Exchange:
    def __init__(self, values, distance):
        self.sent, self.distance = values, distance

    def start(self):
        self.received = rep_exchange(self.sent, self.distance)

    def finish(self):
        pass


class RingSum:
    def __init__(self, block, rows):
        count = lax.axis_size("ep")
        self.block, self.middle, self.step = block, rows // 2, 0
        self.half = count // 2
        self.slot = {offset: j for j, offset in enumerate(ring_slots(count))}
        far = block(self.slot[self.half])
        self.sent = (far[: self.middle], far[self.middle :])

    def start(self):
        self.received = (ring_shift(self.sent[0], 1), ring_shift(self.sent[1], -1))

    def finish(self):
        self.step += 1
        onward, backward = self.received
        left = self.half - self.step
        middle = self.middle
        if left:
            up, down = self.block(self.slot[left]), self.block(self.slot[-left])
            if self.step == 1:
                onward = jnp.concatenate([add_low(onward, up[:middle]), up[middle:]], axis=0)
                backward = jnp.concatenate(
                    [down[:middle], add_low(backward, down[middle:])], axis=0
                )
            else:
                onward, backward = add_low(onward, up), add_low(backward, down)
        self.sent = (onward, backward)

    def total(self):
        return (
            self.block(self.slot[0]).astype(wide_type)
            + self.sent[0].astype(wide_type)
            + self.sent[1].astype(wide_type)
        )


def window(rings, work, *inputs, waits=()):
    for ring in rings:
        ring.start()
    inputs, _ = tie(inputs, [ring.sent for ring in rings])
    received, waits, results = tie([ring.received for ring in rings], waits, work(*inputs))
    for ring, pair in zip(rings, received):
        ring.received = pair
        ring.finish()
    return (results, *waits) if waits else results


def add_low(left, right):
    return (left.astype(wide_type) + right.astype(wide_type)).astype(low_type)


def ring_place(member, count):
    return jnp.where(member % 2 == 0, member // 2, count - 1 - member // 2)


def ring_member(place, count):
    return jnp.where(place < count // 2, 2 * place, 2 * (count - 1 - place) + 1)


def ring_indices(device, count):
    place = ring_place(device, count)
    half = count // 2
    members = [ring_member((place + offset) % count, count) for offset in ring_slots(count)]
    slots = []
    for other in range(count):
        ahead = (ring_place(jnp.int32(other), count) - place) % count
        slot = jnp.where(ahead < half, 2 * ahead - 1, 2 * (count - ahead))
        slots.append(jnp.where(ahead == 0, 0, jnp.where(ahead == half, count - 1, slot)))
    return members, slots


def rep_exchange(values, distance):
    count = lax.axis_size("rep")
    return lax.ppermute(values, "rep", [(i, i ^ distance) for i in range(count)])


def rep_bit(distance):
    return (lax.axis_index("rep") // distance) % 2


def rep_distances():
    count, distance, distances = lax.axis_size("rep"), 1, []
    while distance < count:
        distances.append(distance)
        distance *= 2
    return distances


def rep_gather(gathered, distances):
    for distance in distances:
        shape = gathered.shape[1:]
        other = rep_exchange(gathered, distance)
        mine_first = jnp.stack([gathered, other], axis=1)
        other_first = jnp.stack([other, gathered], axis=1)
        gathered = jnp.where(rep_bit(distance) == 0, mine_first, other_first)
        gathered = gathered.reshape((-1,) + shape)
    return gathered


def rep_scatter(values, axis, distances):
    for distance in distances:
        shape = values.shape
        pairs = values.reshape(shape[:axis] + (shape[axis] // 2, 2) + shape[axis + 1 :])
        bit = rep_bit(distance)
        keep = lax.dynamic_index_in_dim(pairs, bit, axis + 1, keepdims=False)
        send = lax.dynamic_index_in_dim(pairs, 1 - bit, axis + 1, keepdims=False)
        values = add_low(keep, rep_exchange(send, distance))
    return values


def rep_sum(values):
    distance = 1
    while distance < lax.axis_size("rep"):
        values = values + rep_exchange(values, distance)
        distance *= 2
    return values


def swap_all(values):
    return lax.all_to_all(values, "ep", split_axis=0, concat_axis=0, tiled=True)


def expert_kernel(rows_ref, gate_ref, up_ref, stream_ref, gates_ref, *refs):
    inner_ref, gback_ref, uback_ref, pair_ref = refs[-4:]
    expert, step = pl.program_id(0), pl.program_id(1)
    rows = rows_ref[...]
    gate_linear = jnp.dot(rows, gate_ref[0], preferred_element_type=wide_type)
    up_linear = jnp.dot(rows, up_ref[0], preferred_element_type=wide_type)
    stream = stream_ref[...]
    column = gates_ref[:, 0:1]
    for other in range(1, gates_ref.shape[1]):
        column = jnp.where(expert == other, gates_ref[:, other : other + 1], column)
    sigmoid_gate = jax.nn.sigmoid(gate_linear)
    silu_gate = gate_linear * sigmoid_gate
    inner = silu_gate * up_linear
    inner_ref[...] = (column * inner).astype(low_type)
    hidden_grad = column * stream
    gback_ref[...] = (
        hidden_grad * up_linear * sigmoid_gate * (1.0 + gate_linear * (1.0 - sigmoid_gate))
    ).astype(low_type)
    uback_ref[...] = (hidden_grad * silu_gate).astype(low_type)
    product = inner * stream
    lanes = pair_ref.shape[2]
    folded = product[:, :lanes]
    for start in range(lanes, product.shape[1], lanes):
        folded = folded + product[:, start : start + lanes]

    @pl.when(step == 0)
    def _():
        pair_ref[0] = folded

    @pl.when(step > 0)
    def _():
        pair_ref[0] += folded


def expert_pass(rows, gate_weight, up_weight, stream, gates, chunk, chunks, earlier=()):
    count, depth = rows.shape
    experts, _, hidden = gate_weight.shape
    width = 256
    steps = hidden // width
    weight = pl.BlockSpec((1, depth, width), lambda e, j: (e, 0, j))
    out = pl.BlockSpec((count, width), lambda e, j: (chunk, e * steps + j))
    return pl.pallas_call(
        expert_kernel,
        grid=(experts, steps),
        in_specs=[
            pl.BlockSpec((count, depth), lambda e, j: (0, 0)),
            weight,
            weight,
            pl.BlockSpec((count, width), lambda e, j: (0, e * steps + j)),
            pl.BlockSpec(gates.shape, lambda e, j: (0, 0)),
        ]
        + [pl.BlockSpec(memory_space=pl.ANY)] * len(earlier),
        out_specs=[out, out, out, pl.BlockSpec((1, count, 128), lambda e, j: (e, 0, 0))],
        out_shape=[jax.ShapeDtypeStruct((count * chunks, experts * hidden), low_type)] * 3
        + [jax.ShapeDtypeStruct((experts, count, 128), wide_type)],
        input_output_aliases={5 + i: i for i in range(len(earlier))},
        compiler_params=pltpu.CompilerParams(vmem_limit_bytes=56 << 20),
        cost_estimate=pl.CostEstimate(
            flops=4 * count * depth * experts * hidden,
            bytes_accessed=4 * depth * experts * hidden + 20 * count * depth,
            transcendentals=count * experts * hidden,
        ),
    )(rows, gate_weight, up_weight, stream, gates, *earlier)


def expert_back_kernel(gback_ref, uback_ref, gate_ref, up_ref, out_ref):
    experts, _, hidden = gate_ref.shape
    total = None
    for e in range(experts):
        for grad_ref, weight_ref in ((gback_ref, gate_ref), (uback_ref, up_ref)):
            term = mm(grad_ref[:, e * hidden : (e + 1) * hidden], weight_ref[e], 1, 1)
            total = term if total is None else total + term
    out_ref[...] = total.astype(low_type)


def expert_back(gback, uback, gate_weight, up_weight, chunk, chunks):
    count = gback.shape[0] // chunks
    experts, depth, hidden = gate_weight.shape
    width = 256
    whole = pl.BlockSpec((count, experts * hidden), lambda j: (chunk, 0))
    weight = pl.BlockSpec((experts, width, hidden), lambda j: (0, j, 0))
    return pl.pallas_call(
        expert_back_kernel,
        grid=(depth // width,),
        in_specs=[whole, whole, weight, weight],
        out_specs=pl.BlockSpec((count, width), lambda j: (0, j)),
        out_shape=jax.ShapeDtypeStruct((count, depth), low_type),
        compiler_params=pltpu.CompilerParams(vmem_limit_bytes=56 << 20),
        cost_estimate=pl.CostEstimate(
            flops=4 * count * depth * experts * hidden,
            bytes_accessed=4 * depth * experts * hidden + 6 * count * depth,
            transcendentals=0,
        ),
    )(gback, uback, gate_weight, up_weight)


def attention_back_kernel(
    block, scale, order_ref, query_ref, key_ref, value_ref, swapped_ref, total_ref, column_ref, line_ref,
    query_raw_ref, key_raw_ref, gains_ref, cosine_ref, sine_ref, sent_ref, part_ref, key_sum, value_sum, grad_ref
):
    head, heads = pl.program_id(0), pl.num_programs(0)
    rows, depth = query_ref.shape
    lane = lax.broadcasted_iota(jnp.int32, (1, depth), 1)
    sign = jnp.where(lane < depth // 2, 1.0, -1.0)
    share = swapped_ref.shape[1]
    for slot in range(swapped_ref.shape[0]):
        grad_ref[slot * share : (slot + 1) * share, :] = swapped_ref[order_ref[slot]]
    key_sum[...] = jnp.zeros_like(key_sum)
    value_sum[...] = jnp.zeros_like(value_sum)

    @pl.when(head == 0)
    def _():
        part_ref[...] = jnp.zeros_like(part_ref)

    def finish(back, raw, gain, cosine, sine, row, column, which):
        turned = back * cosine + pltpu.roll(back * sine, depth // 2, axis=1) * sign
        inverse = lax.rsqrt(jnp.mean(raw * raw, axis=-1, keepdims=True) + 1e-5)
        result, part = norm_backward(raw, inverse, gain, turned)
        sent_ref[row, pl.ds(pl.multiple_of(column * depth, depth), depth)] = result.astype(low_type)
        part_ref[which : which + 1, :] += jnp.sum(part, axis=0, keepdims=True)

    @pl.loop(0, rows // block)
    def _(step):
        row = pl.ds(pl.multiple_of(step * block, block), block)
        query, grad = query_ref[row, :], grad_ref[row, :]
        scores = mm(query, key_ref[...], 1, 1) * scale
        scores = jnp.where(column_ref[row, :] == line_ref[...], scores, masked_value)
        weights = jnp.exp(scores - total_ref[row, pl.ds(0, 1)])
        weight_grad = mm(grad, value_ref[...], 1, 1)
        row_dot = jnp.sum(weights * weight_grad, axis=-1, keepdims=True)
        score_grad = (weights * (weight_grad - row_dot)).astype(low_type)
        key_sum[...] += mm(score_grad, query, 0, 0)
        value_sum[...] += mm(weights.astype(low_type), grad, 0, 0)
        query_back = mm(score_grad, key_ref[...], 1, 0) * scale
        finish(query_back, query_raw_ref[row, :], gains_ref[0:1, :], cosine_ref[row, :], sine_ref[row, :], row, head, 0)

    @pl.loop(0, rows // block)
    def _(step):
        row = pl.ds(pl.multiple_of(step * block, block), block)
        finish(key_sum[row, :] * scale, key_raw_ref[row, :], gains_ref[1:2, :], cosine_ref[row, :], sine_ref[row, :], row, heads + head, 1)
        sent_ref[row, pl.ds(pl.multiple_of((2 * heads + head) * depth, depth), depth)] = value_sum[row, :].astype(low_type)


def attention_back(lows, swapped, order, totals, segment, raw, gains, cosine, sine, block=256):
    rows, depth = cosine.shape
    heads = lows.shape[1] // (3 * depth)
    block = block if rows % block == 0 else rows

    def by_head(start):
        return pl.BlockSpec((rows, depth), lambda h, order: (0, start * heads + h))

    def whole(array):
        return pl.BlockSpec(array.shape, lambda h, order: (0, 0))

    column, line = segment[:, None], segment[None, :]
    return pl.pallas_call(
        functools.partial(attention_back_kernel, block, depth**-0.5),
        grid_spec=pltpu.PrefetchScalarGridSpec(
            num_scalar_prefetch=1,
            grid=(heads,),
            in_specs=[
                by_head(0),
                by_head(1),
                by_head(2),
                pl.BlockSpec(swapped.shape[:2] + (depth,), lambda h, order: (0, 0, h)),
                pl.BlockSpec((None, rows, 1), lambda h, order: (h, 0, 0)),
                whole(column),
                whole(line),
                by_head(0),
                by_head(1),
                whole(gains),
                whole(cosine),
                whole(sine),
            ],
            out_specs=[
                pl.BlockSpec((rows, lows.shape[1]), lambda h, order: (0, 0)),
                pl.BlockSpec((2, depth), lambda h, order: (0, 0)),
            ],
            scratch_shapes=[pltpu.VMEM((rows, depth), wide_type)] * 2
            + [pltpu.VMEM((rows, depth), low_type)],
        ),
        out_shape=[
            jax.ShapeDtypeStruct(lows.shape, low_type),
            jax.ShapeDtypeStruct((2, depth), wide_type),
        ],
        compiler_params=pltpu.CompilerParams(vmem_limit_bytes=56 << 20),
        cost_estimate=pl.CostEstimate(
            flops=10 * rows * rows * heads * depth,
            bytes_accessed=30 * rows * heads * depth,
            transcendentals=heads * rows * rows,
        ),
    )(order, lows, lows, lows, swapped, totals, column, line, raw, raw, gains, cosine, sine)


def block_product_kernel(left_ref, *refs):
    out_ref = refs[-1]
    rows = refs[0].shape[0]
    total = None
    for j, ref in enumerate(refs[:-1]):
        term = mm(left_ref[j * rows : (j + 1) * rows, :], ref[...], 0, 0)
        total = term if total is None else total + term
    out_ref[...] = total.astype(low_type)


def block_product(left, blocks):
    rows, width = blocks[0].shape
    tile = 512
    return pl.pallas_call(
        block_product_kernel,
        grid=(width // tile,),
        in_specs=[pl.BlockSpec(left.shape, lambda j: (0, 0))] + [pl.BlockSpec((rows, tile), lambda j: (0, j))] * len(blocks),
        out_specs=pl.BlockSpec((left.shape[1], tile), lambda j: (0, j)),
        out_shape=jax.ShapeDtypeStruct((left.shape[1], width), low_type),
        cost_estimate=pl.CostEstimate(flops=2 * left.size * width, bytes_accessed=2 * left.size + 2 * len(blocks) * rows * width, transcendentals=0),
    )(left, *blocks)


def body(
    tokens,
    cotangent,
    seq_lengths,
    token_order,
    routes,
    slot_index,
    query_weight,
    key_weight,
    value_weight,
    output_weight,
    router_weight,
    prenorm_gain,
    querynorm_gain,
    keynorm_gain,
    postnorm_gain,
    gate_weight,
    up_weight,
    down_weight,
):
    group_count = lax.axis_size("ep")
    device = lax.axis_index("ep")
    row_count, model_width = tokens.shape
    head_dim = querynorm_gain.shape[0]
    width_here = model_width // group_count
    heads_here = width_here // head_dim
    experts_here = gate_weight.shape[0]
    expert_total = experts_here * group_count
    top_count = routes.shape[1]
    capacity = row_count * top_count * 5 // (4 * expert_total)
    group_rows = row_count * group_count
    sequence_count = seq_lengths.shape[1]
    score_scale = head_dim ** (-0.5)

    replica_count = lax.axis_size("rep")
    replica = lax.axis_index("rep")
    share = width_here // replica_count

    device_of_slot, slot_of_device = ring_indices(device, group_count)

    def reorder(blocks, index):
        return jnp.concatenate(
            [lax.dynamic_slice_in_dim(blocks, index[i], 1, 0) for i in range(group_count)], axis=0
        )

    group_order = reorder(token_order[0].reshape(group_count, row_count), device_of_slot)
    segment, position = row_meta(seq_lengths[0], group_order.reshape(group_rows))
    segment_own = segment[:row_count]
    valid_own = (segment_own < sequence_count).astype(wide_type)[:, None]
    valid_all = (segment < sequence_count).astype(wide_type)[:, None]

    expert_ids = jnp.arange(expert_total, dtype=jnp.int32)
    route_code = jnp.zeros((row_count, expert_total), jnp.int32)
    for column in range(top_count):
        hit = routes[:, column, None] == expert_ids[None, :]
        kept = (slot_index[:, column, None] < capacity).astype(jnp.int32)
        route_code = route_code + jnp.where(hit, 1 + kept, 0)
    small_sent = jnp.concatenate([route_code.astype(low_type), router_weight], axis=0)

    projections = jnp.concatenate(
        [
            lax.dynamic_slice_in_dim(piece, replica * share, share, 0).reshape(
                share, group_count, width_here
            )
            for piece in (query_weight, key_weight, value_weight)
        ],
        axis=2,
    ).transpose(1, 0, 2)
    scatter_order = rep_distances()
    gather_order = scatter_order[::-1]
    swapped = swap_all(projections)
    head_weight = (
        rep_gather(swapped[None], gather_order)
        .transpose(1, 0, 2, 3)
        .reshape(model_width, 3 * width_here)
    )
    small_flat = after(small_sent.reshape(-1, head_dim), swapped)
    small_all = swap_all(
        jnp.broadcast_to(small_flat[None], (group_count,) + small_flat.shape)
    ).reshape(group_count, row_count + width_here, expert_total)
    code_all = reorder(small_all[:, :row_count], device_of_slot).reshape(
        group_rows, expert_total
    )
    full_router = small_all[:, row_count:].reshape(model_width, expert_total)
    chunks = 2
    chunk_rows = group_rows // chunks
    blocks_here = group_count // chunks

    def chunk_of(array, chunk):
        return array[chunk * chunk_rows : (chunk + 1) * chunk_rows]

    def slot_rows(array):
        return lambda slot: array[slot * row_count : (slot + 1) * row_count]

    def reorder_rows(rows, index):
        return reorder(
            rows.reshape(group_count, row_count, rows.shape[1]), index
        ).reshape(rows.shape)

    tokens_late, output_late, _ = tie(tokens, output_weight, swapped)
    column_share = model_width // replica_count
    output_share = gather_rows(
        lax.dynamic_slice_in_dim(output_late, replica * column_share, column_share, 1)
    )
    token_ring = RingGather(tokens_late)
    for step in range(group_count // 2):
        if step == group_count // 2 - 1:
            token_ring.sent = (after(token_ring.sent[0], output_share), token_ring.sent[1])
        token_ring.start()
        token_ring.finish()
    cosine, sine_part = rope_tables(position, head_dim)

    hidden_here = down_weight.shape[1]
    flat_down = down_weight.reshape(experts_here * hidden_here, model_width)

    allowed = segment[:, None] == segment[None, :]
    far = replica_count // 2
    steps = group_count // 2
    part_rows = model_width // steps
    far_parts = [
        Exchange(output_share[i * part_rows : (i + 1) * part_rows], far) for i in range(steps)
    ]

    def head_columns(values, block, head):
        start = block * width_here + head * head_dim
        return values[:, start : start + head_dim]

    def project(weight, *blocks):
        token_all = jnp.concatenate(blocks, axis=0)
        token_wide = token_all.astype(wide_type)
        first_all = (token_wide * inverse_rms(token_wide) * prenorm_gain).astype(low_type)
        return token_all, first_all, mm(first_all, weight, 1, 0)

    def attend(head, raw):
        turned = []
        for block, gain in ((0, querynorm_gain), (1, keynorm_gain)):
            part = head_columns(raw, block, head)
            normed = part * inverse_rms(part) * gain
            turned.append((normed * cosine + turn_half(normed) * sine_part).astype(low_type))
        value_low = head_columns(raw, 2, head).astype(low_type)
        scores = jnp.where(allowed, mm(*turned, 1, 1) * score_scale, masked_value)
        top_score = jnp.max(scores, axis=-1, keepdims=True)
        powers = jnp.exp(scores - top_score)
        log_total = top_score + jnp.log(jnp.sum(powers, axis=-1, keepdims=True))
        weights_low = jnp.exp(scores - log_total).astype(low_type)
        return (*turned, value_low, log_total, mm(weights_low, value_low, 1, 0).astype(low_type))

    cot_ring = RingGather(after(cotangent, token_ring.received))
    token_all, first_all, raw = window(
        [cot_ring, far_parts[0]], project, head_weight, *token_ring.blocks
    )
    heads = []
    for head in range(heads_here):
        heads.append(
            window(
                [cot_ring, far_parts[1 + head]],
                lambda raw, head=head: attend(head, raw),
                raw,
            )
        )

    def order_work(*mixed):
        mixed_low = jnp.concatenate(mixed, axis=1)
        return mixed_low, reorder_rows(mixed_low, slot_of_device)

    mixed_low, mixed_ordered = window(
        [cot_ring, *far_parts[1 + heads_here :]], order_work, *[head[4] for head in heads]
    )
    cot_all = jnp.concatenate(cot_ring.blocks, axis=0)
    lows = jnp.concatenate([head[part] for part in range(3) for head in heads], axis=1)
    log_totals = jnp.stack([head[3] for head in heads])
    output_pieces = {
        0: output_share,
        far: jnp.concatenate([part.received for part in far_parts], axis=0),
    }
    for distance in gather_order[1:]:
        for j in list(output_pieces):
            output_pieces[j ^ distance] = rep_exchange(output_pieces[j], distance)
    mixed_own = (
        swap_all(mixed_ordered.reshape(group_count, row_count, width_here))
        .transpose(1, 0, 2)
        .reshape(row_count, model_width)
    )
    attention = jnp.zeros((row_count, model_width), wide_type)
    for j, piece in output_pieces.items():
        attention = lax.dynamic_update_slice_in_dim(
            attention, mm(mixed_own, piece, 1, 0), (replica ^ j) * column_share, 1
        )
    residual = tokens.astype(wide_type) + attention
    inverse_two = inverse_rms(residual)
    second_input = (residual * inverse_two * postnorm_gain).astype(low_type)

    def gate_table(rows, code):
        logits = mm(rows, full_router, 1, 0)
        shifted = jnp.where(code > 0, logits, masked_value)
        powers = jnp.exp(shifted - jnp.max(shifted, axis=1, keepdims=True))
        return powers / jnp.sum(powers, axis=1, keepdims=True)

    kept_all = jnp.where(code_all > 1, valid_all, 0.0)
    kept_here = lax.dynamic_slice_in_dim(kept_all, device * experts_here, experts_here, 1)

    def stream_of(cot_part):
        return mm(cot_part, flat_down, 1, 1)

    def expert_chunk(chunk, rows, stream, *earlier):
        gates = gate_table(rows, chunk_of(code_all, chunk)) * chunk_of(kept_all, chunk)
        gates_here = lax.dynamic_slice_in_dim(gates, device * experts_here, experts_here, 1)
        return expert_pass(
            rows, gate_weight, up_weight, stream, gates_here, chunk, chunks, earlier
        )

    second_ring = RingGather(second_input)
    stream_first = window([second_ring], lambda part: stream_of(part), chunk_of(cot_all, 0))
    stream_last = window([second_ring], lambda part: stream_of(part), chunk_of(cot_all, 1))
    rows_first = jnp.concatenate(second_ring.blocks[:blocks_here], axis=0)
    *earlier, pair_first = window(
        [second_ring],
        lambda rows, stream: expert_chunk(0, rows, stream),
        rows_first,
        stream_first,
    )
    window([second_ring], lambda: ())
    rows_last = jnp.concatenate(second_ring.blocks[blocks_here:], axis=0)
    inner_all, gback_all, uback_all, pair_last = expert_chunk(
        1, rows_last, stream_last, *earlier
    )
    second_all = jnp.concatenate([rows_first, rows_last], axis=0)
    back_last = expert_back(gback_all, uback_all, gate_weight, up_weight, 1, chunks)
    back_parts = {1: back_last}

    def back_block(slot):
        start = (slot % blocks_here) * row_count
        return back_parts[slot // blocks_here][start : start + row_count]

    def grad_of(left, right):
        return mm(left, right, 0, 0).astype(low_type)

    pair_lanes = jnp.concatenate([pair_first, pair_last], axis=1)
    pair_sent = (kept_here * jnp.sum(pair_lanes, axis=2).transpose(1, 0)).reshape(
        group_count, row_count, experts_here
    )
    code_own = route_code
    gates_own = gate_table(second_input, code_own)

    back_ring = RingSum(back_block, row_count)
    back_parts[0] = window(
        [back_ring],
        lambda gback, uback: expert_back(gback, uback, gate_weight, up_weight, 0, chunks),
        gback_all,
        uback_all,
    )

    def mixture_work(inner, pair):
        return (
            mm(inner, flat_down, 1, 0).astype(low_type),
            swap_all(reorder(pair, slot_of_device)),
        )

    mixture_part, pair_grad = window([back_ring], mixture_work, inner_all, pair_sent)
    mixture_ring = RingSum(slot_rows(mixture_part), row_count)

    def down_work(inner, pair):
        pair_grad = pair.transpose(1, 0, 2).reshape(row_count, expert_total)
        chosen_grad = gates_own * (
            pair_grad - jnp.sum(gates_own * pair_grad, axis=1, keepdims=True)
        )
        logits_grad = jnp.where(code_own > 0, chosen_grad, 0.0).astype(low_type)
        router_back = mm(logits_grad, full_router, 1, 1)
        router_part = mm(second_input, logits_grad, 0, 0)
        return grad_of(inner, cot_all), router_back, router_part

    down_part, router_back, router_part = window(
        [back_ring, mixture_ring], down_work, inner_all, pair_grad
    )
    gate_part = window(
        [back_ring, mixture_ring], lambda gback: grad_of(second_all, gback), gback_all
    )
    second_scattered = back_ring.total()
    second_grad = router_back + second_scattered
    upstream = valid_own * cotangent.astype(wide_type)
    def residual_work(second_grad):
        post_back, postnorm_part = norm_backward(
            residual, inverse_two, postnorm_gain, second_grad
        )
        residual_grad = upstream + post_back
        attention_low = residual_grad.astype(low_type)
        mixed_grad_own = jnp.zeros((row_count, model_width), wide_type)
        for j, piece in output_pieces.items():
            mixed_grad_own = mixed_grad_own + mm(
                lax.dynamic_slice_in_dim(
                    attention_low, (replica ^ j) * column_share, column_share, 1
                ),
                piece,
                1,
                1,
            )
        swap_sent = (
            mixed_grad_own.astype(low_type)
            .reshape(row_count, group_count, width_here)
            .transpose(1, 0, 2)
        )
        return swap_sent, residual_grad, attention_low, jnp.sum(postnorm_part, axis=0)

    swap_sent, residual_grad, attention_low, postnorm_part = window(
        [mixture_ring], residual_work, second_grad
    )
    class Swap(Exchange):
        def start(self):
            self.received = swap_all(self.sent)

    swap = Swap(swap_sent, 0)
    up_part = window(
        [mixture_ring, swap], lambda uback: grad_of(second_all, uback), uback_all
    )
    mixture = mixture_ring.total()
    layer_out = (valid_own * (residual + mixture)).astype(low_type)
    mixed_grad = swap.received

    attention_gather = RingGather(attention_low)
    sent, gain_parts = window(
        [attention_gather],
        lambda grads: tuple(
            attention_back(
                lows,
                grads,
                jnp.stack(device_of_slot),
                log_totals,
                segment,
                raw,
                jnp.stack([querynorm_gain, keynorm_gain]),
                cosine,
                sine_part,
            )
        ),
        mixed_grad,
    )
    querynorm_part, keynorm_part = gain_parts[0], gain_parts[1]
    down_sum = lax.psum_scatter(
        down_part.reshape(experts_here, hidden_here, model_width),
        "rep",
        scatter_dimension=1,
        tiled=True,
    )
    sent, down_sum = tie(sent, down_sum)

    def first_work(sent, head):
        first_part = mm(sent, head_weight, 1, 1)
        token_wide = token_all.astype(wide_type)
        prenorm_part = jnp.sum(first_part * token_wide * inverse_rms(token_wide), axis=0)
        return first_part.astype(low_type), prenorm_part, rep_scatter(head, 1, scatter_order[:1])

    head_part = window([attention_gather], grad_of, first_all, sent)
    first_low, prenorm_part, head_part = window(
        [attention_gather],
        first_work,
        sent,
        head_part.reshape(group_count, replica_count, share, 3 * width_here),
    )

    def small_swap(parts):
        return swap_all(
            jnp.concatenate([part.reshape(group_count, -1) for part in parts], axis=1)
        )

    def small_pieces(swapped, parts):
        total = rep_sum(jnp.sum(swapped, axis=0))
        pieces, start = [], 0
        for part in parts:
            size = part.size // group_count
            pieces.append(total[start : start + size])
            start += size
        return pieces

    first_ring = RingSum(slot_rows(first_low), row_count)
    small_parts = [router_part, postnorm_part, prenorm_part, querynorm_part, keynorm_part]
    head_part = rep_scatter(head_part, 1, scatter_order[1:])
    small_swapped = window(
        [attention_gather, first_ring], lambda *small: small_swap(small), *small_parts
    )
    gate_sum = lax.psum_scatter(gate_part, "rep", scatter_dimension=0, tiled=True)
    up_sum = lax.psum_scatter(up_part, "rep", scatter_dimension=0, tiled=True)
    output_part, head_part = window(
        [first_ring],
        lambda mixed, *blocks: block_product(mixed, blocks),
        mixed_low,
        *attention_gather.blocks,
        waits=(head_part,),
    )
    head_rows = swap_all(head_part.reshape(group_count, share, 3 * width_here))
    (output_part, small_sums), head_rows = window(
        [first_ring],
        lambda output, small: (
            rep_scatter(output, 0, scatter_order[:1]),
            small_pieces(small, small_parts),
        ),
        output_part.reshape(replica_count, share, model_width),
        small_swapped,
        waits=(head_rows,),
    )
    head_rows = rep_gather(
        head_rows.reshape(group_count, share, 3, width_here)
        .transpose(2, 1, 0, 3)
        .reshape(1, 3, share, model_width),
        gather_order[:-1],
    )
    output_part, head_rows = window(
        [first_ring],
        lambda output: rep_scatter(output, 0, scatter_order[1:]),
        output_part,
        waits=(head_rows,),
    )
    head_rows = rep_gather(head_rows, gather_order[-1:])
    first_grad = first_ring.total()
    output_grad = (
        rep_gather(output_part, gather_order)
        .reshape(width_here, model_width)
        .astype(wide_type)
    )
    query_grad, key_grad, value_grad = (
        head_rows[:, block].reshape(width_here, model_width).astype(wide_type)
        for block in range(3)
    )
    router_grad, postnorm_grad, prenorm_grad, querynorm_grad, keynorm_grad = small_sums
    router_grad = router_grad.reshape(width_here, expert_total)

    token_own = tokens.astype(wide_type)
    inverse_one = inverse_rms(token_own)
    pre_back, _ = norm_backward(token_own, inverse_one, prenorm_gain, first_grad)
    token_grad = residual_grad + pre_back

    down_total = down_sum.astype(wide_type)
    gate_total, up_total = (
        jnp.stack(
            [
                total[:, e * hidden_here : (e + 1) * hidden_here].astype(wide_type)
                for e in range(experts_here)
            ]
        )
        for total in (gate_sum, up_sum)
    )
    return (
        layer_out,
        token_grad,
        query_grad,
        key_grad,
        value_grad,
        output_grad,
        router_grad,
        prenorm_grad,
        querynorm_grad,
        keynorm_grad,
        postnorm_grad,
        gate_total,
        up_total,
        down_total,
    )


def solution(mesh):
    in_specs = (
        P(("rep", "ep"), None),
        P(("rep", "ep"), None),
        P("rep", None),
        P("rep", None),
        P(("rep", "ep"), None),
        P(("rep", "ep"), None),
        P("ep", None),
        P("ep", None),
        P("ep", None),
        P("ep", None),
        P("ep", None),
        P(),
        P(),
        P(),
        P(),
        P("ep", None, None),
        P("ep", None, None),
        P("ep", None, None),
    )
    out_specs = (
        P(("rep", "ep"), None),
        P(("rep", "ep"), None),
        P("ep", None),
        P("ep", None),
        P("ep", None),
        P("ep", None),
        P("ep", None),
        P("ep"),
        P("ep"),
        P("ep"),
        P("ep"),
        P("ep", "rep", None),
        P("ep", "rep", None),
        P("ep", "rep", None),
    )
    return jax.shard_map(body, mesh=mesh, in_specs=in_specs, out_specs=out_specs, check_vma=False)
```

```python
import functools

import jax
import jax.numpy as jnp
from jax import lax
from jax.experimental import pallas as pl
from jax.experimental.pallas import tpu as pltpu
from jax.sharding import PartitionSpec as P

epsilon = 1e-05
rope_base = 10000.0
masked_value = -1e30
low_type = jnp.bfloat16
wide_type = jnp.float32


def inverse_rms(values):
    return lax.rsqrt(jnp.mean(values * values, axis=-1, keepdims=True) + epsilon)


def norm_backward(values, inverse, gain_vector, upstream):
    scaled = upstream * gain_vector
    inner_mean = jnp.mean(scaled * values, axis=-1, keepdims=True)
    result = inverse * scaled - values * (inverse * inverse * inverse) * inner_mean
    return (result, upstream * values * inverse)


def rope_tables(position, dimension):
    halfway = dimension // 2
    indices = jnp.arange(halfway, dtype=wide_type)
    frequency = rope_base ** (-2.0 * indices / dimension)
    angles = position.astype(wide_type)[:, None] * frequency[None, :]
    cosine = jnp.cos(angles)
    sine_part = jnp.sin(angles)
    return (
        jnp.concatenate([cosine, cosine], axis=-1),
        jnp.concatenate([sine_part, sine_part], axis=-1),
    )


def turn_half(values):
    halfway = values.shape[-1] // 2
    return jnp.concatenate([-values[..., halfway:], values[..., :halfway]], axis=-1)


def turn_back(values):
    halfway = values.shape[-1] // 2
    return jnp.concatenate([values[..., halfway:], -values[..., :halfway]], axis=-1)


def row_meta(lengths, group_order):
    boundary = jnp.cumsum(lengths)
    passed = (group_order[:, None] >= boundary[None, :]).astype(jnp.int32)
    segment = jnp.sum(passed, axis=1)
    offset = jnp.sum(passed * lengths[None, :], axis=1)
    return (segment, group_order - offset)


def mm(left, right, left_dim, right_dim):
    return lax.dot_general(
        left,
        right,
        (((left_dim,), (right_dim,)), ((), ())),
        preferred_element_type=wide_type,
    )


def gather_rows(values):
    return lax.all_gather(values, "ep", axis=0, tiled=True)


def ring_order(count):
    return [i for i in range(count) if i % 2 == 0] + [i for i in reversed(range(count)) if i % 2]


def ring_slots(count):
    half = count // 2
    offsets = [0]
    for step in range(1, half):
        offsets += [step, -step]
    return offsets + [half]


def ring_shift(values, direction):
    order = ring_order(lax.axis_size("ep"))
    count = len(order)
    pairs = [(order[i], order[(i + direction) % count]) for i in range(count)]
    return lax.ppermute(values, "ep", pairs)


def tie(*arrays):
    return lax.optimization_barrier(arrays)


def after(value, *others):
    return lax.optimization_barrier((value,) + others)[0]


class RingGather:
    def __init__(self, values):
        self.middle = values.shape[0] // 2
        self.half, self.step = lax.axis_size("ep") // 2, 0
        self.sent = (values, values)
        self.blocks = [values]

    def start(self):
        if self.step == self.half - 1:
            self.sent = (self.sent[0][: self.middle], self.sent[1][self.middle :])
        self.received = (ring_shift(self.sent[0], 1), ring_shift(self.sent[1], -1))

    def finish(self):
        self.step += 1
        onward, backward = self.sent = self.received
        if self.step < self.half:
            self.blocks += [backward, onward]
        else:
            self.blocks += [jnp.concatenate([onward, backward], axis=0)]


class Exchange:
    def __init__(self, values, distance):
        self.sent, self.distance = values, distance

    def start(self):
        self.received = rep_exchange(self.sent, self.distance)

    def finish(self):
        pass


class RingSum:
    def __init__(self, block, rows):
        count = lax.axis_size("ep")
        self.block, self.middle, self.step = block, rows // 2, 0
        self.half = count // 2
        self.slot = {offset: j for j, offset in enumerate(ring_slots(count))}
        far = block(self.slot[self.half])
        self.sent = (far[: self.middle], far[self.middle :])

    def start(self):
        self.received = (ring_shift(self.sent[0], 1), ring_shift(self.sent[1], -1))

    def finish(self):
        self.step += 1
        onward, backward = self.received
        left = self.half - self.step
        middle = self.middle
        if left:
            up, down = self.block(self.slot[left]), self.block(self.slot[-left])
            if self.step == 1:
                onward = jnp.concatenate([add_low(onward, up[:middle]), up[middle:]], axis=0)
                backward = jnp.concatenate(
                    [down[:middle], add_low(backward, down[middle:])], axis=0
                )
            else:
                onward, backward = add_low(onward, up), add_low(backward, down)
        self.sent = (onward, backward)

    def total(self):
        return (
            self.block(self.slot[0]).astype(wide_type)
            + self.sent[0].astype(wide_type)
            + self.sent[1].astype(wide_type)
        )


def window(rings, work, *inputs, waits=()):
    for ring in rings:
        ring.start()
    inputs, _ = tie(inputs, [ring.sent for ring in rings])
    received, waits, results = tie([ring.received for ring in rings], waits, work(*inputs))
    for ring, pair in zip(rings, received):
        ring.received = pair
        ring.finish()
    return (results, *waits) if waits else results


def add_low(left, right):
    return (left.astype(wide_type) + right.astype(wide_type)).astype(low_type)


def ring_place(member, count):
    return jnp.where(member % 2 == 0, member // 2, count - 1 - member // 2)


def ring_member(place, count):
    return jnp.where(place < count // 2, 2 * place, 2 * (count - 1 - place) + 1)


def ring_indices(device, count):
    place = ring_place(device, count)
    half = count // 2
    members = [ring_member((place + offset) % count, count) for offset in ring_slots(count)]
    slots = []
    for other in range(count):
        ahead = (ring_place(jnp.int32(other), count) - place) % count
        slot = jnp.where(ahead < half, 2 * ahead - 1, 2 * (count - ahead))
        slots.append(jnp.where(ahead == 0, 0, jnp.where(ahead == half, count - 1, slot)))
    return members, slots


def rep_exchange(values, distance):
    count = lax.axis_size("rep")
    return lax.ppermute(values, "rep", [(i, i ^ distance) for i in range(count)])


def rep_bit(distance):
    return (lax.axis_index("rep") // distance) % 2


def rep_distances():
    count, distance, distances = lax.axis_size("rep"), 1, []
    while distance < count:
        distances.append(distance)
        distance *= 2
    return distances


def rep_gather(gathered, distances):
    for distance in distances:
        shape = gathered.shape[1:]
        other = rep_exchange(gathered, distance)
        mine_first = jnp.stack([gathered, other], axis=1)
        other_first = jnp.stack([other, gathered], axis=1)
        gathered = jnp.where(rep_bit(distance) == 0, mine_first, other_first)
        gathered = gathered.reshape((-1,) + shape)
    return gathered


def rep_scatter(values, axis, distances):
    for distance in distances:
        shape = values.shape
        pairs = values.reshape(shape[:axis] + (shape[axis] // 2, 2) + shape[axis + 1 :])
        bit = rep_bit(distance)
        keep = lax.dynamic_index_in_dim(pairs, bit, axis + 1, keepdims=False)
        send = lax.dynamic_index_in_dim(pairs, 1 - bit, axis + 1, keepdims=False)
        values = add_low(keep, rep_exchange(send, distance))
    return values


def rep_sum(values):
    distance = 1
    while distance < lax.axis_size("rep"):
        values = values + rep_exchange(values, distance)
        distance *= 2
    return values


def swap_all(values):
    return lax.all_to_all(values, "ep", split_axis=0, concat_axis=0, tiled=True)


def expert_kernel(rows_ref, gate_ref, up_ref, stream_ref, gates_ref, *refs):
    inner_ref, gback_ref, uback_ref, pair_ref = refs[-4:]
    expert, step = pl.program_id(0), pl.program_id(1)
    rows = rows_ref[...]
    gate_linear = jnp.dot(rows, gate_ref[0], preferred_element_type=wide_type)
    up_linear = jnp.dot(rows, up_ref[0], preferred_element_type=wide_type)
    stream = stream_ref[...]
    column = gates_ref[:, 0:1]
    for other in range(1, gates_ref.shape[1]):
        column = jnp.where(expert == other, gates_ref[:, other : other + 1], column)
    sigmoid_gate = jax.nn.sigmoid(gate_linear)
    silu_gate = gate_linear * sigmoid_gate
    inner = silu_gate * up_linear
    inner_ref[...] = (column * inner).astype(low_type)
    hidden_grad = column * stream
    gback_ref[...] = (
        hidden_grad * up_linear * sigmoid_gate * (1.0 + gate_linear * (1.0 - sigmoid_gate))
    ).astype(low_type)
    uback_ref[...] = (hidden_grad * silu_gate).astype(low_type)
    product = inner * stream
    lanes = pair_ref.shape[2]
    folded = product[:, :lanes]
    for start in range(lanes, product.shape[1], lanes):
        folded = folded + product[:, start : start + lanes]

    @pl.when(step == 0)
    def _():
        pair_ref[0] = folded

    @pl.when(step > 0)
    def _():
        pair_ref[0] += folded


def expert_pass(rows, gate_weight, up_weight, stream, gates, chunk, chunks, earlier=()):
    count, depth = rows.shape
    experts, _, hidden = gate_weight.shape
    width = 256
    steps = hidden // width
    weight = pl.BlockSpec((1, depth, width), lambda e, j: (e, 0, j))
    out = pl.BlockSpec((count, width), lambda e, j: (chunk, e * steps + j))
    return pl.pallas_call(
        expert_kernel,
        grid=(experts, steps),
        in_specs=[
            pl.BlockSpec((count, depth), lambda e, j: (0, 0)),
            weight,
            weight,
            pl.BlockSpec((count, width), lambda e, j: (0, e * steps + j)),
            pl.BlockSpec(gates.shape, lambda e, j: (0, 0)),
        ]
        + [pl.BlockSpec(memory_space=pl.ANY)] * len(earlier),
        out_specs=[out, out, out, pl.BlockSpec((1, count, 128), lambda e, j: (e, 0, 0))],
        out_shape=[jax.ShapeDtypeStruct((count * chunks, experts * hidden), low_type)] * 3
        + [jax.ShapeDtypeStruct((experts, count, 128), wide_type)],
        input_output_aliases={5 + i: i for i in range(len(earlier))},
        compiler_params=pltpu.CompilerParams(vmem_limit_bytes=56 << 20),
        cost_estimate=pl.CostEstimate(
            flops=4 * count * depth * experts * hidden,
            bytes_accessed=4 * depth * experts * hidden + 20 * count * depth,
            transcendentals=count * experts * hidden,
        ),
    )(rows, gate_weight, up_weight, stream, gates, *earlier)


def expert_back_kernel(gback_ref, uback_ref, gate_ref, up_ref, out_ref):
    experts, _, hidden = gate_ref.shape
    total = None
    for e in range(experts):
        for grad_ref, weight_ref in ((gback_ref, gate_ref), (uback_ref, up_ref)):
            term = mm(grad_ref[:, e * hidden : (e + 1) * hidden], weight_ref[e], 1, 1)
            total = term if total is None else total + term
    out_ref[...] = total.astype(low_type)


def expert_back(gback, uback, gate_weight, up_weight, chunk, chunks):
    count = gback.shape[0] // chunks
    experts, depth, hidden = gate_weight.shape
    width = 256
    whole = pl.BlockSpec((count, experts * hidden), lambda j: (chunk, 0))
    weight = pl.BlockSpec((experts, width, hidden), lambda j: (0, j, 0))
    return pl.pallas_call(
        expert_back_kernel,
        grid=(depth // width,),
        in_specs=[whole, whole, weight, weight],
        out_specs=pl.BlockSpec((count, width), lambda j: (0, j)),
        out_shape=jax.ShapeDtypeStruct((count, depth), low_type),
        compiler_params=pltpu.CompilerParams(vmem_limit_bytes=56 << 20),
        cost_estimate=pl.CostEstimate(
            flops=4 * count * depth * experts * hidden,
            bytes_accessed=4 * depth * experts * hidden + 6 * count * depth,
            transcendentals=0,
        ),
    )(gback, uback, gate_weight, up_weight)


def attention_back_kernel(
    block,
    scale,
    order_ref,
    query_ref,
    key_ref,
    value_ref,
    swapped_ref,
    total_ref,
    column_ref,
    line_ref,
    query_raw_ref,
    key_raw_ref,
    gains_ref,
    cosine_ref,
    sine_ref,
    *refs,
):
    sent_ref, part_ref, key_sum, value_sum, grad_ref = refs[-5:]
    rows, depth = query_ref.shape
    lane = lax.broadcasted_iota(jnp.int32, (1, depth), 1)
    sign = jnp.where(lane < depth // 2, 1.0, -1.0)
    share = swapped_ref.shape[1]
    for slot in range(swapped_ref.shape[0]):
        grad_ref[slot * share : (slot + 1) * share, :] = swapped_ref[order_ref[slot]]
    key_sum[...] = jnp.zeros_like(key_sum)
    value_sum[...] = jnp.zeros_like(value_sum)
    part_ref[...] = jnp.zeros_like(part_ref)

    def finish(back, raw, row, which):
        turned = back * cosine_ref[row, :]
        turned += pltpu.roll(back * sine_ref[row, :], depth // 2, axis=1) * sign
        inverse = inverse_rms(raw)
        result, part = norm_backward(raw, inverse, gains_ref[which : which + 1, :], turned)
        sent_ref[row, which * depth : (which + 1) * depth] = result.astype(low_type)
        part_ref[which : which + 1, :] += jnp.sum(part, axis=0, keepdims=True)

    @pl.loop(0, rows // block)
    def _(step):
        row = pl.ds(pl.multiple_of(step * block, block), block)
        query, grad = query_ref[row, :], grad_ref[row, :]
        scores = mm(query, key_ref[...], 1, 1) * scale
        scores = jnp.where(column_ref[row, :] == line_ref[...], scores, masked_value)
        weights = jnp.exp(scores - total_ref[row, :])
        weight_grad = mm(grad, value_ref[...], 1, 1)
        row_dot = jnp.sum(weights * weight_grad, axis=-1, keepdims=True)
        score_grad = (weights * (weight_grad - row_dot)).astype(low_type)
        key_sum[...] += mm(score_grad, query, 0, 0)
        value_sum[...] += mm(weights.astype(low_type), grad, 0, 0)
        finish(mm(score_grad, key_ref[...], 1, 0) * scale, query_raw_ref[row, :], row, 0)

    @pl.loop(0, rows // block)
    def _(step):
        row = pl.ds(pl.multiple_of(step * block, block), block)
        finish(key_sum[row, :] * scale, key_raw_ref[row, :], row, 1)
        sent_ref[row, 2 * depth : 3 * depth] = value_sum[row, :].astype(low_type)


def attention_back(head, kept, swapped, order, column, line, raw, gains, tables, earlier=()):
    rows, depth = kept[0].shape
    block = 256 if rows % 256 == 0 else rows

    def whole(array):
        return pl.BlockSpec(array.shape, lambda i, order: (0,) * array.ndim)

    def columns(index):
        return pl.BlockSpec((rows, depth), lambda i, order: (0, index))

    operands = (*kept[:3], swapped, kept[3], column, line, raw, raw, gains, *tables)
    specs = [whole(operand) for operand in operands]
    specs[3] = pl.BlockSpec(swapped.shape[:2] + (depth,), lambda i, order: (0, 0, head))
    specs[7], specs[8] = columns(3 * head), columns(3 * head + 1)
    return pl.pallas_call(
        functools.partial(attention_back_kernel, block, depth**-0.5),
        grid_spec=pltpu.PrefetchScalarGridSpec(
            num_scalar_prefetch=1,
            grid=(1,),
            in_specs=specs + [pl.BlockSpec(memory_space=pl.ANY)] * len(earlier),
            out_specs=[
                pl.BlockSpec((rows, 3 * depth), lambda i, order: (0, head)),
                pl.BlockSpec((2, depth), lambda i, order: (0, 0)),
            ],
            scratch_shapes=[pltpu.VMEM((rows, depth), wide_type)] * 2
            + [pltpu.VMEM((rows, depth), low_type)],
        ),
        out_shape=[
            jax.ShapeDtypeStruct(raw.shape, low_type),
            jax.ShapeDtypeStruct((2, depth), wide_type),
        ],
        input_output_aliases={1 + len(operands) + i: i for i in range(len(earlier))},
        compiler_params=pltpu.CompilerParams(vmem_limit_bytes=56 << 20),
        cost_estimate=pl.CostEstimate(
            flops=10 * rows * rows * depth,
            bytes_accessed=30 * rows * depth,
            transcendentals=rows * rows,
        ),
    )(order, *operands, *earlier)


def block_product_kernel(left_ref, *refs):
    out_ref = refs[-1]
    rows = refs[0].shape[0]
    total = None
    for j, ref in enumerate(refs[:-1]):
        term = mm(left_ref[j * rows : (j + 1) * rows, :], ref[...], 0, 0)
        total = term if total is None else total + term
    out_ref[...] = total.astype(low_type)


def block_product(left, blocks):
    rows, width = blocks[0].shape
    tile = 512
    return pl.pallas_call(
        block_product_kernel,
        grid=(width // tile,),
        in_specs=[pl.BlockSpec(left.shape, lambda j: (0, 0))] + [pl.BlockSpec((rows, tile), lambda j: (0, j))] * len(blocks),
        out_specs=pl.BlockSpec((left.shape[1], tile), lambda j: (0, j)),
        out_shape=jax.ShapeDtypeStruct((left.shape[1], width), low_type),
        cost_estimate=pl.CostEstimate(flops=2 * left.size * width, bytes_accessed=2 * left.size + 2 * len(blocks) * rows * width, transcendentals=0),
    )(left, *blocks)


def body(
    tokens,
    cotangent,
    seq_lengths,
    token_order,
    routes,
    slot_index,
    query_weight,
    key_weight,
    value_weight,
    output_weight,
    router_weight,
    prenorm_gain,
    querynorm_gain,
    keynorm_gain,
    postnorm_gain,
    gate_weight,
    up_weight,
    down_weight,
):
    group_count = lax.axis_size("ep")
    device = lax.axis_index("ep")
    row_count, model_width = tokens.shape
    head_dim = querynorm_gain.shape[0]
    width_here = model_width // group_count
    heads_here = width_here // head_dim
    experts_here = gate_weight.shape[0]
    expert_total = experts_here * group_count
    top_count = routes.shape[1]
    capacity = row_count * top_count * 5 // (4 * expert_total)
    group_rows = row_count * group_count
    sequence_count = seq_lengths.shape[1]
    score_scale = head_dim ** (-0.5)

    replica_count = lax.axis_size("rep")
    replica = lax.axis_index("rep")
    share = width_here // replica_count

    device_of_slot, slot_of_device = ring_indices(device, group_count)

    def reorder(blocks, index):
        return jnp.concatenate(
            [lax.dynamic_slice_in_dim(blocks, index[i], 1, 0) for i in range(group_count)], axis=0
        )

    group_order = reorder(token_order[0].reshape(group_count, row_count), device_of_slot)
    segment, position = row_meta(seq_lengths[0], group_order.reshape(group_rows))
    segment_own = segment[:row_count]
    valid_own = (segment_own < sequence_count).astype(wide_type)[:, None]
    valid_all = (segment < sequence_count).astype(wide_type)[:, None]

    expert_ids = jnp.arange(expert_total, dtype=jnp.int32)
    route_code = jnp.zeros((row_count, expert_total), jnp.int32)
    for column in range(top_count):
        hit = routes[:, column, None] == expert_ids[None, :]
        kept = (slot_index[:, column, None] < capacity).astype(jnp.int32)
        route_code = route_code + jnp.where(hit, 1 + kept, 0)
    small_sent = jnp.concatenate([route_code.astype(low_type), router_weight], axis=0)

    projections = (
        jnp.stack(
            [
                lax.dynamic_slice_in_dim(piece, replica * share, share, 0).reshape(
                    share, group_count, heads_here, head_dim
                )
                for piece in (query_weight, key_weight, value_weight)
            ],
            axis=3,
        )
        .reshape(share, group_count, 3 * width_here)
        .transpose(1, 0, 2)
    )
    scatter_order = rep_distances()
    gather_order = scatter_order[::-1]
    swapped = swap_all(projections)
    head_weight = (
        rep_gather(swapped[None], gather_order)
        .transpose(1, 0, 2, 3)
        .reshape(model_width, 3 * width_here)
    )
    tokens_late, output_late, _ = tie(tokens, output_weight, swapped)
    token_ring = RingGather(tokens_late)
    token_ring.start()
    small_flat = after(small_sent.reshape(-1, head_dim), token_ring.received)
    small_all = swap_all(
        jnp.broadcast_to(small_flat[None], (group_count,) + small_flat.shape)
    ).reshape(group_count, row_count + width_here, expert_total)
    code_all = reorder(small_all[:, :row_count], device_of_slot).reshape(
        group_rows, expert_total
    )
    full_router = small_all[:, row_count:].reshape(model_width, expert_total)
    chunks = 2
    chunk_rows = group_rows // chunks
    blocks_here = group_count // chunks

    def chunk_of(array, chunk):
        return array[chunk * chunk_rows : (chunk + 1) * chunk_rows]

    def slot_rows(array):
        return lambda slot: array[slot * row_count : (slot + 1) * row_count]

    def reorder_rows(rows, index):
        return reorder(
            rows.reshape(group_count, row_count, rows.shape[1]), index
        ).reshape(rows.shape)

    column_share = model_width // replica_count
    output_share = gather_rows(
        lax.dynamic_slice_in_dim(output_late, replica * column_share, column_share, 1)
    )
    token_ring.finish()
    for step in range(1, group_count // 2):
        if step == group_count // 2 - 1:
            token_ring.sent = (after(token_ring.sent[0], output_share), token_ring.sent[1])
        token_ring.start()
        token_ring.finish()
    cosine, sine_part = rope_tables(after(position, token_ring.blocks[1]), head_dim)

    hidden_here = down_weight.shape[1]
    flat_down = down_weight.reshape(experts_here * hidden_here, model_width)

    allowed = segment[:, None] == segment[None, :]
    far = replica_count // 2
    steps = group_count // 2
    part_rows = model_width // steps
    far_parts = [
        Exchange(output_share[i * part_rows : (i + 1) * part_rows], far) for i in range(steps)
    ]

    def head_columns(values, block, head):
        start = (3 * head + block) * head_dim
        return values[:, start : start + head_dim]

    def project(weight, *blocks):
        token_all = jnp.concatenate(blocks, axis=0)
        token_wide = token_all.astype(wide_type)
        first_all = (token_wide * inverse_rms(token_wide) * prenorm_gain).astype(low_type)
        return token_all, first_all, mm(first_all, weight, 1, 0)

    def attend(head, raw):
        turned = []
        for block, gain in ((0, querynorm_gain), (1, keynorm_gain)):
            part = head_columns(raw, block, head)
            normed = part * inverse_rms(part) * gain
            turned.append((normed * cosine + turn_half(normed) * sine_part).astype(low_type))
        value_low = head_columns(raw, 2, head).astype(low_type)
        scores = jnp.where(allowed, mm(*turned, 1, 1) * score_scale, masked_value)
        top_score = jnp.max(scores, axis=-1, keepdims=True)
        powers = jnp.exp(scores - top_score)
        log_total = top_score + jnp.log(jnp.sum(powers, axis=-1, keepdims=True))
        weights_low = jnp.exp(scores - log_total).astype(low_type)
        return (*turned, value_low, log_total, mm(weights_low, value_low, 1, 0).astype(low_type))

    cot_ring = RingGather(after(cotangent, token_ring.received))
    token_all, first_all, raw = window(
        [cot_ring, far_parts[0]], project, head_weight, *token_ring.blocks
    )
    heads = []
    for head in range(heads_here):
        heads.append(
            window(
                [cot_ring, far_parts[1 + head]],
                lambda raw, head=head: attend(head, raw),
                raw,
            )
        )

    def order_work(*mixed):
        mixed_low = jnp.concatenate(mixed, axis=1)
        return (
            mixed_low,
            reorder_rows(mixed_low, slot_of_device),
            segment[:, None],
            segment[None, :],
            jnp.stack([querynorm_gain, keynorm_gain]),
            jnp.stack(device_of_slot),
        )

    mixed_low, mixed_ordered, segment_column, segment_line, norm_gains, slot_order = window(
        [cot_ring, *far_parts[1 + heads_here :]], order_work, *[head[4] for head in heads]
    )
    cot_all = jnp.concatenate(cot_ring.blocks, axis=0)
    output_pieces = {
        0: output_share,
        far: jnp.concatenate([part.received for part in far_parts], axis=0),
    }
    for distance in gather_order[1:]:
        for j in list(output_pieces):
            output_pieces[j ^ distance] = rep_exchange(output_pieces[j], distance)
    mixed_own = (
        swap_all(mixed_ordered.reshape(group_count, row_count, width_here))
        .transpose(1, 0, 2)
        .reshape(row_count, model_width)
    )
    attention = jnp.zeros((row_count, model_width), wide_type)
    for j, piece in output_pieces.items():
        attention = lax.dynamic_update_slice_in_dim(
            attention, mm(mixed_own, piece, 1, 0), (replica ^ j) * column_share, 1
        )
    residual = tokens.astype(wide_type) + attention
    inverse_two = inverse_rms(residual)
    second_input = (residual * inverse_two * postnorm_gain).astype(low_type)

    def gate_table(rows, code):
        logits = mm(rows, full_router, 1, 0)
        shifted = jnp.where(code > 0, logits, masked_value)
        powers = jnp.exp(shifted - jnp.max(shifted, axis=1, keepdims=True))
        return powers / jnp.sum(powers, axis=1, keepdims=True)

    kept_all = jnp.where(code_all > 1, valid_all, 0.0)
    kept_here = lax.dynamic_slice_in_dim(kept_all, device * experts_here, experts_here, 1)

    def stream_of(cot_part):
        return mm(cot_part, flat_down, 1, 1)

    def expert_chunk(chunk, rows, stream, *earlier):
        gates = gate_table(rows, chunk_of(code_all, chunk)) * chunk_of(kept_all, chunk)
        gates_here = lax.dynamic_slice_in_dim(gates, device * experts_here, experts_here, 1)
        return expert_pass(
            rows, gate_weight, up_weight, stream, gates_here, chunk, chunks, earlier
        )

    second_ring = RingGather(second_input)
    stream_first = window([second_ring], lambda part: stream_of(part), chunk_of(cot_all, 0))
    stream_last = window([second_ring], lambda part: stream_of(part), chunk_of(cot_all, 1))
    rows_first = jnp.concatenate(second_ring.blocks[:blocks_here], axis=0)
    *earlier, pair_first = window(
        [second_ring],
        lambda rows, stream: expert_chunk(0, rows, stream),
        rows_first,
        stream_first,
    )
    window([second_ring], lambda: ())
    rows_last = jnp.concatenate(second_ring.blocks[blocks_here:], axis=0)
    inner_all, gback_all, uback_all, pair_last = expert_chunk(
        1, rows_last, stream_last, *earlier
    )
    second_all = jnp.concatenate([rows_first, rows_last], axis=0)
    back_last = expert_back(gback_all, uback_all, gate_weight, up_weight, 1, chunks)
    back_parts = {1: back_last}

    def back_block(slot):
        start = (slot % blocks_here) * row_count
        return back_parts[slot // blocks_here][start : start + row_count]

    def grad_of(left, right):
        return mm(left, right, 0, 0).astype(low_type)

    pair_lanes = jnp.concatenate([pair_first, pair_last], axis=1)
    pair_sent = (kept_here * jnp.sum(pair_lanes, axis=2).transpose(1, 0)).reshape(
        group_count, row_count, experts_here
    )
    code_own = route_code
    gates_own = gate_table(second_input, code_own)

    back_ring = RingSum(back_block, row_count)
    back_parts[0] = window(
        [back_ring],
        lambda gback, uback: expert_back(gback, uback, gate_weight, up_weight, 0, chunks),
        gback_all,
        uback_all,
    )

    def mixture_work(inner, pair):
        return (
            mm(inner, flat_down, 1, 0).astype(low_type),
            swap_all(reorder(pair, slot_of_device)),
        )

    mixture_part, pair_grad = window([back_ring], mixture_work, inner_all, pair_sent)
    mixture_ring = RingSum(slot_rows(mixture_part), row_count)

    def down_work(inner, pair):
        pair_grad = pair.transpose(1, 0, 2).reshape(row_count, expert_total)
        chosen_grad = gates_own * (
            pair_grad - jnp.sum(gates_own * pair_grad, axis=1, keepdims=True)
        )
        logits_grad = jnp.where(code_own > 0, chosen_grad, 0.0).astype(low_type)
        router_back = mm(logits_grad, full_router, 1, 1)
        router_part = mm(second_input, logits_grad, 0, 0)
        return grad_of(inner, cot_all), router_back, router_part

    down_part, router_back, router_part = window(
        [back_ring, mixture_ring], down_work, inner_all, pair_grad
    )
    gate_part = window(
        [back_ring, mixture_ring], lambda gback: grad_of(second_all, gback), gback_all
    )
    second_scattered = back_ring.total()
    second_grad = router_back + second_scattered
    upstream = valid_own * cotangent.astype(wide_type)
    def residual_work(second_grad):
        post_back, postnorm_part = norm_backward(
            residual, inverse_two, postnorm_gain, second_grad
        )
        residual_grad = upstream + post_back
        attention_low = residual_grad.astype(low_type)
        mixed_grad_own = jnp.zeros((row_count, model_width), wide_type)
        for j, piece in output_pieces.items():
            mixed_grad_own = mixed_grad_own + mm(
                lax.dynamic_slice_in_dim(
                    attention_low, (replica ^ j) * column_share, column_share, 1
                ),
                piece,
                1,
                1,
            )
        swap_sent = (
            mixed_grad_own.astype(low_type)
            .reshape(row_count, group_count, width_here)
            .transpose(1, 0, 2)
        )
        return swap_sent, residual_grad, attention_low, jnp.sum(postnorm_part, axis=0)

    swap_sent, residual_grad, attention_low, postnorm_part = window(
        [mixture_ring], residual_work, second_grad
    )
    class Swap(Exchange):
        def start(self):
            self.received = swap_all(self.sent)

    swap = Swap(swap_sent, 0)
    attention_gather = RingGather(attention_low)
    up_part = window(
        [mixture_ring, swap, attention_gather],
        lambda uback: grad_of(second_all, uback),
        uback_all,
    )
    mixture = mixture_ring.total()
    layer_out = (valid_own * (residual + mixture)).astype(low_type)
    mixed_grad = swap.received

    sent, gain_parts = (), 0.0
    for head in range(heads_here):

        def head_work(grads, *earlier, head=head):
            return tuple(
                attention_back(
                    head,
                    heads[head][:4],
                    grads,
                    slot_order,
                    segment_column,
                    segment_line,
                    raw,
                    norm_gains,
                    (cosine, sine_part),
                    earlier,
                )
            )

        *sent, gain_part = window([attention_gather], head_work, mixed_grad, *sent)
        gain_parts = gain_parts + gain_part
    (sent,) = sent
    querynorm_part, keynorm_part = gain_parts[0], gain_parts[1]
    down_sum = lax.psum_scatter(
        down_part.reshape(experts_here, hidden_here, model_width),
        "rep",
        scatter_dimension=1,
        tiled=True,
    )
    sent, down_sum = tie(sent, down_sum)

    def first_work(sent, head):
        first_part = mm(sent, head_weight, 1, 1)
        token_wide = token_all.astype(wide_type)
        prenorm_part = jnp.sum(first_part * token_wide * inverse_rms(token_wide), axis=0)
        return first_part.astype(low_type), prenorm_part, rep_scatter(head, 1, scatter_order[:1])

    head_part = window([attention_gather], grad_of, first_all, sent)
    while attention_gather.step < group_count // 2:
        window([attention_gather], lambda: ())
    first_low, prenorm_part, head_part = window(
        [],
        first_work,
        sent,
        head_part.reshape(group_count, replica_count, share, 3 * width_here),
    )

    def small_swap(parts):
        return swap_all(
            jnp.concatenate([part.reshape(group_count, -1) for part in parts], axis=1)
        )

    def small_pieces(swapped, parts):
        total = rep_sum(jnp.sum(swapped, axis=0))
        pieces, start = [], 0
        for part in parts:
            size = part.size // group_count
            pieces.append(total[start : start + size])
            start += size
        return pieces

    first_ring = RingSum(slot_rows(first_low), row_count)
    small_parts = [router_part, postnorm_part, prenorm_part, querynorm_part, keynorm_part]
    head_part = rep_scatter(head_part, 1, scatter_order[1:])
    output_part = window(
        [first_ring],
        lambda mixed, *blocks: block_product(mixed, blocks),
        mixed_low,
        *attention_gather.blocks,
    )
    gate_sum = lax.psum_scatter(gate_part, "rep", scatter_dimension=0, tiled=True)
    up_sum = lax.psum_scatter(up_part, "rep", scatter_dimension=0, tiled=True)
    (small_swapped, output_part), head_part = window(
        [first_ring],
        lambda output, *small: (small_swap(small), rep_scatter(output, 0, scatter_order[:1])),
        output_part.reshape(replica_count, share, model_width),
        *small_parts,
        waits=(head_part,),
    )
    head_rows = swap_all(head_part.reshape(group_count, share, 3 * width_here))
    (output_part, small_sums), head_rows = window(
        [first_ring],
        lambda output, small: (
            rep_scatter(output, 0, scatter_order[1:]),
            small_pieces(small, small_parts),
        ),
        output_part,
        small_swapped,
        waits=(head_rows,),
    )
    head_rows = rep_gather(
        head_rows.reshape(group_count, share, heads_here, 3, head_dim)
        .transpose(3, 1, 0, 2, 4)
        .reshape(1, 3, share, model_width),
        gather_order[:-1],
    )
    output_rows, head_rows = window(
        [first_ring],
        lambda output: rep_gather(output, gather_order[:-1]),
        output_part,
        waits=(head_rows,),
    )
    head_rows = rep_gather(head_rows, gather_order[-1:])
    output_rows = rep_gather(output_rows, gather_order[-1:])
    first_grad = first_ring.total()
    query_grad, key_grad, value_grad = (
        head_rows[:, block].reshape(width_here, model_width).astype(wide_type)
        for block in range(3)
    )
    output_grad = output_rows.reshape(width_here, model_width).astype(wide_type)
    router_grad, postnorm_grad, prenorm_grad, querynorm_grad, keynorm_grad = small_sums
    router_grad = router_grad.reshape(width_here, expert_total)

    token_own = tokens.astype(wide_type)
    inverse_one = inverse_rms(token_own)
    pre_back, _ = norm_backward(token_own, inverse_one, prenorm_gain, first_grad)
    token_grad = residual_grad + pre_back

    down_total = down_sum.astype(wide_type)
    gate_total, up_total = (
        jnp.stack(
            [
                total[:, e * hidden_here : (e + 1) * hidden_here].astype(wide_type)
                for e in range(experts_here)
            ]
        )
        for total in (gate_sum, up_sum)
    )
    return (
        layer_out,
        token_grad,
        query_grad,
        key_grad,
        value_grad,
        output_grad,
        router_grad,
        prenorm_grad,
        querynorm_grad,
        keynorm_grad,
        postnorm_grad,
        gate_total,
        up_total,
        down_total,
    )


def solution(mesh):
    in_specs = (
        P(("rep", "ep"), None),
        P(("rep", "ep"), None),
        P("rep", None),
        P("rep", None),
        P(("rep", "ep"), None),
        P(("rep", "ep"), None),
        P("ep", None),
        P("ep", None),
        P("ep", None),
        P("ep", None),
        P("ep", None),
        P(),
        P(),
        P(),
        P(),
        P("ep", None, None),
        P("ep", None, None),
        P("ep", None, None),
    )
    out_specs = (
        P(("rep", "ep"), None),
        P(("rep", "ep"), None),
        P("ep", None),
        P("ep", None),
        P("ep", None),
        P("ep", None),
        P("ep", None),
        P("ep"),
        P("ep"),
        P("ep"),
        P("ep"),
        P("ep", "rep", None),
        P("ep", "rep", None),
        P("ep", "rep", None),
    )
    return jax.shard_map(body, mesh=mesh, in_specs=in_specs, out_specs=out_specs, check_vma=False)
```

```python
import functools

import jax
import jax.numpy as jnp
from jax import lax
from jax.experimental import pallas as pl
from jax.experimental.pallas import tpu as pltpu
from jax.sharding import PartitionSpec as P

epsilon = 1e-05
rope_base = 10000.0
masked_value = -1e30
low_type = jnp.bfloat16
wide_type = jnp.float32


def inverse_rms(values):
    return lax.rsqrt(jnp.mean(values * values, axis=-1, keepdims=True) + epsilon)


def norm_backward(values, inverse, gain_vector, upstream):
    scaled = upstream * gain_vector
    inner_mean = jnp.mean(scaled * values, axis=-1, keepdims=True)
    result = inverse * scaled - values * (inverse * inverse * inverse) * inner_mean
    return (result, upstream * values * inverse)


def rope_tables(position, dimension):
    halfway = dimension // 2
    indices = jnp.arange(halfway, dtype=wide_type)
    frequency = rope_base ** (-2.0 * indices / dimension)
    angles = position.astype(wide_type)[:, None] * frequency[None, :]
    cosine = jnp.cos(angles)
    sine_part = jnp.sin(angles)
    return (
        jnp.concatenate([cosine, cosine], axis=-1),
        jnp.concatenate([sine_part, sine_part], axis=-1),
    )


def turn_half(values):
    halfway = values.shape[-1] // 2
    return jnp.concatenate([-values[..., halfway:], values[..., :halfway]], axis=-1)


def turn_back(values):
    halfway = values.shape[-1] // 2
    return jnp.concatenate([values[..., halfway:], -values[..., :halfway]], axis=-1)


def row_meta(lengths, group_order):
    boundary = jnp.cumsum(lengths)
    passed = (group_order[:, None] >= boundary[None, :]).astype(jnp.int32)
    segment = jnp.sum(passed, axis=1)
    offset = jnp.sum(passed * lengths[None, :], axis=1)
    return (segment, group_order - offset)


def mm(left, right, left_dim, right_dim):
    return lax.dot_general(
        left,
        right,
        (((left_dim,), (right_dim,)), ((), ())),
        preferred_element_type=wide_type,
    )


def gather_rows(values):
    return lax.all_gather(values, "ep", axis=0, tiled=True)


def ring_order(count):
    return [i for i in range(count) if i % 2 == 0] + [i for i in reversed(range(count)) if i % 2]


def ring_slots(count):
    half = count // 2
    offsets = [0]
    for step in range(1, half):
        offsets += [step, -step]
    return offsets + [half]


def ring_shift(values, direction):
    order = ring_order(lax.axis_size("ep"))
    count = len(order)
    pairs = [(order[i], order[(i + direction) % count]) for i in range(count)]
    return lax.ppermute(values, "ep", pairs)


def tie(*arrays):
    return lax.optimization_barrier(arrays)


def after(value, *others):
    return lax.optimization_barrier((value,) + others)[0]


class RingGather:
    def __init__(self, values):
        self.middle = values.shape[0] // 2
        self.half, self.step = lax.axis_size("ep") // 2, 0
        self.sent = (values, values)
        self.blocks = [values]

    def start(self):
        if self.step == self.half - 1:
            self.sent = (self.sent[0][: self.middle], self.sent[1][self.middle :])
        self.received = (ring_shift(self.sent[0], 1), ring_shift(self.sent[1], -1))

    def finish(self):
        self.step += 1
        onward, backward = self.sent = self.received
        if self.step < self.half:
            self.blocks += [backward, onward]
        else:
            self.blocks += [jnp.concatenate([onward, backward], axis=0)]


class Exchange:
    def __init__(self, values, distance):
        self.sent, self.distance = values, distance

    def start(self):
        self.received = rep_exchange(self.sent, self.distance)

    def finish(self):
        pass


class RingSum:
    def __init__(self, block, rows):
        count = lax.axis_size("ep")
        self.block, self.middle, self.step = block, rows // 2, 0
        self.half = count // 2
        self.slot = {offset: j for j, offset in enumerate(ring_slots(count))}
        far = block(self.slot[self.half])
        self.sent = (far[: self.middle], far[self.middle :])

    def start(self):
        self.received = (ring_shift(self.sent[0], 1), ring_shift(self.sent[1], -1))

    def finish(self):
        self.step += 1
        onward, backward = self.received
        left = self.half - self.step
        middle = self.middle
        if left:
            up, down = self.block(self.slot[left]), self.block(self.slot[-left])
            if self.step == 1:
                onward = jnp.concatenate([add_low(onward, up[:middle]), up[middle:]], axis=0)
                backward = jnp.concatenate(
                    [down[:middle], add_low(backward, down[middle:])], axis=0
                )
            else:
                onward, backward = add_low(onward, up), add_low(backward, down)
        self.sent = (onward, backward)

    def total(self):
        return (
            self.block(self.slot[0]).astype(wide_type)
            + self.sent[0].astype(wide_type)
            + self.sent[1].astype(wide_type)
        )


def window(rings, work, *inputs, waits=()):
    for ring in rings:
        ring.start()
    inputs, _ = tie(inputs, [ring.sent for ring in rings])
    received, waits, results = tie([ring.received for ring in rings], waits, work(*inputs))
    for ring, pair in zip(rings, received):
        ring.received = pair
        ring.finish()
    return (results, *waits) if waits else results


def add_low(left, right):
    return (left.astype(wide_type) + right.astype(wide_type)).astype(low_type)


def ring_place(member, count):
    return jnp.where(member % 2 == 0, member // 2, count - 1 - member // 2)


def ring_member(place, count):
    return jnp.where(place < count // 2, 2 * place, 2 * (count - 1 - place) + 1)


def ring_indices(device, count):
    place = ring_place(device, count)
    half = count // 2
    members = [ring_member((place + offset) % count, count) for offset in ring_slots(count)]
    slots = []
    for other in range(count):
        ahead = (ring_place(jnp.int32(other), count) - place) % count
        slot = jnp.where(ahead < half, 2 * ahead - 1, 2 * (count - ahead))
        slots.append(jnp.where(ahead == 0, 0, jnp.where(ahead == half, count - 1, slot)))
    return members, slots


def rep_exchange(values, distance):
    count = lax.axis_size("rep")
    return lax.ppermute(values, "rep", [(i, i ^ distance) for i in range(count)])


def rep_bit(distance):
    return (lax.axis_index("rep") // distance) % 2


def rep_distances():
    count, distance, distances = lax.axis_size("rep"), 1, []
    while distance < count:
        distances.append(distance)
        distance *= 2
    return distances


def rep_gather(gathered, distances):
    for distance in distances:
        shape = gathered.shape[1:]
        other = rep_exchange(gathered, distance)
        mine_first = jnp.stack([gathered, other], axis=1)
        other_first = jnp.stack([other, gathered], axis=1)
        gathered = jnp.where(rep_bit(distance) == 0, mine_first, other_first)
        gathered = gathered.reshape((-1,) + shape)
    return gathered


def rep_scatter(values, axis, distances):
    for distance in distances:
        shape = values.shape
        pairs = values.reshape(shape[:axis] + (shape[axis] // 2, 2) + shape[axis + 1 :])
        bit = rep_bit(distance)
        keep = lax.dynamic_index_in_dim(pairs, bit, axis + 1, keepdims=False)
        send = lax.dynamic_index_in_dim(pairs, 1 - bit, axis + 1, keepdims=False)
        values = add_low(keep, rep_exchange(send, distance))
    return values


def rep_sum(values):
    distance = 1
    while distance < lax.axis_size("rep"):
        values = values + rep_exchange(values, distance)
        distance *= 2
    return values


def swap_all(values):
    return lax.all_to_all(values, "ep", split_axis=0, concat_axis=0, tiled=True)


def expert_kernel(rows_ref, gate_ref, up_ref, stream_ref, gates_ref, *refs):
    inner_ref, gback_ref, uback_ref, pair_ref = refs[-4:]
    expert, step = pl.program_id(0), pl.program_id(1)
    rows = rows_ref[...]
    gate_linear = jnp.dot(rows, gate_ref[0], preferred_element_type=wide_type)
    up_linear = jnp.dot(rows, up_ref[0], preferred_element_type=wide_type)
    stream = stream_ref[...]
    column = gates_ref[:, 0:1]
    for other in range(1, gates_ref.shape[1]):
        column = jnp.where(expert == other, gates_ref[:, other : other + 1], column)
    sigmoid_gate = jax.nn.sigmoid(gate_linear)
    silu_gate = gate_linear * sigmoid_gate
    inner = silu_gate * up_linear
    inner_ref[...] = (column * inner).astype(low_type)
    hidden_grad = column * stream
    gback_ref[...] = (
        hidden_grad * up_linear * sigmoid_gate * (1.0 + gate_linear * (1.0 - sigmoid_gate))
    ).astype(low_type)
    uback_ref[...] = (hidden_grad * silu_gate).astype(low_type)
    product = inner * stream
    lanes = pair_ref.shape[2]
    folded = product[:, :lanes]
    for start in range(lanes, product.shape[1], lanes):
        folded = folded + product[:, start : start + lanes]

    @pl.when(step == 0)
    def _():
        pair_ref[0] = folded

    @pl.when(step > 0)
    def _():
        pair_ref[0] += folded


def expert_pass(rows, gate_weight, up_weight, stream, gates, chunk, chunks, earlier=()):
    count, depth = rows.shape
    experts, _, hidden = gate_weight.shape
    width = 256
    steps = hidden // width
    weight = pl.BlockSpec((1, depth, width), lambda e, j: (e, 0, j))
    out = pl.BlockSpec((count, width), lambda e, j: (chunk, e * steps + j))
    return pl.pallas_call(
        expert_kernel,
        grid=(experts, steps),
        in_specs=[
            pl.BlockSpec((count, depth), lambda e, j: (0, 0)),
            weight,
            weight,
            pl.BlockSpec((count, width), lambda e, j: (0, e * steps + j)),
            pl.BlockSpec(gates.shape, lambda e, j: (0, 0)),
        ]
        + [pl.BlockSpec(memory_space=pl.ANY)] * len(earlier),
        out_specs=[out, out, out, pl.BlockSpec((1, count, 128), lambda e, j: (e, 0, 0))],
        out_shape=[jax.ShapeDtypeStruct((count * chunks, experts * hidden), low_type)] * 3
        + [jax.ShapeDtypeStruct((experts, count, 128), wide_type)],
        input_output_aliases={5 + i: i for i in range(len(earlier))},
        compiler_params=pltpu.CompilerParams(vmem_limit_bytes=56 << 20),
        cost_estimate=pl.CostEstimate(
            flops=4 * count * depth * experts * hidden,
            bytes_accessed=4 * depth * experts * hidden + 20 * count * depth,
            transcendentals=count * experts * hidden,
        ),
    )(rows, gate_weight, up_weight, stream, gates, *earlier)


def expert_back_kernel(gback_ref, uback_ref, gate_ref, up_ref, out_ref):
    experts, _, hidden = gate_ref.shape
    total = None
    for e in range(experts):
        for grad_ref, weight_ref in ((gback_ref, gate_ref), (uback_ref, up_ref)):
            term = mm(grad_ref[:, e * hidden : (e + 1) * hidden], weight_ref[e], 1, 1)
            total = term if total is None else total + term
    out_ref[...] = total.astype(low_type)


def expert_back(gback, uback, gate_weight, up_weight, chunk, chunks):
    count = gback.shape[0] // chunks
    experts, depth, hidden = gate_weight.shape
    width = 256
    whole = pl.BlockSpec((count, experts * hidden), lambda j: (chunk, 0))
    weight = pl.BlockSpec((experts, width, hidden), lambda j: (0, j, 0))
    return pl.pallas_call(
        expert_back_kernel,
        grid=(depth // width,),
        in_specs=[whole, whole, weight, weight],
        out_specs=pl.BlockSpec((count, width), lambda j: (0, j)),
        out_shape=jax.ShapeDtypeStruct((count, depth), low_type),
        compiler_params=pltpu.CompilerParams(vmem_limit_bytes=56 << 20),
        cost_estimate=pl.CostEstimate(
            flops=4 * count * depth * experts * hidden,
            bytes_accessed=4 * depth * experts * hidden + 6 * count * depth,
            transcendentals=0,
        ),
    )(gback, uback, gate_weight, up_weight)


def attention_back_kernel(
    block,
    scale,
    order_ref,
    query_ref,
    key_ref,
    value_ref,
    swapped_ref,
    total_ref,
    column_ref,
    line_ref,
    query_raw_ref,
    key_raw_ref,
    gains_ref,
    cosine_ref,
    sine_ref,
    *refs,
):
    sent_ref, part_ref, key_sum, value_sum, grad_ref = refs[-5:]
    rows, depth = query_ref.shape
    lane = lax.broadcasted_iota(jnp.int32, (1, depth), 1)
    sign = jnp.where(lane < depth // 2, 1.0, -1.0)
    share = swapped_ref.shape[1]
    for slot in range(swapped_ref.shape[0]):
        grad_ref[slot * share : (slot + 1) * share, :] = swapped_ref[order_ref[slot]]
    key_sum[...] = jnp.zeros_like(key_sum)
    value_sum[...] = jnp.zeros_like(value_sum)
    part_ref[...] = jnp.zeros_like(part_ref)

    def finish(back, raw, row, which):
        turned = back * cosine_ref[row, :]
        turned += pltpu.roll(back * sine_ref[row, :], depth // 2, axis=1) * sign
        inverse = inverse_rms(raw)
        result, part = norm_backward(raw, inverse, gains_ref[which : which + 1, :], turned)
        sent_ref[row, which * depth : (which + 1) * depth] = result.astype(low_type)
        part_ref[which : which + 1, :] += jnp.sum(part, axis=0, keepdims=True)

    @pl.loop(0, rows // block)
    def _(step):
        row = pl.ds(pl.multiple_of(step * block, block), block)
        query, grad = query_ref[row, :], grad_ref[row, :]
        scores = mm(query, key_ref[...], 1, 1) * scale
        scores = jnp.where(column_ref[row, :] == line_ref[...], scores, masked_value)
        weights = jnp.exp(scores - total_ref[row, :])
        weight_grad = mm(grad, value_ref[...], 1, 1)
        row_dot = jnp.sum(weights * weight_grad, axis=-1, keepdims=True)
        score_grad = (weights * (weight_grad - row_dot)).astype(low_type)
        key_sum[...] += mm(score_grad, query, 0, 0)
        value_sum[...] += mm(weights.astype(low_type), grad, 0, 0)
        finish(mm(score_grad, key_ref[...], 1, 0) * scale, query_raw_ref[row, :], row, 0)

    @pl.loop(0, rows // block)
    def _(step):
        row = pl.ds(pl.multiple_of(step * block, block), block)
        finish(key_sum[row, :] * scale, key_raw_ref[row, :], row, 1)
        sent_ref[row, 2 * depth : 3 * depth] = value_sum[row, :].astype(low_type)


def attention_back(head, kept, swapped, order, column, line, raw, gains, tables, earlier=()):
    rows, depth = kept[0].shape
    block = 256 if rows % 256 == 0 else rows

    def whole(array):
        return pl.BlockSpec(array.shape, lambda i, order: (0,) * array.ndim)

    def columns(index):
        return pl.BlockSpec((rows, depth), lambda i, order: (0, index))

    operands = (*kept[:3], swapped, kept[3], column, line, raw, raw, gains, *tables)
    specs = [whole(operand) for operand in operands]
    specs[3] = pl.BlockSpec(swapped.shape[:2] + (depth,), lambda i, order: (0, 0, head))
    specs[7], specs[8] = columns(3 * head), columns(3 * head + 1)
    return pl.pallas_call(
        functools.partial(attention_back_kernel, block, depth**-0.5),
        grid_spec=pltpu.PrefetchScalarGridSpec(
            num_scalar_prefetch=1,
            grid=(1,),
            in_specs=specs + [pl.BlockSpec(memory_space=pl.ANY)] * len(earlier),
            out_specs=[
                pl.BlockSpec((rows, 3 * depth), lambda i, order: (0, head)),
                pl.BlockSpec((2, depth), lambda i, order: (0, 0)),
            ],
            scratch_shapes=[pltpu.VMEM((rows, depth), wide_type)] * 2
            + [pltpu.VMEM((rows, depth), low_type)],
        ),
        out_shape=[
            jax.ShapeDtypeStruct(raw.shape, low_type),
            jax.ShapeDtypeStruct((2, depth), wide_type),
        ],
        input_output_aliases={1 + len(operands) + i: i for i in range(len(earlier))},
        compiler_params=pltpu.CompilerParams(vmem_limit_bytes=56 << 20),
        cost_estimate=pl.CostEstimate(
            flops=10 * rows * rows * depth,
            bytes_accessed=30 * rows * depth,
            transcendentals=rows * rows,
        ),
    )(order, *operands, *earlier)


def block_product_kernel(left_ref, *refs):
    out_ref = refs[-1]
    rows = refs[0].shape[0]
    total = None
    for j, ref in enumerate(refs[:-1]):
        term = mm(left_ref[j * rows : (j + 1) * rows, :], ref[...], 0, 0)
        total = term if total is None else total + term
    out_ref[...] = total.astype(low_type)


def block_product(left, blocks):
    rows, width = blocks[0].shape
    tile = 512
    return pl.pallas_call(
        block_product_kernel,
        grid=(width // tile,),
        in_specs=[pl.BlockSpec(left.shape, lambda j: (0, 0))] + [pl.BlockSpec((rows, tile), lambda j: (0, j))] * len(blocks),
        out_specs=pl.BlockSpec((left.shape[1], tile), lambda j: (0, j)),
        out_shape=jax.ShapeDtypeStruct((left.shape[1], width), low_type),
        cost_estimate=pl.CostEstimate(flops=2 * left.size * width, bytes_accessed=2 * left.size + 2 * len(blocks) * rows * width, transcendentals=0),
    )(left, *blocks)


def body(
    tokens,
    cotangent,
    seq_lengths,
    token_order,
    routes,
    slot_index,
    query_weight,
    key_weight,
    value_weight,
    output_weight,
    router_weight,
    prenorm_gain,
    querynorm_gain,
    keynorm_gain,
    postnorm_gain,
    gate_weight,
    up_weight,
    down_weight,
):
    group_count = lax.axis_size("ep")
    device = lax.axis_index("ep")
    row_count, model_width = tokens.shape
    head_dim = querynorm_gain.shape[0]
    width_here = model_width // group_count
    heads_here = width_here // head_dim
    experts_here = gate_weight.shape[0]
    expert_total = experts_here * group_count
    top_count = routes.shape[1]
    capacity = row_count * top_count * 5 // (4 * expert_total)
    group_rows = row_count * group_count
    sequence_count = seq_lengths.shape[1]
    score_scale = head_dim ** (-0.5)

    replica_count = lax.axis_size("rep")
    replica = lax.axis_index("rep")
    share = width_here // replica_count

    device_of_slot, slot_of_device = ring_indices(device, group_count)

    def reorder(blocks, index):
        return jnp.concatenate(
            [lax.dynamic_slice_in_dim(blocks, index[i], 1, 0) for i in range(group_count)], axis=0
        )

    group_order = reorder(token_order[0].reshape(group_count, row_count), device_of_slot)
    segment, position = row_meta(seq_lengths[0], group_order.reshape(group_rows))
    segment_own = segment[:row_count]
    valid_own = (segment_own < sequence_count).astype(wide_type)[:, None]
    valid_all = (segment < sequence_count).astype(wide_type)[:, None]

    expert_ids = jnp.arange(expert_total, dtype=jnp.int32)
    route_code = jnp.zeros((row_count, expert_total), jnp.int32)
    for column in range(top_count):
        hit = routes[:, column, None] == expert_ids[None, :]
        kept = (slot_index[:, column, None] < capacity).astype(jnp.int32)
        route_code = route_code + jnp.where(hit, 1 + kept, 0)
    small_sent = jnp.concatenate([route_code.astype(low_type), router_weight], axis=0)

    projections = (
        jnp.stack(
            [
                lax.dynamic_slice_in_dim(piece, replica * share, share, 0).reshape(
                    share, group_count, heads_here, head_dim
                )
                for piece in (query_weight, key_weight, value_weight)
            ],
            axis=3,
        )
        .reshape(share, group_count, 3 * width_here)
        .transpose(1, 0, 2)
    )
    scatter_order = rep_distances()
    gather_order = scatter_order[::-1]
    swapped = swap_all(projections)
    head_weight = (
        rep_gather(swapped[None], gather_order)
        .transpose(1, 0, 2, 3)
        .reshape(model_width, 3 * width_here)
    )
    tokens_late, output_late, _ = tie(tokens, output_weight, swapped)
    token_ring = RingGather(tokens_late)
    token_ring.start()
    small_flat = after(small_sent.reshape(-1, head_dim), token_ring.received)
    small_all = swap_all(
        jnp.broadcast_to(small_flat[None], (group_count,) + small_flat.shape)
    ).reshape(group_count, row_count + width_here, expert_total)
    code_all = reorder(small_all[:, :row_count], device_of_slot).reshape(
        group_rows, expert_total
    )
    full_router = small_all[:, row_count:].reshape(model_width, expert_total)
    chunks = 2
    chunk_rows = group_rows // chunks
    blocks_here = group_count // chunks

    def chunk_of(array, chunk):
        return array[chunk * chunk_rows : (chunk + 1) * chunk_rows]

    def slot_rows(array):
        return lambda slot: array[slot * row_count : (slot + 1) * row_count]

    def reorder_rows(rows, index):
        return reorder(
            rows.reshape(group_count, row_count, rows.shape[1]), index
        ).reshape(rows.shape)

    column_share = model_width // replica_count
    output_share = gather_rows(
        lax.dynamic_slice_in_dim(output_late, replica * column_share, column_share, 1)
    )
    token_ring.finish()
    for step in range(1, group_count // 2):
        if step == group_count // 2 - 1:
            token_ring.sent = (after(token_ring.sent[0], output_share), token_ring.sent[1])
        token_ring.start()
        token_ring.finish()
    cosine, sine_part = rope_tables(after(position, token_ring.blocks[1]), head_dim)

    hidden_here = down_weight.shape[1]
    flat_down = down_weight.reshape(experts_here * hidden_here, model_width)

    allowed = segment[:, None] == segment[None, :]
    far = replica_count // 2
    steps = group_count // 2
    part_rows = model_width // steps
    far_parts = [
        Exchange(output_share[i * part_rows : (i + 1) * part_rows], far) for i in range(steps)
    ]

    def head_columns(values, block, head):
        start = (3 * head + block) * head_dim
        return values[:, start : start + head_dim]

    def project(weight, *blocks):
        token_all = jnp.concatenate(blocks, axis=0)
        token_wide = token_all.astype(wide_type)
        first_all = (token_wide * inverse_rms(token_wide) * prenorm_gain).astype(low_type)
        return token_all, first_all, mm(first_all, weight, 1, 0)

    def attend(head, raw):
        turned = []
        for block, gain in ((0, querynorm_gain), (1, keynorm_gain)):
            part = head_columns(raw, block, head)
            normed = part * inverse_rms(part) * gain
            turned.append((normed * cosine + turn_half(normed) * sine_part).astype(low_type))
        value_low = head_columns(raw, 2, head).astype(low_type)
        scores = jnp.where(allowed, mm(*turned, 1, 1) * score_scale, masked_value)
        top_score = jnp.max(scores, axis=-1, keepdims=True)
        powers = jnp.exp(scores - top_score)
        log_total = top_score + jnp.log(jnp.sum(powers, axis=-1, keepdims=True))
        weights_low = jnp.exp(scores - log_total).astype(low_type)
        return (*turned, value_low, log_total, mm(weights_low, value_low, 1, 0).astype(low_type))

    cot_ring = RingGather(after(cotangent, token_ring.received))
    token_all, first_all, raw = window(
        [cot_ring, far_parts[0]], project, head_weight, *token_ring.blocks
    )
    heads = []
    for head in range(heads_here):
        heads.append(
            window(
                [cot_ring, far_parts[1 + head]],
                lambda raw, head=head: attend(head, raw),
                raw,
            )
        )

    def order_work(*mixed):
        mixed_low = jnp.concatenate(mixed, axis=1)
        return (
            mixed_low,
            reorder_rows(mixed_low, slot_of_device),
            segment[:, None],
            segment[None, :],
            jnp.stack([querynorm_gain, keynorm_gain]),
            jnp.stack(device_of_slot),
        )

    mixed_low, mixed_ordered, segment_column, segment_line, norm_gains, slot_order = window(
        [cot_ring, *far_parts[1 + heads_here :]], order_work, *[head[4] for head in heads]
    )
    cot_all = jnp.concatenate(cot_ring.blocks, axis=0)
    output_pieces = {
        0: output_share,
        far: jnp.concatenate([part.received for part in far_parts], axis=0),
    }
    for distance in gather_order[1:]:
        for j in list(output_pieces):
            output_pieces[j ^ distance] = rep_exchange(output_pieces[j], distance)
    mixed_own = (
        swap_all(mixed_ordered.reshape(group_count, row_count, width_here))
        .transpose(1, 0, 2)
        .reshape(row_count, model_width)
    )
    attention = jnp.zeros((row_count, model_width), wide_type)
    for j, piece in output_pieces.items():
        attention = lax.dynamic_update_slice_in_dim(
            attention, mm(mixed_own, piece, 1, 0), (replica ^ j) * column_share, 1
        )
    residual = tokens.astype(wide_type) + attention
    inverse_two = inverse_rms(residual)
    second_input = (residual * inverse_two * postnorm_gain).astype(low_type)

    def gate_table(rows, code):
        logits = mm(rows, full_router, 1, 0)
        shifted = jnp.where(code > 0, logits, masked_value)
        powers = jnp.exp(shifted - jnp.max(shifted, axis=1, keepdims=True))
        return powers / jnp.sum(powers, axis=1, keepdims=True)

    kept_all = jnp.where(code_all > 1, valid_all, 0.0)
    kept_here = lax.dynamic_slice_in_dim(kept_all, device * experts_here, experts_here, 1)

    def stream_of(cot_part):
        return mm(cot_part, flat_down, 1, 1)

    def expert_chunk(chunk, rows, stream, *earlier):
        gates = gate_table(rows, chunk_of(code_all, chunk)) * chunk_of(kept_all, chunk)
        gates_here = lax.dynamic_slice_in_dim(gates, device * experts_here, experts_here, 1)
        return expert_pass(
            rows, gate_weight, up_weight, stream, gates_here, chunk, chunks, earlier
        )

    second_ring = RingGather(second_input)
    stream_first = window([second_ring], lambda part: stream_of(part), chunk_of(cot_all, 0))
    stream_last = window([second_ring], lambda part: stream_of(part), chunk_of(cot_all, 1))
    rows_first = jnp.concatenate(second_ring.blocks[:blocks_here], axis=0)
    *earlier, pair_first = window(
        [second_ring],
        lambda rows, stream: expert_chunk(0, rows, stream),
        rows_first,
        stream_first,
    )
    window([second_ring], lambda: ())
    rows_last = jnp.concatenate(second_ring.blocks[blocks_here:], axis=0)
    inner_all, gback_all, uback_all, pair_last = expert_chunk(
        1, rows_last, stream_last, *earlier
    )
    second_all = jnp.concatenate([rows_first, rows_last], axis=0)
    back_last = expert_back(gback_all, uback_all, gate_weight, up_weight, 1, chunks)
    back_parts = {1: back_last}

    def back_block(slot):
        start = (slot % blocks_here) * row_count
        return back_parts[slot // blocks_here][start : start + row_count]

    def grad_of(left, right):
        return mm(left, right, 0, 0).astype(low_type)

    pair_lanes = jnp.concatenate([pair_first, pair_last], axis=1)
    pair_sent = (kept_here * jnp.sum(pair_lanes, axis=2).transpose(1, 0)).reshape(
        group_count, row_count, experts_here
    )
    code_own = route_code
    gates_own = gate_table(second_input, code_own)

    back_ring = RingSum(back_block, row_count)

    def mixture_work(inner, pair):
        return (
            mm(inner, flat_down, 1, 0).astype(low_type),
            swap_all(reorder(pair, slot_of_device)),
        )

    mixture_part, pair_grad = window([back_ring], mixture_work, inner_all, pair_sent)
    mixture_ring = RingSum(slot_rows(mixture_part), row_count)

    def back_work(gback, uback, stage=back_parts):
        stage[0] = expert_back(gback, uback, gate_weight, up_weight, 0, chunks)
        return stage[0]

    back_parts[0] = window([back_ring, mixture_ring], back_work, gback_all, uback_all)

    def down_work(inner, pair):
        pair_grad = pair.transpose(1, 0, 2).reshape(row_count, expert_total)
        chosen_grad = gates_own * (
            pair_grad - jnp.sum(gates_own * pair_grad, axis=1, keepdims=True)
        )
        logits_grad = jnp.where(code_own > 0, chosen_grad, 0.0).astype(low_type)
        router_back = mm(logits_grad, full_router, 1, 1)
        router_part = mm(second_input, logits_grad, 0, 0)
        return grad_of(inner, cot_all), router_back, router_part

    down_part, router_back, router_part = window(
        [back_ring, mixture_ring], down_work, inner_all, pair_grad
    )
    gate_part = window(
        [back_ring, mixture_ring], lambda gback: grad_of(second_all, gback), gback_all
    )
    second_scattered = back_ring.total()
    second_grad = router_back + second_scattered
    upstream = valid_own * cotangent.astype(wide_type)
    def residual_work(second_grad):
        post_back, postnorm_part = norm_backward(
            residual, inverse_two, postnorm_gain, second_grad
        )
        residual_grad = upstream + post_back
        attention_low = residual_grad.astype(low_type)
        mixed_grad_own = jnp.zeros((row_count, model_width), wide_type)
        for j, piece in output_pieces.items():
            mixed_grad_own = mixed_grad_own + mm(
                lax.dynamic_slice_in_dim(
                    attention_low, (replica ^ j) * column_share, column_share, 1
                ),
                piece,
                1,
                1,
            )
        swap_sent = (
            mixed_grad_own.astype(low_type)
            .reshape(row_count, group_count, width_here)
            .transpose(1, 0, 2)
        )
        return swap_sent, residual_grad, attention_low, jnp.sum(postnorm_part, axis=0)

    swap_sent, residual_grad, attention_low, postnorm_part = window(
        [mixture_ring], residual_work, second_grad
    )
    class Swap(Exchange):
        def start(self):
            self.received = swap_all(self.sent)

    swap = Swap(swap_sent, 0)
    attention_gather = RingGather(attention_low)
    up_part = window(
        [swap, attention_gather],
        lambda uback: grad_of(second_all, uback),
        uback_all,
    )
    mixture = mixture_ring.total()
    mixed_grad = swap.received

    head_width = 3 * head_dim

    def head_grad(head, sent):
        start = head * head_width
        return grad_of(first_all, sent[:, start : start + head_width])

    def chain_start(head_part):
        shape = (group_count, replica_count, share, head_width)
        return rep_scatter(head_part.reshape(shape), 1, scatter_order)

    sent, gain_parts, chains = (), 0.0, []
    for head in range(heads_here):

        def head_work(grads, *earlier, head=head):
            part = [head_grad(head - 1, earlier[0])] if head else []
            return part, attention_back(
                head,
                heads[head][:4],
                grads,
                slot_order,
                segment_column,
                segment_line,
                raw,
                norm_gains,
                (cosine, sine_part),
                earlier,
            )

        part, (*sent, gain_part) = window([attention_gather], head_work, mixed_grad, *sent)
        chains += [chain_start(grad) for grad in part]
        gain_parts = gain_parts + gain_part
    (sent,) = sent
    querynorm_part, keynorm_part = gain_parts[0], gain_parts[1]
    down_sum = lax.psum_scatter(
        down_part.reshape(experts_here, hidden_here, model_width),
        "rep",
        scatter_dimension=1,
        tiled=True,
    )
    sent, down_sum = tie(sent, down_sum)

    def first_work(sent):
        first_part = mm(sent, head_weight, 1, 1)
        token_wide = token_all.astype(wide_type)
        prenorm_part = jnp.sum(first_part * token_wide * inverse_rms(token_wide), axis=0)
        return first_part.astype(low_type), prenorm_part

    head_part = window([], functools.partial(head_grad, heads_here - 1), sent)
    chains.append(chain_start(head_part))
    first_low, prenorm_part = window(
        [attention_gather] if attention_gather.step < steps else [], first_work, sent
    )
    while attention_gather.step < steps:
        window([attention_gather], lambda: ())

    def small_swap(parts):
        return swap_all(
            jnp.concatenate([part.reshape(group_count, -1) for part in parts], axis=1)
        )

    def small_pieces(swapped, parts):
        total = rep_sum(jnp.sum(swapped, axis=0))
        pieces, start = [], 0
        for part in parts:
            size = part.size // group_count
            pieces.append(total[start : start + size])
            start += size
        return pieces

    first_ring = RingSum(slot_rows(first_low), row_count)
    small_parts = [router_part, postnorm_part, prenorm_part, querynorm_part, keynorm_part]
    gate_sum = lax.psum_scatter(gate_part, "rep", scatter_dimension=0, tiled=True)
    up_sum = lax.psum_scatter(up_part, "rep", scatter_dimension=0, tiled=True)

    def split_experts(total):
        return jnp.stack(
            [
                total[:, e * hidden_here : (e + 1) * hidden_here].astype(wide_type)
                for e in range(experts_here)
            ]
        )

    def chain_swap(part):
        return swap_all(part.reshape(group_count, share, head_width))

    def chain_gather(part):
        rows = part.reshape(group_count, share, 3, head_dim).transpose(2, 1, 0, 3)
        return rep_gather(rows[None], gather_order[:-1])

    output_part, *chains[:-1] = window(
        [first_ring],
        lambda mixed, *blocks: block_product(mixed, blocks),
        mixed_low,
        *attention_gather.blocks,
        waits=tuple(chains[:-1]),
    )
    swaps = [chain_swap(part) for part in chains[:-1]]
    (output_part, down_total), last, *swaps = window(
        [first_ring],
        lambda output, down: (
            rep_scatter(output, 0, scatter_order[:1]),
            down.astype(wide_type),
        ),
        output_part.reshape(replica_count, share, model_width),
        down_sum,
        waits=(chains[-1], *swaps),
    )
    gathers = [chain_gather(part) for part in swaps]
    last = chain_swap(last)
    (output_part, small_swapped, gate_total, layer_out), last, *gathers = window(
        [first_ring],
        lambda output, total, sums, *small: (
            rep_scatter(output, 0, scatter_order[1:]),
            small_swap(small),
            split_experts(total),
            (valid_own * (residual + sums)).astype(low_type),
        ),
        output_part,
        gate_sum,
        mixture,
        *small_parts,
        waits=(last, *gathers),
    )
    last = chain_gather(last)
    (output_rows, small_sums), last = window(
        [first_ring],
        lambda output, small: (
            rep_gather(output, gather_order[:-1]),
            small_pieces(small, small_parts),
        ),
        output_part,
        small_swapped,
        waits=(last,),
    )
    head_rows = jnp.stack([*gathers, last], axis=4).reshape(-1, 3, share, model_width)
    head_rows = rep_gather(head_rows, gather_order[-1:])
    output_rows = rep_gather(output_rows, gather_order[-1:])
    first_grad = first_ring.total()
    query_grad, key_grad, value_grad = (
        head_rows[:, block].reshape(width_here, model_width).astype(wide_type)
        for block in range(3)
    )
    output_grad = output_rows.reshape(width_here, model_width).astype(wide_type)
    router_grad, postnorm_grad, prenorm_grad, querynorm_grad, keynorm_grad = small_sums
    router_grad = router_grad.reshape(width_here, expert_total)

    token_own = tokens.astype(wide_type)
    inverse_one = inverse_rms(token_own)
    pre_back, _ = norm_backward(token_own, inverse_one, prenorm_gain, first_grad)
    token_grad = residual_grad + pre_back

    up_total = split_experts(up_sum)
    return (
        layer_out,
        token_grad,
        query_grad,
        key_grad,
        value_grad,
        output_grad,
        router_grad,
        prenorm_grad,
        querynorm_grad,
        keynorm_grad,
        postnorm_grad,
        gate_total,
        up_total,
        down_total,
    )


def solution(mesh):
    in_specs = (
        P(("rep", "ep"), None),
        P(("rep", "ep"), None),
        P("rep", None),
        P("rep", None),
        P(("rep", "ep"), None),
        P(("rep", "ep"), None),
        P("ep", None),
        P("ep", None),
        P("ep", None),
        P("ep", None),
        P("ep", None),
        P(),
        P(),
        P(),
        P(),
        P("ep", None, None),
        P("ep", None, None),
        P("ep", None, None),
    )
    out_specs = (
        P(("rep", "ep"), None),
        P(("rep", "ep"), None),
        P("ep", None),
        P("ep", None),
        P("ep", None),
        P("ep", None),
        P("ep", None),
        P("ep"),
        P("ep"),
        P("ep"),
        P("ep"),
        P("ep", "rep", None),
        P("ep", "rep", None),
        P("ep", "rep", None),
    )
    return jax.shard_map(body, mesh=mesh, in_specs=in_specs, out_specs=out_specs, check_vma=False)
```

```python
import functools

import jax
import jax.numpy as jnp
from jax import lax
from jax.experimental import pallas as pl
from jax.experimental.pallas import tpu as pltpu
from jax.sharding import PartitionSpec as P

epsilon = 1e-05
rope_base = 10000.0
masked_value = -1e30
low_type = jnp.bfloat16
wide_type = jnp.float32


def inverse_rms(values):
    return lax.rsqrt(jnp.mean(values * values, axis=-1, keepdims=True) + epsilon)


def norm_backward(values, inverse, gain_vector, upstream):
    scaled = upstream * gain_vector
    inner_mean = jnp.mean(scaled * values, axis=-1, keepdims=True)
    result = inverse * scaled - values * (inverse * inverse * inverse) * inner_mean
    return (result, upstream * values * inverse)


def rope_tables(position, dimension):
    halfway = dimension // 2
    indices = jnp.arange(halfway, dtype=wide_type)
    frequency = rope_base ** (-2.0 * indices / dimension)
    angles = position.astype(wide_type)[:, None] * frequency[None, :]
    cosine = jnp.cos(angles)
    sine_part = jnp.sin(angles)
    return (
        jnp.concatenate([cosine, cosine], axis=-1),
        jnp.concatenate([sine_part, sine_part], axis=-1),
    )


def turn_half(values):
    halfway = values.shape[-1] // 2
    return jnp.concatenate([-values[..., halfway:], values[..., :halfway]], axis=-1)


def turn_back(values):
    halfway = values.shape[-1] // 2
    return jnp.concatenate([values[..., halfway:], -values[..., :halfway]], axis=-1)


def row_meta(lengths, group_order):
    boundary = jnp.cumsum(lengths)
    passed = (group_order[:, None] >= boundary[None, :]).astype(jnp.int32)
    segment = jnp.sum(passed, axis=1)
    offset = jnp.sum(passed * lengths[None, :], axis=1)
    return (segment, group_order - offset)


def mm(left, right, left_dim, right_dim):
    return lax.dot_general(
        left,
        right,
        (((left_dim,), (right_dim,)), ((), ())),
        preferred_element_type=wide_type,
    )


def gather_rows(values):
    return lax.all_gather(values, "ep", axis=0, tiled=True)


def ring_order(count):
    return [i for i in range(count) if i % 2 == 0] + [i for i in reversed(range(count)) if i % 2]


def ring_slots(count):
    half = count // 2
    offsets = [0]
    for step in range(1, half):
        offsets += [step, -step]
    return offsets + [half]


def ring_shift(values, direction):
    order = ring_order(lax.axis_size("ep"))
    count = len(order)
    pairs = [(order[i], order[(i + direction) % count]) for i in range(count)]
    return lax.ppermute(values, "ep", pairs)


def tie(*arrays):
    return lax.optimization_barrier(arrays)


def after(value, *others):
    return lax.optimization_barrier((value,) + others)[0]


class RingGather:
    def __init__(self, values):
        self.middle = values.shape[0] // 2
        self.half, self.step = lax.axis_size("ep") // 2, 0
        self.sent = (values, values)
        self.blocks = [values]

    def start(self):
        if self.step == self.half - 1:
            self.sent = (self.sent[0][: self.middle], self.sent[1][self.middle :])
        self.received = (ring_shift(self.sent[0], 1), ring_shift(self.sent[1], -1))

    def finish(self):
        self.step += 1
        onward, backward = self.sent = self.received
        if self.step < self.half:
            self.blocks += [backward, onward]
        else:
            self.blocks += [jnp.concatenate([onward, backward], axis=0)]


class Exchange:
    def __init__(self, values, distance):
        self.sent, self.distance = values, distance

    def start(self):
        self.received = rep_exchange(self.sent, self.distance)

    def finish(self):
        pass


class RingSum:
    def __init__(self, block, rows):
        count = lax.axis_size("ep")
        self.block, self.middle, self.step = block, rows // 2, 0
        self.half = count // 2
        self.slot = {offset: j for j, offset in enumerate(ring_slots(count))}
        far = block(self.slot[self.half])
        self.sent = (far[: self.middle], far[self.middle :])

    def start(self):
        self.received = (ring_shift(self.sent[0], 1), ring_shift(self.sent[1], -1))

    def finish(self):
        self.step += 1
        onward, backward = self.received
        left = self.half - self.step
        middle = self.middle
        if left:
            up, down = self.block(self.slot[left]), self.block(self.slot[-left])
            if self.step == 1:
                onward = jnp.concatenate([add_low(onward, up[:middle]), up[middle:]], axis=0)
                backward = jnp.concatenate(
                    [down[:middle], add_low(backward, down[middle:])], axis=0
                )
            else:
                onward, backward = add_low(onward, up), add_low(backward, down)
        self.sent = (onward, backward)

    def total(self):
        return (
            self.block(self.slot[0]).astype(wide_type)
            + self.sent[0].astype(wide_type)
            + self.sent[1].astype(wide_type)
        )


def window(rings, work, *inputs, waits=()):
    for ring in rings:
        ring.start()
    inputs, _ = tie(inputs, [ring.sent for ring in rings])
    received, waits, results = tie([ring.received for ring in rings], waits, work(*inputs))
    for ring, pair in zip(rings, received):
        ring.received = pair
        ring.finish()
    return (results, *waits) if waits else results


def add_low(left, right):
    return (left.astype(wide_type) + right.astype(wide_type)).astype(low_type)


def ring_place(member, count):
    return jnp.where(member % 2 == 0, member // 2, count - 1 - member // 2)


def ring_member(place, count):
    return jnp.where(place < count // 2, 2 * place, 2 * (count - 1 - place) + 1)


def ring_indices(device, count):
    place = ring_place(device, count)
    half = count // 2
    members = [ring_member((place + offset) % count, count) for offset in ring_slots(count)]
    slots = []
    for other in range(count):
        ahead = (ring_place(jnp.int32(other), count) - place) % count
        slot = jnp.where(ahead < half, 2 * ahead - 1, 2 * (count - ahead))
        slots.append(jnp.where(ahead == 0, 0, jnp.where(ahead == half, count - 1, slot)))
    return members, slots


def rep_exchange(values, distance):
    count = lax.axis_size("rep")
    return lax.ppermute(values, "rep", [(i, i ^ distance) for i in range(count)])


def rep_bit(distance):
    return (lax.axis_index("rep") // distance) % 2


def rep_distances():
    count, distance, distances = lax.axis_size("rep"), 1, []
    while distance < count:
        distances.append(distance)
        distance *= 2
    return distances


def rep_gather(gathered, distances):
    for distance in distances:
        shape = gathered.shape[1:]
        other = rep_exchange(gathered, distance)
        mine_first = jnp.stack([gathered, other], axis=1)
        other_first = jnp.stack([other, gathered], axis=1)
        gathered = jnp.where(rep_bit(distance) == 0, mine_first, other_first)
        gathered = gathered.reshape((-1,) + shape)
    return gathered


def rep_scatter(values, axis, distances):
    for distance in distances:
        shape = values.shape
        pairs = values.reshape(shape[:axis] + (shape[axis] // 2, 2) + shape[axis + 1 :])
        bit = rep_bit(distance)
        keep = lax.dynamic_index_in_dim(pairs, bit, axis + 1, keepdims=False)
        send = lax.dynamic_index_in_dim(pairs, 1 - bit, axis + 1, keepdims=False)
        values = add_low(keep, rep_exchange(send, distance))
    return values


def rep_sum(values):
    distance = 1
    while distance < lax.axis_size("rep"):
        values = values + rep_exchange(values, distance)
        distance *= 2
    return values


def swap_all(values):
    return lax.all_to_all(values, "ep", split_axis=0, concat_axis=0, tiled=True)


def expert_kernel(rows_ref, gate_ref, up_ref, stream_ref, gates_ref, *refs):
    inner_ref, gback_ref, uback_ref, pair_ref = refs[-4:]
    expert, step = pl.program_id(0), pl.program_id(1)
    rows = rows_ref[...]
    gate_linear = jnp.dot(rows, gate_ref[0], preferred_element_type=wide_type)
    up_linear = jnp.dot(rows, up_ref[0], preferred_element_type=wide_type)
    stream = stream_ref[...]
    column = gates_ref[:, 0:1]
    for other in range(1, gates_ref.shape[1]):
        column = jnp.where(expert == other, gates_ref[:, other : other + 1], column)
    sigmoid_gate = jax.nn.sigmoid(gate_linear)
    silu_gate = gate_linear * sigmoid_gate
    inner = silu_gate * up_linear
    inner_ref[...] = (column * inner).astype(low_type)
    hidden_grad = column * stream
    gback_ref[...] = (
        hidden_grad * up_linear * sigmoid_gate * (1.0 + gate_linear * (1.0 - sigmoid_gate))
    ).astype(low_type)
    uback_ref[...] = (hidden_grad * silu_gate).astype(low_type)
    product = inner * stream
    lanes = pair_ref.shape[2]
    folded = product[:, :lanes]
    for start in range(lanes, product.shape[1], lanes):
        folded = folded + product[:, start : start + lanes]

    @pl.when(step == 0)
    def _():
        pair_ref[0] = folded

    @pl.when(step > 0)
    def _():
        pair_ref[0] += folded


def expert_pass(rows, gate_weight, up_weight, stream, gates, chunk, chunks, earlier=()):
    count, depth = rows.shape
    experts, _, hidden = gate_weight.shape
    width = 256
    steps = hidden // width
    weight = pl.BlockSpec((1, depth, width), lambda e, j: (e, 0, j))
    out = pl.BlockSpec((count, width), lambda e, j: (chunk, e * steps + j))
    return pl.pallas_call(
        expert_kernel,
        grid=(experts, steps),
        in_specs=[
            pl.BlockSpec((count, depth), lambda e, j: (0, 0)),
            weight,
            weight,
            pl.BlockSpec((count, width), lambda e, j: (0, e * steps + j)),
            pl.BlockSpec(gates.shape, lambda e, j: (0, 0)),
        ]
        + [pl.BlockSpec(memory_space=pl.ANY)] * len(earlier),
        out_specs=[out, out, out, pl.BlockSpec((1, count, 128), lambda e, j: (e, 0, 0))],
        out_shape=[jax.ShapeDtypeStruct((count * chunks, experts * hidden), low_type)] * 3
        + [jax.ShapeDtypeStruct((experts, count, 128), wide_type)],
        input_output_aliases={5 + i: i for i in range(len(earlier))},
        compiler_params=pltpu.CompilerParams(vmem_limit_bytes=56 << 20),
        cost_estimate=pl.CostEstimate(
            flops=4 * count * depth * experts * hidden,
            bytes_accessed=4 * depth * experts * hidden + 20 * count * depth,
            transcendentals=count * experts * hidden,
        ),
    )(rows, gate_weight, up_weight, stream, gates, *earlier)


def expert_back_kernel(gback_ref, uback_ref, gate_ref, up_ref, out_ref):
    experts, _, hidden = gate_ref.shape
    total = None
    for e in range(experts):
        for grad_ref, weight_ref in ((gback_ref, gate_ref), (uback_ref, up_ref)):
            term = mm(grad_ref[:, e * hidden : (e + 1) * hidden], weight_ref[e], 1, 1)
            total = term if total is None else total + term
    out_ref[...] = total.astype(low_type)


def expert_back(gback, uback, gate_weight, up_weight, chunk, chunks):
    count = gback.shape[0] // chunks
    experts, depth, hidden = gate_weight.shape
    width = 256
    whole = pl.BlockSpec((count, experts * hidden), lambda j: (chunk, 0))
    weight = pl.BlockSpec((experts, width, hidden), lambda j: (0, j, 0))
    return pl.pallas_call(
        expert_back_kernel,
        grid=(depth // width,),
        in_specs=[whole, whole, weight, weight],
        out_specs=pl.BlockSpec((count, width), lambda j: (0, j)),
        out_shape=jax.ShapeDtypeStruct((count, depth), low_type),
        compiler_params=pltpu.CompilerParams(vmem_limit_bytes=56 << 20),
        cost_estimate=pl.CostEstimate(
            flops=4 * count * depth * experts * hidden,
            bytes_accessed=4 * depth * experts * hidden + 6 * count * depth,
            transcendentals=0,
        ),
    )(gback, uback, gate_weight, up_weight)


def attention_back_kernel(
    block,
    scale,
    order_ref,
    query_ref,
    key_ref,
    value_ref,
    swapped_ref,
    total_ref,
    column_ref,
    line_ref,
    query_raw_ref,
    key_raw_ref,
    gains_ref,
    cosine_ref,
    sine_ref,
    *refs,
):
    sent_ref, part_ref, key_sum, value_sum, grad_ref = refs[-5:]
    rows, depth = query_ref.shape
    lane = lax.broadcasted_iota(jnp.int32, (1, depth), 1)
    sign = jnp.where(lane < depth // 2, 1.0, -1.0)
    share = swapped_ref.shape[1]
    for slot in range(swapped_ref.shape[0]):
        grad_ref[slot * share : (slot + 1) * share, :] = swapped_ref[order_ref[slot]]
    key_sum[...] = jnp.zeros_like(key_sum)
    value_sum[...] = jnp.zeros_like(value_sum)
    part_ref[...] = jnp.zeros_like(part_ref)

    def finish(back, raw, row, which):
        turned = back * cosine_ref[row, :]
        turned += pltpu.roll(back * sine_ref[row, :], depth // 2, axis=1) * sign
        inverse = inverse_rms(raw)
        result, part = norm_backward(raw, inverse, gains_ref[which : which + 1, :], turned)
        sent_ref[row, which * depth : (which + 1) * depth] = result.astype(low_type)
        part_ref[which : which + 1, :] += jnp.sum(part, axis=0, keepdims=True)

    @pl.loop(0, rows // block)
    def _(step):
        row = pl.ds(pl.multiple_of(step * block, block), block)
        query, grad = query_ref[row, :], grad_ref[row, :]
        scores = mm(query, key_ref[...], 1, 1) * scale
        scores = jnp.where(column_ref[row, :] == line_ref[...], scores, masked_value)
        weights = jnp.exp(scores - total_ref[row, :])
        weight_grad = mm(grad, value_ref[...], 1, 1)
        row_dot = jnp.sum(weights * weight_grad, axis=-1, keepdims=True)
        score_grad = (weights * (weight_grad - row_dot)).astype(low_type)
        key_sum[...] += mm(score_grad, query, 0, 0)
        value_sum[...] += mm(weights.astype(low_type), grad, 0, 0)
        finish(mm(score_grad, key_ref[...], 1, 0) * scale, query_raw_ref[row, :], row, 0)

    @pl.loop(0, rows // block)
    def _(step):
        row = pl.ds(pl.multiple_of(step * block, block), block)
        finish(key_sum[row, :] * scale, key_raw_ref[row, :], row, 1)
        sent_ref[row, 2 * depth : 3 * depth] = value_sum[row, :].astype(low_type)


def attention_back(head, kept, swapped, order, column, line, raw, gains, tables, earlier=()):
    rows, depth = kept[0].shape
    block = 256 if rows % 256 == 0 else rows

    def whole(array):
        return pl.BlockSpec(array.shape, lambda i, order: (0,) * array.ndim)

    def columns(index):
        return pl.BlockSpec((rows, depth), lambda i, order: (0, index))

    operands = (*kept[:3], swapped, kept[3], column, line, raw, raw, gains, *tables)
    specs = [whole(operand) for operand in operands]
    specs[3] = pl.BlockSpec(swapped.shape[:2] + (depth,), lambda i, order: (0, 0, head))
    specs[7], specs[8] = columns(3 * head), columns(3 * head + 1)
    return pl.pallas_call(
        functools.partial(attention_back_kernel, block, depth**-0.5),
        grid_spec=pltpu.PrefetchScalarGridSpec(
            num_scalar_prefetch=1,
            grid=(1,),
            in_specs=specs + [pl.BlockSpec(memory_space=pl.ANY)] * len(earlier),
            out_specs=[
                pl.BlockSpec((rows, 3 * depth), lambda i, order: (0, head)),
                pl.BlockSpec((2, depth), lambda i, order: (0, 0)),
            ],
            scratch_shapes=[pltpu.VMEM((rows, depth), wide_type)] * 2
            + [pltpu.VMEM((rows, depth), low_type)],
        ),
        out_shape=[
            jax.ShapeDtypeStruct(raw.shape, low_type),
            jax.ShapeDtypeStruct((2, depth), wide_type),
        ],
        input_output_aliases={1 + len(operands) + i: i for i in range(len(earlier))},
        compiler_params=pltpu.CompilerParams(vmem_limit_bytes=56 << 20),
        cost_estimate=pl.CostEstimate(
            flops=10 * rows * rows * depth,
            bytes_accessed=30 * rows * depth,
            transcendentals=rows * rows,
        ),
    )(order, *operands, *earlier)


def block_product_kernel(left_ref, *refs):
    out_ref = refs[-1]
    rows = refs[0].shape[0]
    total = None
    for j, ref in enumerate(refs[:-1]):
        term = mm(left_ref[j * rows : (j + 1) * rows, :], ref[...], 0, 0)
        total = term if total is None else total + term
    out_ref[...] = total.astype(low_type)


def block_product(left, blocks):
    rows, width = blocks[0].shape
    tile = 512
    return pl.pallas_call(
        block_product_kernel,
        grid=(width // tile,),
        in_specs=[pl.BlockSpec(left.shape, lambda j: (0, 0))] + [pl.BlockSpec((rows, tile), lambda j: (0, j))] * len(blocks),
        out_specs=pl.BlockSpec((left.shape[1], tile), lambda j: (0, j)),
        out_shape=jax.ShapeDtypeStruct((left.shape[1], width), low_type),
        cost_estimate=pl.CostEstimate(flops=2 * left.size * width, bytes_accessed=2 * left.size + 2 * len(blocks) * rows * width, transcendentals=0),
    )(left, *blocks)


def body(
    tokens,
    cotangent,
    seq_lengths,
    token_order,
    routes,
    slot_index,
    query_weight,
    key_weight,
    value_weight,
    output_weight,
    router_weight,
    prenorm_gain,
    querynorm_gain,
    keynorm_gain,
    postnorm_gain,
    gate_weight,
    up_weight,
    down_weight,
):
    group_count = lax.axis_size("ep")
    device = lax.axis_index("ep")
    row_count, model_width = tokens.shape
    head_dim = querynorm_gain.shape[0]
    width_here = model_width // group_count
    heads_here = width_here // head_dim
    experts_here = gate_weight.shape[0]
    expert_total = experts_here * group_count
    top_count = routes.shape[1]
    capacity = row_count * top_count * 5 // (4 * expert_total)
    group_rows = row_count * group_count
    sequence_count = seq_lengths.shape[1]
    score_scale = head_dim ** (-0.5)

    replica_count = lax.axis_size("rep")
    replica = lax.axis_index("rep")
    share = width_here // replica_count

    device_of_slot, slot_of_device = ring_indices(device, group_count)

    def reorder(blocks, index):
        return jnp.concatenate(
            [lax.dynamic_slice_in_dim(blocks, index[i], 1, 0) for i in range(group_count)], axis=0
        )

    group_order = reorder(token_order[0].reshape(group_count, row_count), device_of_slot)
    segment, position = row_meta(seq_lengths[0], group_order.reshape(group_rows))
    segment_own = segment[:row_count]
    valid_own = (segment_own < sequence_count).astype(wide_type)[:, None]
    valid_all = (segment < sequence_count).astype(wide_type)[:, None]

    expert_ids = jnp.arange(expert_total, dtype=jnp.int32)
    route_code = jnp.zeros((row_count, expert_total), jnp.int32)
    for column in range(top_count):
        hit = routes[:, column, None] == expert_ids[None, :]
        kept = (slot_index[:, column, None] < capacity).astype(jnp.int32)
        route_code = route_code + jnp.where(hit, 1 + kept, 0)
    small_sent = jnp.concatenate([route_code.astype(low_type), router_weight], axis=0)

    projections = (
        jnp.stack(
            [
                lax.dynamic_slice_in_dim(piece, replica * share, share, 0).reshape(
                    share, group_count, heads_here, head_dim
                )
                for piece in (query_weight, key_weight, value_weight)
            ],
            axis=3,
        )
        .reshape(share, group_count, 3 * width_here)
        .transpose(1, 0, 2)
    )
    scatter_order = rep_distances()
    gather_order = scatter_order[::-1]
    swapped = swap_all(projections)
    head_weight = (
        rep_gather(swapped[None], gather_order)
        .transpose(1, 0, 2, 3)
        .reshape(model_width, 3 * width_here)
    )
    tokens_late, output_late, _ = tie(tokens, output_weight, swapped)
    token_ring = RingGather(tokens_late)
    token_ring.start()
    small_flat = after(small_sent.reshape(-1, head_dim), token_ring.received)
    small_all = swap_all(
        jnp.broadcast_to(small_flat[None], (group_count,) + small_flat.shape)
    ).reshape(group_count, row_count + width_here, expert_total)
    code_all = reorder(small_all[:, :row_count], device_of_slot).reshape(
        group_rows, expert_total
    )
    full_router = small_all[:, row_count:].reshape(model_width, expert_total)
    chunks = 2
    chunk_rows = group_rows // chunks
    blocks_here = group_count // chunks

    def chunk_of(array, chunk):
        return array[chunk * chunk_rows : (chunk + 1) * chunk_rows]

    def slot_rows(array):
        return lambda slot: array[slot * row_count : (slot + 1) * row_count]

    def reorder_rows(rows, index):
        return reorder(
            rows.reshape(group_count, row_count, rows.shape[1]), index
        ).reshape(rows.shape)

    column_share = model_width // replica_count
    output_share = gather_rows(
        lax.dynamic_slice_in_dim(output_late, replica * column_share, column_share, 1)
    )
    token_ring.finish()
    for step in range(1, group_count // 2):
        if step == group_count // 2 - 1:
            token_ring.sent = (after(token_ring.sent[0], output_share), token_ring.sent[1])
        token_ring.start()
        token_ring.finish()
    cosine, sine_part = rope_tables(after(position, token_ring.blocks[1]), head_dim)

    hidden_here = down_weight.shape[1]
    flat_down = down_weight.reshape(experts_here * hidden_here, model_width)

    allowed = segment[:, None] == segment[None, :]
    far = replica_count // 2
    steps = group_count // 2
    part_rows = model_width // steps
    far_parts = [
        Exchange(output_share[i * part_rows : (i + 1) * part_rows], far) for i in range(steps)
    ]

    def head_columns(values, block, head):
        start = (3 * head + block) * head_dim
        return values[:, start : start + head_dim]

    def project(weight, *blocks):
        token_all = jnp.concatenate(blocks, axis=0)
        token_wide = token_all.astype(wide_type)
        first_all = (token_wide * inverse_rms(token_wide) * prenorm_gain).astype(low_type)
        return token_all, first_all, mm(first_all, weight, 1, 0)

    def attend(head, raw):
        turned = []
        for block, gain in ((0, querynorm_gain), (1, keynorm_gain)):
            part = head_columns(raw, block, head)
            normed = part * inverse_rms(part) * gain
            turned.append((normed * cosine + turn_half(normed) * sine_part).astype(low_type))
        value_low = head_columns(raw, 2, head).astype(low_type)
        scores = jnp.where(allowed, mm(*turned, 1, 1) * score_scale, masked_value)
        top_score = jnp.max(scores, axis=-1, keepdims=True)
        powers = jnp.exp(scores - top_score)
        log_total = top_score + jnp.log(jnp.sum(powers, axis=-1, keepdims=True))
        weights_low = jnp.exp(scores - log_total).astype(low_type)
        return (*turned, value_low, log_total, mm(weights_low, value_low, 1, 0).astype(low_type))

    cot_ring = RingGather(after(cotangent, token_ring.received))
    token_all, first_all, raw = window(
        [cot_ring, far_parts[0]], project, head_weight, *token_ring.blocks
    )
    heads = []
    for head in range(heads_here):
        heads.append(
            window(
                [cot_ring, far_parts[1 + head]],
                lambda raw, head=head: attend(head, raw),
                raw,
            )
        )

    def order_work(*mixed):
        mixed_low = jnp.concatenate(mixed, axis=1)
        return (
            mixed_low,
            reorder_rows(mixed_low, slot_of_device),
            segment[:, None],
            segment[None, :],
            jnp.stack([querynorm_gain, keynorm_gain]),
            jnp.stack(device_of_slot),
        )

    mixed_low, mixed_ordered, segment_column, segment_line, norm_gains, slot_order = window(
        [cot_ring, *far_parts[1 + heads_here :]], order_work, *[head[4] for head in heads]
    )
    cot_all = jnp.concatenate(cot_ring.blocks, axis=0)
    output_pieces = {
        0: output_share,
        far: jnp.concatenate([part.received for part in far_parts], axis=0),
    }
    for distance in gather_order[1:]:
        for j in list(output_pieces):
            output_pieces[j ^ distance] = rep_exchange(output_pieces[j], distance)
    mixed_own = (
        swap_all(mixed_ordered.reshape(group_count, row_count, width_here))
        .transpose(1, 0, 2)
        .reshape(row_count, model_width)
    )
    attention = jnp.zeros((row_count, model_width), wide_type)
    for j, piece in output_pieces.items():
        attention = lax.dynamic_update_slice_in_dim(
            attention, mm(mixed_own, piece, 1, 0), (replica ^ j) * column_share, 1
        )
    residual = tokens.astype(wide_type) + attention
    inverse_two = inverse_rms(residual)
    second_input = (residual * inverse_two * postnorm_gain).astype(low_type)

    def gate_table(rows, code):
        logits = mm(rows, full_router, 1, 0)
        shifted = jnp.where(code > 0, logits, masked_value)
        powers = jnp.exp(shifted - jnp.max(shifted, axis=1, keepdims=True))
        return powers / jnp.sum(powers, axis=1, keepdims=True)

    kept_all = jnp.where(code_all > 1, valid_all, 0.0)
    kept_here = lax.dynamic_slice_in_dim(kept_all, device * experts_here, experts_here, 1)

    def stream_of(cot_part):
        return mm(cot_part, flat_down, 1, 1)

    def expert_chunk(chunk, rows, stream, *earlier):
        gates = gate_table(rows, chunk_of(code_all, chunk)) * chunk_of(kept_all, chunk)
        gates_here = lax.dynamic_slice_in_dim(gates, device * experts_here, experts_here, 1)
        return expert_pass(
            rows, gate_weight, up_weight, stream, gates_here, chunk, chunks, earlier
        )

    second_ring = RingGather(second_input)
    stream_first = window([second_ring], lambda part: stream_of(part), chunk_of(cot_all, 0))
    stream_last = window([second_ring], lambda part: stream_of(part), chunk_of(cot_all, 1))
    rows_first = jnp.concatenate(second_ring.blocks[:blocks_here], axis=0)
    *earlier, pair_first = window(
        [second_ring],
        lambda rows, stream: expert_chunk(0, rows, stream),
        rows_first,
        stream_first,
    )
    window([second_ring], lambda: ())
    rows_last = jnp.concatenate(second_ring.blocks[blocks_here:], axis=0)
    inner_all, gback_all, uback_all, pair_last = expert_chunk(
        1, rows_last, stream_last, *earlier
    )
    second_all = jnp.concatenate([rows_first, rows_last], axis=0)
    back_last = expert_back(gback_all, uback_all, gate_weight, up_weight, 1, chunks)
    back_parts = {1: back_last}

    def back_block(slot):
        start = (slot % blocks_here) * row_count
        return back_parts[slot // blocks_here][start : start + row_count]

    def grad_of(left, right):
        return mm(left, right, 0, 0).astype(low_type)

    pair_lanes = jnp.concatenate([pair_first, pair_last], axis=1)
    pair_sent = (kept_here * jnp.sum(pair_lanes, axis=2).transpose(1, 0)).reshape(
        group_count, row_count, experts_here
    )
    code_own = route_code
    gates_own = gate_table(second_input, code_own)

    back_ring = RingSum(back_block, row_count)

    def mixture_work(inner, pair):
        return (
            mm(inner, flat_down, 1, 0).astype(low_type),
            swap_all(reorder(pair, slot_of_device)),
        )

    mixture_part, pair_grad = window([back_ring], mixture_work, inner_all, pair_sent)
    mixture_ring = RingSum(slot_rows(mixture_part), row_count)

    def back_work(gback, uback):
        back_parts[0] = expert_back(gback, uback, gate_weight, up_weight, 0, chunks)
        return back_parts[0]

    back_parts[0] = window([back_ring, mixture_ring], back_work, gback_all, uback_all)

    def down_work(inner, pair):
        pair_grad = pair.transpose(1, 0, 2).reshape(row_count, expert_total)
        chosen_grad = gates_own * (
            pair_grad - jnp.sum(gates_own * pair_grad, axis=1, keepdims=True)
        )
        logits_grad = jnp.where(code_own > 0, chosen_grad, 0.0).astype(low_type)
        router_back = mm(logits_grad, full_router, 1, 1)
        router_part = mm(second_input, logits_grad, 0, 0)
        return grad_of(inner, cot_all), router_back, router_part

    down_part, router_back, router_part = window(
        [back_ring, mixture_ring], down_work, inner_all, pair_grad
    )
    gate_part = window(
        [back_ring, mixture_ring], lambda gback: grad_of(second_all, gback), gback_all
    )
    second_scattered = back_ring.total()
    second_grad = router_back + second_scattered
    upstream = valid_own * cotangent.astype(wide_type)
    def residual_work(second_grad):
        post_back, postnorm_part = norm_backward(
            residual, inverse_two, postnorm_gain, second_grad
        )
        residual_grad = upstream + post_back
        attention_low = residual_grad.astype(low_type)
        mixed_grad_own = jnp.zeros((row_count, model_width), wide_type)
        for j, piece in output_pieces.items():
            mixed_grad_own = mixed_grad_own + mm(
                lax.dynamic_slice_in_dim(
                    attention_low, (replica ^ j) * column_share, column_share, 1
                ),
                piece,
                1,
                1,
            )
        swap_sent = (
            mixed_grad_own.astype(low_type)
            .reshape(row_count, group_count, width_here)
            .transpose(1, 0, 2)
        )
        return swap_sent, residual_grad, attention_low, jnp.sum(postnorm_part, axis=0)

    swap_sent, residual_grad, attention_low, postnorm_part = window(
        [mixture_ring], residual_work, second_grad
    )
    class Swap(Exchange):
        def start(self):
            self.received = swap_all(self.sent)

    swap = Swap(swap_sent, 0)
    attention_gather = RingGather(attention_low)
    up_part = window(
        [swap, attention_gather],
        lambda uback: grad_of(second_all, uback),
        uback_all,
    )
    mixture = mixture_ring.total()
    mixed_grad = swap.received

    sent, gain_parts = (), 0.0
    for head in range(heads_here):

        def head_work(grads, *earlier, head=head):
            return tuple(
                attention_back(
                    head,
                    heads[head][:4],
                    grads,
                    slot_order,
                    segment_column,
                    segment_line,
                    raw,
                    norm_gains,
                    (cosine, sine_part),
                    earlier,
                )
            )

        *sent, gain_part = window([attention_gather], head_work, mixed_grad, *sent)
        gain_parts = gain_parts + gain_part
    (sent,) = sent
    querynorm_part, keynorm_part = gain_parts[0], gain_parts[1]
    down_sum = lax.psum_scatter(
        down_part.reshape(experts_here, hidden_here, model_width),
        "rep",
        scatter_dimension=1,
        tiled=True,
    )
    sent, down_sum = tie(sent, down_sum)

    def first_work(sent, head):
        first_part = mm(sent, head_weight, 1, 1)
        token_wide = token_all.astype(wide_type)
        prenorm_part = jnp.sum(first_part * token_wide * inverse_rms(token_wide), axis=0)
        return first_part.astype(low_type), prenorm_part, rep_scatter(head, 1, scatter_order[:1])

    head_part = window([attention_gather], grad_of, first_all, sent)
    while attention_gather.step < group_count // 2:
        window([attention_gather], lambda: ())
    first_low, prenorm_part, head_part = window(
        [],
        first_work,
        sent,
        head_part.reshape(group_count, replica_count, share, 3 * width_here),
    )

    def small_swap(parts):
        return swap_all(
            jnp.concatenate([part.reshape(group_count, -1) for part in parts], axis=1)
        )

    def small_pieces(swapped, parts):
        total = rep_sum(jnp.sum(swapped, axis=0))
        pieces, start = [], 0
        for part in parts:
            size = part.size // group_count
            pieces.append(total[start : start + size])
            start += size
        return pieces

    first_ring = RingSum(slot_rows(first_low), row_count)
    small_parts = [router_part, postnorm_part, prenorm_part, querynorm_part, keynorm_part]
    head_part = rep_scatter(head_part, 1, scatter_order[1:])
    output_part = window(
        [first_ring],
        lambda mixed, *blocks: block_product(mixed, blocks),
        mixed_low,
        *attention_gather.blocks,
    )
    gate_sum = lax.psum_scatter(gate_part, "rep", scatter_dimension=0, tiled=True)
    up_sum = lax.psum_scatter(up_part, "rep", scatter_dimension=0, tiled=True)
    def split_experts(total):
        return jnp.stack(
            [
                total[:, e * hidden_here : (e + 1) * hidden_here].astype(wide_type)
                for e in range(experts_here)
            ]
        )

    (small_swapped, output_part, down_total), head_part = window(
        [first_ring],
        lambda output, down, *small: (
            small_swap(small),
            rep_scatter(output, 0, scatter_order[:1]),
            down.astype(wide_type),
        ),
        output_part.reshape(replica_count, share, model_width),
        down_sum,
        *small_parts,
        waits=(head_part,),
    )
    head_rows = swap_all(head_part.reshape(group_count, share, 3 * width_here))
    (output_part, small_sums, gate_total, layer_out), head_rows = window(
        [first_ring],
        lambda output, small, total, sums: (
            rep_scatter(output, 0, scatter_order[1:]),
            small_pieces(small, small_parts),
            split_experts(total),
            (valid_own * (residual + sums)).astype(low_type),
        ),
        output_part,
        small_swapped,
        gate_sum,
        mixture,
        waits=(head_rows,),
    )
    head_rows = rep_gather(
        head_rows.reshape(group_count, share, heads_here, 3, head_dim)
        .transpose(3, 1, 0, 2, 4)
        .reshape(1, 3, share, model_width),
        gather_order[:-1],
    )
    output_rows, head_rows = window(
        [first_ring],
        lambda output: rep_gather(output, gather_order[:-1]),
        output_part,
        waits=(head_rows,),
    )
    head_rows = rep_gather(head_rows, gather_order[-1:])
    output_rows = rep_gather(output_rows, gather_order[-1:])
    first_grad = first_ring.total()
    query_grad, key_grad, value_grad = (
        head_rows[:, block].reshape(width_here, model_width).astype(wide_type)
        for block in range(3)
    )
    output_grad = output_rows.reshape(width_here, model_width).astype(wide_type)
    router_grad, postnorm_grad, prenorm_grad, querynorm_grad, keynorm_grad = small_sums
    router_grad = router_grad.reshape(width_here, expert_total)

    token_own = tokens.astype(wide_type)
    inverse_one = inverse_rms(token_own)
    pre_back, _ = norm_backward(token_own, inverse_one, prenorm_gain, first_grad)
    token_grad = residual_grad + pre_back

    up_total = split_experts(up_sum)
    return (
        layer_out,
        token_grad,
        query_grad,
        key_grad,
        value_grad,
        output_grad,
        router_grad,
        prenorm_grad,
        querynorm_grad,
        keynorm_grad,
        postnorm_grad,
        gate_total,
        up_total,
        down_total,
    )


def solution(mesh):
    in_specs = (
        P(("rep", "ep"), None),
        P(("rep", "ep"), None),
        P("rep", None),
        P("rep", None),
        P(("rep", "ep"), None),
        P(("rep", "ep"), None),
        P("ep", None),
        P("ep", None),
        P("ep", None),
        P("ep", None),
        P("ep", None),
        P(),
        P(),
        P(),
        P(),
        P("ep", None, None),
        P("ep", None, None),
        P("ep", None, None),
    )
    out_specs = (
        P(("rep", "ep"), None),
        P(("rep", "ep"), None),
        P("ep", None),
        P("ep", None),
        P("ep", None),
        P("ep", None),
        P("ep", None),
        P("ep"),
        P("ep"),
        P("ep"),
        P("ep"),
        P("ep", "rep", None),
        P("ep", "rep", None),
        P("ep", "rep", None),
    )
    return jax.shard_map(body, mesh=mesh, in_specs=in_specs, out_specs=out_specs, check_vma=False)
```

```python
import functools

import jax
import jax.numpy as jnp
from jax import lax
from jax.experimental import pallas as pl
from jax.experimental.pallas import tpu as pltpu
from jax.sharding import PartitionSpec as P

epsilon = 1e-05
rope_base = 10000.0
masked_value = -1e30
low_type = jnp.bfloat16
wide_type = jnp.float32


def inverse_rms(values):
    return lax.rsqrt(jnp.mean(values * values, axis=-1, keepdims=True) + epsilon)


def norm_backward(values, inverse, gain_vector, upstream):
    scaled = upstream * gain_vector
    inner_mean = jnp.mean(scaled * values, axis=-1, keepdims=True)
    result = inverse * scaled - values * (inverse * inverse * inverse) * inner_mean
    return (result, upstream * values * inverse)


def rope_tables(position, dimension):
    halfway = dimension // 2
    indices = jnp.arange(halfway, dtype=wide_type)
    frequency = rope_base ** (-2.0 * indices / dimension)
    angles = position.astype(wide_type)[:, None] * frequency[None, :]
    cosine = jnp.cos(angles)
    sine_part = jnp.sin(angles)
    return (
        jnp.concatenate([cosine, cosine], axis=-1),
        jnp.concatenate([sine_part, sine_part], axis=-1),
    )


def turn_half(values):
    halfway = values.shape[-1] // 2
    return jnp.concatenate([-values[..., halfway:], values[..., :halfway]], axis=-1)


def turn_back(values):
    halfway = values.shape[-1] // 2
    return jnp.concatenate([values[..., halfway:], -values[..., :halfway]], axis=-1)


def row_meta(lengths, group_order):
    boundary = jnp.cumsum(lengths)
    passed = (group_order[:, None] >= boundary[None, :]).astype(jnp.int32)
    segment = jnp.sum(passed, axis=1)
    offset = jnp.sum(passed * lengths[None, :], axis=1)
    return (segment, group_order - offset)


def mm(left, right, left_dim, right_dim):
    return lax.dot_general(
        left,
        right,
        (((left_dim,), (right_dim,)), ((), ())),
        preferred_element_type=wide_type,
    )


def gather_rows(values):
    return lax.all_gather(values, "ep", axis=0, tiled=True)


def ring_order(count):
    return [i for i in range(count) if i % 2 == 0] + [i for i in reversed(range(count)) if i % 2]


def ring_slots(count):
    half = count // 2
    offsets = [0]
    for step in range(1, half):
        offsets += [step, -step]
    return offsets + [half]


def ring_shift(values, direction):
    order = ring_order(lax.axis_size("ep"))
    count = len(order)
    pairs = [(order[i], order[(i + direction) % count]) for i in range(count)]
    return lax.ppermute(values, "ep", pairs)


def tie(*arrays):
    return lax.optimization_barrier(arrays)


def after(value, *others):
    return lax.optimization_barrier((value,) + others)[0]


class RingGather:
    def __init__(self, values):
        self.middle = values.shape[0] // 2
        self.half, self.step = lax.axis_size("ep") // 2, 0
        self.sent = (values, values)
        self.blocks = [values]

    def start(self):
        if self.step == self.half - 1:
            self.sent = (self.sent[0][: self.middle], self.sent[1][self.middle :])
        self.received = (ring_shift(self.sent[0], 1), ring_shift(self.sent[1], -1))

    def finish(self):
        self.step += 1
        onward, backward = self.sent = self.received
        if self.step < self.half:
            self.blocks += [backward, onward]
        else:
            self.blocks += [jnp.concatenate([onward, backward], axis=0)]


class Exchange:
    def __init__(self, values, distance):
        self.sent, self.distance = values, distance

    def start(self):
        self.received = rep_exchange(self.sent, self.distance)

    def finish(self):
        pass


class RingSum:
    def __init__(self, block, rows):
        count = lax.axis_size("ep")
        self.block, self.middle, self.step = block, rows // 2, 0
        self.half = count // 2
        self.slot = {offset: j for j, offset in enumerate(ring_slots(count))}
        far = block(self.slot[self.half])
        self.sent = (far[: self.middle], far[self.middle :])

    def start(self):
        self.received = (ring_shift(self.sent[0], 1), ring_shift(self.sent[1], -1))

    def finish(self):
        self.step += 1
        onward, backward = self.received
        left = self.half - self.step
        middle = self.middle
        if left:
            up, down = self.block(self.slot[left]), self.block(self.slot[-left])
            if self.step == 1:
                onward = jnp.concatenate([add_low(onward, up[:middle]), up[middle:]], axis=0)
                backward = jnp.concatenate(
                    [down[:middle], add_low(backward, down[middle:])], axis=0
                )
            else:
                onward, backward = add_low(onward, up), add_low(backward, down)
        self.sent = (onward, backward)

    def total(self):
        return (
            self.block(self.slot[0]).astype(wide_type)
            + self.sent[0].astype(wide_type)
            + self.sent[1].astype(wide_type)
        )


def window(rings, work, *inputs, waits=()):
    for ring in rings:
        ring.start()
    inputs, _ = tie(inputs, [ring.sent for ring in rings])
    received, waits, results = tie([ring.received for ring in rings], waits, work(*inputs))
    for ring, pair in zip(rings, received):
        ring.received = pair
        ring.finish()
    return (results, *waits) if waits else results


def add_low(left, right):
    return (left.astype(wide_type) + right.astype(wide_type)).astype(low_type)


def ring_place(member, count):
    return jnp.where(member % 2 == 0, member // 2, count - 1 - member // 2)


def ring_member(place, count):
    return jnp.where(place < count // 2, 2 * place, 2 * (count - 1 - place) + 1)


def ring_indices(device, count):
    place = ring_place(device, count)
    half = count // 2
    members = [ring_member((place + offset) % count, count) for offset in ring_slots(count)]
    slots = []
    for other in range(count):
        ahead = (ring_place(jnp.int32(other), count) - place) % count
        slot = jnp.where(ahead < half, 2 * ahead - 1, 2 * (count - ahead))
        slots.append(jnp.where(ahead == 0, 0, jnp.where(ahead == half, count - 1, slot)))
    return members, slots


def rep_exchange(values, distance):
    count = lax.axis_size("rep")
    return lax.ppermute(values, "rep", [(i, i ^ distance) for i in range(count)])


def rep_bit(distance):
    return (lax.axis_index("rep") // distance) % 2


def rep_distances():
    count, distance, distances = lax.axis_size("rep"), 1, []
    while distance < count:
        distances.append(distance)
        distance *= 2
    return distances


def rep_gather(gathered, distances):
    for distance in distances:
        shape = gathered.shape[1:]
        other = rep_exchange(gathered, distance)
        mine_first = jnp.stack([gathered, other], axis=1)
        other_first = jnp.stack([other, gathered], axis=1)
        gathered = jnp.where(rep_bit(distance) == 0, mine_first, other_first)
        gathered = gathered.reshape((-1,) + shape)
    return gathered


def rep_scatter(values, axis, distances):
    for distance in distances:
        shape = values.shape
        pairs = values.reshape(shape[:axis] + (shape[axis] // 2, 2) + shape[axis + 1 :])
        bit = rep_bit(distance)
        keep = lax.dynamic_index_in_dim(pairs, bit, axis + 1, keepdims=False)
        send = lax.dynamic_index_in_dim(pairs, 1 - bit, axis + 1, keepdims=False)
        values = add_low(keep, rep_exchange(send, distance))
    return values


def rep_sum(values):
    distance = 1
    while distance < lax.axis_size("rep"):
        values = values + rep_exchange(values, distance)
        distance *= 2
    return values


def swap_all(values):
    return lax.all_to_all(values, "ep", split_axis=0, concat_axis=0, tiled=True)


def expert_kernel(rows_ref, gate_ref, up_ref, stream_ref, gates_ref, *refs):
    inner_ref, gback_ref, uback_ref, pair_ref = refs[-4:]
    expert, step = pl.program_id(0), pl.program_id(1)
    rows = rows_ref[...]
    gate_linear = jnp.dot(rows, gate_ref[0], preferred_element_type=wide_type)
    up_linear = jnp.dot(rows, up_ref[0], preferred_element_type=wide_type)
    stream = stream_ref[...]
    column = gates_ref[:, 0:1]
    for other in range(1, gates_ref.shape[1]):
        column = jnp.where(expert == other, gates_ref[:, other : other + 1], column)
    sigmoid_gate = jax.nn.sigmoid(gate_linear)
    silu_gate = gate_linear * sigmoid_gate
    inner = silu_gate * up_linear
    inner_ref[...] = (column * inner).astype(low_type)
    hidden_grad = column * stream
    gback_ref[...] = (
        hidden_grad * up_linear * sigmoid_gate * (1.0 + gate_linear * (1.0 - sigmoid_gate))
    ).astype(low_type)
    uback_ref[...] = (hidden_grad * silu_gate).astype(low_type)
    product = inner * stream
    lanes = pair_ref.shape[2]
    folded = product[:, :lanes]
    for start in range(lanes, product.shape[1], lanes):
        folded = folded + product[:, start : start + lanes]

    @pl.when(step == 0)
    def _():
        pair_ref[0] = folded

    @pl.when(step > 0)
    def _():
        pair_ref[0] += folded


def expert_pass(rows, gate_weight, up_weight, stream, gates, chunk, chunks, earlier=()):
    count, depth = rows.shape
    experts, _, hidden = gate_weight.shape
    width = 256
    steps = hidden // width
    weight = pl.BlockSpec((1, depth, width), lambda e, j: (e, 0, j))
    out = pl.BlockSpec((count, width), lambda e, j: (chunk, e * steps + j))
    return pl.pallas_call(
        expert_kernel,
        grid=(experts, steps),
        in_specs=[
            pl.BlockSpec((count, depth), lambda e, j: (0, 0)),
            weight,
            weight,
            pl.BlockSpec((count, width), lambda e, j: (0, e * steps + j)),
            pl.BlockSpec(gates.shape, lambda e, j: (0, 0)),
        ]
        + [pl.BlockSpec(memory_space=pl.ANY)] * len(earlier),
        out_specs=[out, out, out, pl.BlockSpec((1, count, 128), lambda e, j: (e, 0, 0))],
        out_shape=[jax.ShapeDtypeStruct((count * chunks, experts * hidden), low_type)] * 3
        + [jax.ShapeDtypeStruct((experts, count, 128), wide_type)],
        input_output_aliases={5 + i: i for i in range(len(earlier))},
        compiler_params=pltpu.CompilerParams(vmem_limit_bytes=56 << 20),
        cost_estimate=pl.CostEstimate(
            flops=4 * count * depth * experts * hidden,
            bytes_accessed=4 * depth * experts * hidden + 20 * count * depth,
            transcendentals=count * experts * hidden,
        ),
    )(rows, gate_weight, up_weight, stream, gates, *earlier)


def expert_back_kernel(gback_ref, uback_ref, gate_ref, up_ref, out_ref):
    experts, _, hidden = gate_ref.shape
    total = None
    for e in range(experts):
        for grad_ref, weight_ref in ((gback_ref, gate_ref), (uback_ref, up_ref)):
            term = mm(grad_ref[:, e * hidden : (e + 1) * hidden], weight_ref[e], 1, 1)
            total = term if total is None else total + term
    out_ref[...] = total.astype(low_type)


def expert_back(gback, uback, gate_weight, up_weight, chunk, chunks):
    count = gback.shape[0] // chunks
    experts, depth, hidden = gate_weight.shape
    width = 256
    whole = pl.BlockSpec((count, experts * hidden), lambda j: (chunk, 0))
    weight = pl.BlockSpec((experts, width, hidden), lambda j: (0, j, 0))
    return pl.pallas_call(
        expert_back_kernel,
        grid=(depth // width,),
        in_specs=[whole, whole, weight, weight],
        out_specs=pl.BlockSpec((count, width), lambda j: (0, j)),
        out_shape=jax.ShapeDtypeStruct((count, depth), low_type),
        compiler_params=pltpu.CompilerParams(vmem_limit_bytes=56 << 20),
        cost_estimate=pl.CostEstimate(
            flops=4 * count * depth * experts * hidden,
            bytes_accessed=4 * depth * experts * hidden + 6 * count * depth,
            transcendentals=0,
        ),
    )(gback, uback, gate_weight, up_weight)


def attention_back_kernel(
    block,
    scale,
    order_ref,
    query_ref,
    key_ref,
    value_ref,
    swapped_ref,
    total_ref,
    column_ref,
    line_ref,
    query_raw_ref,
    key_raw_ref,
    gains_ref,
    cosine_ref,
    sine_ref,
    *refs,
):
    sent_ref, part_ref, key_sum, value_sum, grad_ref = refs[-5:]
    rows, depth = query_ref.shape
    lane = lax.broadcasted_iota(jnp.int32, (1, depth), 1)
    sign = jnp.where(lane < depth // 2, 1.0, -1.0)
    share = swapped_ref.shape[1]
    for slot in range(swapped_ref.shape[0]):
        grad_ref[slot * share : (slot + 1) * share, :] = swapped_ref[order_ref[slot]]
    key_sum[...] = jnp.zeros_like(key_sum)
    value_sum[...] = jnp.zeros_like(value_sum)
    part_ref[...] = jnp.zeros_like(part_ref)

    def finish(back, raw, row, which):
        turned = back * cosine_ref[row, :]
        turned += pltpu.roll(back * sine_ref[row, :], depth // 2, axis=1) * sign
        inverse = inverse_rms(raw)
        result, part = norm_backward(raw, inverse, gains_ref[which : which + 1, :], turned)
        sent_ref[row, which * depth : (which + 1) * depth] = result.astype(low_type)
        part_ref[which : which + 1, :] += jnp.sum(part, axis=0, keepdims=True)

    @pl.loop(0, rows // block)
    def _(step):
        row = pl.ds(pl.multiple_of(step * block, block), block)
        query, grad = query_ref[row, :], grad_ref[row, :]
        scores = mm(query, key_ref[...], 1, 1) * scale
        scores = jnp.where(column_ref[row, :] == line_ref[...], scores, masked_value)
        weights = jnp.exp(scores - total_ref[row, :])
        weight_grad = mm(grad, value_ref[...], 1, 1)
        row_dot = jnp.sum(weights * weight_grad, axis=-1, keepdims=True)
        score_grad = (weights * (weight_grad - row_dot)).astype(low_type)
        key_sum[...] += mm(score_grad, query, 0, 0)
        value_sum[...] += mm(weights.astype(low_type), grad, 0, 0)
        finish(mm(score_grad, key_ref[...], 1, 0) * scale, query_raw_ref[row, :], row, 0)

    @pl.loop(0, rows // block)
    def _(step):
        row = pl.ds(pl.multiple_of(step * block, block), block)
        finish(key_sum[row, :] * scale, key_raw_ref[row, :], row, 1)
        sent_ref[row, 2 * depth : 3 * depth] = value_sum[row, :].astype(low_type)


def attention_back(head, kept, swapped, order, column, line, raw, gains, tables, earlier=()):
    rows, depth = kept[0].shape
    block = 256 if rows % 256 == 0 else rows

    def whole(array):
        return pl.BlockSpec(array.shape, lambda i, order: (0,) * array.ndim)

    def columns(index):
        return pl.BlockSpec((rows, depth), lambda i, order: (0, index))

    operands = (*kept[:3], swapped, kept[3], column, line, raw, raw, gains, *tables)
    specs = [whole(operand) for operand in operands]
    specs[3] = pl.BlockSpec(swapped.shape[:2] + (depth,), lambda i, order: (0, 0, head))
    specs[7], specs[8] = columns(3 * head), columns(3 * head + 1)
    return pl.pallas_call(
        functools.partial(attention_back_kernel, block, depth**-0.5),
        grid_spec=pltpu.PrefetchScalarGridSpec(
            num_scalar_prefetch=1,
            grid=(1,),
            in_specs=specs + [pl.BlockSpec(memory_space=pl.ANY)] * len(earlier),
            out_specs=[
                pl.BlockSpec((rows, 3 * depth), lambda i, order: (0, head)),
                pl.BlockSpec((2, depth), lambda i, order: (0, 0)),
            ],
            scratch_shapes=[pltpu.VMEM((rows, depth), wide_type)] * 2
            + [pltpu.VMEM((rows, depth), low_type)],
        ),
        out_shape=[
            jax.ShapeDtypeStruct(raw.shape, low_type),
            jax.ShapeDtypeStruct((2, depth), wide_type),
        ],
        input_output_aliases={1 + len(operands) + i: i for i in range(len(earlier))},
        compiler_params=pltpu.CompilerParams(vmem_limit_bytes=56 << 20),
        cost_estimate=pl.CostEstimate(
            flops=10 * rows * rows * depth,
            bytes_accessed=30 * rows * depth,
            transcendentals=rows * rows,
        ),
    )(order, *operands, *earlier)


def output_forward_kernel(starts_ref, mixed_ref, token_ref, gain_ref, *refs):
    residual_ref, normed_ref, total = refs[-3:]
    step = pl.program_id(0)

    @pl.when(step == 0)
    def _():
        total[...] = token_ref[...].astype(wide_type)

    for j, piece_ref in enumerate(refs[:-3]):
        width = piece_ref.shape[1]
        columns = pl.ds(pl.multiple_of(starts_ref[j], width), width)
        total[:, columns] += mm(mixed_ref[0], piece_ref[...], 1, 0)

    @pl.when(step == pl.num_programs(0) - 1)
    def _():
        residual = total[...]
        residual_ref[...] = residual
        normed_ref[...] = (residual * inverse_rms(residual) * gain_ref[...]).astype(low_type)


def output_forward(swapped, tokens, gain, pieces, starts):
    count, rows, width = swapped.shape
    depth = tokens.shape[1]
    whole = pl.BlockSpec((rows, depth), lambda i, starts: (0, 0))
    return pl.pallas_call(
        output_forward_kernel,
        grid_spec=pltpu.PrefetchScalarGridSpec(
            num_scalar_prefetch=1,
            grid=(count,),
            in_specs=[
                pl.BlockSpec((1, rows, width), lambda i, starts: (i, 0, 0)),
                whole,
                pl.BlockSpec((1, depth), lambda i, starts: (0, 0)),
            ]
            + [
                pl.BlockSpec((width, piece.shape[1]), lambda i, starts: (i, 0))
                for piece in pieces
            ],
            out_specs=[whole, whole],
            scratch_shapes=[pltpu.VMEM((rows, depth), wide_type)],
        ),
        out_shape=[
            jax.ShapeDtypeStruct((rows, depth), wide_type),
            jax.ShapeDtypeStruct((rows, depth), low_type),
        ],
        compiler_params=pltpu.CompilerParams(vmem_limit_bytes=40 << 20),
        cost_estimate=pl.CostEstimate(
            flops=2 * rows * depth * depth,
            bytes_accessed=2 * depth * depth + 10 * rows * depth,
            transcendentals=0,
        ),
    )(starts, swapped, tokens, gain[None, :], *pieces)


def output_back_kernel(starts_ref, grad_ref, *refs):
    out_ref = refs[-1]
    total = None
    for j, piece_ref in enumerate(refs[:-1]):
        width = piece_ref.shape[1]
        columns = pl.ds(pl.multiple_of(starts_ref[j], width), width)
        term = mm(grad_ref[:, columns], piece_ref[...], 1, 1)
        total = term if total is None else total + term
    width = out_ref.shape[2]
    for i in range(out_ref.shape[0]):
        out_ref[i] = total[:, i * width : (i + 1) * width].astype(low_type)


def output_back(grads, pieces, starts, count):
    rows, depth = grads.shape
    width = depth // count
    group = 2 if count % 2 == 0 else 1
    return pl.pallas_call(
        output_back_kernel,
        grid_spec=pltpu.PrefetchScalarGridSpec(
            num_scalar_prefetch=1,
            grid=(count // group,),
            in_specs=[pl.BlockSpec((rows, depth), lambda i, starts: (0, 0))]
            + [
                pl.BlockSpec((group * width, piece.shape[1]), lambda i, starts: (i, 0))
                for piece in pieces
            ],
            out_specs=pl.BlockSpec((group, rows, width), lambda i, starts: (i, 0, 0)),
        ),
        out_shape=jax.ShapeDtypeStruct((count, rows, width), low_type),
        compiler_params=pltpu.CompilerParams(vmem_limit_bytes=40 << 20),
        cost_estimate=pl.CostEstimate(
            flops=2 * rows * depth * depth,
            bytes_accessed=2 * depth * depth + 4 * rows * depth,
            transcendentals=0,
        ),
    )(starts, grads, *pieces)


def block_product_kernel(left_ref, *refs):
    out_ref = refs[-1]
    rows = refs[0].shape[0]
    total = None
    for j, ref in enumerate(refs[:-1]):
        term = mm(left_ref[j * rows : (j + 1) * rows, :], ref[...], 0, 0)
        total = term if total is None else total + term
    out_ref[...] = total.astype(low_type)


def block_product(left, blocks):
    rows, width = blocks[0].shape
    tile = 512
    return pl.pallas_call(
        block_product_kernel,
        grid=(width // tile,),
        in_specs=[pl.BlockSpec(left.shape, lambda j: (0, 0))] + [pl.BlockSpec((rows, tile), lambda j: (0, j))] * len(blocks),
        out_specs=pl.BlockSpec((left.shape[1], tile), lambda j: (0, j)),
        out_shape=jax.ShapeDtypeStruct((left.shape[1], width), low_type),
        cost_estimate=pl.CostEstimate(flops=2 * left.size * width, bytes_accessed=2 * left.size + 2 * len(blocks) * rows * width, transcendentals=0),
    )(left, *blocks)


def body(
    tokens,
    cotangent,
    seq_lengths,
    token_order,
    routes,
    slot_index,
    query_weight,
    key_weight,
    value_weight,
    output_weight,
    router_weight,
    prenorm_gain,
    querynorm_gain,
    keynorm_gain,
    postnorm_gain,
    gate_weight,
    up_weight,
    down_weight,
):
    group_count = lax.axis_size("ep")
    device = lax.axis_index("ep")
    row_count, model_width = tokens.shape
    head_dim = querynorm_gain.shape[0]
    width_here = model_width // group_count
    heads_here = width_here // head_dim
    experts_here = gate_weight.shape[0]
    expert_total = experts_here * group_count
    top_count = routes.shape[1]
    capacity = row_count * top_count * 5 // (4 * expert_total)
    group_rows = row_count * group_count
    sequence_count = seq_lengths.shape[1]
    score_scale = head_dim ** (-0.5)

    replica_count = lax.axis_size("rep")
    replica = lax.axis_index("rep")
    share = width_here // replica_count

    device_of_slot, slot_of_device = ring_indices(device, group_count)

    def reorder(blocks, index):
        return jnp.concatenate(
            [lax.dynamic_slice_in_dim(blocks, index[i], 1, 0) for i in range(group_count)], axis=0
        )

    group_order = reorder(token_order[0].reshape(group_count, row_count), device_of_slot)
    segment, position = row_meta(seq_lengths[0], group_order.reshape(group_rows))
    segment_own = segment[:row_count]
    valid_own = (segment_own < sequence_count).astype(wide_type)[:, None]
    valid_all = (segment < sequence_count).astype(wide_type)[:, None]

    expert_ids = jnp.arange(expert_total, dtype=jnp.int32)
    route_code = jnp.zeros((row_count, expert_total), jnp.int32)
    for column in range(top_count):
        hit = routes[:, column, None] == expert_ids[None, :]
        kept = (slot_index[:, column, None] < capacity).astype(jnp.int32)
        route_code = route_code + jnp.where(hit, 1 + kept, 0)
    small_sent = jnp.concatenate([route_code.astype(low_type), router_weight], axis=0)

    projections = (
        jnp.stack(
            [
                lax.dynamic_slice_in_dim(piece, replica * share, share, 0).reshape(
                    share, group_count, heads_here, head_dim
                )
                for piece in (query_weight, key_weight, value_weight)
            ],
            axis=3,
        )
        .reshape(share, group_count, 3 * width_here)
        .transpose(1, 0, 2)
    )
    scatter_order = rep_distances()
    gather_order = scatter_order[::-1]
    swapped = swap_all(projections)
    head_weight = (
        rep_gather(swapped[None], gather_order)
        .transpose(1, 0, 2, 3)
        .reshape(model_width, 3 * width_here)
    )
    tokens_late, output_late, _ = tie(tokens, output_weight, swapped)
    token_ring = RingGather(tokens_late)
    token_ring.start()
    chunks = 2
    chunk_rows = group_rows // chunks
    blocks_here = group_count // chunks

    def chunk_of(array, chunk):
        return array[chunk * chunk_rows : (chunk + 1) * chunk_rows]

    def slot_rows(array):
        return lambda slot: array[slot * row_count : (slot + 1) * row_count]

    def reorder_rows(rows, index):
        return reorder(
            rows.reshape(group_count, row_count, rows.shape[1]), index
        ).reshape(rows.shape)

    column_share = model_width // replica_count
    output_share = gather_rows(
        lax.dynamic_slice_in_dim(output_late, replica * column_share, column_share, 1)
    )
    token_ring.finish()
    for step in range(1, group_count // 2):
        if step == group_count // 2 - 1:
            token_ring.sent = (after(token_ring.sent[0], output_share), token_ring.sent[1])
        token_ring.start()
        token_ring.finish()
    cosine, sine_part = rope_tables(after(position, token_ring.blocks[1]), head_dim)

    hidden_here = down_weight.shape[1]
    flat_down = down_weight.reshape(experts_here * hidden_here, model_width)

    allowed = segment[:, None] == segment[None, :]
    far = replica_count // 2
    steps = group_count // 2
    part_rows = model_width // steps
    far_parts = [
        Exchange(output_share[i * part_rows : (i + 1) * part_rows], far) for i in range(steps)
    ]

    def head_columns(values, block, head):
        start = (3 * head + block) * head_dim
        return values[:, start : start + head_dim]

    def project(weight, *blocks):
        token_all = jnp.concatenate(blocks, axis=0)
        token_wide = token_all.astype(wide_type)
        first_all = (token_wide * inverse_rms(token_wide) * prenorm_gain).astype(low_type)
        return token_all, first_all, mm(first_all, weight, 1, 0)

    def attend(head, raw):
        turned = []
        for block, gain in ((0, querynorm_gain), (1, keynorm_gain)):
            part = head_columns(raw, block, head)
            normed = part * inverse_rms(part) * gain
            turned.append((normed * cosine + turn_half(normed) * sine_part).astype(low_type))
        value_low = head_columns(raw, 2, head).astype(low_type)
        scores = jnp.where(allowed, mm(*turned, 1, 1) * score_scale, masked_value)
        top_score = jnp.max(scores, axis=-1, keepdims=True)
        powers = jnp.exp(scores - top_score)
        log_total = top_score + jnp.log(jnp.sum(powers, axis=-1, keepdims=True))
        weights_low = jnp.exp(scores - log_total).astype(low_type)
        return (*turned, value_low, log_total, mm(weights_low, value_low, 1, 0).astype(low_type))

    cot_ring = RingGather(after(cotangent, token_ring.received))
    token_all, first_all, raw = window(
        [cot_ring, far_parts[0]], project, head_weight, *token_ring.blocks
    )
    heads = []
    for head in range(heads_here):
        heads.append(
            window(
                [cot_ring, far_parts[1 + head]],
                lambda raw, head=head: attend(head, raw),
                raw,
            )
        )

    def order_work(*mixed):
        mixed_low = jnp.concatenate(mixed, axis=1)
        return (
            mixed_low,
            reorder_rows(mixed_low, slot_of_device),
            segment[:, None],
            segment[None, :],
            jnp.stack([querynorm_gain, keynorm_gain]),
            jnp.stack(device_of_slot),
        )

    mixed_low, mixed_ordered, segment_column, segment_line, norm_gains, slot_order = window(
        [cot_ring, *far_parts[1 + heads_here :]], order_work, *[head[4] for head in heads]
    )
    cot_all = jnp.concatenate(cot_ring.blocks, axis=0)
    output_pieces = {
        0: output_share,
        far: jnp.concatenate([part.received for part in far_parts], axis=0),
    }
    for distance in gather_order[1:]:
        for j in list(output_pieces):
            output_pieces[j ^ distance] = rep_exchange(output_pieces[j], distance)
    small_flat = after(small_sent.reshape(-1, head_dim), mixed_ordered)
    small_all = swap_all(
        jnp.broadcast_to(small_flat[None], (group_count,) + small_flat.shape)
    ).reshape(group_count, row_count + width_here, expert_total)
    code_all = reorder(small_all[:, :row_count], device_of_slot).reshape(
        group_rows, expert_total
    )
    full_router = small_all[:, row_count:].reshape(model_width, expert_total)
    piece_starts = jnp.stack([(replica ^ j) * column_share for j in output_pieces])
    piece_list = list(output_pieces.values())
    residual, second_input = output_forward(
        swap_all(mixed_ordered.reshape(group_count, row_count, width_here)),
        tokens,
        postnorm_gain,
        piece_list,
        piece_starts,
    )
    inverse_two = inverse_rms(residual)

    def gate_table(rows, code):
        logits = mm(rows, full_router, 1, 0)
        shifted = jnp.where(code > 0, logits, masked_value)
        powers = jnp.exp(shifted - jnp.max(shifted, axis=1, keepdims=True))
        return powers / jnp.sum(powers, axis=1, keepdims=True)

    kept_all = jnp.where(code_all > 1, valid_all, 0.0)
    kept_here = lax.dynamic_slice_in_dim(kept_all, device * experts_here, experts_here, 1)

    def stream_of(cot_part):
        return mm(cot_part, flat_down, 1, 1)

    def expert_chunk(chunk, rows, stream, *earlier):
        gates = gate_table(rows, chunk_of(code_all, chunk)) * chunk_of(kept_all, chunk)
        gates_here = lax.dynamic_slice_in_dim(gates, device * experts_here, experts_here, 1)
        return expert_pass(
            rows, gate_weight, up_weight, stream, gates_here, chunk, chunks, earlier
        )

    second_ring = RingGather(second_input)
    stream_first = window([second_ring], lambda part: stream_of(part), chunk_of(cot_all, 0))
    stream_last = window([second_ring], lambda part: stream_of(part), chunk_of(cot_all, 1))
    rows_first = jnp.concatenate(second_ring.blocks[:blocks_here], axis=0)
    *earlier, pair_first = window(
        [second_ring],
        lambda rows, stream: expert_chunk(0, rows, stream),
        rows_first,
        stream_first,
    )
    window([second_ring], lambda: ())
    rows_last = jnp.concatenate(second_ring.blocks[blocks_here:], axis=0)
    inner_all, gback_all, uback_all, pair_last = expert_chunk(
        1, rows_last, stream_last, *earlier
    )
    second_all = jnp.concatenate([rows_first, rows_last], axis=0)
    back_last = expert_back(gback_all, uback_all, gate_weight, up_weight, 1, chunks)
    back_parts = {1: back_last}

    def back_block(slot):
        start = (slot % blocks_here) * row_count
        return back_parts[slot // blocks_here][start : start + row_count]

    def grad_of(left, right):
        return mm(left, right, 0, 0).astype(low_type)

    pair_lanes = jnp.concatenate([pair_first, pair_last], axis=1)
    pair_sent = (kept_here * jnp.sum(pair_lanes, axis=2).transpose(1, 0)).reshape(
        group_count, row_count, experts_here
    )
    code_own = route_code
    gates_own = gate_table(second_input, code_own)

    back_ring = RingSum(back_block, row_count)

    def mixture_work(inner, pair):
        return (
            mm(inner, flat_down, 1, 0).astype(low_type),
            swap_all(reorder(pair, slot_of_device)),
        )

    mixture_part, pair_grad = window([back_ring], mixture_work, inner_all, pair_sent)
    mixture_ring = RingSum(slot_rows(mixture_part), row_count)

    def back_work(gback, uback):
        back_parts[0] = expert_back(gback, uback, gate_weight, up_weight, 0, chunks)
        return back_parts[0]

    back_parts[0] = window([back_ring, mixture_ring], back_work, gback_all, uback_all)

    def down_work(inner, pair):
        pair_grad = pair.transpose(1, 0, 2).reshape(row_count, expert_total)
        chosen_grad = gates_own * (
            pair_grad - jnp.sum(gates_own * pair_grad, axis=1, keepdims=True)
        )
        logits_grad = jnp.where(code_own > 0, chosen_grad, 0.0).astype(low_type)
        router_back = mm(logits_grad, full_router, 1, 1)
        router_part = mm(second_input, logits_grad, 0, 0)
        return grad_of(inner, cot_all), router_back, router_part

    down_part, router_back, router_part = window(
        [back_ring, mixture_ring], down_work, inner_all, pair_grad
    )
    gate_part = window(
        [back_ring, mixture_ring], lambda gback: grad_of(second_all, gback), gback_all
    )
    second_scattered = back_ring.total()
    second_grad = router_back + second_scattered
    upstream = valid_own * cotangent.astype(wide_type)
    def residual_work(second_grad):
        post_back, postnorm_part = norm_backward(
            residual, inverse_two, postnorm_gain, second_grad
        )
        residual_grad = upstream + post_back
        attention_low = residual_grad.astype(low_type)
        swap_sent = output_back(attention_low, piece_list, piece_starts, group_count)
        return swap_sent, residual_grad, attention_low, jnp.sum(postnorm_part, axis=0)

    swap_sent, residual_grad, attention_low, postnorm_part = window(
        [mixture_ring], residual_work, second_grad
    )
    class Swap(Exchange):
        def start(self):
            self.received = swap_all(self.sent)

    swap = Swap(swap_sent, 0)
    attention_gather = RingGather(attention_low)
    up_part = window(
        [swap, attention_gather],
        lambda uback: grad_of(second_all, uback),
        uback_all,
    )
    mixed_grad = swap.received

    sent, gain_parts = (), 0.0
    for head in range(heads_here):

        def head_work(grads, *earlier, head=head):
            return tuple(
                attention_back(
                    head,
                    heads[head][:4],
                    grads,
                    slot_order,
                    segment_column,
                    segment_line,
                    raw,
                    norm_gains,
                    (cosine, sine_part),
                    earlier,
                )
            )

        *sent, gain_part = window([attention_gather], head_work, mixed_grad, *sent)
        gain_parts = gain_parts + gain_part
    (sent,) = sent
    querynorm_part, keynorm_part = gain_parts[0], gain_parts[1]
    down_sum = lax.psum_scatter(
        down_part.reshape(experts_here, hidden_here, model_width),
        "rep",
        scatter_dimension=1,
        tiled=True,
    )
    sent, down_sum = tie(sent, down_sum)

    def first_work(sent, head):
        first_part = mm(sent, head_weight, 1, 1)
        token_wide = token_all.astype(wide_type)
        prenorm_part = jnp.sum(first_part * token_wide * inverse_rms(token_wide), axis=0)
        return first_part.astype(low_type), prenorm_part, rep_scatter(head, 1, scatter_order[:1])

    head_part = window([attention_gather], grad_of, first_all, sent)
    while attention_gather.step < group_count // 2:
        window([attention_gather], lambda: ())
    first_low, prenorm_part, head_part = window(
        [],
        first_work,
        sent,
        head_part.reshape(group_count, replica_count, share, 3 * width_here),
    )

    def small_swap(parts):
        return swap_all(
            jnp.concatenate([part.reshape(group_count, -1) for part in parts], axis=1)
        )

    def small_pieces(swapped, parts):
        total = rep_sum(jnp.sum(swapped, axis=0))
        pieces, start = [], 0
        for part in parts:
            size = part.size // group_count
            pieces.append(total[start : start + size])
            start += size
        return pieces

    first_ring = RingSum(slot_rows(first_low), row_count)
    small_parts = [router_part, postnorm_part, prenorm_part, querynorm_part, keynorm_part]
    head_part = rep_scatter(head_part, 1, scatter_order[1:])
    output_part = window(
        [first_ring],
        lambda mixed, *blocks: block_product(mixed, blocks),
        mixed_low,
        *attention_gather.blocks,
    )
    gate_sum = lax.psum_scatter(gate_part, "rep", scatter_dimension=0, tiled=True)
    up_sum = lax.psum_scatter(up_part, "rep", scatter_dimension=0, tiled=True)
    def split_experts(total):
        return jnp.stack(
            [
                total[:, e * hidden_here : (e + 1) * hidden_here].astype(wide_type)
                for e in range(experts_here)
            ]
        )

    (output_part, down_total), head_part = window(
        [first_ring],
        lambda output, down: (
            rep_scatter(output, 0, scatter_order[:1]),
            down.astype(wide_type),
        ),
        output_part.reshape(replica_count, share, model_width),
        down_sum,
        waits=(head_part,),
    )
    head_rows = swap_all(head_part.reshape(group_count, share, 3 * width_here))
    def layer_work(own, *sums):
        mixture = sum((part.astype(wide_type) for part in sums), own.astype(wide_type))
        return (valid_own * (residual + mixture)).astype(low_type)

    (output_part, small_swapped, gate_total, layer_out), head_rows = window(
        [first_ring],
        lambda output, total, sums, *small: (
            rep_scatter(output, 0, scatter_order[1:]),
            small_swap(small),
            split_experts(total),
            layer_work(*sums),
        ),
        output_part,
        gate_sum,
        (mixture_part[:row_count], *mixture_ring.sent),
        *small_parts,
        waits=(head_rows,),
    )
    head_rows = rep_gather(
        head_rows.reshape(group_count, share, heads_here, 3, head_dim)
        .transpose(3, 1, 0, 2, 4)
        .reshape(1, 3, share, model_width),
        gather_order[:-1],
    )
    (output_rows, small_sums), head_rows = window(
        [first_ring],
        lambda output, small: (
            rep_gather(output, gather_order[:-1]),
            small_pieces(small, small_parts),
        ),
        output_part,
        small_swapped,
        waits=(head_rows,),
    )
    head_rows = rep_gather(head_rows, gather_order[-1:])
    output_rows = rep_gather(output_rows, gather_order[-1:])
    first_grad = first_ring.total()
    query_grad, key_grad, value_grad = (
        head_rows[:, block].reshape(width_here, model_width).astype(wide_type)
        for block in range(3)
    )
    output_grad = output_rows.reshape(width_here, model_width).astype(wide_type)
    router_grad, postnorm_grad, prenorm_grad, querynorm_grad, keynorm_grad = small_sums
    router_grad = router_grad.reshape(width_here, expert_total)

    token_own = tokens.astype(wide_type)
    inverse_one = inverse_rms(token_own)
    pre_back, _ = norm_backward(token_own, inverse_one, prenorm_gain, first_grad)
    token_grad = residual_grad + pre_back

    up_total = split_experts(up_sum)
    return (
        layer_out,
        token_grad,
        query_grad,
        key_grad,
        value_grad,
        output_grad,
        router_grad,
        prenorm_grad,
        querynorm_grad,
        keynorm_grad,
        postnorm_grad,
        gate_total,
        up_total,
        down_total,
    )


def solution(mesh):
    in_specs = (
        P(("rep", "ep"), None),
        P(("rep", "ep"), None),
        P("rep", None),
        P("rep", None),
        P(("rep", "ep"), None),
        P(("rep", "ep"), None),
        P("ep", None),
        P("ep", None),
        P("ep", None),
        P("ep", None),
        P("ep", None),
        P(),
        P(),
        P(),
        P(),
        P("ep", None, None),
        P("ep", None, None),
        P("ep", None, None),
    )
    out_specs = (
        P(("rep", "ep"), None),
        P(("rep", "ep"), None),
        P("ep", None),
        P("ep", None),
        P("ep", None),
        P("ep", None),
        P("ep", None),
        P("ep"),
        P("ep"),
        P("ep"),
        P("ep"),
        P("ep", "rep", None),
        P("ep", "rep", None),
        P("ep", "rep", None),
    )
    return jax.shard_map(body, mesh=mesh, in_specs=in_specs, out_specs=out_specs, check_vma=False)
```

```python
import functools

import jax
import jax.numpy as jnp
from jax import lax
from jax.experimental import pallas as pl
from jax.experimental.pallas import tpu as pltpu
from jax.sharding import PartitionSpec as P

epsilon = 1e-05
rope_base = 10000.0
masked_value = -1e30
low_type = jnp.bfloat16
wide_type = jnp.float32


def inverse_rms(values):
    return lax.rsqrt(jnp.mean(values * values, axis=-1, keepdims=True) + epsilon)


def norm_backward(values, inverse, gain_vector, upstream):
    scaled = upstream * gain_vector
    inner_mean = jnp.mean(scaled * values, axis=-1, keepdims=True)
    result = inverse * scaled - values * (inverse * inverse * inverse) * inner_mean
    return (result, upstream * values * inverse)


def rope_tables(position, dimension):
    halfway = dimension // 2
    indices = jnp.arange(halfway, dtype=wide_type)
    frequency = rope_base ** (-2.0 * indices / dimension)
    angles = position.astype(wide_type)[:, None] * frequency[None, :]
    cosine = jnp.cos(angles)
    sine_part = jnp.sin(angles)
    return (
        jnp.concatenate([cosine, cosine], axis=-1),
        jnp.concatenate([sine_part, sine_part], axis=-1),
    )


def turn_half(values):
    halfway = values.shape[-1] // 2
    return jnp.concatenate([-values[..., halfway:], values[..., :halfway]], axis=-1)


def turn_back(values):
    halfway = values.shape[-1] // 2
    return jnp.concatenate([values[..., halfway:], -values[..., :halfway]], axis=-1)


def row_meta(lengths, group_order):
    boundary = jnp.cumsum(lengths)
    passed = (group_order[:, None] >= boundary[None, :]).astype(jnp.int32)
    segment = jnp.sum(passed, axis=1)
    offset = jnp.sum(passed * lengths[None, :], axis=1)
    return (segment, group_order - offset)


def mm(left, right, left_dim, right_dim):
    return lax.dot_general(
        left,
        right,
        (((left_dim,), (right_dim,)), ((), ())),
        preferred_element_type=wide_type,
    )


def gather_rows(values):
    return lax.all_gather(values, "ep", axis=0, tiled=True)


def ring_order(count):
    return [i for i in range(count) if i % 2 == 0] + [i for i in reversed(range(count)) if i % 2]


def ring_slots(count):
    half = count // 2
    offsets = [0]
    for step in range(1, half):
        offsets += [step, -step]
    return offsets + [half]


def ring_shift(values, direction):
    order = ring_order(lax.axis_size("ep"))
    count = len(order)
    pairs = [(order[i], order[(i + direction) % count]) for i in range(count)]
    return lax.ppermute(values, "ep", pairs)


def tie(*arrays):
    return lax.optimization_barrier(arrays)


def after(value, *others):
    return lax.optimization_barrier((value,) + others)[0]


class RingGather:
    def __init__(self, values):
        self.middle = values.shape[0] // 2
        self.half, self.step = lax.axis_size("ep") // 2, 0
        self.sent = (values, values)
        self.blocks = [values]

    def start(self):
        if self.step == self.half - 1:
            self.sent = (self.sent[0][: self.middle], self.sent[1][self.middle :])
        self.received = (ring_shift(self.sent[0], 1), ring_shift(self.sent[1], -1))

    def finish(self):
        self.step += 1
        onward, backward = self.sent = self.received
        if self.step < self.half:
            self.blocks += [backward, onward]
        else:
            self.blocks += [jnp.concatenate([onward, backward], axis=0)]


class Exchange:
    def __init__(self, values, distance):
        self.sent, self.distance = values, distance

    def start(self):
        self.received = rep_exchange(self.sent, self.distance)

    def finish(self):
        pass


class RingSum:
    def __init__(self, block, rows):
        count = lax.axis_size("ep")
        self.block, self.middle, self.step = block, rows // 2, 0
        self.half = count // 2
        self.slot = {offset: j for j, offset in enumerate(ring_slots(count))}
        far = block(self.slot[self.half])
        self.sent = (far[: self.middle], far[self.middle :])

    def start(self):
        self.received = (ring_shift(self.sent[0], 1), ring_shift(self.sent[1], -1))

    def finish(self):
        self.step += 1
        onward, backward = self.received
        left = self.half - self.step
        middle = self.middle
        if left:
            up, down = self.block(self.slot[left]), self.block(self.slot[-left])
            if self.step == 1:
                onward = jnp.concatenate([add_low(onward, up[:middle]), up[middle:]], axis=0)
                backward = jnp.concatenate(
                    [down[:middle], add_low(backward, down[middle:])], axis=0
                )
            else:
                onward, backward = add_low(onward, up), add_low(backward, down)
        self.sent = (onward, backward)

    def total(self):
        return (
            self.block(self.slot[0]).astype(wide_type)
            + self.sent[0].astype(wide_type)
            + self.sent[1].astype(wide_type)
        )


def window(rings, work, *inputs, waits=()):
    for ring in rings:
        ring.start()
    inputs, _ = tie(inputs, [ring.sent for ring in rings])
    received, waits, results = tie([ring.received for ring in rings], waits, work(*inputs))
    for ring, pair in zip(rings, received):
        ring.received = pair
        ring.finish()
    return (results, *waits) if waits else results


def add_low(left, right):
    return (left.astype(wide_type) + right.astype(wide_type)).astype(low_type)


def ring_place(member, count):
    return jnp.where(member % 2 == 0, member // 2, count - 1 - member // 2)


def ring_member(place, count):
    return jnp.where(place < count // 2, 2 * place, 2 * (count - 1 - place) + 1)


def ring_indices(device, count):
    place = ring_place(device, count)
    half = count // 2
    members = [ring_member((place + offset) % count, count) for offset in ring_slots(count)]
    slots = []
    for other in range(count):
        ahead = (ring_place(jnp.int32(other), count) - place) % count
        slot = jnp.where(ahead < half, 2 * ahead - 1, 2 * (count - ahead))
        slots.append(jnp.where(ahead == 0, 0, jnp.where(ahead == half, count - 1, slot)))
    return members, slots


def rep_exchange(values, distance):
    count = lax.axis_size("rep")
    return lax.ppermute(values, "rep", [(i, i ^ distance) for i in range(count)])


def rep_bit(distance):
    return (lax.axis_index("rep") // distance) % 2


def rep_distances():
    count, distance, distances = lax.axis_size("rep"), 1, []
    while distance < count:
        distances.append(distance)
        distance *= 2
    return distances


def rep_gather(gathered, distances):
    for distance in distances:
        shape = gathered.shape[1:]
        other = rep_exchange(gathered, distance)
        mine_first = jnp.stack([gathered, other], axis=1)
        other_first = jnp.stack([other, gathered], axis=1)
        gathered = jnp.where(rep_bit(distance) == 0, mine_first, other_first)
        gathered = gathered.reshape((-1,) + shape)
    return gathered


def rep_scatter(values, axis, distances):
    for distance in distances:
        shape = values.shape
        pairs = values.reshape(shape[:axis] + (shape[axis] // 2, 2) + shape[axis + 1 :])
        bit = rep_bit(distance)
        keep = lax.dynamic_index_in_dim(pairs, bit, axis + 1, keepdims=False)
        send = lax.dynamic_index_in_dim(pairs, 1 - bit, axis + 1, keepdims=False)
        values = add_low(keep, rep_exchange(send, distance))
    return values


def rep_sum(values):
    distance = 1
    while distance < lax.axis_size("rep"):
        values = values + rep_exchange(values, distance)
        distance *= 2
    return values


def swap_all(values):
    return lax.all_to_all(values, "ep", split_axis=0, concat_axis=0, tiled=True)


def expert_kernel(rows_ref, gate_ref, up_ref, stream_ref, gates_ref, *refs):
    inner_ref, gback_ref, uback_ref, pair_ref = refs[-4:]
    expert, step = pl.program_id(0), pl.program_id(1)
    rows = rows_ref[...]
    gate_linear = jnp.dot(rows, gate_ref[0], preferred_element_type=wide_type)
    up_linear = jnp.dot(rows, up_ref[0], preferred_element_type=wide_type)
    stream = stream_ref[...]
    column = gates_ref[:, 0:1]
    for other in range(1, gates_ref.shape[1]):
        column = jnp.where(expert == other, gates_ref[:, other : other + 1], column)
    sigmoid_gate = jax.nn.sigmoid(gate_linear)
    silu_gate = gate_linear * sigmoid_gate
    inner = silu_gate * up_linear
    inner_ref[...] = (column * inner).astype(low_type)
    hidden_grad = column * stream
    gback_ref[...] = (
        hidden_grad * up_linear * sigmoid_gate * (1.0 + gate_linear * (1.0 - sigmoid_gate))
    ).astype(low_type)
    uback_ref[...] = (hidden_grad * silu_gate).astype(low_type)
    product = inner * stream
    lanes = pair_ref.shape[2]
    folded = product[:, :lanes]
    for start in range(lanes, product.shape[1], lanes):
        folded = folded + product[:, start : start + lanes]

    @pl.when(step == 0)
    def _():
        pair_ref[0] = folded

    @pl.when(step > 0)
    def _():
        pair_ref[0] += folded


def expert_pass(rows, gate_weight, up_weight, stream, gates, chunk, chunks, earlier=()):
    count, depth = rows.shape
    experts, _, hidden = gate_weight.shape
    width = 256
    steps = hidden // width
    weight = pl.BlockSpec((1, depth, width), lambda e, j: (e, 0, j))
    out = pl.BlockSpec((count, width), lambda e, j: (chunk, e * steps + j))
    return pl.pallas_call(
        expert_kernel,
        grid=(experts, steps),
        in_specs=[
            pl.BlockSpec((count, depth), lambda e, j: (0, 0)),
            weight,
            weight,
            pl.BlockSpec((count, width), lambda e, j: (0, e * steps + j)),
            pl.BlockSpec(gates.shape, lambda e, j: (0, 0)),
        ]
        + [pl.BlockSpec(memory_space=pl.ANY)] * len(earlier),
        out_specs=[out, out, out, pl.BlockSpec((1, count, 128), lambda e, j: (e, 0, 0))],
        out_shape=[jax.ShapeDtypeStruct((count * chunks, experts * hidden), low_type)] * 3
        + [jax.ShapeDtypeStruct((experts, count, 128), wide_type)],
        input_output_aliases={5 + i: i for i in range(len(earlier))},
        compiler_params=pltpu.CompilerParams(vmem_limit_bytes=56 << 20),
        cost_estimate=pl.CostEstimate(
            flops=4 * count * depth * experts * hidden,
            bytes_accessed=4 * depth * experts * hidden + 20 * count * depth,
            transcendentals=count * experts * hidden,
        ),
    )(rows, gate_weight, up_weight, stream, gates, *earlier)


def expert_back_kernel(gback_ref, uback_ref, gate_ref, up_ref, out_ref):
    experts, _, hidden = gate_ref.shape
    total = None
    for e in range(experts):
        for grad_ref, weight_ref in ((gback_ref, gate_ref), (uback_ref, up_ref)):
            term = mm(grad_ref[:, e * hidden : (e + 1) * hidden], weight_ref[e], 1, 1)
            total = term if total is None else total + term
    out_ref[...] = total.astype(low_type)


def expert_back(gback, uback, gate_weight, up_weight, chunk, chunks):
    count = gback.shape[0] // chunks
    experts, depth, hidden = gate_weight.shape
    width = 256
    whole = pl.BlockSpec((count, experts * hidden), lambda j: (chunk, 0))
    weight = pl.BlockSpec((experts, width, hidden), lambda j: (0, j, 0))
    return pl.pallas_call(
        expert_back_kernel,
        grid=(depth // width,),
        in_specs=[whole, whole, weight, weight],
        out_specs=pl.BlockSpec((count, width), lambda j: (0, j)),
        out_shape=jax.ShapeDtypeStruct((count, depth), low_type),
        compiler_params=pltpu.CompilerParams(vmem_limit_bytes=56 << 20),
        cost_estimate=pl.CostEstimate(
            flops=4 * count * depth * experts * hidden,
            bytes_accessed=4 * depth * experts * hidden + 6 * count * depth,
            transcendentals=0,
        ),
    )(gback, uback, gate_weight, up_weight)


def attention_back_kernel(
    block,
    scale,
    order_ref,
    query_ref,
    key_ref,
    value_ref,
    swapped_ref,
    total_ref,
    column_ref,
    line_ref,
    query_raw_ref,
    key_raw_ref,
    gains_ref,
    cosine_ref,
    sine_ref,
    *refs,
):
    sent_ref, part_ref, key_sum, value_sum, grad_ref = refs[-5:]
    rows, depth = query_ref.shape
    lane = lax.broadcasted_iota(jnp.int32, (1, depth), 1)
    sign = jnp.where(lane < depth // 2, 1.0, -1.0)
    share = swapped_ref.shape[1]
    for slot in range(swapped_ref.shape[0]):
        grad_ref[slot * share : (slot + 1) * share, :] = swapped_ref[order_ref[slot]]
    key_sum[...] = jnp.zeros_like(key_sum)
    value_sum[...] = jnp.zeros_like(value_sum)
    part_ref[...] = jnp.zeros_like(part_ref)

    def finish(back, raw, row, which):
        turned = back * cosine_ref[row, :]
        turned += pltpu.roll(back * sine_ref[row, :], depth // 2, axis=1) * sign
        inverse = inverse_rms(raw)
        result, part = norm_backward(raw, inverse, gains_ref[which : which + 1, :], turned)
        sent_ref[row, which * depth : (which + 1) * depth] = result.astype(low_type)
        part_ref[which : which + 1, :] += jnp.sum(part, axis=0, keepdims=True)

    @pl.loop(0, rows // block)
    def _(step):
        row = pl.ds(pl.multiple_of(step * block, block), block)
        query, grad = query_ref[row, :], grad_ref[row, :]
        scores = mm(query, key_ref[...], 1, 1) * scale
        scores = jnp.where(column_ref[row, :] == line_ref[...], scores, masked_value)
        weights = jnp.exp(scores - total_ref[row, :])
        weight_grad = mm(grad, value_ref[...], 1, 1)
        row_dot = jnp.sum(weights * weight_grad, axis=-1, keepdims=True)
        score_grad = (weights * (weight_grad - row_dot)).astype(low_type)
        key_sum[...] += mm(score_grad, query, 0, 0)
        value_sum[...] += mm(weights.astype(low_type), grad, 0, 0)
        finish(mm(score_grad, key_ref[...], 1, 0) * scale, query_raw_ref[row, :], row, 0)

    @pl.loop(0, rows // block)
    def _(step):
        row = pl.ds(pl.multiple_of(step * block, block), block)
        finish(key_sum[row, :] * scale, key_raw_ref[row, :], row, 1)
        sent_ref[row, 2 * depth : 3 * depth] = value_sum[row, :].astype(low_type)


def attention_back(head, kept, swapped, order, column, line, raw, gains, tables, earlier=()):
    rows, depth = kept[0].shape
    block = 256 if rows % 256 == 0 else rows

    def whole(array):
        return pl.BlockSpec(array.shape, lambda i, order: (0,) * array.ndim)

    def columns(index):
        return pl.BlockSpec((rows, depth), lambda i, order: (0, index))

    operands = (*kept[:3], swapped, kept[3], column, line, raw, raw, gains, *tables)
    specs = [whole(operand) for operand in operands]
    specs[3] = pl.BlockSpec(swapped.shape[:2] + (depth,), lambda i, order: (0, 0, head))
    specs[7], specs[8] = columns(3 * head), columns(3 * head + 1)
    return pl.pallas_call(
        functools.partial(attention_back_kernel, block, depth**-0.5),
        grid_spec=pltpu.PrefetchScalarGridSpec(
            num_scalar_prefetch=1,
            grid=(1,),
            in_specs=specs + [pl.BlockSpec(memory_space=pl.ANY)] * len(earlier),
            out_specs=[
                pl.BlockSpec((rows, 3 * depth), lambda i, order: (0, head)),
                pl.BlockSpec((2, depth), lambda i, order: (0, 0)),
            ],
            scratch_shapes=[pltpu.VMEM((rows, depth), wide_type)] * 2
            + [pltpu.VMEM((rows, depth), low_type)],
        ),
        out_shape=[
            jax.ShapeDtypeStruct(raw.shape, low_type),
            jax.ShapeDtypeStruct((2, depth), wide_type),
        ],
        input_output_aliases={1 + len(operands) + i: i for i in range(len(earlier))},
        compiler_params=pltpu.CompilerParams(vmem_limit_bytes=56 << 20),
        cost_estimate=pl.CostEstimate(
            flops=10 * rows * rows * depth,
            bytes_accessed=30 * rows * depth,
            transcendentals=rows * rows,
        ),
    )(order, *operands, *earlier)


def block_product_kernel(left_ref, *refs):
    out_ref = refs[-1]
    rows = refs[0].shape[0]
    total = None
    for j, ref in enumerate(refs[:-1]):
        term = mm(left_ref[j * rows : (j + 1) * rows, :], ref[...], 0, 0)
        total = term if total is None else total + term
    out_ref[...] = total.astype(low_type)


def block_product(left, blocks):
    rows, width = blocks[0].shape
    tile = 512
    return pl.pallas_call(
        block_product_kernel,
        grid=(width // tile,),
        in_specs=[pl.BlockSpec(left.shape, lambda j: (0, 0))] + [pl.BlockSpec((rows, tile), lambda j: (0, j))] * len(blocks),
        out_specs=pl.BlockSpec((left.shape[1], tile), lambda j: (0, j)),
        out_shape=jax.ShapeDtypeStruct((left.shape[1], width), low_type),
        cost_estimate=pl.CostEstimate(flops=2 * left.size * width, bytes_accessed=2 * left.size + 2 * len(blocks) * rows * width, transcendentals=0),
    )(left, *blocks)


def body(
    tokens,
    cotangent,
    seq_lengths,
    token_order,
    routes,
    slot_index,
    query_weight,
    key_weight,
    value_weight,
    output_weight,
    router_weight,
    prenorm_gain,
    querynorm_gain,
    keynorm_gain,
    postnorm_gain,
    gate_weight,
    up_weight,
    down_weight,
):
    group_count = lax.axis_size("ep")
    device = lax.axis_index("ep")
    row_count, model_width = tokens.shape
    head_dim = querynorm_gain.shape[0]
    width_here = model_width // group_count
    heads_here = width_here // head_dim
    experts_here = gate_weight.shape[0]
    expert_total = experts_here * group_count
    top_count = routes.shape[1]
    capacity = row_count * top_count * 5 // (4 * expert_total)
    group_rows = row_count * group_count
    sequence_count = seq_lengths.shape[1]
    score_scale = head_dim ** (-0.5)

    replica_count = lax.axis_size("rep")
    replica = lax.axis_index("rep")
    share = width_here // replica_count

    device_of_slot, slot_of_device = ring_indices(device, group_count)

    def reorder(blocks, index):
        return jnp.concatenate(
            [lax.dynamic_slice_in_dim(blocks, index[i], 1, 0) for i in range(group_count)], axis=0
        )

    group_order = reorder(token_order[0].reshape(group_count, row_count), device_of_slot)
    segment, position = row_meta(seq_lengths[0], group_order.reshape(group_rows))
    segment_own = segment[:row_count]
    valid_own = (segment_own < sequence_count).astype(wide_type)[:, None]
    valid_all = (segment < sequence_count).astype(wide_type)[:, None]

    expert_ids = jnp.arange(expert_total, dtype=jnp.int32)
    route_code = jnp.zeros((row_count, expert_total), jnp.int32)
    for column in range(top_count):
        hit = routes[:, column, None] == expert_ids[None, :]
        kept = (slot_index[:, column, None] < capacity).astype(jnp.int32)
        route_code = route_code + jnp.where(hit, 1 + kept, 0)
    small_sent = jnp.concatenate([route_code.astype(low_type), router_weight], axis=0)

    projections = (
        jnp.stack(
            [
                lax.dynamic_slice_in_dim(piece, replica * share, share, 0).reshape(
                    share, group_count, heads_here, head_dim
                )
                for piece in (query_weight, key_weight, value_weight)
            ],
            axis=3,
        )
        .reshape(share, group_count, 3 * width_here)
        .transpose(1, 0, 2)
    )
    scatter_order = rep_distances()
    gather_order = scatter_order[::-1]
    swapped = swap_all(projections)
    head_weight = (
        rep_gather(swapped[None], gather_order)
        .transpose(1, 0, 2, 3)
        .reshape(model_width, 3 * width_here)
    )
    output_late = after(output_weight, swapped)
    token_ring = RingGather(tokens)
    token_ring.start()
    small_flat = after(small_sent.reshape(-1, head_dim), token_ring.received)
    small_all = swap_all(
        jnp.broadcast_to(small_flat[None], (group_count,) + small_flat.shape)
    ).reshape(group_count, row_count + width_here, expert_total)
    code_all = reorder(small_all[:, :row_count], device_of_slot).reshape(
        group_rows, expert_total
    )
    full_router = small_all[:, row_count:].reshape(model_width, expert_total)
    chunks = 2
    chunk_rows = group_rows // chunks
    blocks_here = group_count // chunks

    def chunk_of(array, chunk):
        return array[chunk * chunk_rows : (chunk + 1) * chunk_rows]

    def slot_rows(array):
        return lambda slot: array[slot * row_count : (slot + 1) * row_count]

    def reorder_rows(rows, index):
        return reorder(
            rows.reshape(group_count, row_count, rows.shape[1]), index
        ).reshape(rows.shape)

    column_share = model_width // replica_count
    output_share = gather_rows(
        lax.dynamic_slice_in_dim(output_late, replica * column_share, column_share, 1)
    )
    token_ring.finish()
    for step in range(1, group_count // 2):
        if step == group_count // 2 - 1:
            token_ring.sent = (after(token_ring.sent[0], output_share), token_ring.sent[1])
        token_ring.start()
        token_ring.finish()
    cosine, sine_part = rope_tables(after(position, token_ring.blocks[1]), head_dim)

    hidden_here = down_weight.shape[1]
    flat_down = down_weight.reshape(experts_here * hidden_here, model_width)

    allowed = segment[:, None] == segment[None, :]
    far = replica_count // 2
    steps = group_count // 2
    part_rows = model_width // steps
    far_parts = [
        Exchange(output_share[i * part_rows : (i + 1) * part_rows], far) for i in range(steps)
    ]

    def head_columns(values, block, head):
        start = (3 * head + block) * head_dim
        return values[:, start : start + head_dim]

    def project(weight, *blocks):
        token_all = jnp.concatenate(blocks, axis=0)
        token_wide = token_all.astype(wide_type)
        inverse = inverse_rms(token_wide)
        first_all = (token_wide * inverse * prenorm_gain).astype(low_type)
        return token_all, inverse, first_all, mm(first_all, weight, 1, 0)

    def attend(head, raw):
        turned = []
        for block, gain in ((0, querynorm_gain), (1, keynorm_gain)):
            part = head_columns(raw, block, head)
            normed = part * inverse_rms(part) * gain
            turned.append((normed * cosine + turn_half(normed) * sine_part).astype(low_type))
        value_low = head_columns(raw, 2, head).astype(low_type)
        scores = jnp.where(allowed, mm(*turned, 1, 1) * score_scale, masked_value)
        top_score = jnp.max(scores, axis=-1, keepdims=True)
        powers = jnp.exp(scores - top_score)
        log_total = top_score + jnp.log(jnp.sum(powers, axis=-1, keepdims=True))
        weights_low = jnp.exp(scores - log_total).astype(low_type)
        return (*turned, value_low, log_total, mm(weights_low, value_low, 1, 0).astype(low_type))

    cot_ring = RingGather(after(cotangent, token_ring.received))
    token_all, inverse_all, first_all, raw = window(
        [cot_ring, far_parts[0]], project, head_weight, *token_ring.blocks
    )
    heads = []
    for head in range(heads_here):
        heads.append(
            window(
                [cot_ring, far_parts[1 + head]],
                lambda raw, head=head: attend(head, raw),
                raw,
            )
        )

    def order_work(*mixed):
        mixed_low = jnp.concatenate(mixed, axis=1)
        return (
            mixed_low,
            reorder_rows(mixed_low, slot_of_device),
            segment[:, None],
            segment[None, :],
            jnp.stack([querynorm_gain, keynorm_gain]),
            jnp.stack(device_of_slot),
        )

    mixed_low, mixed_ordered, segment_column, segment_line, norm_gains, slot_order = window(
        [cot_ring, *far_parts[1 + heads_here :]], order_work, *[head[4] for head in heads]
    )
    cot_all = jnp.concatenate(cot_ring.blocks, axis=0)
    output_pieces = {
        0: output_share,
        far: jnp.concatenate([part.received for part in far_parts], axis=0),
    }
    for distance in gather_order[1:]:
        for j in list(output_pieces):
            output_pieces[j ^ distance] = rep_exchange(output_pieces[j], distance)
    mixed_own = (
        swap_all(mixed_ordered.reshape(group_count, row_count, width_here))
        .transpose(1, 0, 2)
        .reshape(row_count, model_width)
    )
    attention = jnp.zeros((row_count, model_width), wide_type)
    for j, piece in output_pieces.items():
        attention = lax.dynamic_update_slice_in_dim(
            attention, mm(mixed_own, piece, 1, 0), (replica ^ j) * column_share, 1
        )
    residual = tokens.astype(wide_type) + attention
    inverse_two = inverse_rms(residual)
    second_input = (residual * inverse_two * postnorm_gain).astype(low_type)

    def gate_table(rows, code):
        logits = mm(rows, full_router, 1, 0)
        shifted = jnp.where(code > 0, logits, masked_value)
        powers = jnp.exp(shifted - jnp.max(shifted, axis=1, keepdims=True))
        return powers / jnp.sum(powers, axis=1, keepdims=True)

    kept_all = jnp.where(code_all > 1, valid_all, 0.0)
    kept_here = lax.dynamic_slice_in_dim(kept_all, device * experts_here, experts_here, 1)

    def stream_of(cot_part):
        return mm(cot_part, flat_down, 1, 1)

    def expert_chunk(chunk, rows, stream, *earlier):
        gates = gate_table(rows, chunk_of(code_all, chunk)) * chunk_of(kept_all, chunk)
        gates_here = lax.dynamic_slice_in_dim(gates, device * experts_here, experts_here, 1)
        return expert_pass(
            rows, gate_weight, up_weight, stream, gates_here, chunk, chunks, earlier
        )

    second_ring = RingGather(second_input)
    stream_first = window([second_ring], lambda part: stream_of(part), chunk_of(cot_all, 0))
    stream_last = window([second_ring], lambda part: stream_of(part), chunk_of(cot_all, 1))
    rows_first = jnp.concatenate(second_ring.blocks[:blocks_here], axis=0)
    *earlier, pair_first = window(
        [second_ring],
        lambda rows, stream: expert_chunk(0, rows, stream),
        rows_first,
        stream_first,
    )
    window([second_ring], lambda: ())
    rows_last = jnp.concatenate(second_ring.blocks[blocks_here:], axis=0)
    inner_all, gback_all, uback_all, pair_last = expert_chunk(
        1, rows_last, stream_last, *earlier
    )
    second_all = jnp.concatenate([rows_first, rows_last], axis=0)
    back_last = expert_back(gback_all, uback_all, gate_weight, up_weight, 1, chunks)
    back_parts = {1: back_last}

    def back_block(slot):
        start = (slot % blocks_here) * row_count
        return back_parts[slot // blocks_here][start : start + row_count]

    def grad_of(left, right):
        return mm(left, right, 0, 0).astype(low_type)

    pair_lanes = jnp.concatenate([pair_first, pair_last], axis=1)
    pair_sent = (kept_here * jnp.sum(pair_lanes, axis=2).transpose(1, 0)).reshape(
        group_count, row_count, experts_here
    )
    code_own = route_code
    gates_own = gate_table(second_input, code_own)

    back_ring = RingSum(back_block, row_count)

    def mixture_work(inner, pair):
        return (
            mm(inner, flat_down, 1, 0).astype(low_type),
            swap_all(reorder(pair, slot_of_device)),
        )

    mixture_part, pair_grad = window([back_ring], mixture_work, inner_all, pair_sent)
    mixture_ring = RingSum(slot_rows(mixture_part), row_count)

    def back_work(gback, uback):
        back_parts[0] = expert_back(gback, uback, gate_weight, up_weight, 0, chunks)
        return back_parts[0]

    back_parts[0] = window([back_ring, mixture_ring], back_work, gback_all, uback_all)

    def down_work(inner, pair):
        pair_grad = pair.transpose(1, 0, 2).reshape(row_count, expert_total)
        chosen_grad = gates_own * (
            pair_grad - jnp.sum(gates_own * pair_grad, axis=1, keepdims=True)
        )
        logits_grad = jnp.where(code_own > 0, chosen_grad, 0.0).astype(low_type)
        router_back = mm(logits_grad, full_router, 1, 1)
        router_part = mm(second_input, logits_grad, 0, 0)
        return grad_of(inner, cot_all), router_back, router_part

    down_part, router_back, router_part = window(
        [back_ring, mixture_ring], down_work, inner_all, pair_grad
    )
    gate_part = window(
        [back_ring, mixture_ring], lambda gback: grad_of(second_all, gback), gback_all
    )
    second_scattered = back_ring.total()
    second_grad = router_back + second_scattered
    upstream = valid_own * cotangent.astype(wide_type)
    def residual_work(second_grad):
        post_back, postnorm_part = norm_backward(
            residual, inverse_two, postnorm_gain, second_grad
        )
        residual_grad = upstream + post_back
        attention_low = residual_grad.astype(low_type)
        mixed_grad_own = jnp.zeros((row_count, model_width), wide_type)
        for j, piece in output_pieces.items():
            mixed_grad_own = mixed_grad_own + mm(
                lax.dynamic_slice_in_dim(
                    attention_low, (replica ^ j) * column_share, column_share, 1
                ),
                piece,
                1,
                1,
            )
        swap_sent = (
            mixed_grad_own.astype(low_type)
            .reshape(row_count, group_count, width_here)
            .transpose(1, 0, 2)
        )
        return swap_sent, residual_grad, attention_low, jnp.sum(postnorm_part, axis=0)

    swap_sent, residual_grad, attention_low, postnorm_part = window(
        [mixture_ring], residual_work, second_grad
    )
    class Swap(Exchange):
        def start(self):
            self.received = swap_all(self.sent)

    swap = Swap(swap_sent, 0)
    attention_gather = RingGather(attention_low)
    up_part = window(
        [swap, attention_gather],
        lambda uback: grad_of(second_all, uback),
        uback_all,
    )
    mixed_grad = swap.received

    sent, gain_parts = (), 0.0
    for head in range(heads_here):

        def head_work(grads, *earlier, head=head):
            return tuple(
                attention_back(
                    head,
                    heads[head][:4],
                    grads,
                    slot_order,
                    segment_column,
                    segment_line,
                    raw,
                    norm_gains,
                    (cosine, sine_part),
                    earlier,
                )
            )

        *sent, gain_part = window([attention_gather], head_work, mixed_grad, *sent)
        gain_parts = gain_parts + gain_part
    (sent,) = sent
    querynorm_part, keynorm_part = gain_parts[0], gain_parts[1]
    down_sum = lax.psum_scatter(
        down_part.reshape(experts_here, hidden_here, model_width),
        "rep",
        scatter_dimension=1,
        tiled=True,
    )
    sent, down_sum = tie(sent, down_sum)

    def first_work(sent, head):
        first_part = mm(sent, head_weight, 1, 1)
        token_wide = token_all.astype(wide_type)
        prenorm_part = jnp.sum(first_part * token_wide * inverse_all, axis=0)
        return first_part.astype(low_type), prenorm_part, rep_scatter(head, 1, scatter_order[:1])

    head_part = window([attention_gather], grad_of, first_all, sent)
    while attention_gather.step < group_count // 2:
        window([attention_gather], lambda: ())
    first_low, prenorm_part, head_part = window(
        [],
        first_work,
        sent,
        head_part.reshape(group_count, replica_count, share, 3 * width_here),
    )

    def small_swap(parts):
        return swap_all(
            jnp.concatenate([part.reshape(group_count, -1) for part in parts], axis=1)
        )

    def small_pieces(swapped, parts):
        total = rep_sum(jnp.sum(swapped, axis=0))
        pieces, start = [], 0
        for part in parts:
            size = part.size // group_count
            pieces.append(total[start : start + size])
            start += size
        return pieces

    first_ring = RingSum(slot_rows(first_low), row_count)
    small_parts = [router_part, postnorm_part, prenorm_part, querynorm_part, keynorm_part]
    head_part = rep_scatter(head_part, 1, scatter_order[1:])
    output_part = window(
        [first_ring],
        lambda mixed, *blocks: block_product(mixed, blocks),
        mixed_low,
        *attention_gather.blocks,
    )
    gate_sum = lax.psum_scatter(gate_part, "rep", scatter_dimension=0, tiled=True)
    up_sum = lax.psum_scatter(up_part, "rep", scatter_dimension=0, tiled=True)
    def split_experts(total):
        return jnp.stack(
            [
                total[:, e * hidden_here : (e + 1) * hidden_here].astype(wide_type)
                for e in range(experts_here)
            ]
        )

    (small_swapped, output_part, down_total), head_part = window(
        [first_ring],
        lambda output, down, *small: (
            small_swap(small),
            rep_scatter(output, 0, scatter_order[:1]),
            down.astype(wide_type),
        ),
        output_part.reshape(replica_count, share, model_width),
        down_sum,
        *small_parts,
        waits=(head_part,),
    )
    head_rows = swap_all(head_part.reshape(group_count, share, 3 * width_here))
    def layer_work(own, *sums):
        mixture = sum((part.astype(wide_type) for part in sums), own.astype(wide_type))
        return (valid_own * (residual + mixture)).astype(low_type)

    (output_part, small_sums, gate_total, layer_out), head_rows = window(
        [first_ring],
        lambda output, small, total, sums: (
            rep_scatter(output, 0, scatter_order[1:]),
            small_pieces(small, small_parts),
            split_experts(total),
            layer_work(*sums),
        ),
        output_part,
        small_swapped,
        gate_sum,
        (mixture_part[:row_count], *mixture_ring.sent),
        waits=(head_rows,),
    )
    head_rows = rep_gather(
        head_rows.reshape(group_count, share, heads_here, 3, head_dim)
        .transpose(3, 1, 0, 2, 4)
        .reshape(1, 3, share, model_width),
        gather_order[:-1],
    )
    output_rows, head_rows = window(
        [first_ring],
        lambda output: rep_gather(output, gather_order[:-1]),
        output_part,
        waits=(head_rows,),
    )
    head_rows = rep_gather(head_rows, gather_order[-1:])
    output_rows = rep_gather(output_rows, gather_order[-1:])
    first_grad = first_ring.total()
    query_grad, key_grad, value_grad = (
        head_rows[:, block].reshape(width_here, model_width).astype(wide_type)
        for block in range(3)
    )
    output_grad = output_rows.reshape(width_here, model_width).astype(wide_type)
    router_grad, postnorm_grad, prenorm_grad, querynorm_grad, keynorm_grad = small_sums
    router_grad = router_grad.reshape(width_here, expert_total)

    token_own = tokens.astype(wide_type)
    inverse_one = inverse_rms(token_own)
    pre_back, _ = norm_backward(token_own, inverse_one, prenorm_gain, first_grad)
    token_grad = residual_grad + pre_back

    up_total = split_experts(up_sum)
    return (
        layer_out,
        token_grad,
        query_grad,
        key_grad,
        value_grad,
        output_grad,
        router_grad,
        prenorm_grad,
        querynorm_grad,
        keynorm_grad,
        postnorm_grad,
        gate_total,
        up_total,
        down_total,
    )


def solution(mesh):
    in_specs = (
        P(("rep", "ep"), None),
        P(("rep", "ep"), None),
        P("rep", None),
        P("rep", None),
        P(("rep", "ep"), None),
        P(("rep", "ep"), None),
        P("ep", None),
        P("ep", None),
        P("ep", None),
        P("ep", None),
        P("ep", None),
        P(),
        P(),
        P(),
        P(),
        P("ep", None, None),
        P("ep", None, None),
        P("ep", None, None),
    )
    out_specs = (
        P(("rep", "ep"), None),
        P(("rep", "ep"), None),
        P("ep", None),
        P("ep", None),
        P("ep", None),
        P("ep", None),
        P("ep", None),
        P("ep"),
        P("ep"),
        P("ep"),
        P("ep"),
        P("ep", "rep", None),
        P("ep", "rep", None),
        P("ep", "rep", None),
    )
    return jax.shard_map(body, mesh=mesh, in_specs=in_specs, out_specs=out_specs, check_vma=False)
```

```python
import functools

import jax
import jax.numpy as jnp
from jax import lax
from jax.experimental import pallas as pl
from jax.experimental.pallas import tpu as pltpu
from jax.sharding import PartitionSpec as P

epsilon = 1e-05
rope_base = 10000.0
masked_value = -1e30
low_type = jnp.bfloat16
wide_type = jnp.float32


def inverse_rms(values):
    return lax.rsqrt(jnp.mean(values * values, axis=-1, keepdims=True) + epsilon)


def norm_backward(values, inverse, gain_vector, upstream):
    scaled = upstream * gain_vector
    inner_mean = jnp.mean(scaled * values, axis=-1, keepdims=True)
    result = inverse * scaled - values * (inverse * inverse * inverse) * inner_mean
    return (result, upstream * values * inverse)


def rope_tables(position, dimension):
    halfway = dimension // 2
    indices = jnp.arange(halfway, dtype=wide_type)
    frequency = rope_base ** (-2.0 * indices / dimension)
    angles = position.astype(wide_type)[:, None] * frequency[None, :]
    cosine = jnp.cos(angles)
    sine_part = jnp.sin(angles)
    return (
        jnp.concatenate([cosine, cosine], axis=-1),
        jnp.concatenate([sine_part, sine_part], axis=-1),
    )


def turn_half(values):
    halfway = values.shape[-1] // 2
    return jnp.concatenate([-values[..., halfway:], values[..., :halfway]], axis=-1)


def turn_back(values):
    halfway = values.shape[-1] // 2
    return jnp.concatenate([values[..., halfway:], -values[..., :halfway]], axis=-1)


def row_meta(lengths, group_order):
    boundary = jnp.cumsum(lengths)
    passed = (group_order[:, None] >= boundary[None, :]).astype(jnp.int32)
    segment = jnp.sum(passed, axis=1)
    offset = jnp.sum(passed * lengths[None, :], axis=1)
    return (segment, group_order - offset)


def mm(left, right, left_dim, right_dim):
    return lax.dot_general(
        left,
        right,
        (((left_dim,), (right_dim,)), ((), ())),
        preferred_element_type=wide_type,
    )


def gather_rows(values):
    return lax.all_gather(values, "ep", axis=0, tiled=True)


def ring_order(count):
    return [i for i in range(count) if i % 2 == 0] + [i for i in reversed(range(count)) if i % 2]


def ring_slots(count):
    half = count // 2
    offsets = [0]
    for step in range(1, half):
        offsets += [step, -step]
    return offsets + [half]


def ring_shift(values, direction):
    order = ring_order(lax.axis_size("ep"))
    count = len(order)
    pairs = [(order[i], order[(i + direction) % count]) for i in range(count)]
    return lax.ppermute(values, "ep", pairs)


def tie(*arrays):
    return lax.optimization_barrier(arrays)


def after(value, *others):
    return lax.optimization_barrier((value,) + others)[0]


class RingGather:
    def __init__(self, values):
        self.middle = values.shape[0] // 2
        self.half, self.step = lax.axis_size("ep") // 2, 0
        self.sent = (values, values)
        self.blocks = [values]

    def start(self):
        if self.step == self.half - 1:
            self.sent = (self.sent[0][: self.middle], self.sent[1][self.middle :])
        self.received = (ring_shift(self.sent[0], 1), ring_shift(self.sent[1], -1))

    def finish(self):
        self.step += 1
        onward, backward = self.sent = self.received
        if self.step < self.half:
            self.blocks += [backward, onward]
        else:
            self.blocks += [jnp.concatenate([onward, backward], axis=0)]


class Exchange:
    def __init__(self, values, distance):
        self.sent, self.distance = values, distance

    def start(self):
        self.received = rep_exchange(self.sent, self.distance)

    def finish(self):
        pass


class RingSum:
    def __init__(self, block, rows):
        count = lax.axis_size("ep")
        self.block, self.middle, self.step = block, rows // 2, 0
        self.half = count // 2
        self.slot = {offset: j for j, offset in enumerate(ring_slots(count))}
        far = block(self.slot[self.half])
        self.sent = (far[: self.middle], far[self.middle :])

    def start(self):
        self.received = (ring_shift(self.sent[0], 1), ring_shift(self.sent[1], -1))

    def finish(self):
        self.step += 1
        onward, backward = self.received
        left = self.half - self.step
        middle = self.middle
        if left:
            up, down = self.block(self.slot[left]), self.block(self.slot[-left])
            if self.step == 1:
                onward = jnp.concatenate([add_low(onward, up[:middle]), up[middle:]], axis=0)
                backward = jnp.concatenate(
                    [down[:middle], add_low(backward, down[middle:])], axis=0
                )
            else:
                onward, backward = add_low(onward, up), add_low(backward, down)
        self.sent = (onward, backward)

    def total(self):
        return (
            self.block(self.slot[0]).astype(wide_type)
            + self.sent[0].astype(wide_type)
            + self.sent[1].astype(wide_type)
        )


def window(rings, work, *inputs, waits=()):
    for ring in rings:
        ring.start()
    inputs, _ = tie(inputs, [ring.sent for ring in rings])
    received, waits, results = tie([ring.received for ring in rings], waits, work(*inputs))
    for ring, pair in zip(rings, received):
        ring.received = pair
        ring.finish()
    return (results, *waits) if waits else results


def add_low(left, right):
    return (left.astype(wide_type) + right.astype(wide_type)).astype(low_type)


def ring_place(member, count):
    return jnp.where(member % 2 == 0, member // 2, count - 1 - member // 2)


def ring_member(place, count):
    return jnp.where(place < count // 2, 2 * place, 2 * (count - 1 - place) + 1)


def ring_indices(device, count):
    place = ring_place(device, count)
    half = count // 2
    members = [ring_member((place + offset) % count, count) for offset in ring_slots(count)]
    slots = []
    for other in range(count):
        ahead = (ring_place(jnp.int32(other), count) - place) % count
        slot = jnp.where(ahead < half, 2 * ahead - 1, 2 * (count - ahead))
        slots.append(jnp.where(ahead == 0, 0, jnp.where(ahead == half, count - 1, slot)))
    return members, slots


def rep_exchange(values, distance):
    count = lax.axis_size("rep")
    return lax.ppermute(values, "rep", [(i, i ^ distance) for i in range(count)])


def rep_bit(distance):
    return (lax.axis_index("rep") // distance) % 2


def rep_distances():
    count, distance, distances = lax.axis_size("rep"), 1, []
    while distance < count:
        distances.append(distance)
        distance *= 2
    return distances


def rep_gather(gathered, distances):
    for distance in distances:
        shape = gathered.shape[1:]
        other = rep_exchange(gathered, distance)
        mine_first = jnp.stack([gathered, other], axis=1)
        other_first = jnp.stack([other, gathered], axis=1)
        gathered = jnp.where(rep_bit(distance) == 0, mine_first, other_first)
        gathered = gathered.reshape((-1,) + shape)
    return gathered


def rep_scatter(values, axis, distances):
    for distance in distances:
        shape = values.shape
        pairs = values.reshape(shape[:axis] + (shape[axis] // 2, 2) + shape[axis + 1 :])
        bit = rep_bit(distance)
        keep = lax.dynamic_index_in_dim(pairs, bit, axis + 1, keepdims=False)
        send = lax.dynamic_index_in_dim(pairs, 1 - bit, axis + 1, keepdims=False)
        values = add_low(keep, rep_exchange(send, distance))
    return values


def rep_sum(values):
    distance = 1
    while distance < lax.axis_size("rep"):
        values = values + rep_exchange(values, distance)
        distance *= 2
    return values


def swap_all(values):
    return lax.all_to_all(values, "ep", split_axis=0, concat_axis=0, tiled=True)


def expert_kernel(rows_ref, gate_ref, up_ref, stream_ref, gates_ref, *refs):
    inner_ref, gback_ref, uback_ref, pair_ref = refs[-4:]
    expert, step = pl.program_id(0), pl.program_id(1)
    rows = rows_ref[...]
    gate_linear = jnp.dot(rows, gate_ref[0], preferred_element_type=wide_type)
    up_linear = jnp.dot(rows, up_ref[0], preferred_element_type=wide_type)
    stream = stream_ref[...]
    column = gates_ref[:, 0:1]
    for other in range(1, gates_ref.shape[1]):
        column = jnp.where(expert == other, gates_ref[:, other : other + 1], column)
    sigmoid_gate = jax.nn.sigmoid(gate_linear)
    silu_gate = gate_linear * sigmoid_gate
    inner = silu_gate * up_linear
    inner_ref[...] = (column * inner).astype(low_type)
    hidden_grad = column * stream
    gback_ref[...] = (
        hidden_grad * up_linear * sigmoid_gate * (1.0 + gate_linear * (1.0 - sigmoid_gate))
    ).astype(low_type)
    uback_ref[...] = (hidden_grad * silu_gate).astype(low_type)
    product = inner * stream
    lanes = pair_ref.shape[2]
    folded = product[:, :lanes]
    for start in range(lanes, product.shape[1], lanes):
        folded = folded + product[:, start : start + lanes]

    @pl.when(step == 0)
    def _():
        pair_ref[0] = folded

    @pl.when(step > 0)
    def _():
        pair_ref[0] += folded


def expert_pass(rows, gate_weight, up_weight, stream, gates, chunk, chunks, earlier=()):
    count, depth = rows.shape
    experts, _, hidden = gate_weight.shape
    width = 256
    steps = hidden // width
    weight = pl.BlockSpec((1, depth, width), lambda e, j: (e, 0, j))
    out = pl.BlockSpec((count, width), lambda e, j: (chunk, e * steps + j))
    return pl.pallas_call(
        expert_kernel,
        grid=(experts, steps),
        in_specs=[
            pl.BlockSpec((count, depth), lambda e, j: (0, 0)),
            weight,
            weight,
            pl.BlockSpec((count, width), lambda e, j: (0, e * steps + j)),
            pl.BlockSpec(gates.shape, lambda e, j: (0, 0)),
        ]
        + [pl.BlockSpec(memory_space=pl.ANY)] * len(earlier),
        out_specs=[out, out, out, pl.BlockSpec((1, count, 128), lambda e, j: (e, 0, 0))],
        out_shape=[jax.ShapeDtypeStruct((count * chunks, experts * hidden), low_type)] * 3
        + [jax.ShapeDtypeStruct((experts, count, 128), wide_type)],
        input_output_aliases={5 + i: i for i in range(len(earlier))},
        compiler_params=pltpu.CompilerParams(vmem_limit_bytes=56 << 20),
        cost_estimate=pl.CostEstimate(
            flops=4 * count * depth * experts * hidden,
            bytes_accessed=4 * depth * experts * hidden + 20 * count * depth,
            transcendentals=count * experts * hidden,
        ),
    )(rows, gate_weight, up_weight, stream, gates, *earlier)


def expert_back_kernel(gback_ref, uback_ref, gate_ref, up_ref, out_ref):
    experts, _, hidden = gate_ref.shape
    total = None
    for e in range(experts):
        for grad_ref, weight_ref in ((gback_ref, gate_ref), (uback_ref, up_ref)):
            term = mm(grad_ref[:, e * hidden : (e + 1) * hidden], weight_ref[e], 1, 1)
            total = term if total is None else total + term
    out_ref[...] = total.astype(low_type)


def expert_back(gback, uback, gate_weight, up_weight, chunk, chunks):
    count = gback.shape[0] // chunks
    experts, depth, hidden = gate_weight.shape
    width = 256
    whole = pl.BlockSpec((count, experts * hidden), lambda j: (chunk, 0))
    weight = pl.BlockSpec((experts, width, hidden), lambda j: (0, j, 0))
    return pl.pallas_call(
        expert_back_kernel,
        grid=(depth // width,),
        in_specs=[whole, whole, weight, weight],
        out_specs=pl.BlockSpec((count, width), lambda j: (0, j)),
        out_shape=jax.ShapeDtypeStruct((count, depth), low_type),
        compiler_params=pltpu.CompilerParams(vmem_limit_bytes=56 << 20),
        cost_estimate=pl.CostEstimate(
            flops=4 * count * depth * experts * hidden,
            bytes_accessed=4 * depth * experts * hidden + 6 * count * depth,
            transcendentals=0,
        ),
    )(gback, uback, gate_weight, up_weight)


def attention_back_kernel(
    block,
    scale,
    order_ref,
    query_ref,
    key_ref,
    value_ref,
    swapped_ref,
    total_ref,
    column_ref,
    line_ref,
    query_raw_ref,
    key_raw_ref,
    gains_ref,
    cosine_ref,
    sine_ref,
    *refs,
):
    sent_ref, part_ref, key_sum, value_sum, grad_ref = refs[-5:]
    rows, depth = query_ref.shape
    lane = lax.broadcasted_iota(jnp.int32, (1, depth), 1)
    sign = jnp.where(lane < depth // 2, 1.0, -1.0)
    share = swapped_ref.shape[1]
    for slot in range(swapped_ref.shape[0]):
        grad_ref[slot * share : (slot + 1) * share, :] = swapped_ref[order_ref[slot]]
    key_sum[...] = jnp.zeros_like(key_sum)
    value_sum[...] = jnp.zeros_like(value_sum)
    part_ref[...] = jnp.zeros_like(part_ref)

    def finish(back, raw, row, which):
        turned = back * cosine_ref[row, :]
        turned += pltpu.roll(back * sine_ref[row, :], depth // 2, axis=1) * sign
        inverse = inverse_rms(raw)
        result, part = norm_backward(raw, inverse, gains_ref[which : which + 1, :], turned)
        sent_ref[row, which * depth : (which + 1) * depth] = result.astype(low_type)
        part_ref[which : which + 1, :] += jnp.sum(part, axis=0, keepdims=True)

    @pl.loop(0, rows // block)
    def _(step):
        row = pl.ds(pl.multiple_of(step * block, block), block)
        query, grad = query_ref[row, :], grad_ref[row, :]
        scores = mm(query, key_ref[...], 1, 1) * scale
        scores = jnp.where(column_ref[row, :] == line_ref[...], scores, masked_value)
        weights = jnp.exp(scores - total_ref[row, :])
        weight_grad = mm(grad, value_ref[...], 1, 1)
        row_dot = jnp.sum(weights * weight_grad, axis=-1, keepdims=True)
        score_grad = (weights * (weight_grad - row_dot)).astype(low_type)
        key_sum[...] += mm(score_grad, query, 0, 0)
        value_sum[...] += mm(weights.astype(low_type), grad, 0, 0)
        finish(mm(score_grad, key_ref[...], 1, 0) * scale, query_raw_ref[row, :], row, 0)

    @pl.loop(0, rows // block)
    def _(step):
        row = pl.ds(pl.multiple_of(step * block, block), block)
        finish(key_sum[row, :] * scale, key_raw_ref[row, :], row, 1)
        sent_ref[row, 2 * depth : 3 * depth] = value_sum[row, :].astype(low_type)


def attention_back(head, kept, swapped, order, column, line, raw, gains, tables, earlier=()):
    rows, depth = kept[0].shape
    block = 256 if rows % 256 == 0 else rows

    def whole(array):
        return pl.BlockSpec(array.shape, lambda i, order: (0,) * array.ndim)

    def columns(index):
        return pl.BlockSpec((rows, depth), lambda i, order: (0, index))

    operands = (*kept[:3], swapped, kept[3], column, line, raw, raw, gains, *tables)
    specs = [whole(operand) for operand in operands]
    specs[3] = pl.BlockSpec(swapped.shape[:2] + (depth,), lambda i, order: (0, 0, head))
    specs[7], specs[8] = columns(3 * head), columns(3 * head + 1)
    return pl.pallas_call(
        functools.partial(attention_back_kernel, block, depth**-0.5),
        grid_spec=pltpu.PrefetchScalarGridSpec(
            num_scalar_prefetch=1,
            grid=(1,),
            in_specs=specs + [pl.BlockSpec(memory_space=pl.ANY)] * len(earlier),
            out_specs=[
                pl.BlockSpec((rows, 3 * depth), lambda i, order: (0, head)),
                pl.BlockSpec((2, depth), lambda i, order: (0, 0)),
            ],
            scratch_shapes=[pltpu.VMEM((rows, depth), wide_type)] * 2
            + [pltpu.VMEM((rows, depth), low_type)],
        ),
        out_shape=[
            jax.ShapeDtypeStruct(raw.shape, low_type),
            jax.ShapeDtypeStruct((2, depth), wide_type),
        ],
        input_output_aliases={1 + len(operands) + i: i for i in range(len(earlier))},
        compiler_params=pltpu.CompilerParams(vmem_limit_bytes=56 << 20),
        cost_estimate=pl.CostEstimate(
            flops=10 * rows * rows * depth,
            bytes_accessed=30 * rows * depth,
            transcendentals=rows * rows,
        ),
    )(order, *operands, *earlier)


def block_product_kernel(left_ref, *refs):
    out_ref = refs[-1]
    rows = refs[0].shape[0]
    total = None
    for j, ref in enumerate(refs[:-1]):
        term = mm(left_ref[j * rows : (j + 1) * rows, :], ref[...], 0, 0)
        total = term if total is None else total + term
    out_ref[...] = total.astype(low_type)


def block_product(left, blocks):
    rows, width = blocks[0].shape
    tile = 512
    return pl.pallas_call(
        block_product_kernel,
        grid=(width // tile,),
        in_specs=[pl.BlockSpec(left.shape, lambda j: (0, 0))] + [pl.BlockSpec((rows, tile), lambda j: (0, j))] * len(blocks),
        out_specs=pl.BlockSpec((left.shape[1], tile), lambda j: (0, j)),
        out_shape=jax.ShapeDtypeStruct((left.shape[1], width), low_type),
        cost_estimate=pl.CostEstimate(flops=2 * left.size * width, bytes_accessed=2 * left.size + 2 * len(blocks) * rows * width, transcendentals=0),
    )(left, *blocks)


def body(
    tokens,
    cotangent,
    seq_lengths,
    token_order,
    routes,
    slot_index,
    query_weight,
    key_weight,
    value_weight,
    output_weight,
    router_weight,
    prenorm_gain,
    querynorm_gain,
    keynorm_gain,
    postnorm_gain,
    gate_weight,
    up_weight,
    down_weight,
):
    group_count = lax.axis_size("ep")
    device = lax.axis_index("ep")
    row_count, model_width = tokens.shape
    head_dim = querynorm_gain.shape[0]
    width_here = model_width // group_count
    heads_here = width_here // head_dim
    experts_here = gate_weight.shape[0]
    expert_total = experts_here * group_count
    top_count = routes.shape[1]
    capacity = row_count * top_count * 5 // (4 * expert_total)
    group_rows = row_count * group_count
    sequence_count = seq_lengths.shape[1]
    score_scale = head_dim ** (-0.5)

    replica_count = lax.axis_size("rep")
    replica = lax.axis_index("rep")
    share = width_here // replica_count

    device_of_slot, slot_of_device = ring_indices(device, group_count)

    def reorder(blocks, index):
        return jnp.concatenate(
            [lax.dynamic_slice_in_dim(blocks, index[i], 1, 0) for i in range(group_count)], axis=0
        )

    group_order = reorder(token_order[0].reshape(group_count, row_count), device_of_slot)
    segment, position = row_meta(seq_lengths[0], group_order.reshape(group_rows))
    segment_own = segment[:row_count]
    valid_own = (segment_own < sequence_count).astype(wide_type)[:, None]
    valid_all = (segment < sequence_count).astype(wide_type)[:, None]

    expert_ids = jnp.arange(expert_total, dtype=jnp.int32)
    route_code = jnp.zeros((row_count, expert_total), jnp.int32)
    for column in range(top_count):
        hit = routes[:, column, None] == expert_ids[None, :]
        kept = (slot_index[:, column, None] < capacity).astype(jnp.int32)
        route_code = route_code + jnp.where(hit, 1 + kept, 0)
    small_sent = jnp.concatenate([route_code.astype(low_type), router_weight], axis=0)

    projections = (
        jnp.stack(
            [
                lax.dynamic_slice_in_dim(piece, replica * share, share, 0).reshape(
                    share, group_count, heads_here, head_dim
                )
                for piece in (query_weight, key_weight, value_weight)
            ],
            axis=3,
        )
        .reshape(share, group_count, 3 * width_here)
        .transpose(1, 0, 2)
    )
    scatter_order = rep_distances()
    gather_order = scatter_order[::-1]
    swapped = swap_all(projections)
    head_weight = (
        rep_gather(swapped[None], gather_order)
        .transpose(1, 0, 2, 3)
        .reshape(model_width, 3 * width_here)
    )
    output_late = after(output_weight, swapped)
    token_ring = RingGather(tokens)
    token_ring.start()
    chunks = 2
    chunk_rows = group_rows // chunks
    blocks_here = group_count // chunks

    def chunk_of(array, chunk):
        return array[chunk * chunk_rows : (chunk + 1) * chunk_rows]

    def slot_rows(array):
        return lambda slot: array[slot * row_count : (slot + 1) * row_count]

    def reorder_rows(rows, index):
        return reorder(
            rows.reshape(group_count, row_count, rows.shape[1]), index
        ).reshape(rows.shape)

    column_share = model_width // replica_count
    output_share = gather_rows(
        lax.dynamic_slice_in_dim(output_late, replica * column_share, column_share, 1)
    )
    token_ring.finish()
    for step in range(1, group_count // 2):
        if step == group_count // 2 - 1:
            token_ring.sent = (after(token_ring.sent[0], output_share), token_ring.sent[1])
        token_ring.start()
        token_ring.finish()
    cosine, sine_part = rope_tables(after(position, token_ring.blocks[1]), head_dim)

    hidden_here = down_weight.shape[1]
    flat_down = down_weight.reshape(experts_here * hidden_here, model_width)

    allowed = segment[:, None] == segment[None, :]
    far = replica_count // 2
    steps = group_count // 2
    part_rows = model_width // steps
    far_parts = [
        Exchange(output_share[i * part_rows : (i + 1) * part_rows], far) for i in range(steps)
    ]

    def head_columns(values, block, head):
        start = (3 * head + block) * head_dim
        return values[:, start : start + head_dim]

    def project(weight, *blocks):
        token_all = jnp.concatenate(blocks, axis=0)
        token_wide = token_all.astype(wide_type)
        first_all = (token_wide * inverse_rms(token_wide) * prenorm_gain).astype(low_type)
        return token_all, first_all, mm(first_all, weight, 1, 0)

    def attend(head, raw):
        turned = []
        for block, gain in ((0, querynorm_gain), (1, keynorm_gain)):
            part = head_columns(raw, block, head)
            normed = part * inverse_rms(part) * gain
            turned.append((normed * cosine + turn_half(normed) * sine_part).astype(low_type))
        value_low = head_columns(raw, 2, head).astype(low_type)
        scores = jnp.where(allowed, mm(*turned, 1, 1) * score_scale, masked_value)
        top_score = jnp.max(scores, axis=-1, keepdims=True)
        powers = jnp.exp(scores - top_score)
        log_total = top_score + jnp.log(jnp.sum(powers, axis=-1, keepdims=True))
        weights_low = jnp.exp(scores - log_total).astype(low_type)
        return (*turned, value_low, log_total, mm(weights_low, value_low, 1, 0).astype(low_type))

    cot_ring = RingGather(after(cotangent, token_ring.received))
    token_all, first_all, raw = window(
        [cot_ring, far_parts[0]], project, head_weight, *token_ring.blocks
    )
    heads = []
    for head in range(heads_here):
        heads.append(
            window(
                [cot_ring, far_parts[1 + head]],
                lambda raw, head=head: attend(head, raw),
                raw,
            )
        )

    def order_work(small, *mixed):
        mixed_low = jnp.concatenate(mixed, axis=1)
        return (
            mixed_low,
            reorder_rows(mixed_low, slot_of_device),
            segment[:, None],
            segment[None, :],
            jnp.stack([querynorm_gain, keynorm_gain]),
            jnp.stack(device_of_slot),
            swap_all(jnp.broadcast_to(small[None], (group_count,) + small.shape)),
        )

    (
        mixed_low,
        mixed_ordered,
        segment_column,
        segment_line,
        norm_gains,
        slot_order,
        small_all,
    ) = window(
        [cot_ring, *far_parts[1 + heads_here :]],
        order_work,
        small_sent.reshape(-1, head_dim),
        *[head[4] for head in heads],
    )
    small_all = small_all.reshape(group_count, row_count + width_here, expert_total)
    code_all = reorder(small_all[:, :row_count], device_of_slot).reshape(
        group_rows, expert_total
    )
    full_router = small_all[:, row_count:].reshape(model_width, expert_total)
    cot_all = jnp.concatenate(cot_ring.blocks, axis=0)
    output_pieces = {
        0: output_share,
        far: jnp.concatenate([part.received for part in far_parts], axis=0),
    }
    for distance in gather_order[1:]:
        for j in list(output_pieces):
            output_pieces[j ^ distance] = rep_exchange(output_pieces[j], distance)
    mixed_own = (
        swap_all(mixed_ordered.reshape(group_count, row_count, width_here))
        .transpose(1, 0, 2)
        .reshape(row_count, model_width)
    )
    attention = jnp.zeros((row_count, model_width), wide_type)
    for j, piece in output_pieces.items():
        attention = lax.dynamic_update_slice_in_dim(
            attention, mm(mixed_own, piece, 1, 0), (replica ^ j) * column_share, 1
        )
    residual = tokens.astype(wide_type) + attention
    inverse_two = inverse_rms(residual)
    second_input = (residual * inverse_two * postnorm_gain).astype(low_type)

    def gate_table(rows, code):
        logits = mm(rows, full_router, 1, 0)
        shifted = jnp.where(code > 0, logits, masked_value)
        powers = jnp.exp(shifted - jnp.max(shifted, axis=1, keepdims=True))
        return powers / jnp.sum(powers, axis=1, keepdims=True)

    kept_all = jnp.where(code_all > 1, valid_all, 0.0)
    kept_here = lax.dynamic_slice_in_dim(kept_all, device * experts_here, experts_here, 1)

    def stream_of(cot_part):
        return mm(cot_part, flat_down, 1, 1)

    def expert_chunk(chunk, rows, stream, *earlier):
        gates = gate_table(rows, chunk_of(code_all, chunk)) * chunk_of(kept_all, chunk)
        gates_here = lax.dynamic_slice_in_dim(gates, device * experts_here, experts_here, 1)
        return expert_pass(
            rows, gate_weight, up_weight, stream, gates_here, chunk, chunks, earlier
        )

    second_ring = RingGather(second_input)
    stream_first = window([second_ring], lambda part: stream_of(part), chunk_of(cot_all, 0))
    stream_last = window([second_ring], lambda part: stream_of(part), chunk_of(cot_all, 1))
    rows_first = jnp.concatenate(second_ring.blocks[:blocks_here], axis=0)
    *earlier, pair_first = window(
        [second_ring],
        lambda rows, stream: expert_chunk(0, rows, stream),
        rows_first,
        stream_first,
    )
    window([second_ring], lambda: ())
    rows_last = jnp.concatenate(second_ring.blocks[blocks_here:], axis=0)
    inner_all, gback_all, uback_all, pair_last = expert_chunk(
        1, rows_last, stream_last, *earlier
    )
    second_all = jnp.concatenate([rows_first, rows_last], axis=0)
    back_last = expert_back(gback_all, uback_all, gate_weight, up_weight, 1, chunks)
    back_parts = {1: back_last}

    def back_block(slot):
        start = (slot % blocks_here) * row_count
        return back_parts[slot // blocks_here][start : start + row_count]

    def grad_of(left, right):
        return mm(left, right, 0, 0).astype(low_type)

    pair_lanes = jnp.concatenate([pair_first, pair_last], axis=1)
    pair_sent = (kept_here * jnp.sum(pair_lanes, axis=2).transpose(1, 0)).reshape(
        group_count, row_count, experts_here
    )
    code_own = route_code
    gates_own = gate_table(second_input, code_own)

    back_ring = RingSum(back_block, row_count)

    def mixture_work(inner, pair):
        return (
            mm(inner, flat_down, 1, 0).astype(low_type),
            swap_all(reorder(pair, slot_of_device)),
        )

    mixture_part, pair_grad = window([back_ring], mixture_work, inner_all, pair_sent)
    mixture_ring = RingSum(slot_rows(mixture_part), row_count)

    def back_work(gback, uback):
        back_parts[0] = expert_back(gback, uback, gate_weight, up_weight, 0, chunks)
        return back_parts[0]

    back_parts[0] = window([back_ring, mixture_ring], back_work, gback_all, uback_all)

    def down_work(inner, pair):
        pair_grad = pair.transpose(1, 0, 2).reshape(row_count, expert_total)
        chosen_grad = gates_own * (
            pair_grad - jnp.sum(gates_own * pair_grad, axis=1, keepdims=True)
        )
        logits_grad = jnp.where(code_own > 0, chosen_grad, 0.0).astype(low_type)
        router_back = mm(logits_grad, full_router, 1, 1)
        router_part = mm(second_input, logits_grad, 0, 0)
        return grad_of(inner, cot_all), router_back, router_part

    down_part, router_back, router_part = window(
        [back_ring, mixture_ring], down_work, inner_all, pair_grad
    )
    gate_part = window(
        [back_ring, mixture_ring], lambda gback: grad_of(second_all, gback), gback_all
    )
    second_scattered = back_ring.total()
    second_grad = router_back + second_scattered
    upstream = valid_own * cotangent.astype(wide_type)
    def residual_work(second_grad):
        post_back, postnorm_part = norm_backward(
            residual, inverse_two, postnorm_gain, second_grad
        )
        residual_grad = upstream + post_back
        attention_low = residual_grad.astype(low_type)
        mixed_grad_own = jnp.zeros((row_count, model_width), wide_type)
        for j, piece in output_pieces.items():
            mixed_grad_own = mixed_grad_own + mm(
                lax.dynamic_slice_in_dim(
                    attention_low, (replica ^ j) * column_share, column_share, 1
                ),
                piece,
                1,
                1,
            )
        swap_sent = (
            mixed_grad_own.astype(low_type)
            .reshape(row_count, group_count, width_here)
            .transpose(1, 0, 2)
        )
        return swap_sent, residual_grad, attention_low, jnp.sum(postnorm_part, axis=0)

    swap_sent, residual_grad, attention_low, postnorm_part = window(
        [mixture_ring], residual_work, second_grad
    )
    class Swap(Exchange):
        def start(self):
            self.received = swap_all(self.sent)

    swap = Swap(swap_sent, 0)
    attention_gather = RingGather(attention_low)
    up_part = window(
        [swap, attention_gather],
        lambda uback: grad_of(second_all, uback),
        uback_all,
    )
    mixed_grad = swap.received

    sent, gain_parts = (), 0.0
    for head in range(heads_here):

        def head_work(grads, *earlier, head=head):
            return tuple(
                attention_back(
                    head,
                    heads[head][:4],
                    grads,
                    slot_order,
                    segment_column,
                    segment_line,
                    raw,
                    norm_gains,
                    (cosine, sine_part),
                    earlier,
                )
            )

        *sent, gain_part = window([attention_gather], head_work, mixed_grad, *sent)
        gain_parts = gain_parts + gain_part
    (sent,) = sent
    querynorm_part, keynorm_part = gain_parts[0], gain_parts[1]
    down_sum = lax.psum_scatter(
        down_part.reshape(experts_here, hidden_here, model_width),
        "rep",
        scatter_dimension=1,
        tiled=True,
    )
    sent, down_sum = tie(sent, down_sum)

    def first_work(sent, head):
        first_part = mm(sent, head_weight, 1, 1)
        token_wide = token_all.astype(wide_type)
        prenorm_part = jnp.sum(first_part * token_wide * inverse_rms(token_wide), axis=0)
        return first_part.astype(low_type), prenorm_part, rep_scatter(head, 1, scatter_order[:1])

    head_part = window([attention_gather], grad_of, first_all, sent)
    while attention_gather.step < group_count // 2:
        window([attention_gather], lambda: ())
    first_low, prenorm_part, head_part = window(
        [],
        first_work,
        sent,
        head_part.reshape(group_count, replica_count, share, 3 * width_here),
    )

    def small_swap(parts):
        return swap_all(
            jnp.concatenate([part.reshape(group_count, -1) for part in parts], axis=1)
        )

    def small_pieces(swapped, parts):
        total = rep_sum(jnp.sum(swapped, axis=0))
        pieces, start = [], 0
        for part in parts:
            size = part.size // group_count
            pieces.append(total[start : start + size])
            start += size
        return pieces

    first_ring = RingSum(slot_rows(first_low), row_count)
    small_parts = [router_part, postnorm_part, prenorm_part, querynorm_part, keynorm_part]
    head_part = rep_scatter(head_part, 1, scatter_order[1:])
    output_part = window(
        [first_ring],
        lambda mixed, *blocks: block_product(mixed, blocks),
        mixed_low,
        *attention_gather.blocks,
    )
    gate_sum = lax.psum_scatter(gate_part, "rep", scatter_dimension=0, tiled=True)
    up_sum = lax.psum_scatter(up_part, "rep", scatter_dimension=0, tiled=True)
    def split_experts(total):
        return jnp.stack(
            [
                total[:, e * hidden_here : (e + 1) * hidden_here].astype(wide_type)
                for e in range(experts_here)
            ]
        )

    (small_swapped, output_part, down_total), head_part = window(
        [first_ring],
        lambda output, down, *small: (
            small_swap(small),
            rep_scatter(output, 0, scatter_order[:1]),
            down.astype(wide_type),
        ),
        output_part.reshape(replica_count, share, model_width),
        down_sum,
        *small_parts,
        waits=(head_part,),
    )
    head_rows = swap_all(head_part.reshape(group_count, share, 3 * width_here))
    def layer_work(own, *sums):
        mixture = sum((part.astype(wide_type) for part in sums), own.astype(wide_type))
        return (valid_own * (residual + mixture)).astype(low_type)

    (output_part, small_sums, gate_total, layer_out), head_rows = window(
        [first_ring],
        lambda output, small, total, sums: (
            rep_scatter(output, 0, scatter_order[1:]),
            small_pieces(small, small_parts),
            split_experts(total),
            layer_work(*sums),
        ),
        output_part,
        small_swapped,
        gate_sum,
        (mixture_part[:row_count], *mixture_ring.sent),
        waits=(head_rows,),
    )
    head_rows = rep_gather(
        head_rows.reshape(group_count, share, heads_here, 3, head_dim)
        .transpose(3, 1, 0, 2, 4)
        .reshape(1, 3, share, model_width),
        gather_order[:-1],
    )
    output_rows, head_rows = window(
        [first_ring],
        lambda output: rep_gather(output, gather_order[:-1]),
        output_part,
        waits=(head_rows,),
    )
    head_rows = rep_gather(head_rows, gather_order[-1:])
    output_rows = rep_gather(output_rows, gather_order[-1:])
    first_grad = first_ring.total()
    query_grad, key_grad, value_grad = (
        head_rows[:, block].reshape(width_here, model_width).astype(wide_type)
        for block in range(3)
    )
    output_grad = output_rows.reshape(width_here, model_width).astype(wide_type)
    router_grad, postnorm_grad, prenorm_grad, querynorm_grad, keynorm_grad = small_sums
    router_grad = router_grad.reshape(width_here, expert_total)

    token_own = tokens.astype(wide_type)
    inverse_one = inverse_rms(token_own)
    pre_back, _ = norm_backward(token_own, inverse_one, prenorm_gain, first_grad)
    token_grad = residual_grad + pre_back

    up_total = split_experts(up_sum)
    return (
        layer_out,
        token_grad,
        query_grad,
        key_grad,
        value_grad,
        output_grad,
        router_grad,
        prenorm_grad,
        querynorm_grad,
        keynorm_grad,
        postnorm_grad,
        gate_total,
        up_total,
        down_total,
    )


def solution(mesh):
    in_specs = (
        P(("rep", "ep"), None),
        P(("rep", "ep"), None),
        P("rep", None),
        P("rep", None),
        P(("rep", "ep"), None),
        P(("rep", "ep"), None),
        P("ep", None),
        P("ep", None),
        P("ep", None),
        P("ep", None),
        P("ep", None),
        P(),
        P(),
        P(),
        P(),
        P("ep", None, None),
        P("ep", None, None),
        P("ep", None, None),
    )
    out_specs = (
        P(("rep", "ep"), None),
        P(("rep", "ep"), None),
        P("ep", None),
        P("ep", None),
        P("ep", None),
        P("ep", None),
        P("ep", None),
        P("ep"),
        P("ep"),
        P("ep"),
        P("ep"),
        P("ep", "rep", None),
        P("ep", "rep", None),
        P("ep", "rep", None),
    )
    return jax.shard_map(body, mesh=mesh, in_specs=in_specs, out_specs=out_specs, check_vma=False)
```

```python
import functools

import jax
import jax.numpy as jnp
from jax import lax
from jax.experimental import pallas as pl
from jax.experimental.pallas import tpu as pltpu
from jax.sharding import PartitionSpec as P

epsilon = 1e-05
rope_base = 10000.0
masked_value = -1e30
low_type = jnp.bfloat16
wide_type = jnp.float32


def inverse_rms(values):
    return lax.rsqrt(jnp.mean(values * values, axis=-1, keepdims=True) + epsilon)


def norm_backward(values, inverse, gain_vector, upstream):
    scaled = upstream * gain_vector
    inner_mean = jnp.mean(scaled * values, axis=-1, keepdims=True)
    result = inverse * scaled - values * (inverse * inverse * inverse) * inner_mean
    return (result, upstream * values * inverse)


def rope_tables(position, dimension):
    halfway = dimension // 2
    indices = jnp.arange(halfway, dtype=wide_type)
    frequency = rope_base ** (-2.0 * indices / dimension)
    angles = position.astype(wide_type)[:, None] * frequency[None, :]
    cosine = jnp.cos(angles)
    sine_part = jnp.sin(angles)
    return (
        jnp.concatenate([cosine, cosine], axis=-1),
        jnp.concatenate([sine_part, sine_part], axis=-1),
    )


def turn_half(values):
    halfway = values.shape[-1] // 2
    return jnp.concatenate([-values[..., halfway:], values[..., :halfway]], axis=-1)


def turn_back(values):
    halfway = values.shape[-1] // 2
    return jnp.concatenate([values[..., halfway:], -values[..., :halfway]], axis=-1)


def row_meta(lengths, group_order):
    boundary = jnp.cumsum(lengths)
    passed = (group_order[:, None] >= boundary[None, :]).astype(jnp.int32)
    segment = jnp.sum(passed, axis=1)
    offset = jnp.sum(passed * lengths[None, :], axis=1)
    return (segment, group_order - offset)


def mm(left, right, left_dim, right_dim):
    return lax.dot_general(
        left,
        right,
        (((left_dim,), (right_dim,)), ((), ())),
        preferred_element_type=wide_type,
    )


def gather_rows(values):
    return lax.all_gather(values, "ep", axis=0, tiled=True)


def ring_order(count):
    return [i for i in range(count) if i % 2 == 0] + [i for i in reversed(range(count)) if i % 2]


def ring_slots(count):
    half = count // 2
    offsets = [0]
    for step in range(1, half):
        offsets += [step, -step]
    return offsets + [half]


def ring_shift(values, direction):
    order = ring_order(lax.axis_size("ep"))
    count = len(order)
    pairs = [(order[i], order[(i + direction) % count]) for i in range(count)]
    return lax.ppermute(values, "ep", pairs)


def tie(*arrays):
    return lax.optimization_barrier(arrays)


def after(value, *others):
    return lax.optimization_barrier((value,) + others)[0]


class RingGather:
    def __init__(self, values):
        self.middle = values.shape[0] // 2
        self.half, self.step = lax.axis_size("ep") // 2, 0
        self.sent = (values, values)
        self.blocks = [values]

    def start(self):
        if self.step == self.half - 1:
            self.sent = (self.sent[0][: self.middle], self.sent[1][self.middle :])
        self.received = (ring_shift(self.sent[0], 1), ring_shift(self.sent[1], -1))

    def finish(self):
        self.step += 1
        onward, backward = self.sent = self.received
        if self.step < self.half:
            self.blocks += [backward, onward]
        else:
            self.blocks += [jnp.concatenate([onward, backward], axis=0)]


class Exchange:
    def __init__(self, values, distance):
        self.sent, self.distance = values, distance

    def start(self):
        self.received = rep_exchange(self.sent, self.distance)

    def finish(self):
        pass


class RingSum:
    def __init__(self, block, rows):
        count = lax.axis_size("ep")
        self.block, self.middle, self.step = block, rows // 2, 0
        self.half = count // 2
        self.slot = {offset: j for j, offset in enumerate(ring_slots(count))}
        far = block(self.slot[self.half])
        self.sent = (far[: self.middle], far[self.middle :])

    def start(self):
        self.received = (ring_shift(self.sent[0], 1), ring_shift(self.sent[1], -1))

    def finish(self):
        self.step += 1
        onward, backward = self.received
        left = self.half - self.step
        middle = self.middle
        if left:
            up, down = self.block(self.slot[left]), self.block(self.slot[-left])
            if self.step == 1:
                onward = jnp.concatenate([add_low(onward, up[:middle]), up[middle:]], axis=0)
                backward = jnp.concatenate(
                    [down[:middle], add_low(backward, down[middle:])], axis=0
                )
            else:
                onward, backward = add_low(onward, up), add_low(backward, down)
        self.sent = (onward, backward)

    def total(self):
        return (
            self.block(self.slot[0]).astype(wide_type)
            + self.sent[0].astype(wide_type)
            + self.sent[1].astype(wide_type)
        )


def window(rings, work, *inputs, waits=()):
    for ring in rings:
        ring.start()
    inputs, _ = tie(inputs, [ring.sent for ring in rings])
    received, waits, results = tie([ring.received for ring in rings], waits, work(*inputs))
    for ring, pair in zip(rings, received):
        ring.received = pair
        ring.finish()
    return (results, *waits) if waits else results


def add_low(left, right):
    return (left.astype(wide_type) + right.astype(wide_type)).astype(low_type)


def ring_place(member, count):
    return jnp.where(member % 2 == 0, member // 2, count - 1 - member // 2)


def ring_member(place, count):
    return jnp.where(place < count // 2, 2 * place, 2 * (count - 1 - place) + 1)


def ring_indices(device, count):
    place = ring_place(device, count)
    half = count // 2
    members = [ring_member((place + offset) % count, count) for offset in ring_slots(count)]
    slots = []
    for other in range(count):
        ahead = (ring_place(jnp.int32(other), count) - place) % count
        slot = jnp.where(ahead < half, 2 * ahead - 1, 2 * (count - ahead))
        slots.append(jnp.where(ahead == 0, 0, jnp.where(ahead == half, count - 1, slot)))
    return members, slots


def rep_exchange(values, distance):
    count = lax.axis_size("rep")
    return lax.ppermute(values, "rep", [(i, i ^ distance) for i in range(count)])


def rep_bit(distance):
    return (lax.axis_index("rep") // distance) % 2


def rep_distances():
    count, distance, distances = lax.axis_size("rep"), 1, []
    while distance < count:
        distances.append(distance)
        distance *= 2
    return distances


def rep_gather(gathered, distances):
    for distance in distances:
        shape = gathered.shape[1:]
        other = rep_exchange(gathered, distance)
        mine_first = jnp.stack([gathered, other], axis=1)
        other_first = jnp.stack([other, gathered], axis=1)
        gathered = jnp.where(rep_bit(distance) == 0, mine_first, other_first)
        gathered = gathered.reshape((-1,) + shape)
    return gathered


def rep_scatter(values, axis, distances):
    for distance in distances:
        shape = values.shape
        pairs = values.reshape(shape[:axis] + (shape[axis] // 2, 2) + shape[axis + 1 :])
        bit = rep_bit(distance)
        keep = lax.dynamic_index_in_dim(pairs, bit, axis + 1, keepdims=False)
        send = lax.dynamic_index_in_dim(pairs, 1 - bit, axis + 1, keepdims=False)
        values = add_low(keep, rep_exchange(send, distance))
    return values


def rep_sum(values):
    distance = 1
    while distance < lax.axis_size("rep"):
        values = values + rep_exchange(values, distance)
        distance *= 2
    return values


def swap_all(values):
    return lax.all_to_all(values, "ep", split_axis=0, concat_axis=0, tiled=True)


def expert_kernel(rows_ref, gate_ref, up_ref, stream_ref, gates_ref, *refs):
    inner_ref, gback_ref, uback_ref, pair_ref = refs[-4:]
    expert, step = pl.program_id(0), pl.program_id(1)
    rows = rows_ref[...]
    gate_linear = jnp.dot(rows, gate_ref[0], preferred_element_type=wide_type)
    up_linear = jnp.dot(rows, up_ref[0], preferred_element_type=wide_type)
    stream = stream_ref[...]
    column = gates_ref[:, 0:1]
    for other in range(1, gates_ref.shape[1]):
        column = jnp.where(expert == other, gates_ref[:, other : other + 1], column)
    sigmoid_gate = jax.nn.sigmoid(gate_linear)
    silu_gate = gate_linear * sigmoid_gate
    inner = silu_gate * up_linear
    inner_ref[...] = (column * inner).astype(low_type)
    hidden_grad = column * stream
    gback_ref[...] = (
        hidden_grad * up_linear * sigmoid_gate * (1.0 + gate_linear * (1.0 - sigmoid_gate))
    ).astype(low_type)
    uback_ref[...] = (hidden_grad * silu_gate).astype(low_type)
    product = inner * stream
    lanes = pair_ref.shape[2]
    folded = product[:, :lanes]
    for start in range(lanes, product.shape[1], lanes):
        folded = folded + product[:, start : start + lanes]

    @pl.when(step == 0)
    def _():
        pair_ref[0] = folded

    @pl.when(step > 0)
    def _():
        pair_ref[0] += folded


def expert_pass(rows, gate_weight, up_weight, stream, gates, chunk, chunks, earlier=()):
    count, depth = rows.shape
    experts, _, hidden = gate_weight.shape
    width = 256
    steps = hidden // width
    weight = pl.BlockSpec((1, depth, width), lambda e, j: (e, 0, j))
    out = pl.BlockSpec((count, width), lambda e, j: (chunk, e * steps + j))
    return pl.pallas_call(
        expert_kernel,
        grid=(experts, steps),
        in_specs=[
            pl.BlockSpec((count, depth), lambda e, j: (0, 0)),
            weight,
            weight,
            pl.BlockSpec((count, width), lambda e, j: (0, e * steps + j)),
            pl.BlockSpec(gates.shape, lambda e, j: (0, 0)),
        ]
        + [pl.BlockSpec(memory_space=pl.ANY)] * len(earlier),
        out_specs=[out, out, out, pl.BlockSpec((1, count, 128), lambda e, j: (e, 0, 0))],
        out_shape=[jax.ShapeDtypeStruct((count * chunks, experts * hidden), low_type)] * 3
        + [jax.ShapeDtypeStruct((experts, count, 128), wide_type)],
        input_output_aliases={5 + i: i for i in range(len(earlier))},
        compiler_params=pltpu.CompilerParams(vmem_limit_bytes=56 << 20),
        cost_estimate=pl.CostEstimate(
            flops=4 * count * depth * experts * hidden,
            bytes_accessed=4 * depth * experts * hidden + 20 * count * depth,
            transcendentals=count * experts * hidden,
        ),
    )(rows, gate_weight, up_weight, stream, gates, *earlier)


def expert_back_kernel(gback_ref, uback_ref, gate_ref, up_ref, out_ref):
    experts, _, hidden = gate_ref.shape
    total = None
    for e in range(experts):
        for grad_ref, weight_ref in ((gback_ref, gate_ref), (uback_ref, up_ref)):
            term = mm(grad_ref[:, e * hidden : (e + 1) * hidden], weight_ref[e], 1, 1)
            total = term if total is None else total + term
    out_ref[...] = total.astype(low_type)


def expert_back(gback, uback, gate_weight, up_weight, chunk, chunks):
    count = gback.shape[0] // chunks
    experts, depth, hidden = gate_weight.shape
    width = 256
    whole = pl.BlockSpec((count, experts * hidden), lambda j: (chunk, 0))
    weight = pl.BlockSpec((experts, width, hidden), lambda j: (0, j, 0))
    return pl.pallas_call(
        expert_back_kernel,
        grid=(depth // width,),
        in_specs=[whole, whole, weight, weight],
        out_specs=pl.BlockSpec((count, width), lambda j: (0, j)),
        out_shape=jax.ShapeDtypeStruct((count, depth), low_type),
        compiler_params=pltpu.CompilerParams(vmem_limit_bytes=56 << 20),
        cost_estimate=pl.CostEstimate(
            flops=4 * count * depth * experts * hidden,
            bytes_accessed=4 * depth * experts * hidden + 6 * count * depth,
            transcendentals=0,
        ),
    )(gback, uback, gate_weight, up_weight)


def attention_back_kernel(
    block,
    scale,
    order_ref,
    query_ref,
    key_ref,
    value_ref,
    swapped_ref,
    total_ref,
    column_ref,
    line_ref,
    query_raw_ref,
    key_raw_ref,
    gains_ref,
    cosine_ref,
    sine_ref,
    *refs,
):
    sent_ref, part_ref, key_sum, value_sum, grad_ref = refs[-5:]
    rows, depth = query_ref.shape
    lane = lax.broadcasted_iota(jnp.int32, (1, depth), 1)
    sign = jnp.where(lane < depth // 2, 1.0, -1.0)
    share = swapped_ref.shape[1]
    for slot in range(swapped_ref.shape[0]):
        grad_ref[slot * share : (slot + 1) * share, :] = swapped_ref[order_ref[slot]]
    key_sum[...] = jnp.zeros_like(key_sum)
    value_sum[...] = jnp.zeros_like(value_sum)
    part_ref[...] = jnp.zeros_like(part_ref)

    def finish(back, raw, row, which):
        turned = back * cosine_ref[row, :]
        turned += pltpu.roll(back * sine_ref[row, :], depth // 2, axis=1) * sign
        inverse = inverse_rms(raw)
        result, part = norm_backward(raw, inverse, gains_ref[which : which + 1, :], turned)
        sent_ref[row, which * depth : (which + 1) * depth] = result.astype(low_type)
        part_ref[which : which + 1, :] += jnp.sum(part, axis=0, keepdims=True)

    @pl.loop(0, rows // block)
    def _(step):
        row = pl.ds(pl.multiple_of(step * block, block), block)
        query, grad = query_ref[row, :], grad_ref[row, :]
        scores = mm(query, key_ref[...], 1, 1) * scale
        scores = jnp.where(column_ref[row, :] == line_ref[...], scores, masked_value)
        weights = jnp.exp(scores - total_ref[row, :])
        weight_grad = mm(grad, value_ref[...], 1, 1)
        row_dot = jnp.sum(weights * weight_grad, axis=-1, keepdims=True)
        score_grad = (weights * (weight_grad - row_dot)).astype(low_type)
        key_sum[...] += mm(score_grad, query, 0, 0)
        value_sum[...] += mm(weights.astype(low_type), grad, 0, 0)
        finish(mm(score_grad, key_ref[...], 1, 0) * scale, query_raw_ref[row, :], row, 0)

    @pl.loop(0, rows // block)
    def _(step):
        row = pl.ds(pl.multiple_of(step * block, block), block)
        finish(key_sum[row, :] * scale, key_raw_ref[row, :], row, 1)
        sent_ref[row, 2 * depth : 3 * depth] = value_sum[row, :].astype(low_type)


def attention_back(head, kept, swapped, order, column, line, raw, gains, tables, earlier=()):
    rows, depth = kept[0].shape
    block = 256 if rows % 256 == 0 else rows

    def whole(array):
        return pl.BlockSpec(array.shape, lambda i, order: (0,) * array.ndim)

    def columns(index):
        return pl.BlockSpec((rows, depth), lambda i, order: (0, index))

    operands = (*kept[:3], swapped, kept[3], column, line, raw, raw, gains, *tables)
    specs = [whole(operand) for operand in operands]
    specs[3] = pl.BlockSpec(swapped.shape[:2] + (depth,), lambda i, order: (0, 0, head))
    specs[7], specs[8] = columns(3 * head), columns(3 * head + 1)
    return pl.pallas_call(
        functools.partial(attention_back_kernel, block, depth**-0.5),
        grid_spec=pltpu.PrefetchScalarGridSpec(
            num_scalar_prefetch=1,
            grid=(1,),
            in_specs=specs + [pl.BlockSpec(memory_space=pl.ANY)] * len(earlier),
            out_specs=[
                pl.BlockSpec((rows, 3 * depth), lambda i, order: (0, head)),
                pl.BlockSpec((2, depth), lambda i, order: (0, 0)),
            ],
            scratch_shapes=[pltpu.VMEM((rows, depth), wide_type)] * 2
            + [pltpu.VMEM((rows, depth), low_type)],
        ),
        out_shape=[
            jax.ShapeDtypeStruct(raw.shape, low_type),
            jax.ShapeDtypeStruct((2, depth), wide_type),
        ],
        input_output_aliases={1 + len(operands) + i: i for i in range(len(earlier))},
        compiler_params=pltpu.CompilerParams(vmem_limit_bytes=56 << 20),
        cost_estimate=pl.CostEstimate(
            flops=10 * rows * rows * depth,
            bytes_accessed=30 * rows * depth,
            transcendentals=rows * rows,
        ),
    )(order, *operands, *earlier)


def first_product_kernel(sent_ref, weight_ref, token_ref, inverse_ref, out_ref, part_ref):
    first = mm(sent_ref[...], weight_ref[...], 1, 1)
    out_ref[...] = first.astype(low_type)
    scaled = token_ref[...].astype(wide_type) * inverse_ref[...]
    part_ref[...] = jnp.sum(first * scaled, axis=0, keepdims=True)


def first_product(sent, weight, tokens, inverse):
    rows, depth = tokens.shape
    width = 256
    tile = pl.BlockSpec((rows, width), lambda j: (0, j))
    first, part = pl.pallas_call(
        first_product_kernel,
        grid=(depth // width,),
        in_specs=[
            pl.BlockSpec(sent.shape, lambda j: (0, 0)),
            pl.BlockSpec((width, weight.shape[1]), lambda j: (j, 0)),
            tile,
            pl.BlockSpec((rows, 1), lambda j: (0, 0)),
        ],
        out_specs=[tile, pl.BlockSpec((1, width), lambda j: (0, j))],
        out_shape=[
            jax.ShapeDtypeStruct((rows, depth), low_type),
            jax.ShapeDtypeStruct((1, depth), wide_type),
        ],
        compiler_params=pltpu.CompilerParams(vmem_limit_bytes=40 << 20),
        cost_estimate=pl.CostEstimate(
            flops=2 * sent.size * depth,
            bytes_accessed=2 * (sent.size + weight.size) + 4 * rows * depth,
            transcendentals=0,
        ),
    )(sent, weight, tokens, inverse)
    return first, part[0]


def block_product_kernel(left_ref, *refs):
    out_ref = refs[-1]
    rows = refs[0].shape[0]
    total = None
    for j, ref in enumerate(refs[:-1]):
        term = mm(left_ref[j * rows : (j + 1) * rows, :], ref[...], 0, 0)
        total = term if total is None else total + term
    out_ref[...] = total.astype(low_type)


def block_product(left, blocks):
    rows, width = blocks[0].shape
    tile = 512
    return pl.pallas_call(
        block_product_kernel,
        grid=(width // tile,),
        in_specs=[pl.BlockSpec(left.shape, lambda j: (0, 0))] + [pl.BlockSpec((rows, tile), lambda j: (0, j))] * len(blocks),
        out_specs=pl.BlockSpec((left.shape[1], tile), lambda j: (0, j)),
        out_shape=jax.ShapeDtypeStruct((left.shape[1], width), low_type),
        cost_estimate=pl.CostEstimate(flops=2 * left.size * width, bytes_accessed=2 * left.size + 2 * len(blocks) * rows * width, transcendentals=0),
    )(left, *blocks)


def body(
    tokens,
    cotangent,
    seq_lengths,
    token_order,
    routes,
    slot_index,
    query_weight,
    key_weight,
    value_weight,
    output_weight,
    router_weight,
    prenorm_gain,
    querynorm_gain,
    keynorm_gain,
    postnorm_gain,
    gate_weight,
    up_weight,
    down_weight,
):
    group_count = lax.axis_size("ep")
    device = lax.axis_index("ep")
    row_count, model_width = tokens.shape
    head_dim = querynorm_gain.shape[0]
    width_here = model_width // group_count
    heads_here = width_here // head_dim
    experts_here = gate_weight.shape[0]
    expert_total = experts_here * group_count
    top_count = routes.shape[1]
    capacity = row_count * top_count * 5 // (4 * expert_total)
    group_rows = row_count * group_count
    sequence_count = seq_lengths.shape[1]
    score_scale = head_dim ** (-0.5)

    replica_count = lax.axis_size("rep")
    replica = lax.axis_index("rep")
    share = width_here // replica_count

    device_of_slot, slot_of_device = ring_indices(device, group_count)

    def reorder(blocks, index):
        return jnp.concatenate(
            [lax.dynamic_slice_in_dim(blocks, index[i], 1, 0) for i in range(group_count)], axis=0
        )

    group_order = reorder(token_order[0].reshape(group_count, row_count), device_of_slot)
    segment, position = row_meta(seq_lengths[0], group_order.reshape(group_rows))
    segment_own = segment[:row_count]
    valid_own = (segment_own < sequence_count).astype(wide_type)[:, None]
    valid_all = (segment < sequence_count).astype(wide_type)[:, None]

    expert_ids = jnp.arange(expert_total, dtype=jnp.int32)
    route_code = jnp.zeros((row_count, expert_total), jnp.int32)
    for column in range(top_count):
        hit = routes[:, column, None] == expert_ids[None, :]
        kept = (slot_index[:, column, None] < capacity).astype(jnp.int32)
        route_code = route_code + jnp.where(hit, 1 + kept, 0)
    small_sent = jnp.concatenate([route_code.astype(low_type), router_weight], axis=0)

    projections = (
        jnp.stack(
            [
                lax.dynamic_slice_in_dim(piece, replica * share, share, 0).reshape(
                    share, group_count, heads_here, head_dim
                )
                for piece in (query_weight, key_weight, value_weight)
            ],
            axis=3,
        )
        .reshape(share, group_count, 3 * width_here)
        .transpose(1, 0, 2)
    )
    scatter_order = rep_distances()
    gather_order = scatter_order[::-1]
    swapped = swap_all(projections)
    head_weight = (
        rep_gather(swapped[None], gather_order)
        .transpose(1, 0, 2, 3)
        .reshape(model_width, 3 * width_here)
    )
    tokens_late, output_late, _ = tie(tokens, output_weight, swapped)
    token_ring = RingGather(tokens_late)
    token_ring.start()
    small_flat = after(small_sent.reshape(-1, head_dim), token_ring.received)
    small_all = swap_all(
        jnp.broadcast_to(small_flat[None], (group_count,) + small_flat.shape)
    ).reshape(group_count, row_count + width_here, expert_total)
    code_all = reorder(small_all[:, :row_count], device_of_slot).reshape(
        group_rows, expert_total
    )
    full_router = small_all[:, row_count:].reshape(model_width, expert_total)
    chunks = 2
    chunk_rows = group_rows // chunks
    blocks_here = group_count // chunks

    def chunk_of(array, chunk):
        return array[chunk * chunk_rows : (chunk + 1) * chunk_rows]

    def slot_rows(array):
        return lambda slot: array[slot * row_count : (slot + 1) * row_count]

    def reorder_rows(rows, index):
        return reorder(
            rows.reshape(group_count, row_count, rows.shape[1]), index
        ).reshape(rows.shape)

    column_share = model_width // replica_count
    output_share = gather_rows(
        lax.dynamic_slice_in_dim(output_late, replica * column_share, column_share, 1)
    )
    token_ring.finish()
    for step in range(1, group_count // 2):
        if step == group_count // 2 - 1:
            token_ring.sent = (after(token_ring.sent[0], output_share), token_ring.sent[1])
        token_ring.start()
        token_ring.finish()
    cosine, sine_part = rope_tables(after(position, token_ring.blocks[1]), head_dim)

    hidden_here = down_weight.shape[1]
    flat_down = down_weight.reshape(experts_here * hidden_here, model_width)

    allowed = segment[:, None] == segment[None, :]
    far = replica_count // 2
    steps = group_count // 2
    part_rows = model_width // steps
    far_parts = [
        Exchange(output_share[i * part_rows : (i + 1) * part_rows], far) for i in range(steps)
    ]

    def head_columns(values, block, head):
        start = (3 * head + block) * head_dim
        return values[:, start : start + head_dim]

    def project(weight, *blocks):
        token_all = jnp.concatenate(blocks, axis=0)
        token_wide = token_all.astype(wide_type)
        inverse = inverse_rms(token_wide)
        first_all = (token_wide * inverse * prenorm_gain).astype(low_type)
        return token_all, inverse, first_all, mm(first_all, weight, 1, 0)

    def attend(head, raw):
        turned = []
        for block, gain in ((0, querynorm_gain), (1, keynorm_gain)):
            part = head_columns(raw, block, head)
            normed = part * inverse_rms(part) * gain
            turned.append((normed * cosine + turn_half(normed) * sine_part).astype(low_type))
        value_low = head_columns(raw, 2, head).astype(low_type)
        scores = jnp.where(allowed, mm(*turned, 1, 1) * score_scale, masked_value)
        top_score = jnp.max(scores, axis=-1, keepdims=True)
        powers = jnp.exp(scores - top_score)
        log_total = top_score + jnp.log(jnp.sum(powers, axis=-1, keepdims=True))
        weights_low = jnp.exp(scores - log_total).astype(low_type)
        return (*turned, value_low, log_total, mm(weights_low, value_low, 1, 0).astype(low_type))

    cot_ring = RingGather(after(cotangent, token_ring.received))
    token_all, inverse_all, first_all, raw = window(
        [cot_ring, far_parts[0]], project, head_weight, *token_ring.blocks
    )
    heads = []
    for head in range(heads_here):
        heads.append(
            window(
                [cot_ring, far_parts[1 + head]],
                lambda raw, head=head: attend(head, raw),
                raw,
            )
        )

    def order_work(*mixed):
        mixed_low = jnp.concatenate(mixed, axis=1)
        return (
            mixed_low,
            reorder_rows(mixed_low, slot_of_device),
            segment[:, None],
            segment[None, :],
            jnp.stack([querynorm_gain, keynorm_gain]),
            jnp.stack(device_of_slot),
        )

    mixed_low, mixed_ordered, segment_column, segment_line, norm_gains, slot_order = window(
        [cot_ring, *far_parts[1 + heads_here :]], order_work, *[head[4] for head in heads]
    )
    cot_all = jnp.concatenate(cot_ring.blocks, axis=0)
    output_pieces = {
        0: output_share,
        far: jnp.concatenate([part.received for part in far_parts], axis=0),
    }
    for distance in gather_order[1:]:
        for j in list(output_pieces):
            output_pieces[j ^ distance] = rep_exchange(output_pieces[j], distance)
    mixed_own = (
        swap_all(mixed_ordered.reshape(group_count, row_count, width_here))
        .transpose(1, 0, 2)
        .reshape(row_count, model_width)
    )
    attention = jnp.zeros((row_count, model_width), wide_type)
    for j, piece in output_pieces.items():
        attention = lax.dynamic_update_slice_in_dim(
            attention, mm(mixed_own, piece, 1, 0), (replica ^ j) * column_share, 1
        )
    residual = tokens.astype(wide_type) + attention
    inverse_two = inverse_rms(residual)
    second_input = (residual * inverse_two * postnorm_gain).astype(low_type)

    def gate_table(rows, code):
        logits = mm(rows, full_router, 1, 0)
        shifted = jnp.where(code > 0, logits, masked_value)
        powers = jnp.exp(shifted - jnp.max(shifted, axis=1, keepdims=True))
        return powers / jnp.sum(powers, axis=1, keepdims=True)

    kept_all = jnp.where(code_all > 1, valid_all, 0.0)
    kept_here = lax.dynamic_slice_in_dim(kept_all, device * experts_here, experts_here, 1)

    def stream_of(cot_part):
        return mm(cot_part, flat_down, 1, 1)

    def expert_chunk(chunk, rows, stream, *earlier):
        gates = gate_table(rows, chunk_of(code_all, chunk)) * chunk_of(kept_all, chunk)
        gates_here = lax.dynamic_slice_in_dim(gates, device * experts_here, experts_here, 1)
        return expert_pass(
            rows, gate_weight, up_weight, stream, gates_here, chunk, chunks, earlier
        )

    second_ring = RingGather(second_input)
    stream_first = window([second_ring], lambda part: stream_of(part), chunk_of(cot_all, 0))
    stream_last = window([second_ring], lambda part: stream_of(part), chunk_of(cot_all, 1))
    rows_first = jnp.concatenate(second_ring.blocks[:blocks_here], axis=0)
    *earlier, pair_first = window(
        [second_ring],
        lambda rows, stream: expert_chunk(0, rows, stream),
        rows_first,
        stream_first,
    )
    window([second_ring], lambda: ())
    rows_last = jnp.concatenate(second_ring.blocks[blocks_here:], axis=0)
    inner_all, gback_all, uback_all, pair_last = expert_chunk(
        1, rows_last, stream_last, *earlier
    )
    second_all = jnp.concatenate([rows_first, rows_last], axis=0)
    back_last = expert_back(gback_all, uback_all, gate_weight, up_weight, 1, chunks)
    back_parts = {1: back_last}

    def back_block(slot):
        start = (slot % blocks_here) * row_count
        return back_parts[slot // blocks_here][start : start + row_count]

    def grad_of(left, right):
        return mm(left, right, 0, 0).astype(low_type)

    pair_lanes = jnp.concatenate([pair_first, pair_last], axis=1)
    pair_sent = (kept_here * jnp.sum(pair_lanes, axis=2).transpose(1, 0)).reshape(
        group_count, row_count, experts_here
    )
    code_own = route_code
    gates_own = gate_table(second_input, code_own)

    back_ring = RingSum(back_block, row_count)

    def mixture_work(inner, pair):
        return (
            mm(inner, flat_down, 1, 0).astype(low_type),
            swap_all(reorder(pair, slot_of_device)),
        )

    mixture_part, pair_grad = window([back_ring], mixture_work, inner_all, pair_sent)
    mixture_ring = RingSum(slot_rows(mixture_part), row_count)

    def back_work(gback, uback):
        back_parts[0] = expert_back(gback, uback, gate_weight, up_weight, 0, chunks)
        return back_parts[0]

    back_parts[0] = window([back_ring, mixture_ring], back_work, gback_all, uback_all)

    def down_work(inner, pair):
        pair_grad = pair.transpose(1, 0, 2).reshape(row_count, expert_total)
        chosen_grad = gates_own * (
            pair_grad - jnp.sum(gates_own * pair_grad, axis=1, keepdims=True)
        )
        logits_grad = jnp.where(code_own > 0, chosen_grad, 0.0).astype(low_type)
        router_back = mm(logits_grad, full_router, 1, 1)
        router_part = mm(second_input, logits_grad, 0, 0)
        return grad_of(inner, cot_all), router_back, router_part

    down_part, router_back, router_part = window(
        [back_ring, mixture_ring], down_work, inner_all, pair_grad
    )
    gate_part = window(
        [back_ring, mixture_ring], lambda gback: grad_of(second_all, gback), gback_all
    )
    second_scattered = back_ring.total()
    second_grad = router_back + second_scattered
    upstream = valid_own * cotangent.astype(wide_type)
    def residual_work(second_grad):
        post_back, postnorm_part = norm_backward(
            residual, inverse_two, postnorm_gain, second_grad
        )
        residual_grad = upstream + post_back
        attention_low = residual_grad.astype(low_type)
        mixed_grad_own = jnp.zeros((row_count, model_width), wide_type)
        for j, piece in output_pieces.items():
            mixed_grad_own = mixed_grad_own + mm(
                lax.dynamic_slice_in_dim(
                    attention_low, (replica ^ j) * column_share, column_share, 1
                ),
                piece,
                1,
                1,
            )
        swap_sent = (
            mixed_grad_own.astype(low_type)
            .reshape(row_count, group_count, width_here)
            .transpose(1, 0, 2)
        )
        return swap_sent, residual_grad, attention_low, jnp.sum(postnorm_part, axis=0)

    swap_sent, residual_grad, attention_low, postnorm_part = window(
        [mixture_ring], residual_work, second_grad
    )
    class Swap(Exchange):
        def start(self):
            self.received = swap_all(self.sent)

    swap = Swap(swap_sent, 0)
    attention_gather = RingGather(attention_low)
    up_part = window(
        [swap, attention_gather],
        lambda uback: grad_of(second_all, uback),
        uback_all,
    )
    mixed_grad = swap.received

    sent, gain_parts = (), 0.0
    for head in range(heads_here):

        def head_work(grads, *earlier, head=head):
            return tuple(
                attention_back(
                    head,
                    heads[head][:4],
                    grads,
                    slot_order,
                    segment_column,
                    segment_line,
                    raw,
                    norm_gains,
                    (cosine, sine_part),
                    earlier,
                )
            )

        *sent, gain_part = window([attention_gather], head_work, mixed_grad, *sent)
        gain_parts = gain_parts + gain_part
    (sent,) = sent
    querynorm_part, keynorm_part = gain_parts[0], gain_parts[1]
    down_sum = lax.psum_scatter(
        down_part.reshape(experts_here, hidden_here, model_width),
        "rep",
        scatter_dimension=1,
        tiled=True,
    )
    sent, down_sum = tie(sent, down_sum)

    def first_work(sent, head):
        return (
            *first_product(sent, head_weight, token_all, inverse_all),
            rep_scatter(head, 1, scatter_order[:1]),
        )

    head_part = window([attention_gather], grad_of, first_all, sent)
    while attention_gather.step < group_count // 2:
        window([attention_gather], lambda: ())
    first_low, prenorm_part, head_part = window(
        [],
        first_work,
        sent,
        head_part.reshape(group_count, replica_count, share, 3 * width_here),
    )

    def small_swap(parts):
        return swap_all(
            jnp.concatenate([part.reshape(group_count, -1) for part in parts], axis=1)
        )

    def small_pieces(swapped, parts):
        total = rep_sum(jnp.sum(swapped, axis=0))
        pieces, start = [], 0
        for part in parts:
            size = part.size // group_count
            pieces.append(total[start : start + size])
            start += size
        return pieces

    first_ring = RingSum(slot_rows(first_low), row_count)
    small_parts = [router_part, postnorm_part, prenorm_part, querynorm_part, keynorm_part]
    head_part = rep_scatter(head_part, 1, scatter_order[1:])
    output_part = window(
        [first_ring],
        lambda mixed, *blocks: block_product(mixed, blocks),
        mixed_low,
        *attention_gather.blocks,
    )
    gate_sum = lax.psum_scatter(gate_part, "rep", scatter_dimension=0, tiled=True)
    up_sum = lax.psum_scatter(up_part, "rep", scatter_dimension=0, tiled=True)
    def split_experts(total):
        return jnp.stack(
            [
                total[:, e * hidden_here : (e + 1) * hidden_here].astype(wide_type)
                for e in range(experts_here)
            ]
        )

    (small_swapped, output_part, down_total), head_part = window(
        [first_ring],
        lambda output, down, *small: (
            small_swap(small),
            rep_scatter(output, 0, scatter_order[:1]),
            down.astype(wide_type),
        ),
        output_part.reshape(replica_count, share, model_width),
        down_sum,
        *small_parts,
        waits=(head_part,),
    )
    head_rows = swap_all(head_part.reshape(group_count, share, 3 * width_here))
    def layer_work(own, *sums):
        mixture = sum((part.astype(wide_type) for part in sums), own.astype(wide_type))
        return (valid_own * (residual + mixture)).astype(low_type)

    (output_part, small_sums, gate_total, layer_out), head_rows = window(
        [first_ring],
        lambda output, small, total, sums: (
            rep_scatter(output, 0, scatter_order[1:]),
            small_pieces(small, small_parts),
            split_experts(total),
            layer_work(*sums),
        ),
        output_part,
        small_swapped,
        gate_sum,
        (mixture_part[:row_count], *mixture_ring.sent),
        waits=(head_rows,),
    )
    head_rows = rep_gather(
        head_rows.reshape(group_count, share, heads_here, 3, head_dim)
        .transpose(3, 1, 0, 2, 4)
        .reshape(1, 3, share, model_width),
        gather_order[:-1],
    )
    output_rows, head_rows = window(
        [first_ring],
        lambda output: rep_gather(output, gather_order[:-1]),
        output_part,
        waits=(head_rows,),
    )
    head_rows = rep_gather(head_rows, gather_order[-1:])
    output_rows = rep_gather(output_rows, gather_order[-1:])
    first_grad = first_ring.total()
    query_grad, key_grad, value_grad = (
        head_rows[:, block].reshape(width_here, model_width).astype(wide_type)
        for block in range(3)
    )
    output_grad = output_rows.reshape(width_here, model_width).astype(wide_type)
    router_grad, postnorm_grad, prenorm_grad, querynorm_grad, keynorm_grad = small_sums
    router_grad = router_grad.reshape(width_here, expert_total)

    token_own = tokens.astype(wide_type)
    inverse_one = inverse_rms(token_own)
    pre_back, _ = norm_backward(token_own, inverse_one, prenorm_gain, first_grad)
    token_grad = residual_grad + pre_back

    up_total = split_experts(up_sum)
    return (
        layer_out,
        token_grad,
        query_grad,
        key_grad,
        value_grad,
        output_grad,
        router_grad,
        prenorm_grad,
        querynorm_grad,
        keynorm_grad,
        postnorm_grad,
        gate_total,
        up_total,
        down_total,
    )


def solution(mesh):
    in_specs = (
        P(("rep", "ep"), None),
        P(("rep", "ep"), None),
        P("rep", None),
        P("rep", None),
        P(("rep", "ep"), None),
        P(("rep", "ep"), None),
        P("ep", None),
        P("ep", None),
        P("ep", None),
        P("ep", None),
        P("ep", None),
        P(),
        P(),
        P(),
        P(),
        P("ep", None, None),
        P("ep", None, None),
        P("ep", None, None),
    )
    out_specs = (
        P(("rep", "ep"), None),
        P(("rep", "ep"), None),
        P("ep", None),
        P("ep", None),
        P("ep", None),
        P("ep", None),
        P("ep", None),
        P("ep"),
        P("ep"),
        P("ep"),
        P("ep"),
        P("ep", "rep", None),
        P("ep", "rep", None),
        P("ep", "rep", None),
    )
    return jax.shard_map(body, mesh=mesh, in_specs=in_specs, out_specs=out_specs, check_vma=False)
```

```python
import functools

import jax
import jax.numpy as jnp
from jax import lax
from jax.experimental import pallas as pl
from jax.experimental.pallas import tpu as pltpu
from jax.sharding import PartitionSpec as P

epsilon = 1e-05
rope_base = 10000.0
masked_value = -1e30
low_type = jnp.bfloat16
wide_type = jnp.float32


def inverse_rms(values):
    return lax.rsqrt(jnp.mean(values * values, axis=-1, keepdims=True) + epsilon)


def norm_backward(values, inverse, gain_vector, upstream):
    scaled = upstream * gain_vector
    inner_mean = jnp.mean(scaled * values, axis=-1, keepdims=True)
    result = inverse * scaled - values * (inverse * inverse * inverse) * inner_mean
    return (result, upstream * values * inverse)


def rope_tables(position, dimension):
    halfway = dimension // 2
    indices = jnp.arange(halfway, dtype=wide_type)
    frequency = rope_base ** (-2.0 * indices / dimension)
    angles = position.astype(wide_type)[:, None] * frequency[None, :]
    cosine = jnp.cos(angles)
    sine_part = jnp.sin(angles)
    return (
        jnp.concatenate([cosine, cosine], axis=-1),
        jnp.concatenate([sine_part, sine_part], axis=-1),
    )


def turn_half(values):
    halfway = values.shape[-1] // 2
    return jnp.concatenate([-values[..., halfway:], values[..., :halfway]], axis=-1)


def turn_back(values):
    halfway = values.shape[-1] // 2
    return jnp.concatenate([values[..., halfway:], -values[..., :halfway]], axis=-1)


def row_meta(lengths, group_order):
    boundary = jnp.cumsum(lengths)
    passed = (group_order[:, None] >= boundary[None, :]).astype(jnp.int32)
    segment = jnp.sum(passed, axis=1)
    offset = jnp.sum(passed * lengths[None, :], axis=1)
    return (segment, group_order - offset)


def mm(left, right, left_dim, right_dim):
    return lax.dot_general(
        left,
        right,
        (((left_dim,), (right_dim,)), ((), ())),
        preferred_element_type=wide_type,
    )


def gather_rows(values):
    return lax.all_gather(values, "ep", axis=0, tiled=True)


def ring_order(count):
    return [i for i in range(count) if i % 2 == 0] + [i for i in reversed(range(count)) if i % 2]


def ring_slots(count):
    half = count // 2
    offsets = [0]
    for step in range(1, half):
        offsets += [step, -step]
    return offsets + [half]


def ring_shift(values, direction):
    order = ring_order(lax.axis_size("ep"))
    count = len(order)
    pairs = [(order[i], order[(i + direction) % count]) for i in range(count)]
    return lax.ppermute(values, "ep", pairs)


def tie(*arrays):
    return lax.optimization_barrier(arrays)


def after(value, *others):
    return lax.optimization_barrier((value,) + others)[0]


class RingGather:
    def __init__(self, values):
        self.middle = values.shape[0] // 2
        self.half, self.step = lax.axis_size("ep") // 2, 0
        self.sent = (values, values)
        self.blocks = [values]

    def start(self):
        if self.step == self.half - 1:
            self.sent = (self.sent[0][: self.middle], self.sent[1][self.middle :])
        self.received = (ring_shift(self.sent[0], 1), ring_shift(self.sent[1], -1))

    def finish(self):
        self.step += 1
        onward, backward = self.sent = self.received
        if self.step < self.half:
            self.blocks += [backward, onward]
        else:
            self.blocks += [jnp.concatenate([onward, backward], axis=0)]


class Exchange:
    def __init__(self, values, distance):
        self.sent, self.distance = values, distance

    def start(self):
        self.received = rep_exchange(self.sent, self.distance)

    def finish(self):
        pass


class RingSum:
    def __init__(self, block, rows):
        count = lax.axis_size("ep")
        self.block, self.middle, self.step = block, rows // 2, 0
        self.half = count // 2
        self.slot = {offset: j for j, offset in enumerate(ring_slots(count))}
        far = block(self.slot[self.half])
        self.sent = (far[: self.middle], far[self.middle :])

    def start(self):
        self.received = (ring_shift(self.sent[0], 1), ring_shift(self.sent[1], -1))

    def finish(self):
        self.step += 1
        onward, backward = self.received
        left = self.half - self.step
        middle = self.middle
        if left:
            up, down = self.block(self.slot[left]), self.block(self.slot[-left])
            if self.step == 1:
                onward = jnp.concatenate([add_low(onward, up[:middle]), up[middle:]], axis=0)
                backward = jnp.concatenate(
                    [down[:middle], add_low(backward, down[middle:])], axis=0
                )
            else:
                onward, backward = add_low(onward, up), add_low(backward, down)
        self.sent = (onward, backward)

    def total(self):
        return (
            self.block(self.slot[0]).astype(wide_type)
            + self.sent[0].astype(wide_type)
            + self.sent[1].astype(wide_type)
        )


def window(rings, work, *inputs, waits=()):
    for ring in rings:
        ring.start()
    inputs, _ = tie(inputs, [ring.sent for ring in rings])
    received, waits, results = tie([ring.received for ring in rings], waits, work(*inputs))
    for ring, pair in zip(rings, received):
        ring.received = pair
        ring.finish()
    return (results, *waits) if waits else results


def add_low(left, right):
    return (left.astype(wide_type) + right.astype(wide_type)).astype(low_type)


def ring_place(member, count):
    return jnp.where(member % 2 == 0, member // 2, count - 1 - member // 2)


def ring_member(place, count):
    return jnp.where(place < count // 2, 2 * place, 2 * (count - 1 - place) + 1)


def ring_indices(device, count):
    place = ring_place(device, count)
    half = count // 2
    members = [ring_member((place + offset) % count, count) for offset in ring_slots(count)]
    slots = []
    for other in range(count):
        ahead = (ring_place(jnp.int32(other), count) - place) % count
        slot = jnp.where(ahead < half, 2 * ahead - 1, 2 * (count - ahead))
        slots.append(jnp.where(ahead == 0, 0, jnp.where(ahead == half, count - 1, slot)))
    return members, slots


def rep_exchange(values, distance):
    count = lax.axis_size("rep")
    return lax.ppermute(values, "rep", [(i, i ^ distance) for i in range(count)])


def rep_bit(distance):
    return (lax.axis_index("rep") // distance) % 2


def rep_distances():
    count, distance, distances = lax.axis_size("rep"), 1, []
    while distance < count:
        distances.append(distance)
        distance *= 2
    return distances


def rep_gather(gathered, distances):
    for distance in distances:
        shape = gathered.shape[1:]
        other = rep_exchange(gathered, distance)
        mine_first = jnp.stack([gathered, other], axis=1)
        other_first = jnp.stack([other, gathered], axis=1)
        gathered = jnp.where(rep_bit(distance) == 0, mine_first, other_first)
        gathered = gathered.reshape((-1,) + shape)
    return gathered


def rep_scatter(values, axis, distances):
    for distance in distances:
        shape = values.shape
        pairs = values.reshape(shape[:axis] + (shape[axis] // 2, 2) + shape[axis + 1 :])
        bit = rep_bit(distance)
        keep = lax.dynamic_index_in_dim(pairs, bit, axis + 1, keepdims=False)
        send = lax.dynamic_index_in_dim(pairs, 1 - bit, axis + 1, keepdims=False)
        values = add_low(keep, rep_exchange(send, distance))
    return values


def rep_sum(values):
    distance = 1
    while distance < lax.axis_size("rep"):
        values = values + rep_exchange(values, distance)
        distance *= 2
    return values


def swap_all(values):
    return lax.all_to_all(values, "ep", split_axis=0, concat_axis=0, tiled=True)


def expert_kernel(rows_ref, gate_ref, up_ref, stream_ref, gates_ref, *refs):
    inner_ref, gback_ref, uback_ref, pair_ref = refs[-4:]
    expert, step = pl.program_id(0), pl.program_id(1)
    rows = rows_ref[...]
    gate_linear = jnp.dot(rows, gate_ref[0], preferred_element_type=wide_type)
    up_linear = jnp.dot(rows, up_ref[0], preferred_element_type=wide_type)
    stream = stream_ref[...]
    column = gates_ref[:, 0:1]
    for other in range(1, gates_ref.shape[1]):
        column = jnp.where(expert == other, gates_ref[:, other : other + 1], column)
    sigmoid_gate = jax.nn.sigmoid(gate_linear)
    silu_gate = gate_linear * sigmoid_gate
    inner = silu_gate * up_linear
    inner_ref[...] = (column * inner).astype(low_type)
    hidden_grad = column * stream
    gback_ref[...] = (
        hidden_grad * up_linear * sigmoid_gate * (1.0 + gate_linear * (1.0 - sigmoid_gate))
    ).astype(low_type)
    uback_ref[...] = (hidden_grad * silu_gate).astype(low_type)
    product = inner * stream
    lanes = pair_ref.shape[2]
    folded = product[:, :lanes]
    for start in range(lanes, product.shape[1], lanes):
        folded = folded + product[:, start : start + lanes]

    @pl.when(step == 0)
    def _():
        pair_ref[0] = folded

    @pl.when(step > 0)
    def _():
        pair_ref[0] += folded


def expert_pass(rows, gate_weight, up_weight, stream, gates, chunk, chunks, earlier=()):
    count, depth = rows.shape
    experts, _, hidden = gate_weight.shape
    width = 256
    steps = hidden // width
    weight = pl.BlockSpec((1, depth, width), lambda e, j: (e, 0, j))
    out = pl.BlockSpec((count, width), lambda e, j: (chunk, e * steps + j))
    return pl.pallas_call(
        expert_kernel,
        grid=(experts, steps),
        in_specs=[
            pl.BlockSpec((count, depth), lambda e, j: (0, 0)),
            weight,
            weight,
            pl.BlockSpec((count, width), lambda e, j: (0, e * steps + j)),
            pl.BlockSpec(gates.shape, lambda e, j: (0, 0)),
        ]
        + [pl.BlockSpec(memory_space=pl.ANY)] * len(earlier),
        out_specs=[out, out, out, pl.BlockSpec((1, count, 128), lambda e, j: (e, 0, 0))],
        out_shape=[jax.ShapeDtypeStruct((count * chunks, experts * hidden), low_type)] * 3
        + [jax.ShapeDtypeStruct((experts, count, 128), wide_type)],
        input_output_aliases={5 + i: i for i in range(len(earlier))},
        compiler_params=pltpu.CompilerParams(vmem_limit_bytes=56 << 20),
        cost_estimate=pl.CostEstimate(
            flops=4 * count * depth * experts * hidden,
            bytes_accessed=4 * depth * experts * hidden + 20 * count * depth,
            transcendentals=count * experts * hidden,
        ),
    )(rows, gate_weight, up_weight, stream, gates, *earlier)


def expert_back_kernel(gback_ref, uback_ref, gate_ref, up_ref, out_ref):
    experts, _, hidden = gate_ref.shape
    total = None
    for e in range(experts):
        for grad_ref, weight_ref in ((gback_ref, gate_ref), (uback_ref, up_ref)):
            term = mm(grad_ref[:, e * hidden : (e + 1) * hidden], weight_ref[e], 1, 1)
            total = term if total is None else total + term
    out_ref[...] = total.astype(low_type)


def expert_back(gback, uback, gate_weight, up_weight, chunk, chunks):
    count = gback.shape[0] // chunks
    experts, depth, hidden = gate_weight.shape
    width = 256
    whole = pl.BlockSpec((count, experts * hidden), lambda j: (chunk, 0))
    weight = pl.BlockSpec((experts, width, hidden), lambda j: (0, j, 0))
    return pl.pallas_call(
        expert_back_kernel,
        grid=(depth // width,),
        in_specs=[whole, whole, weight, weight],
        out_specs=pl.BlockSpec((count, width), lambda j: (0, j)),
        out_shape=jax.ShapeDtypeStruct((count, depth), low_type),
        compiler_params=pltpu.CompilerParams(vmem_limit_bytes=56 << 20),
        cost_estimate=pl.CostEstimate(
            flops=4 * count * depth * experts * hidden,
            bytes_accessed=4 * depth * experts * hidden + 6 * count * depth,
            transcendentals=0,
        ),
    )(gback, uback, gate_weight, up_weight)


def attention_back_kernel(
    block,
    scale,
    order_ref,
    query_ref,
    key_ref,
    value_ref,
    swapped_ref,
    total_ref,
    column_ref,
    line_ref,
    query_raw_ref,
    key_raw_ref,
    gains_ref,
    cosine_ref,
    sine_ref,
    *refs,
):
    sent_ref, part_ref, key_sum, value_sum, grad_ref = refs[-5:]
    rows, depth = query_ref.shape
    lane = lax.broadcasted_iota(jnp.int32, (1, depth), 1)
    sign = jnp.where(lane < depth // 2, 1.0, -1.0)
    share = swapped_ref.shape[1]
    for slot in range(swapped_ref.shape[0]):
        grad_ref[slot * share : (slot + 1) * share, :] = swapped_ref[order_ref[slot]]
    key_sum[...] = jnp.zeros_like(key_sum)
    value_sum[...] = jnp.zeros_like(value_sum)
    part_ref[...] = jnp.zeros_like(part_ref)

    def finish(back, raw, row, which):
        turned = back * cosine_ref[row, :]
        turned += pltpu.roll(back * sine_ref[row, :], depth // 2, axis=1) * sign
        inverse = inverse_rms(raw)
        result, part = norm_backward(raw, inverse, gains_ref[which : which + 1, :], turned)
        sent_ref[row, which * depth : (which + 1) * depth] = result.astype(low_type)
        part_ref[which : which + 1, :] += jnp.sum(part, axis=0, keepdims=True)

    @pl.loop(0, rows // block)
    def _(step):
        row = pl.ds(pl.multiple_of(step * block, block), block)
        query, grad = query_ref[row, :], grad_ref[row, :]
        scores = mm(query, key_ref[...], 1, 1) * scale
        scores = jnp.where(column_ref[row, :] == line_ref[...], scores, masked_value)
        weights = jnp.exp(scores - total_ref[row, :])
        weight_grad = mm(grad, value_ref[...], 1, 1)
        row_dot = jnp.sum(weights * weight_grad, axis=-1, keepdims=True)
        score_grad = (weights * (weight_grad - row_dot)).astype(low_type)
        key_sum[...] += mm(score_grad, query, 0, 0)
        value_sum[...] += mm(weights.astype(low_type), grad, 0, 0)
        finish(mm(score_grad, key_ref[...], 1, 0) * scale, query_raw_ref[row, :], row, 0)

    @pl.loop(0, rows // block)
    def _(step):
        row = pl.ds(pl.multiple_of(step * block, block), block)
        finish(key_sum[row, :] * scale, key_raw_ref[row, :], row, 1)
        sent_ref[row, 2 * depth : 3 * depth] = value_sum[row, :].astype(low_type)


def attention_back(head, kept, swapped, order, column, line, raw, gains, tables, earlier=()):
    rows, depth = kept[0].shape
    block = 256 if rows % 256 == 0 else rows

    def whole(array):
        return pl.BlockSpec(array.shape, lambda i, order: (0,) * array.ndim)

    def columns(index):
        return pl.BlockSpec((rows, depth), lambda i, order: (0, index))

    operands = (*kept[:3], swapped, kept[3], column, line, raw, raw, gains, *tables)
    specs = [whole(operand) for operand in operands]
    specs[3] = pl.BlockSpec(swapped.shape[:2] + (depth,), lambda i, order: (0, 0, head))
    specs[7], specs[8] = columns(3 * head), columns(3 * head + 1)
    return pl.pallas_call(
        functools.partial(attention_back_kernel, block, depth**-0.5),
        grid_spec=pltpu.PrefetchScalarGridSpec(
            num_scalar_prefetch=1,
            grid=(1,),
            in_specs=specs + [pl.BlockSpec(memory_space=pl.ANY)] * len(earlier),
            out_specs=[
                pl.BlockSpec((rows, 3 * depth), lambda i, order: (0, head)),
                pl.BlockSpec((2, depth), lambda i, order: (0, 0)),
            ],
            scratch_shapes=[pltpu.VMEM((rows, depth), wide_type)] * 2
            + [pltpu.VMEM((rows, depth), low_type)],
        ),
        out_shape=[
            jax.ShapeDtypeStruct(raw.shape, low_type),
            jax.ShapeDtypeStruct((2, depth), wide_type),
        ],
        input_output_aliases={1 + len(operands) + i: i for i in range(len(earlier))},
        compiler_params=pltpu.CompilerParams(vmem_limit_bytes=56 << 20),
        cost_estimate=pl.CostEstimate(
            flops=10 * rows * rows * depth,
            bytes_accessed=30 * rows * depth,
            transcendentals=rows * rows,
        ),
    )(order, *operands, *earlier)


def block_product_kernel(left_ref, *refs):
    out_ref = refs[-1]
    rows = refs[0].shape[0]
    total = None
    for j, ref in enumerate(refs[:-1]):
        term = mm(left_ref[j * rows : (j + 1) * rows, :], ref[...], 0, 0)
        total = term if total is None else total + term
    out_ref[...] = total.astype(low_type)


def block_product(left, blocks):
    rows, width = blocks[0].shape
    tile = 512
    return pl.pallas_call(
        block_product_kernel,
        grid=(width // tile,),
        in_specs=[pl.BlockSpec(left.shape, lambda j: (0, 0))] + [pl.BlockSpec((rows, tile), lambda j: (0, j))] * len(blocks),
        out_specs=pl.BlockSpec((left.shape[1], tile), lambda j: (0, j)),
        out_shape=jax.ShapeDtypeStruct((left.shape[1], width), low_type),
        cost_estimate=pl.CostEstimate(flops=2 * left.size * width, bytes_accessed=2 * left.size + 2 * len(blocks) * rows * width, transcendentals=0),
    )(left, *blocks)


def body(
    tokens,
    cotangent,
    seq_lengths,
    token_order,
    routes,
    slot_index,
    query_weight,
    key_weight,
    value_weight,
    output_weight,
    router_weight,
    prenorm_gain,
    querynorm_gain,
    keynorm_gain,
    postnorm_gain,
    gate_weight,
    up_weight,
    down_weight,
):
    group_count = lax.axis_size("ep")
    device = lax.axis_index("ep")
    row_count, model_width = tokens.shape
    head_dim = querynorm_gain.shape[0]
    width_here = model_width // group_count
    heads_here = width_here // head_dim
    experts_here = gate_weight.shape[0]
    expert_total = experts_here * group_count
    top_count = routes.shape[1]
    capacity = row_count * top_count * 5 // (4 * expert_total)
    group_rows = row_count * group_count
    sequence_count = seq_lengths.shape[1]
    score_scale = head_dim ** (-0.5)

    replica_count = lax.axis_size("rep")
    replica = lax.axis_index("rep")
    share = width_here // replica_count

    device_of_slot, slot_of_device = ring_indices(device, group_count)

    def reorder(blocks, index):
        return jnp.concatenate(
            [lax.dynamic_slice_in_dim(blocks, index[i], 1, 0) for i in range(group_count)], axis=0
        )

    group_order = reorder(token_order[0].reshape(group_count, row_count), device_of_slot)
    segment, position = row_meta(seq_lengths[0], group_order.reshape(group_rows))
    segment_own = segment[:row_count]
    valid_own = (segment_own < sequence_count).astype(wide_type)[:, None]
    valid_all = (segment < sequence_count).astype(wide_type)[:, None]

    expert_ids = jnp.arange(expert_total, dtype=jnp.int32)
    route_code = jnp.zeros((row_count, expert_total), jnp.int32)
    for column in range(top_count):
        hit = routes[:, column, None] == expert_ids[None, :]
        kept = (slot_index[:, column, None] < capacity).astype(jnp.int32)
        route_code = route_code + jnp.where(hit, 1 + kept, 0)
    small_sent = jnp.concatenate([route_code.astype(low_type), router_weight], axis=0)

    projections = (
        jnp.stack(
            [
                lax.dynamic_slice_in_dim(piece, replica * share, share, 0).reshape(
                    share, group_count, heads_here, head_dim
                )
                for piece in (query_weight, key_weight, value_weight)
            ],
            axis=3,
        )
        .reshape(share, group_count, 3 * width_here)
        .transpose(1, 0, 2)
    )
    scatter_order = rep_distances()
    gather_order = scatter_order[::-1]
    swapped = swap_all(projections)
    head_weight = (
        rep_gather(swapped[None], gather_order)
        .transpose(1, 0, 2, 3)
        .reshape(model_width, 3 * width_here)
    )
    tokens_late, output_late, _ = tie(tokens, output_weight, swapped)
    token_ring = RingGather(tokens_late)
    token_ring.start()
    small_flat = after(small_sent.reshape(-1, head_dim), token_ring.received)
    small_all = swap_all(
        jnp.broadcast_to(small_flat[None], (group_count,) + small_flat.shape)
    ).reshape(group_count, row_count + width_here, expert_total)
    code_all = reorder(small_all[:, :row_count], device_of_slot).reshape(
        group_rows, expert_total
    )
    full_router = small_all[:, row_count:].reshape(model_width, expert_total)
    chunks = 2
    chunk_rows = group_rows // chunks
    blocks_here = group_count // chunks

    def chunk_of(array, chunk):
        return array[chunk * chunk_rows : (chunk + 1) * chunk_rows]

    def slot_rows(array):
        return lambda slot: array[slot * row_count : (slot + 1) * row_count]

    def reorder_rows(rows, index):
        return reorder(
            rows.reshape(group_count, row_count, rows.shape[1]), index
        ).reshape(rows.shape)

    column_share = model_width // replica_count
    output_share = gather_rows(
        lax.dynamic_slice_in_dim(output_late, replica * column_share, column_share, 1)
    )
    token_ring.finish()
    for step in range(1, group_count // 2):
        if step == group_count // 2 - 1:
            token_ring.sent = (after(token_ring.sent[0], output_share), token_ring.sent[1])
        token_ring.start()
        token_ring.finish()
    cosine, sine_part = rope_tables(after(position, token_ring.blocks[1]), head_dim)

    hidden_here = down_weight.shape[1]
    flat_down = down_weight.reshape(experts_here * hidden_here, model_width)

    allowed = segment[:, None] == segment[None, :]
    far = replica_count // 2
    steps = group_count // 2
    part_rows = model_width // steps
    far_parts = [
        Exchange(output_share[i * part_rows : (i + 1) * part_rows], far) for i in range(steps)
    ]

    def head_columns(values, block, head):
        start = (3 * head + block) * head_dim
        return values[:, start : start + head_dim]

    def project(weight, *blocks):
        token_all = jnp.concatenate(blocks, axis=0)
        token_wide = token_all.astype(wide_type)
        first_all = (token_wide * inverse_rms(token_wide) * prenorm_gain).astype(low_type)
        return token_all, first_all, mm(first_all, weight, 1, 0)

    def attend(head, raw):
        turned = []
        for block, gain in ((0, querynorm_gain), (1, keynorm_gain)):
            part = head_columns(raw, block, head)
            normed = part * inverse_rms(part) * gain
            turned.append((normed * cosine + turn_half(normed) * sine_part).astype(low_type))
        value_low = head_columns(raw, 2, head).astype(low_type)
        scores = jnp.where(allowed, mm(*turned, 1, 1) * score_scale, masked_value)
        top_score = jnp.max(scores, axis=-1, keepdims=True)
        powers = jnp.exp(scores - top_score)
        log_total = top_score + jnp.log(jnp.sum(powers, axis=-1, keepdims=True))
        weights_low = jnp.exp(scores - log_total).astype(low_type)
        return (*turned, value_low, log_total, mm(weights_low, value_low, 1, 0).astype(low_type))

    cot_ring = RingGather(after(cotangent, token_ring.received))
    token_all, first_all, raw = window(
        [cot_ring, far_parts[0]], project, head_weight, *token_ring.blocks
    )
    heads = []
    for head in range(heads_here):
        heads.append(
            window(
                [cot_ring, far_parts[1 + head]],
                lambda raw, head=head: attend(head, raw),
                raw,
            )
        )

    def order_work(*mixed):
        mixed_low = jnp.concatenate(mixed, axis=1)
        return (
            mixed_low,
            reorder_rows(mixed_low, slot_of_device),
            segment[:, None],
            segment[None, :],
            jnp.stack([querynorm_gain, keynorm_gain]),
            jnp.stack(device_of_slot),
        )

    mixed_low, mixed_ordered, segment_column, segment_line, norm_gains, slot_order = window(
        [cot_ring, *far_parts[1 + heads_here :]], order_work, *[head[4] for head in heads]
    )
    cot_all = jnp.concatenate(cot_ring.blocks, axis=0)
    output_pieces = {
        0: output_share,
        far: jnp.concatenate([part.received for part in far_parts], axis=0),
    }
    for distance in gather_order[1:]:
        for j in list(output_pieces):
            output_pieces[j ^ distance] = rep_exchange(output_pieces[j], distance)
    mixed_own = (
        swap_all(mixed_ordered.reshape(group_count, row_count, width_here))
        .transpose(1, 0, 2)
        .reshape(row_count, model_width)
    )
    attention = jnp.zeros((row_count, model_width), wide_type)
    for j, piece in output_pieces.items():
        attention = lax.dynamic_update_slice_in_dim(
            attention, mm(mixed_own, piece, 1, 0), (replica ^ j) * column_share, 1
        )
    residual = tokens.astype(wide_type) + attention
    inverse_two = inverse_rms(residual)
    second_input = (residual * inverse_two * postnorm_gain).astype(low_type)

    def gate_table(rows, code):
        logits = mm(rows, full_router, 1, 0)
        shifted = jnp.where(code > 0, logits, masked_value)
        powers = jnp.exp(shifted - jnp.max(shifted, axis=1, keepdims=True))
        return powers / jnp.sum(powers, axis=1, keepdims=True)

    kept_all = jnp.where(code_all > 1, valid_all, 0.0)
    kept_here = lax.dynamic_slice_in_dim(kept_all, device * experts_here, experts_here, 1)

    def stream_of(cot_part):
        return mm(cot_part, flat_down, 1, 1)

    def expert_chunk(chunk, rows, stream, *earlier):
        gates = gate_table(rows, chunk_of(code_all, chunk)) * chunk_of(kept_all, chunk)
        gates_here = lax.dynamic_slice_in_dim(gates, device * experts_here, experts_here, 1)
        return expert_pass(
            rows, gate_weight, up_weight, stream, gates_here, chunk, chunks, earlier
        )

    second_ring = RingGather(second_input)
    stream_first = window([second_ring], lambda part: stream_of(part), chunk_of(cot_all, 0))
    stream_last = window([second_ring], lambda part: stream_of(part), chunk_of(cot_all, 1))
    rows_first = jnp.concatenate(second_ring.blocks[:blocks_here], axis=0)
    *earlier, pair_first = window(
        [second_ring],
        lambda rows, stream: expert_chunk(0, rows, stream),
        rows_first,
        stream_first,
    )
    window([second_ring], lambda: ())
    rows_last = jnp.concatenate(second_ring.blocks[blocks_here:], axis=0)
    inner_all, gback_all, uback_all, pair_last = expert_chunk(
        1, rows_last, stream_last, *earlier
    )
    second_all = jnp.concatenate([rows_first, rows_last], axis=0)
    back_last = expert_back(gback_all, uback_all, gate_weight, up_weight, 1, chunks)
    back_parts = {1: back_last}

    def back_block(slot):
        start = (slot % blocks_here) * row_count
        return back_parts[slot // blocks_here][start : start + row_count]

    def grad_of(left, right):
        return mm(left, right, 0, 0).astype(low_type)

    pair_lanes = jnp.concatenate([pair_first, pair_last], axis=1)
    pair_sent = (kept_here * jnp.sum(pair_lanes, axis=2).transpose(1, 0)).reshape(
        group_count, row_count, experts_here
    )
    code_own = route_code
    gates_own = gate_table(second_input, code_own)

    back_ring = RingSum(back_block, row_count)

    def mixture_work(inner, pair):
        return (
            mm(inner, flat_down, 1, 0).astype(low_type),
            swap_all(reorder(pair, slot_of_device)),
        )

    mixture_part, pair_grad = window([back_ring], mixture_work, inner_all, pair_sent)
    mixture_ring = RingSum(slot_rows(mixture_part), row_count)

    def back_work(gback, uback):
        back_parts[0] = expert_back(gback, uback, gate_weight, up_weight, 0, chunks)
        return back_parts[0]

    back_parts[0] = window([back_ring, mixture_ring], back_work, gback_all, uback_all)

    def down_work(inner, pair):
        pair_grad = pair.transpose(1, 0, 2).reshape(row_count, expert_total)
        chosen_grad = gates_own * (
            pair_grad - jnp.sum(gates_own * pair_grad, axis=1, keepdims=True)
        )
        logits_grad = jnp.where(code_own > 0, chosen_grad, 0.0).astype(low_type)
        router_back = mm(logits_grad, full_router, 1, 1)
        router_part = mm(second_input, logits_grad, 0, 0)
        return grad_of(inner, cot_all), router_back, router_part

    down_part, router_back, router_part = window(
        [back_ring, mixture_ring], down_work, inner_all, pair_grad
    )
    gate_part = window(
        [back_ring, mixture_ring], lambda gback: grad_of(second_all, gback), gback_all
    )
    second_scattered = back_ring.total()
    second_grad = router_back + second_scattered
    upstream = valid_own * cotangent.astype(wide_type)
    def residual_work(second_grad):
        post_back, postnorm_part = norm_backward(
            residual, inverse_two, postnorm_gain, second_grad
        )
        residual_grad = upstream + post_back
        attention_low = residual_grad.astype(low_type)
        mixed_grad_own = jnp.zeros((row_count, model_width), wide_type)
        for j, piece in output_pieces.items():
            mixed_grad_own = mixed_grad_own + mm(
                lax.dynamic_slice_in_dim(
                    attention_low, (replica ^ j) * column_share, column_share, 1
                ),
                piece,
                1,
                1,
            )
        swap_sent = (
            mixed_grad_own.astype(low_type)
            .reshape(row_count, group_count, width_here)
            .transpose(1, 0, 2)
        )
        return swap_sent, residual_grad, attention_low, jnp.sum(postnorm_part, axis=0)

    swap_sent, residual_grad, attention_low, postnorm_part = window(
        [mixture_ring], residual_work, second_grad
    )
    class Swap(Exchange):
        def start(self):
            self.received = swap_all(self.sent)

    swap = Swap(swap_sent, 0)
    attention_gather = RingGather(attention_low)
    up_part = window(
        [swap, attention_gather],
        lambda uback: grad_of(second_all, uback),
        uback_all,
    )
    mixed_grad = swap.received

    sent, gain_parts = (), 0.0
    for head in range(heads_here):

        def head_work(grads, *earlier, head=head):
            return tuple(
                attention_back(
                    head,
                    heads[head][:4],
                    grads,
                    slot_order,
                    segment_column,
                    segment_line,
                    raw,
                    norm_gains,
                    (cosine, sine_part),
                    earlier,
                )
            )

        *sent, gain_part = window([attention_gather], head_work, mixed_grad, *sent)
        gain_parts = gain_parts + gain_part
    (sent,) = sent
    querynorm_part, keynorm_part = gain_parts[0], gain_parts[1]
    down_sum = lax.psum_scatter(
        down_part.reshape(experts_here, hidden_here, model_width),
        "rep",
        scatter_dimension=1,
        tiled=True,
    )
    sent, down_sum = tie(sent, down_sum)

    def first_work(sent, head):
        first_part = mm(sent, head_weight, 1, 1)
        token_wide = token_all.astype(wide_type)
        prenorm_part = jnp.sum(first_part * token_wide * inverse_rms(token_wide), axis=0)
        return first_part.astype(low_type), prenorm_part, rep_scatter(head, 1, scatter_order[:1])

    head_part = window([attention_gather], grad_of, first_all, sent)
    while attention_gather.step < group_count // 2:
        window([attention_gather], lambda: ())
    first_low, prenorm_part, head_part = window(
        [],
        first_work,
        sent,
        head_part.reshape(group_count, replica_count, share, 3 * width_here),
    )

    def small_swap(parts):
        return swap_all(
            jnp.concatenate([part.reshape(group_count, -1) for part in parts], axis=1)
        )

    def small_pieces(swapped, parts):
        total = rep_sum(jnp.sum(swapped, axis=0))
        pieces, start = [], 0
        for part in parts:
            size = part.size // group_count
            pieces.append(total[start : start + size])
            start += size
        return pieces

    first_ring = RingSum(slot_rows(first_low), row_count)
    small_parts = [router_part, postnorm_part, prenorm_part, querynorm_part, keynorm_part]
    head_part = rep_scatter(head_part, 1, scatter_order[1:])
    output_part = window(
        [first_ring],
        lambda mixed, *blocks: block_product(mixed, blocks),
        mixed_low,
        *attention_gather.blocks,
    )
    gate_sum = lax.psum_scatter(gate_part, "rep", scatter_dimension=0, tiled=True)
    up_sum = lax.psum_scatter(up_part, "rep", scatter_dimension=0, tiled=True)
    def split_experts(total):
        return jnp.stack(
            [
                total[:, e * hidden_here : (e + 1) * hidden_here].astype(wide_type)
                for e in range(experts_here)
            ]
        )

    (small_swapped, output_part, down_total), head_part = window(
        [first_ring],
        lambda output, down, *small: (
            small_swap(small),
            rep_scatter(output, 0, scatter_order[:1]),
            down.astype(wide_type),
        ),
        output_part.reshape(replica_count, share, model_width),
        down_sum,
        *small_parts,
        waits=(head_part,),
    )
    head_rows = swap_all(head_part.reshape(group_count, share, 3 * width_here))
    def layer_work(own, *sums):
        mixture = sum((part.astype(wide_type) for part in sums), own.astype(wide_type))
        return (valid_own * (residual + mixture)).astype(low_type)

    (output_part, small_sums, gate_total, layer_out), head_rows = window(
        [first_ring],
        lambda output, small, total, sums: (
            rep_scatter(output, 0, scatter_order[1:]),
            small_pieces(small, small_parts),
            split_experts(total),
            layer_work(*sums),
        ),
        output_part,
        small_swapped,
        gate_sum,
        (mixture_part[:row_count], *mixture_ring.sent),
        waits=(head_rows,),
    )
    head_rows = rep_gather(
        head_rows.reshape(group_count, share, heads_here, 3, head_dim)
        .transpose(3, 1, 0, 2, 4)
        .reshape(1, 3, share, model_width),
        gather_order[:-1],
    )
    output_rows, head_rows = window(
        [first_ring],
        lambda output: rep_gather(output, gather_order[:-1]),
        output_part,
        waits=(head_rows,),
    )
    head_rows = rep_gather(head_rows, gather_order[-1:])
    output_rows = rep_gather(output_rows, gather_order[-1:])
    first_grad = first_ring.total()
    query_grad, key_grad, value_grad = (
        head_rows[:, block].reshape(width_here, model_width).astype(wide_type)
        for block in range(3)
    )
    output_grad = output_rows.reshape(width_here, model_width).astype(wide_type)
    router_grad, postnorm_grad, prenorm_grad, querynorm_grad, keynorm_grad = small_sums
    router_grad = router_grad.reshape(width_here, expert_total)

    token_own = tokens.astype(wide_type)
    inverse_one = inverse_rms(token_own)
    pre_back, _ = norm_backward(token_own, inverse_one, prenorm_gain, first_grad)
    token_grad = residual_grad + pre_back

    up_total = split_experts(up_sum)
    return (
        layer_out,
        token_grad,
        query_grad,
        key_grad,
        value_grad,
        output_grad,
        router_grad,
        prenorm_grad,
        querynorm_grad,
        keynorm_grad,
        postnorm_grad,
        gate_total,
        up_total,
        down_total,
    )


def solution(mesh):
    in_specs = (
        P(("rep", "ep"), None),
        P(("rep", "ep"), None),
        P("rep", None),
        P("rep", None),
        P(("rep", "ep"), None),
        P(("rep", "ep"), None),
        P("ep", None),
        P("ep", None),
        P("ep", None),
        P("ep", None),
        P("ep", None),
        P(),
        P(),
        P(),
        P(),
        P("ep", None, None),
        P("ep", None, None),
        P("ep", None, None),
    )
    out_specs = (
        P(("rep", "ep"), None),
        P(("rep", "ep"), None),
        P("ep", None),
        P("ep", None),
        P("ep", None),
        P("ep", None),
        P("ep", None),
        P("ep"),
        P("ep"),
        P("ep"),
        P("ep"),
        P("ep", "rep", None),
        P("ep", "rep", None),
        P("ep", "rep", None),
    )
    return jax.shard_map(body, mesh=mesh, in_specs=in_specs, out_specs=out_specs, check_vma=False)
```
